128 devices in a mesh: row: 2 (over x_lo), col: 2 (over x_hi), dp: 32 (over y, z, core).
Axes of the slice: x: 4 (x_hi: 2, x_lo: 2; x = x_hi * 2 + x_lo), y: 4, z: 4, core: 2. Of those that a mesh axis runs over, the one named last changes fastest.
Arguments:
- features: bfloat16 [32, 48, 48, 1024], P('dp', 'row', 'col'), may hold values from -6 to 6
- cotangent: bfloat16 [32, 48, 48, 256], P('dp', 'row', 'col'), may hold values from -0.09375 to 0.09375
- w_point: bfloat16 [1024, 256], replicated, may hold values from -0.1875 to 0.1875
- w_rate_a: bfloat16 [3, 3, 1024, 256], replicated, may hold values from -0.0625 to 0.0625
- w_rate_b: bfloat16 [3, 3, 1024, 256], replicated, may hold values from -0.0625 to 0.0625
- w_rate_c: bfloat16 [3, 3, 1024, 256], replicated, may hold values from -0.0625 to 0.0625
- w_proj: bfloat16 [1024, 256], replicated, may hold values from -0.1875 to 0.1875
- bucket_slot: int32 [176], replicated, may hold values from 0 to 191, as said below
Outputs:
- owned_grads: float32 [192, 16384], P('dp', ('row', 'col'))
The draws below stay inside these ranges and needn't reach their ends.
Inputs may be any that keep to these rules, and one draw needn't show every extreme that they name: Distinct slot numbers, one for each of the 176 slices; slice s belongs to data replica bucket_slot[s] // 6. In every draw all 6 slots of some replica are taken. Rows of owned_grads that no slice names are zero.
All inputs are finite; a program needn't handle non-finite values.
Results may differ from the reference program's by a relative error of at most 0.0043.
Values may be sent and summed in bfloat16 or wider, within the bound.
No kernel may reach another device: no remote copies, remote signals or barrier semaphores. Data moves between devices by JAX's collectives and lax.ppermute only.
A program may use at most 192 MiB of HBM per device.

```python
import jax
import jax.numpy as jnp
from jax import lax

CIN = 1024
CO = 256
CAT = 1024
RATE_A = 6
RATE_B = 12
RATE_C = 18
H = 48
W = 48
SROWS = 64
NSLICE = 176
CAP = 6
SLOTS = 192
N_DP = 32


def draw_bucket_slot(key, part):
    key_owner = jax.random.fold_in(key, 11)
    key_score = jax.random.fold_in(key, 12)
    key_order = jax.random.fold_in(key, 13)
    full_owner = jax.random.randint(key_owner, (), 0, SLOTS // CAP)
    slot_ids = jnp.arange(SLOTS, dtype=jnp.int32)
    owners = slot_ids // CAP
    score = jax.random.randint(key_score, (SLOTS,), 0, 1 << 20)
    score = jnp.where(owners == full_owner, 1 << 21, score) * SLOTS + slot_ids
    unused, chosen = lax.top_k(score, NSLICE)
    order = jax.random.permutation(key_order, NSLICE)
    return chosen[order].astype(jnp.int32)


def block_scale(key, dims, cuts, least, top_value):
    factor_of = 1.0
    for axis_at, shards_of in cuts:
        heights = jax.random.uniform(jax.random.fold_in(jax.random.fold_in(key, 6), axis_at), (shards_of,), jnp.float32, least / len(cuts), top_value / len(cuts))
        factor_of = factor_of * jnp.repeat(jnp.exp(heights), dims[axis_at] // shards_of).reshape((-1,) + (1,) * (len(dims) - 1 - axis_at))
    return factor_of


def bell_draw(rng, extent, spread, reach, cuts=(), held_as=jnp.bfloat16):
    array = jax.random.normal(rng, extent, jnp.float32) * spread
    if len(cuts) > 0:
        array = block_scale(rng, extent, cuts, -0.22, 0.18) * array
    return jnp.clip(array, min=-reach, max=reach).astype(held_as)


def setup_inputs(seed: int = 0) -> dict:
    key_list = jax.random.split(jax.random.key(seed), 9)
    features = bell_draw(key_list[0], (N_DP, H, W, CIN), 1.0, 6.0, ((0, 32), (1, 2), (2, 2)))
    cotangent = bell_draw(key_list[1], (N_DP, H, W, CO), 0.006, 0.09375, ((0, 32), (1, 2), (2, 2)))
    w_point = bell_draw(key_list[2], (CIN, CO), CIN ** -0.5, 0.1875)
    w_rate_a = bell_draw(key_list[3], (3, 3, CIN, CO), (9 * CIN) ** -0.5, 0.0625)
    w_rate_b = bell_draw(key_list[4], (3, 3, CIN, CO), (9 * CIN) ** -0.5, 0.0625)
    w_rate_c = bell_draw(key_list[5], (3, 3, CIN, CO), (9 * CIN) ** -0.5, 0.0625)
    w_proj = bell_draw(key_list[6], (CAT, CO), CAT ** -0.5, 0.1875)
    bucket_slot = draw_bucket_slot(jax.random.fold_in(key_list[8], 71), 0)
    return dict(features=features, cotangent=cotangent, w_point=w_point, w_rate_a=w_rate_a, w_rate_b=w_rate_b, w_rate_c=w_rate_c, w_proj=w_proj, bucket_slot=bucket_slot)


def silu_slope(value):
    sig = jax.nn.sigmoid(value)
    return sig * (1.0 + value * (1.0 - sig))


def contract_pixels(left, right):
    return lax.dot_general(left, right, (((0,), (0,)), ((), ())), preferred_element_type=jnp.float32)


def image_grads(image, upstream, w_point, kernels, w_proj):
    rows_img, cols_img, chans = image.shape
    pixels = rows_img * cols_img
    width = RATE_C
    padded = jnp.pad(image, ((width, width), (width, width), (0, 0)))

    def window(rate, above, across):
        top = width + above * rate
        left = width + across * rate
        return padded[top:top + rows_img, left:left + cols_img].reshape(pixels, chans)

    rates = (RATE_A, RATE_B, RATE_C)
    centre = window(0, 0, 0)
    pre_list = [jnp.dot(centre, w_point, preferred_element_type=jnp.float32)]
    for rate, kernel in zip(rates, kernels):
        total = jnp.zeros((pixels, CO), jnp.float32)
        for above in range(3):
            for across in range(3):
                total = total + jnp.dot(window(rate, above - 1, across - 1), kernel[above, across], preferred_element_type=jnp.float32)
        pre_list.append(total)
    joined = jnp.concatenate([jax.nn.silu(pre) for pre in pre_list], 1).astype(jnp.bfloat16)
    proj_pre = jnp.dot(joined, w_proj, preferred_element_type=jnp.float32)
    g_proj = (upstream.reshape(pixels, CO).astype(jnp.float32) * silu_slope(proj_pre)).astype(jnp.bfloat16)
    pieces = [contract_pixels(joined, g_proj)]
    d_joined = lax.dot_general(g_proj, w_proj, (((1,), (1,)), ((), ())), preferred_element_type=jnp.float32)
    for index in (0, 3):
        pre = pre_list[index]
        d_pre = (d_joined[:, index * CO:(index + 1) * CO] * silu_slope(pre)).astype(jnp.bfloat16)
        if index == 0:
            pieces.append(contract_pixels(centre, d_pre))
        else:
            for above in range(3):
                for across in range(3):
                    pieces.append(contract_pixels(window(RATE_C, above - 1, across - 1), d_pre))
    return jnp.concatenate(pieces, 0)


def reference(features, cotangent, w_point, w_rate_a, w_rate_b, w_rate_c, w_proj, bucket_slot):
    kernels = (w_rate_a, w_rate_b, w_rate_c)

    def add_image(total, pair):
        return total + image_grads(pair[0], pair[1], w_point, kernels, w_proj), None

    start = jnp.zeros((CAT + 10 * CIN, CO), jnp.float32)
    total, unused = lax.scan(add_image, start, (features, cotangent))
    slices = total.reshape(NSLICE, SROWS * CO)
    return jnp.zeros((SLOTS, SROWS * CO), jnp.float32).at[bucket_slot].set(slices)
```

```python
import jax
import jax.numpy as jnp
from jax import lax
from jax.experimental import pallas as pl
from jax.experimental.pallas import tpu as pltpu
from jax.sharding import Mesh
from jax.sharding import PartitionSpec as P

RATE_A = 6
RATE_B = 12
RATE_C = 18
SROWS = 64
DP = ("dp_0", "dp_1", "dp_2")


BF = jnp.bfloat16
F32 = jnp.float32
VMEM_LIMIT = 56 * 1024 * 1024


def flip(x, mask):
    if mask == 1:
        return lax.ppermute(x, "col", [(0, 1), (1, 0)])
    if mask == 2:
        return lax.ppermute(x, "row", [(0, 1), (1, 0)])
    return lax.ppermute(x, ("row", "col"), [(0, 3), (3, 0), (1, 2), (2, 1)])


def smem():
    return pl.BlockSpec(memory_space=pltpu.SMEM)


def vmem():
    return pl.BlockSpec(memory_space=pltpu.VMEM)


def call(body, outs, n_smem, n_vmem, flops, nbytes, scratch=(), name=None):
    return pl.pallas_call(
        body,
        out_shape=outs,
        in_specs=[smem()] * n_smem + [vmem()] * n_vmem,
        out_specs=jax.tree.map(lambda _: vmem(), outs),
        scratch_shapes=list(scratch),
        compiler_params=pltpu.CompilerParams(vmem_limit_bytes=VMEM_LIMIT),
        cost_estimate=pl.CostEstimate(flops=flops, bytes_accessed=nbytes, transcendentals=0),
        name=name,
    )


def select_channels(pos_ref, x_ref, *o_refs):
    chans = x_ref.shape[1]
    width = o_refs[0].shape[1]
    source = lax.broadcasted_iota(jnp.int32, (chans, width), 0)
    col = lax.broadcasted_iota(jnp.int32, (chans, width), 1)
    wanted = 64 * (col // 16) + col % 16
    for k, o_ref in enumerate(o_refs):
        c = jnp.bitwise_xor(pos_ref[0], k)
        pick = (source == wanted + 16 * c).astype(F32).astype(BF)
        o_ref[...] = jnp.dot(x_ref[...], pick, preferred_element_type=F32).astype(BF)


def turn_pixels(pos_ref, x0, x1, x2, x3, o_ref, held):
    pixels, width = x0.shape
    for k, x in enumerate((x0, x1, x2, x3)):
        s = jnp.bitwise_xor(pos_ref[0], k)
        held[s % 2, pl.ds((s // 2) * pixels, pixels), :] = x[...]
    eye = (
        lax.broadcasted_iota(jnp.int32, (width, width), 0)
        == lax.broadcasted_iota(jnp.int32, (width, width), 1)
    ).astype(F32).astype(BF)
    for g in range(2):
        o_ref[g] = lax.dot_general(
            eye, held[g], (((1,), (1,)), ((), ())), preferred_element_type=F32
        ).astype(BF)


def roll_cols(x, shift):
    return jnp.concatenate([x[:, x.shape[1] - shift :], x[:, : x.shape[1] - shift]], axis=1)


def tap_grads(pos_ref, place_ref, d0, d1, d2, d3, xt_ref, gp_ref, keep_ref, send_ref, held, padded, buf):
    side = RATE_C
    pixels, width = d0.shape
    cols = 24
    rows = pixels // cols
    for k, d in enumerate((d0, d1, d2, d3)):
        s = jnp.bitwise_xor(pos_ref[0], k)
        held[s % 2, pl.ds((s // 2) * pixels, pixels), :] = d[...]
    buf[...] = jnp.zeros_like(buf)
    tall = 2 * pixels
    lead = side * cols
    zeros = jnp.zeros((2, lead, width), BF)
    halves = [held[g].astype(F32).reshape(2 * rows, cols, width) for g in range(2)]
    at = lax.broadcasted_iota(jnp.int32, (2 * rows, cols, width), 1)
    rest = cols - side
    for across in (-1, 0, 1):
        padded[:, pl.ds(0, lead), :] = zeros
        padded[:, pl.ds(lead + tall, lead), :] = zeros
        if across == 0:
            shifted = halves
        elif across == 1:
            rolled = [roll_cols(h, side) for h in halves]
            shifted = [
                jnp.where(at >= side, rolled[0], 0.0),
                jnp.where(at < side, rolled[0], rolled[1]),
            ]
        else:
            rolled = [roll_cols(h, rest) for h in halves]
            shifted = [
                jnp.where(at < rest, rolled[0], rolled[1]),
                jnp.where(at < rest, rolled[1], 0.0),
            ]
        for g in range(2):
            padded[g, pl.ds(lead, tall), :] = shifted[g].reshape(tall, width).astype(BF)
        for above in (-1, 0, 1):
            first, last = {-1: (0, 32), 0: (0, 48), 1: (16, 48)}[above]
            base = first - side * above + side
            total = None
            for g in range(2):
                part = jnp.dot(
                    xt_ref[g, :, first * cols : last * cols],
                    padded[g, base * cols : (base + last - first) * cols, :],
                    preferred_element_type=F32,
                )
                total = part if total is None else total + part
            tap = 3 * (above + 1) + across + 1
            groups = total.reshape(width // 16, 16, width)
            for m in range(width // 16):
                buf[place_ref[32 + 16 * tap + m]] = groups[m]
    for n in range(gp_ref.shape[0]):
        buf[place_ref[pos_ref[1] + n]] = gp_ref[n]
    half = buf.shape[0] // 2
    keep_ref[...] = buf[:half]
    send_ref[...] = buf[half:].astype(BF)


def exchange_sum(blocks, axis, dtype):
    count = lax.axis_size(axis)
    me = lax.axis_index(axis)
    total = lax.dynamic_index_in_dim(blocks, me, 0, keepdims=False)
    for step in range(1, count):
        out = lax.dynamic_index_in_dim(blocks, (me + step) % count, 0, keepdims=False).astype(dtype)
        got = lax.ppermute(out, axis, [(i, (i + step) % count) for i in range(count)])
        total = total + got.astype(F32)
    return total


def exchange_sum_image(blocks, me, dtype):
    total = lax.dynamic_index_in_dim(blocks, me, 0, keepdims=False)
    for mask in (1, 2, 3):
        out = lax.dynamic_index_in_dim(blocks, jnp.bitwise_xor(me, mask), 0, keepdims=False)
        total = total + flip(out.astype(dtype), mask).astype(F32)
    return total


def swap_core(x):
    return lax.ppermute(x, "dp_2", [(0, 1), (1, 0)])


def share_channels(pos, centre):
    pixels, chans = centre.shape
    width = chans // 4
    block = jax.ShapeDtypeStruct((pixels, width), BF)
    picked = call(select_channels, [block] * 4, 1, 1, 2 * pixels * chans * chans, 4 * pixels * chans, name="pick")(
        pos, centre
    )
    got = [picked[0]] + [flip(picked[k], k) for k in (1, 2, 3)]
    return call(
        turn_pixels,
        jax.ShapeDtypeStruct((2, width, 2 * pixels), BF),
        1,
        4,
        2 * pixels * chans * width,
        4 * pixels * chans,
        [pltpu.VMEM((2, 2 * pixels, width), BF)],
        name="turn",
    )(pos, *got)


def reduce_pair(grad_proj, grad_point, me):
    core = lax.axis_index("dp_2")
    both = jnp.stack([grad_proj, grad_point])
    kept = lax.dynamic_index_in_dim(both, core, 0, keepdims=False)
    sent = lax.dynamic_index_in_dim(both, 1 - core, 0, keepdims=False).astype(BF)
    kept = kept + swap_core(sent).astype(F32)
    ys = lax.axis_size("dp_0")
    width = kept.shape[1]
    mine = exchange_sum(kept.reshape(ys, -1, width), "dp_0", BF)
    blocks = jnp.moveaxis(mine.reshape(-1, 4, 16, width), 1, 0)
    return exchange_sum_image(blocks, me, BF)


def place_slots(bucket_slot, core, slot_count):
    replicas = lax.axis_size(DP)
    capacity = slot_count // replicas
    owner = bucket_slot // capacity
    other = jnp.bitwise_xor(owner % 2, core)
    return other * (slot_count // 2) + (owner // 2) * capacity + bucket_slot % capacity


def reduce_slots(pos, place, deltas, turned, pair, slot_count):
    pixels, width = deltas[0].shape
    half = slot_count // 2
    kept, sent = call(
        tap_grads,
        [
            jax.ShapeDtypeStruct((half, 16, width), F32),
            jax.ShapeDtypeStruct((half, 16, width), BF),
        ],
        2,
        6,
        2 * 7 * 4 * pixels * width * width,
        8 * 1024 * 1024,
        [
            pltpu.VMEM((2, 2 * pixels, width), BF),
            pltpu.VMEM((2, 2 * pixels + 2 * RATE_C * 24, width), BF),
            pltpu.VMEM((slot_count, 16, width), F32),
        ],
        name="taps",
    )(pos, place, *deltas, turned, pair)
    total = kept + swap_core(sent).astype(F32)
    ys, zs = lax.axis_size("dp_0"), lax.axis_size("dp_1")
    total = exchange_sum(total.reshape(ys, half // ys * 16, width), "dp_0", BF)
    total = exchange_sum(total.reshape(zs, half // ys // zs * 16, width), "dp_1", BF)
    return total.reshape(half // ys // zs, 16 * width)


def extended(cells, sides, width):
    for axis, dim in sides:
        count = lax.axis_size(axis)
        ends = count - 1
        head = lax.slice_in_dim(cells, 0, width, axis=dim)
        tail = lax.slice_in_dim(cells, cells.shape[dim] - width, cells.shape[dim], axis=dim)
        cells = jnp.concatenate(
            [
                lax.ppermute(tail, axis, [(i, (i + 1) % count) for i in range(ends)]),
                cells,
                lax.ppermute(head, axis, [((i + 1) % count, i) for i in range(ends)]),
            ],
            axis=dim,
        )
    return cells


def silu_slope(value):
    sig = jax.nn.sigmoid(value)
    return sig * (1.0 + value * (1.0 - sig))


def contract_pixels(left, right):
    return lax.dot_general(
        left, right, (((0,), (0,)), ((), ())), preferred_element_type=jnp.float32
    )


def shards(features, cotangent, w_point, w_rate_a, w_rate_b, w_rate_c, w_proj, bucket_slot):
    image = features[0]
    rows_dev, cols_dev, chans = image.shape
    out_width = w_point.shape[1]
    pixels = rows_dev * cols_dev
    width = RATE_C
    me = 2 * lax.axis_index("row") + lax.axis_index("col")
    core = lax.axis_index("dp_2")
    pos = jnp.stack([me, 16 * core + 4 * lax.axis_index("dp_0")]).astype(jnp.int32)
    replicas = lax.axis_size(DP)
    slot_count = replicas * (bucket_slot.shape[0] // replicas + 1)
    place = place_slots(bucket_slot, core, slot_count)
    turned = share_channels(pos, image.reshape(pixels, chans))
    padded = extended(image, (("row", 0), ("col", 1)), width)

    def window(rate, above, across):
        top = width + above * rate
        left = width + across * rate
        return padded[top : top + rows_dev, left : left + cols_dev].reshape(pixels, chans)

    rates = (RATE_A, RATE_B, RATE_C)
    kernels = (w_rate_a, w_rate_b, w_rate_c)
    centre = window(0, 0, 0)
    pre_list = [jnp.dot(centre, w_point, preferred_element_type=jnp.float32)]
    for rate, kernel in zip(rates, kernels):
        total = jnp.zeros((pixels, out_width), jnp.float32)
        for above in range(3):
            for across in range(3):
                total = total + jnp.dot(
                    window(rate, above - 1, across - 1),
                    kernel[above, across],
                    preferred_element_type=jnp.float32,
                )
        pre_list.append(total)
    joined = jnp.concatenate([jax.nn.silu(pre) for pre in pre_list], 1).astype(jnp.bfloat16)
    proj_pre = jnp.dot(joined, w_proj, preferred_element_type=jnp.float32)
    upstream = cotangent[0].reshape(pixels, out_width).astype(jnp.float32)
    g_proj = (upstream * silu_slope(proj_pre)).astype(jnp.bfloat16)
    grad_proj = contract_pixels(joined, g_proj)
    d_joined = lax.dot_general(
        g_proj, w_proj, (((1,), (1,)), ((), ())), preferred_element_type=jnp.float32
    )
    deltas = [
        (d_joined[:, k * out_width : (k + 1) * out_width] * silu_slope(pre_list[k])).astype(jnp.bfloat16)
        for k in (0, 3)
    ]
    grad_point = contract_pixels(centre, deltas[0])
    shared = [deltas[1]] + [flip(deltas[1], k) for k in (1, 2, 3)]
    pair = reduce_pair(grad_proj, grad_point, me)
    return reduce_slots(pos, place, shared, turned, pair, slot_count)


def solution(mesh):
    torus = Mesh(
        mesh.devices.reshape(mesh.shape["row"], mesh.shape["col"], 4, 4, 2),
        ("row", "col", "dp_0", "dp_1", "dp_2"),
    )
    in_specs = (P(DP, "row", "col", None), P(DP, "row", "col", None), P(), P(), P(), P(), P(), P())
    out_specs = P(DP, ("row", "col"))
    return jax.shard_map(
        shards, mesh=torus, in_specs=in_specs, out_specs=out_specs, check_vma=False
    )
```

```python
import jax
import jax.numpy as jnp
from jax import lax
from jax.experimental import pallas as pl
from jax.experimental.pallas import tpu as pltpu
from jax.sharding import Mesh
from jax.sharding import PartitionSpec as P

RATE_A = 6
RATE_B = 12
RATE_C = 18
DP = ("dp_0", "dp_1", "dp_2")


BF = jnp.bfloat16
F32 = jnp.float32
VMEM_LIMIT = 56 * 1024 * 1024


def flip(x, mask):
    if mask == 1:
        return lax.ppermute(x, "col", [(0, 1), (1, 0)])
    if mask == 2:
        return lax.ppermute(x, "row", [(0, 1), (1, 0)])
    return lax.ppermute(x, ("row", "col"), [(0, 3), (3, 0), (1, 2), (2, 1)])


def smem():
    return pl.BlockSpec(memory_space=pltpu.SMEM)


def vmem():
    return pl.BlockSpec(memory_space=pltpu.VMEM)


def call(body, outs, n_smem, n_vmem, flops, nbytes, scratch=(), name=None):
    return pl.pallas_call(
        body,
        out_shape=outs,
        in_specs=[smem()] * n_smem + [vmem()] * n_vmem,
        out_specs=jax.tree.map(lambda _: vmem(), outs),
        scratch_shapes=list(scratch),
        compiler_params=pltpu.CompilerParams(vmem_limit_bytes=VMEM_LIMIT),
        cost_estimate=pl.CostEstimate(flops=flops, bytes_accessed=nbytes, transcendentals=0),
        name=name,
    )


def select_channels(pos_ref, x_ref, *o_refs):
    chans = x_ref.shape[1]
    width = o_refs[0].shape[1]
    source = lax.broadcasted_iota(jnp.int32, (chans, width), 0)
    col = lax.broadcasted_iota(jnp.int32, (chans, width), 1)
    wanted = 64 * (col // 16) + col % 16
    for k, o_ref in enumerate(o_refs):
        c = jnp.bitwise_xor(pos_ref[0], k)
        pick = (source == wanted + 16 * c).astype(F32).astype(BF)
        o_ref[...] = jnp.dot(x_ref[...], pick, preferred_element_type=F32).astype(BF)


def turn_pixels(pos_ref, x0, x1, x2, x3, o_ref, held):
    pixels, width = x0.shape
    for k, x in enumerate((x0, x1, x2, x3)):
        s = jnp.bitwise_xor(pos_ref[0], k)
        held[s % 2, pl.ds((s // 2) * pixels, pixels), :] = x[...]
    eye = (
        lax.broadcasted_iota(jnp.int32, (width, width), 0)
        == lax.broadcasted_iota(jnp.int32, (width, width), 1)
    ).astype(F32).astype(BF)
    for g in range(2):
        o_ref[g] = lax.dot_general(
            eye, held[g], (((1,), (1,)), ((), ())), preferred_element_type=F32
        ).astype(BF)


def roll_cols(x, shift):
    return jnp.concatenate([x[:, x.shape[1] - shift :], x[:, : x.shape[1] - shift]], axis=1)


def tap_grads(pos_ref, place_ref, d0, d1, d2, d3, xt_ref, gp_ref, keep_ref, send_ref, held, padded, buf):
    side = RATE_C
    pixels, width = d0.shape
    cols = 24
    rows = pixels // cols
    for k, d in enumerate((d0, d1, d2, d3)):
        s = jnp.bitwise_xor(pos_ref[0], k)
        held[s % 2, pl.ds((s // 2) * pixels, pixels), :] = d[...]
    buf[...] = jnp.zeros_like(buf)
    tall = 2 * pixels
    lead = side * cols
    zeros = jnp.zeros((2, lead, width), BF)
    halves = [held[g].astype(F32).reshape(2 * rows, cols, width) for g in range(2)]
    at = lax.broadcasted_iota(jnp.int32, (2 * rows, cols, width), 1)
    rest = cols - side
    for across in (-1, 0, 1):
        padded[:, pl.ds(0, lead), :] = zeros
        padded[:, pl.ds(lead + tall, lead), :] = zeros
        if across == 0:
            shifted = halves
        elif across == 1:
            rolled = [roll_cols(h, side) for h in halves]
            shifted = [
                jnp.where(at >= side, rolled[0], 0.0),
                jnp.where(at < side, rolled[0], rolled[1]),
            ]
        else:
            rolled = [roll_cols(h, rest) for h in halves]
            shifted = [
                jnp.where(at < rest, rolled[0], rolled[1]),
                jnp.where(at < rest, rolled[1], 0.0),
            ]
        for g in range(2):
            padded[g, pl.ds(lead, tall), :] = shifted[g].reshape(tall, width).astype(BF)
        for above in (-1, 0, 1):
            first, last = {-1: (0, 32), 0: (0, 48), 1: (16, 48)}[above]
            base = first - side * above + side
            total = None
            for g in range(2):
                part = jnp.dot(
                    xt_ref[g, :, first * cols : last * cols],
                    padded[g, base * cols : (base + last - first) * cols, :],
                    preferred_element_type=F32,
                )
                total = part if total is None else total + part
            tap = 3 * (above + 1) + across + 1
            groups = total.reshape(width // 16, 16, width)
            for m in range(width // 16):
                buf[place_ref[32 + 16 * tap + m]] = groups[m]
    for n in range(gp_ref.shape[0]):
        buf[place_ref[pos_ref[1] + n]] = gp_ref[n]
    half = buf.shape[0] // 2
    keep_ref[...] = buf[:half]
    send_ref[...] = buf[half:].astype(BF)


def exchange_sum(blocks, axis, dtype):
    count = lax.axis_size(axis)
    me = lax.axis_index(axis)
    total = lax.dynamic_index_in_dim(blocks, me, 0, keepdims=False)
    for step in range(1, count):
        out = lax.dynamic_index_in_dim(blocks, (me + step) % count, 0, keepdims=False).astype(dtype)
        got = lax.ppermute(out, axis, [(i, (i + step) % count) for i in range(count)])
        total = total + got.astype(F32)
    return total


def exchange_sum_image(blocks, me, dtype):
    total = lax.dynamic_index_in_dim(blocks, me, 0, keepdims=False)
    for mask in (1, 2, 3):
        out = lax.dynamic_index_in_dim(blocks, jnp.bitwise_xor(me, mask), 0, keepdims=False)
        total = total + flip(out.astype(dtype), mask).astype(F32)
    return total


def swap_core(x):
    return lax.ppermute(x, "dp_2", [(0, 1), (1, 0)])


def pick(pos, centre):
    pixels, chans = centre.shape
    block = jax.ShapeDtypeStruct((pixels, chans // 4), BF)
    return call(select_channels, [block] * 4, 1, 1, 2 * pixels * chans * chans, 4 * pixels * chans, name="pick")(
        pos, centre
    )


def turn(pos, got):
    pixels, width = got[0].shape
    return call(
        turn_pixels,
        jax.ShapeDtypeStruct((2, width, 2 * pixels), BF),
        1,
        4,
        8 * pixels * width * width,
        16 * pixels * width,
        [pltpu.VMEM((2, 2 * pixels, width), BF)],
        name="turn",
    )(pos, *got)


def reduce_pair(kept, sent, me):
    kept = kept + swap_core(sent).astype(F32)
    ys = lax.axis_size("dp_0")
    width = kept.shape[1]
    mine = exchange_sum(kept.reshape(ys, -1, width), "dp_0", BF)
    blocks = jnp.moveaxis(mine.reshape(-1, 4, 16, width), 1, 0)
    return exchange_sum_image(blocks, me, BF)


def place_slots(bucket_slot, core, slot_count):
    replicas = lax.axis_size(DP)
    capacity = slot_count // replicas
    owner = bucket_slot // capacity
    other = jnp.bitwise_xor(owner % 2, core)
    return other * (slot_count // 2) + (owner // 2) * capacity + bucket_slot % capacity


def reduce_slots(pos, place, deltas, turned, pair, slot_count):
    pixels, width = deltas[0].shape
    half = slot_count // 2
    kept, sent = call(
        tap_grads,
        [
            jax.ShapeDtypeStruct((half, 16, width), F32),
            jax.ShapeDtypeStruct((half, 16, width), BF),
        ],
        2,
        6,
        2 * 7 * 4 * pixels * width * width,
        8 * 1024 * 1024,
        [
            pltpu.VMEM((2, 2 * pixels, width), BF),
            pltpu.VMEM((2, 2 * pixels + 2 * RATE_C * 24, width), BF),
            pltpu.VMEM((slot_count, 16, width), F32),
        ],
        name="taps",
    )(pos, place, *deltas, turned, pair)
    total = kept + swap_core(sent).astype(F32)
    ys, zs = lax.axis_size("dp_0"), lax.axis_size("dp_1")
    total = exchange_sum(total.reshape(ys, half // ys * 16, width), "dp_0", BF)
    total = exchange_sum(total.reshape(zs, half // ys // zs * 16, width), "dp_1", BF)
    return total.reshape(half // ys // zs, 16 * width)


def silu_slope(value):
    sig = jax.nn.sigmoid(value)
    return sig * (1.0 + value * (1.0 - sig))


RATES = (RATE_A, RATE_B, RATE_C)
SIDE = 24


def turned_by(x, shift, far):
    return jnp.where(far == 0, roll_cols(x, shift), roll_cols(x, SIDE - shift))


def rank_of(shape, far):
    at = lax.broadcasted_iota(jnp.int32, shape, 1)
    return jnp.where(far == 0, at, SIDE - 1 - at)


def conv_parts(
    pos_ref, x_ref, wa_ref, wb_ref, wc_ref, wp_ref, pre0_ref, pre_ref, row_ref, col_ref, diag_ref, ext, held
):
    step = pl.program_id(0)
    across = step // 3
    low = pos_ref[2]
    far = pos_ref[3]
    width = x_ref.shape[1] // 4
    whole = SIDE * SIDE

    def blocks(x):
        return x.reshape(x.shape[0] // SIDE, SIDE, width)

    def flat(x):
        return x.reshape(x.shape[0] * SIDE, width)

    def rate_step(index, rate, w_ref):
        lead = rate * SIDE
        inside = (SIDE - rate) * SIDE
        own_at = pl.multiple_of(jnp.where(low == 0, 0, lead), 16)
        out_at = pl.multiple_of(jnp.where(low == 0, lead, 0), 16)
        next_at = pl.multiple_of(jnp.where(low == 0, whole, 0), 16)
        blank_at = pl.multiple_of(jnp.where(low == 0, 0, whole), 16)
        in_from = pl.multiple_of(jnp.where(low == 0, lead, 0), 16)
        in_at = pl.multiple_of(jnp.where(low == 0, 0, 2 * lead), 16)
        out_tap = jnp.where(low == 0, 0, 2)
        in_tap = jnp.where(low == 0, 2, 0)
        ext[pl.ds(blank_at, lead), :] = jnp.zeros((lead, width), F32)
        ext[pl.ds(out_at, whole), :] = jnp.dot(x_ref[...], w_ref[out_tap, 0], preferred_element_type=F32)
        ext[pl.ds(own_at, whole), :] += jnp.dot(x_ref[...], w_ref[1, 0], preferred_element_type=F32)
        ext[pl.ds(in_at, inside), :] += jnp.dot(
            x_ref[pl.ds(in_from, inside), :], w_ref[in_tap, 0], preferred_element_type=F32
        )
        own_rows = pl.ds(own_at, whole)
        next_rows = pl.ds(next_at, lead)
        first = {RATE_C: 0, RATE_B: RATE_C * SIDE, RATE_A: (RATE_C + RATE_B) * SIDE}[rate]
        to_row = slice(first, first + lead)

        @pl.when(across == 0)
        def _():
            pre_ref[index] = ext[own_rows, :]
            held[to_row, :] = ext[next_rows, :]

        @pl.when(across == 1)
        def _():
            own = blocks(ext[own_rows, :])
            ours = turned_by(own, rate, far)
            rank = rank_of(own.shape, far)
            pre_ref[index] += flat(jnp.where(rank >= rate, ours, 0.0))
            below = blocks(ext[next_rows, :])
            theirs = turned_by(below, rate, far)
            place = rank_of(below.shape, far)
            held[to_row, :] += flat(jnp.where(place >= rate, theirs, 0.0))
            if rate == RATE_C:
                col_ref[:whole, :] = flat(jnp.where(rank < rate, ours, 0.0)).astype(BF)
                diag_ref[:lead, :] = flat(jnp.where(place < rate, theirs, 0.0)).astype(BF)
            elif rate == RATE_B:
                half = rate // 2
                part = rank[:rate] < rate
                col_ref[whole:, :] = flat(jnp.where(part, ours[:rate], own[rate:])).astype(BF)
                part = place[:half] < rate
                diag_ref[RATE_C * SIDE :, :] = flat(jnp.where(part, theirs[:half], below[half:])).astype(BF)
            else:
                have = blocks(col_ref[:whole, :].astype(F32))
                col_ref[:whole, :] = flat(jnp.where(rank >= RATE_C, own, have)).astype(BF)
                have = blocks(diag_ref[:lead, :].astype(F32))
                diag_ref[:lead, :] = flat(jnp.where(place >= RATE_C, below, have)).astype(BF)

        @pl.when(across == 2)
        def _():
            own = blocks(ext[own_rows, :])
            rank = rank_of(own.shape, far)
            pre_ref[index] += flat(jnp.where(rank < SIDE - rate, turned_by(own, rate, 1 - far), 0.0))
            below = blocks(ext[next_rows, :])
            place = rank_of(below.shape, far)
            theirs = jnp.where(place < SIDE - rate, turned_by(below, rate, 1 - far), 0.0)
            row_ref[to_row, :] = (held[to_row, :] + flat(theirs)).astype(BF)

    @pl.when(step == 0)
    def _():
        pre0_ref[...] = jnp.dot(x_ref[...], wp_ref[...], preferred_element_type=F32)

    for turn, (index, rate, w_ref) in enumerate(((2, RATE_C, wc_ref), (1, RATE_B, wb_ref), (0, RATE_A, wa_ref))):

        @pl.when(step % 3 == turn)
        def _(index=index, rate=rate, w_ref=w_ref):
            rate_step(index, rate, w_ref)


def convolve(pos, centre, w_rate_a, w_rate_b, w_rate_c, w_point):
    pixels, chans = centre.shape
    width = w_point.shape[1]
    sends = (RATE_A + RATE_B + RATE_C) * SIDE
    corner = pixels

    def taps_spec(turn):
        def at(step, pos_ref):
            across = (step - turn + 2) // 3
            out = jnp.where(pos_ref[3] == 0, 0, 2)
            return (0, jnp.where(across == 0, 1, jnp.where(across == 1, out, 2 - out)), 0, 0)

        return pl.BlockSpec((3, 1, chans, width), at)

    def still(shape):
        return pl.BlockSpec(shape, lambda step, pos_ref: (0,) * len(shape))

    shapes = [
        ((pixels, width), F32),
        ((3, pixels, width), F32),
        ((sends, width), BF),
        ((sends, width), BF),
        ((corner, width), BF),
    ]
    return pl.pallas_call(
        conv_parts,
        out_shape=[jax.ShapeDtypeStruct(*s) for s in shapes],
        grid_spec=pltpu.PrefetchScalarGridSpec(
            num_scalar_prefetch=1,
            grid=(9,),
            in_specs=[
                still((pixels, chans)),
                taps_spec(2),
                taps_spec(1),
                taps_spec(0),
                still((chans, width)),
            ],
            out_specs=[still(s[0]) for s in shapes],
            scratch_shapes=[
                pltpu.VMEM(((SIDE + RATE_C) * SIDE, width), F32),
                pltpu.VMEM((sends, width), F32),
            ],
        ),
        compiler_params=pltpu.CompilerParams(vmem_limit_bytes=VMEM_LIMIT),
        cost_estimate=pl.CostEstimate(
            flops=2 * pixels * chans * width * 25, bytes_accessed=20 * 1024 * 1024, transcendentals=0
        ),
        name="convs",
    )(pos, centre, w_rate_a, w_rate_b, w_rate_c, w_point)


def merge_parts(
    pos_ref, pre0_ref, own_ref, row_ref, col_ref, diag_ref, cot_ref, wp_ref, joined_ref, g_ref, d0_ref, d3_ref, pre
):
    low = pos_ref[2]
    theirs = 1 - pos_ref[3]
    width = pre0_ref.shape[1]
    whole = SIDE * SIDE

    def blocks(x):
        return x.reshape(x.shape[0] // SIDE, SIDE, width)

    def flat(x):
        return x.reshape(x.shape[0] * SIDE, width)

    def rows_of(rate):
        return pl.multiple_of(jnp.where(low == 0, (SIDE - rate) * SIDE, 0), 16)

    pre[...] = own_ref[...]
    first = 0
    for index, rate in ((2, RATE_C), (1, RATE_B), (0, RATE_A)):
        lead = rate * SIDE
        pre[index, pl.ds(rows_of(rate), lead), :] += row_ref[first : first + lead, :].astype(F32)
        first += lead

    part = blocks(col_ref[:whole, :].astype(F32))
    rank = rank_of(part.shape, theirs)
    pre[2] += flat(jnp.where(rank < RATE_C, part, 0.0))
    pre[0] += flat(turned_by(jnp.where(rank >= RATE_C, part, 0.0), RATE_A, theirs))
    part = blocks(col_ref[whole:, :].astype(F32))
    rank = rank_of(part.shape, theirs)
    pre[1, : RATE_B * SIDE, :] += flat(jnp.where(rank < RATE_B, part, 0.0))
    pre[1, RATE_B * SIDE :, :] += flat(roll_cols(jnp.where(rank >= RATE_B, part, 0.0), RATE_B))

    part = blocks(diag_ref[: RATE_C * SIDE, :].astype(F32))
    rank = rank_of(part.shape, theirs)
    pre[2, pl.ds(rows_of(RATE_C), RATE_C * SIDE), :] += flat(jnp.where(rank < RATE_C, part, 0.0))
    few = part[:RATE_A]
    few = turned_by(jnp.where(rank[:RATE_A] >= RATE_C, few, 0.0), RATE_A, theirs)
    pre[0, pl.ds(rows_of(RATE_A), RATE_A * SIDE), :] += flat(few)
    part = blocks(diag_ref[RATE_C * SIDE :, :].astype(F32))
    rank = rank_of(part.shape, theirs)
    half = RATE_B // 2
    at = rows_of(RATE_B)
    pre[1, pl.ds(at, half * SIDE), :] += flat(jnp.where(rank < RATE_B, part, 0.0))
    last = pl.multiple_of(at + half * SIDE, 16)
    pre[1, pl.ds(last, half * SIDE), :] += flat(roll_cols(jnp.where(rank >= RATE_B, part, 0.0), RATE_B))

    slopes = {}
    for k in range(4):
        value = pre0_ref[...] if k == 0 else pre[k - 1]
        sig = jax.nn.sigmoid(value)
        joined_ref[:, k * width : (k + 1) * width] = (value * sig).astype(BF)
        if k in (0, 3):
            slopes[k] = sig * (1.0 + value * (1.0 - sig))
    proj_pre = jnp.dot(joined_ref[...], wp_ref[...], preferred_element_type=F32)
    g_proj = (cot_ref[...].astype(F32) * silu_slope(proj_pre)).astype(BF)
    g_ref[...] = g_proj
    for k, out in ((3, d3_ref), (0, d0_ref)):
        back = lax.dot_general(
            g_proj, wp_ref[k * width : (k + 1) * width, :], (((1,), (1,)), ((), ())), preferred_element_type=F32
        )
        out[...] = (back * slopes[k]).astype(BF)


def merge(pos, pre0, own, row, col, diag, cot, w_proj):
    pixels, width = pre0.shape
    block = jax.ShapeDtypeStruct((pixels, width), BF)
    return call(
        merge_parts,
        [jax.ShapeDtypeStruct((pixels, 4 * width), BF), block, block, block],
        1,
        7,
        2 * pixels * width * width * 6,
        6 * 1024 * 1024,
        [pltpu.VMEM((3, pixels, width), F32)],
        name="merge",
    )(pos, pre0, own, row, col, diag, cot, w_proj)


def pair_grads(pos_ref, joined_ref, g_ref, x_ref, d0_ref, keep_ref, send_ref):
    core = pos_ref[4]
    over = (((0,), (0,)), ((), ()))
    grad_proj = lax.dot_general(joined_ref[...], g_ref[...], over, preferred_element_type=F32)
    grad_point = lax.dot_general(x_ref[...], d0_ref[...], over, preferred_element_type=F32)
    keep_ref[...] = jnp.where(core == 0, grad_proj, grad_point)
    send_ref[...] = jnp.where(core == 0, grad_point, grad_proj).astype(BF)


def shards(features, cotangent, w_point, w_rate_a, w_rate_b, w_rate_c, w_proj, bucket_slot):
    image = features[0]
    rows_dev, cols_dev, chans = image.shape
    pixels = rows_dev * cols_dev
    width = w_point.shape[1]
    row, col, core = (lax.axis_index(n) for n in ("row", "col", "dp_2"))
    me = 2 * row + col
    pos = jnp.stack([me, 16 * core + 4 * lax.axis_index("dp_0"), row, col, core]).astype(jnp.int32)
    replicas = lax.axis_size(DP)
    slot_count = replicas * (bucket_slot.shape[0] // replicas + 1)
    place = place_slots(bucket_slot, core, slot_count)
    centre = image.reshape(pixels, chans)
    picked = pick(pos, centre)
    centre, *picked = lax.optimization_barrier((centre, *picked))
    got = [picked[0]] + [flip(picked[k], k) for k in (1, 2, 3)]
    pre0, own, *parts = convolve(pos, centre, w_rate_a, w_rate_b, w_rate_c, w_point)
    parts, got = lax.optimization_barrier((parts, got))
    to_row, to_col, to_diag = parts
    from_row, from_col, from_diag = flip(to_row, 2), flip(to_col, 1), flip(to_diag, 3)
    turned = turn(pos, got)
    joined, g_proj, delta0, delta3 = merge(
        pos, pre0, own, from_row, from_col, from_diag, cotangent[0].reshape(pixels, width), w_proj
    )
    shared = [delta3] + [flip(delta3, k) for k in (1, 2, 3)]
    block = (4 * width, width)
    kept, sent = call(
        pair_grads,
        [jax.ShapeDtypeStruct(block, F32), jax.ShapeDtypeStruct(block, BF)],
        1,
        4,
        4 * pixels * chans * width,
        4 * 1024 * 1024,
        name="pair",
    )(pos, joined, g_proj, centre, delta0)
    pair = reduce_pair(kept, sent, me)
    return reduce_slots(pos, place, shared, turned, pair, slot_count)


def solution(mesh):
    torus = Mesh(
        mesh.devices.reshape(mesh.shape["row"], mesh.shape["col"], 4, 4, 2),
        ("row", "col", "dp_0", "dp_1", "dp_2"),
    )
    in_specs = (P(DP, "row", "col", None), P(DP, "row", "col", None), P(), P(), P(), P(), P(), P())
    out_specs = P(DP, ("row", "col"))
    return jax.shard_map(
        shards, mesh=torus, in_specs=in_specs, out_specs=out_specs, check_vma=False
    )
```

```python
import jax
import jax.numpy as jnp
from jax import lax
from jax.experimental import pallas as pl
from jax.experimental.pallas import tpu as pltpu
from jax.sharding import Mesh
from jax.sharding import PartitionSpec as P

RATE_A = 6
RATE_B = 12
RATE_C = 18
DP = ("dp_0", "dp_1", "dp_2")


BF = jnp.bfloat16
F32 = jnp.float32
MIB = 1024 * 1024


def flip(x, mask):
    if mask == 1:
        return lax.ppermute(x, "col", [(0, 1), (1, 0)])
    if mask == 2:
        return lax.ppermute(x, "row", [(0, 1), (1, 0)])
    return lax.ppermute(x, ("row", "col"), [(0, 3), (3, 0), (1, 2), (2, 1)])


def smem():
    return pl.BlockSpec(memory_space=pltpu.SMEM)


def vmem():
    return pl.BlockSpec(memory_space=pltpu.VMEM)


def call(body, outs, n_smem, n_vmem, flops, nbytes, limit, scratch=(), name=None, n_any=0):
    return pl.pallas_call(
        body,
        out_shape=outs,
        in_specs=[smem()] * n_smem + [vmem()] * n_vmem + [pl.BlockSpec(memory_space=pltpu.HBM)] * n_any,
        out_specs=jax.tree.map(lambda _: vmem(), outs),
        scratch_shapes=list(scratch),
        compiler_params=pltpu.CompilerParams(vmem_limit_bytes=limit * MIB),
        cost_estimate=pl.CostEstimate(flops=flops, bytes_accessed=nbytes, transcendentals=0),
        name=name,
    )


def select_channels(pos_ref, x_ref, *o_refs):
    chans = x_ref.shape[1]
    width = o_refs[0].shape[1]
    source = lax.broadcasted_iota(jnp.int32, (chans, width), 0)
    col = lax.broadcasted_iota(jnp.int32, (1, width), 1)
    wanted = 64 * (col // 16) + col % 16
    for k, o_ref in enumerate(o_refs):
        c = jnp.bitwise_xor(pos_ref[0], k)
        pick = jnp.where(source == wanted + 16 * c, 1.0, 0.0).astype(BF)
        o_ref[...] = jnp.dot(x_ref[...], pick, preferred_element_type=F32).astype(BF)


def turn_pixels(pos_ref, x0, x1, x2, x3, o_ref, held):
    pixels, width = x0.shape
    for k, x in enumerate((x0, x1, x2, x3)):
        s = jnp.bitwise_xor(pos_ref[0], k)
        held[s % 2, pl.ds((s // 2) * pixels, pixels), :] = x[...]
    eye = (
        lax.broadcasted_iota(jnp.int32, (width, width), 0)
        == lax.broadcasted_iota(jnp.int32, (width, width), 1)
    ).astype(F32).astype(BF)
    for g in range(2):
        o_ref[g] = lax.dot_general(
            eye, held[g], (((1,), (1,)), ((), ())), preferred_element_type=F32
        ).astype(BF)


def roll_cols(x, shift):
    return jnp.concatenate([x[:, x.shape[1] - shift :], x[:, : x.shape[1] - shift]], axis=1)


def tap_grads(pos_ref, place_ref, d0, d1, d2, d3, xt_ref, keep_ref, send_ref, held, padded, buf):
    side = RATE_C
    pixels, width = d0.shape
    cols = 24
    rows = pixels // cols
    for k, d in enumerate((d0, d1, d2, d3)):
        s = jnp.bitwise_xor(pos_ref[0], k)
        held[s % 2, pl.ds((s // 2) * pixels, pixels), :] = d[...]
    buf[...] = jnp.zeros_like(buf)
    tall = 2 * pixels
    lead = side * cols
    zeros = jnp.zeros((2, lead, width), BF)
    halves = [held[g].astype(F32).reshape(2 * rows, cols, width) for g in range(2)]
    at = lax.broadcasted_iota(jnp.int32, (2 * rows, cols, width), 1)
    rest = cols - side
    for across in (-1, 0, 1):
        padded[:, pl.ds(0, lead), :] = zeros
        padded[:, pl.ds(lead + tall, lead), :] = zeros
        if across == 0:
            shifted = halves
        elif across == 1:
            rolled = [roll_cols(h, side) for h in halves]
            shifted = [
                jnp.where(at >= side, rolled[0], 0.0),
                jnp.where(at < side, rolled[0], rolled[1]),
            ]
        else:
            rolled = [roll_cols(h, rest) for h in halves]
            shifted = [
                jnp.where(at < rest, rolled[0], rolled[1]),
                jnp.where(at < rest, rolled[1], 0.0),
            ]
        for g in range(2):
            padded[g, pl.ds(lead, tall), :] = shifted[g].reshape(tall, width).astype(BF)
        for above in (-1, 0, 1):
            first, last = {-1: (0, 32), 0: (0, 48), 1: (16, 48)}[above]
            base = first - side * above + side
            total = None
            for g in range(2):
                part = jnp.dot(
                    xt_ref[g, :, first * cols : last * cols],
                    padded[g, base * cols : (base + last - first) * cols, :],
                    preferred_element_type=F32,
                )
                total = part if total is None else total + part
            tap = 3 * (above + 1) + across + 1
            groups = total.reshape(width // 16, 16, width)
            for m in range(width // 16):
                buf[place_ref[32 + 16 * tap + m]] = groups[m]
    half = buf.shape[0] // 2
    keep_ref[...] = buf[:half]
    send_ref[...] = buf[half:].astype(BF)


def hand_out(total, me, outs):
    outs[0][...] = total[me]
    for s in range(1, len(outs)):
        outs[s][...] = total[lax.rem(me + s, len(outs))].astype(BF)


def join_owners(pos_ref, place_ref, keep_ref, got_ref, mine_ref, other_ref, *rest):
    *outs, total = rest
    count, each = total.shape[0], total.shape[1]
    total[...] = (keep_ref[...] + got_ref[...].astype(F32)).reshape(total.shape)
    core = pos_ref[4]
    for n in range(mine_ref.shape[0]):
        for ref, first in ((mine_ref, 16 * core), (other_ref, 16 * (1 - core))):
            at = place_ref[first + n]

            @pl.when(at < count * each)
            def _(ref=ref, at=at, n=n):
                total[at // each, at % each] = ref[n].astype(F32)

    hand_out(total, pos_ref[1], outs)


def fold_next(pos_ref, *refs):
    total = refs[-1]
    value = refs[0][...]
    for got in refs[1:4]:
        value = value + got[...].astype(F32)
    total[...] = value.reshape(total.shape)
    hand_out(total, pos_ref[5], refs[4:-1])


def fold_last(r0, r1, r2, r3, o_ref):
    total = r0[...] + r1[...].astype(F32) + r2[...].astype(F32) + r3[...].astype(F32)
    width = total.shape[2]
    for i in range(total.shape[1]):
        o_ref[:, i * width : (i + 1) * width] = total[:, i, :]


def share_rows(pos_ref, kept_ref, got0, got1, *rest):
    *outs, total = rest
    half, each = got0.shape[0], total.shape[0] // 2
    for n, got in enumerate((got0, got1)):
        value = kept_ref[n * half : (n + 1) * half, :] + got[...].astype(F32)
        total[n * each : (n + 1) * each] = value.reshape(each, *total.shape[1:])
    for k, out in enumerate(outs):
        out[...] = total[:, jnp.bitwise_xor(pos_ref[0], k)].astype(out.dtype)


def along(blocks, axis):
    count = lax.axis_size(axis)
    return [blocks[0]] + [
        lax.ppermute(blocks[s], axis, [(i, (i + s) % count) for i in range(count)]) for s in range(1, count)
    ]


def swap_core(x):
    return lax.ppermute(x, "dp_2", [(0, 1), (1, 0)])


def pick(pos, centre):
    pixels, chans = centre.shape
    block = jax.ShapeDtypeStruct((pixels, chans // 4), BF)
    return call(select_channels, [block] * 4, 1, 1, 2 * pixels * chans * chans, 4 * pixels * chans, 14, name="pick")(
        pos, centre
    )


def turn(pos, got):
    pixels, width = got[0].shape
    return call(
        turn_pixels,
        jax.ShapeDtypeStruct((2, width, 2 * pixels), BF),
        1,
        4,
        8 * pixels * width * width,
        16 * pixels * width,
        12,
        [pltpu.VMEM((2, 2 * pixels, width), BF)],
        name="turn",
    )(pos, *got)


def split_pair(pos, kept, got):
    width = kept.shape[1]
    slices = kept.shape[0] // 64
    shape = (slices, 16, width)
    return call(
        share_rows,
        [jax.ShapeDtypeStruct(shape, F32)] + [jax.ShapeDtypeStruct(shape, BF)] * 3,
        1,
        3,
        kept.size,
        8 * kept.size,
        10,
        [pltpu.VMEM((slices, 4, 16, width), F32)],
        name="rows",
    )(pos, kept, *got)


def sum_pair(blocks):
    mine = blocks[0] + sum(block.astype(F32) for block in blocks[1:])
    return mine, swap_core(mine.astype(BF))


def place_slots(bucket_slot, core, slot_count):
    replicas = lax.axis_size(DP)
    capacity = slot_count // replicas
    owner = bucket_slot // capacity
    other = jnp.bitwise_xor(owner % 2, core)
    return other * (slot_count // 2) + (owner // 2) * capacity + bucket_slot % capacity


def tap_slots(pos, place, deltas, turned, slot_count):
    pixels, width = deltas[0].shape
    half = slot_count // 2
    return call(
        tap_grads,
        [jax.ShapeDtypeStruct((half, 16, width), F32), jax.ShapeDtypeStruct((half, 16, width), BF)],
        2,
        5,
        2 * 7 * 4 * pixels * width * width,
        8 * 1024 * 1024,
        26,
        [
            pltpu.VMEM((2, 2 * pixels, width), BF),
            pltpu.VMEM((2, 2 * pixels + 2 * RATE_C * SIDE, width), BF),
            pltpu.VMEM((slot_count, 16, width), F32),
        ],
        name="taps",
    )(pos, place, *deltas, turned)


def reduce_slots(pos, place, kept, sent, mine, other):
    half, rows, width = kept.shape
    ys, zs = lax.axis_size("dp_0"), lax.axis_size("dp_1")
    each = half // ys
    last = each // zs

    def blocks(count, n):
        shape = (n, rows, width)
        return [jax.ShapeDtypeStruct(shape, F32)] + [jax.ShapeDtypeStruct(shape, BF)] * (count - 1)

    total = call(
        join_owners,
        blocks(ys, each),
        2,
        4,
        kept.size,
        8 * kept.size,
        12,
        [pltpu.VMEM((ys, each, rows, width), F32)],
        name="owners",
    )(pos, place, kept, swap_core(sent), mine, other)
    total = call(
        fold_next,
        blocks(zs, last),
        1,
        4,
        kept.size // 4,
        2 * kept.size,
        6,
        [pltpu.VMEM((zs, last, rows, width), F32)],
        name="fold",
    )(pos, *along(total, "dp_0"))
    return call(
        fold_last,
        jax.ShapeDtypeStruct((last, rows * width), F32),
        0,
        4,
        kept.size // 16,
        kept.size // 2,
        4,
        name="last",
    )(*along(total, "dp_1"))


def silu_slope(value):
    sig = jax.nn.sigmoid(value)
    return sig * (1.0 + value * (1.0 - sig))


RATES = (RATE_A, RATE_B, RATE_C)
SIDE = 24


def turned_by(x, shift, far):
    return jnp.where(far == 0, roll_cols(x, shift), roll_cols(x, SIDE - shift))


def rank_of(shape, far):
    at = lax.broadcasted_iota(jnp.int32, shape, 1)
    return jnp.where(far == 0, at, SIDE - 1 - at)


def row_marks(low, rate):
    lead = rate * SIDE
    whole = SIDE * SIDE

    def either(upper, lower):
        return pl.multiple_of(jnp.where(low == 0, upper, lower), 16)

    return dict(
        own=either(0, lead),
        out=either(lead, 0),
        theirs=either(whole, 0),
        inward_from=either(lead, 0),
        inward=either(0, 2 * lead),
        kept=either(lead, 0),
        inner=either(0, lead),
    )


def blocks(x):
    return x.reshape(x.shape[0] // SIDE, SIDE, x.shape[1])


def flat(x):
    return x.reshape(x.shape[0] * SIDE, x.shape[2])


def tap_copies(pos_ref, refs, jobs, held, sems):
    copies = []
    for n, (branch, above, across) in enumerate(jobs):
        a = 1 if above == 1 else jnp.where(pos_ref[2] == 0, above, 2 - above)
        b = 1 if across == 1 else jnp.where(pos_ref[3] == 0, across, 2 - across)
        copies.append(pltpu.make_async_copy(refs[branch].at[a, b], held.at[n], sems.at[n]))
    return copies


OUTER = [(k, a, b) for k in (2, 1, 0) for a, b in ((0, 0), (1, 0), (2, 0), (0, 1), (0, 2))]
INNER = [(k, a, b) for k in (2, 1, 0) for a, b in ((1, 1), (2, 1), (1, 2), (2, 2))]


def outer_parts(pos_ref, x_ref, wa_ref, wb_ref, wc_ref, pre_ref, row_ref, col_ref, diag_ref, ext, acc, held, sems):
    low, far = pos_ref[2], pos_ref[3]
    whole = SIDE * SIDE
    width = pre_ref.shape[2]
    copies = tap_copies(pos_ref, (wa_ref, wb_ref, wc_ref), OUTER, held, sems)
    for copy in copies:
        copy.start()
    first = 0
    for turn, (index, rate) in enumerate(((2, RATE_C), (1, RATE_B), (0, RATE_A))):
        lead = rate * SIDE
        inside = whole - lead
        at = row_marks(low, rate)

        def times(n, rows=slice(None)):
            copies[5 * turn + n].wait()
            return jnp.dot(x_ref[rows, :], held[5 * turn + n], preferred_element_type=F32)

        own_rows = pl.ds(at["own"], whole)
        their_rows = pl.ds(at["theirs"], lead)
        kept_rows = pl.ds(at["kept"], inside)
        to_row = slice(first, first + lead)
        first += lead
        ext[pl.ds(pl.multiple_of(whole - at["theirs"], 16), lead), :] = jnp.zeros((lead, width), F32)
        ext[pl.ds(at["out"], whole), :] = times(0)
        ext[own_rows, :] += times(1)
        ext[pl.ds(at["inward"], inside), :] += times(2, pl.ds(at["inward_from"], inside))
        own = blocks(ext[own_rows, :])
        ours = turned_by(own, rate, far)
        rank = rank_of(own.shape, far)
        pre_ref[index] = flat(jnp.where(rank >= rate, ours, 0.0))
        below = blocks(ext[their_rows, :])
        theirs = turned_by(below, rate, far)
        place = rank_of(below.shape, far)
        acc[:lead, :] = flat(jnp.where(place >= rate, theirs, 0.0))
        if rate == RATE_C:
            col_ref[:whole, :] = flat(jnp.where(rank < rate, ours, 0.0)).astype(BF)
            diag_ref[:lead, :] = flat(jnp.where(place < rate, theirs, 0.0)).astype(BF)
        elif rate == RATE_B:
            half = rate // 2
            col_ref[whole:, :] = flat(jnp.where(rank[:rate] < rate, ours[:rate], own[rate:])).astype(BF)
            part = place[:half] < rate
            diag_ref[RATE_C * SIDE :, :] = flat(jnp.where(part, theirs[:half], below[half:])).astype(BF)
        else:
            have = blocks(col_ref[:whole, :].astype(F32))
            col_ref[:whole, :] = flat(jnp.where(rank >= RATE_C, own, have)).astype(BF)
            have = blocks(diag_ref[:lead, :].astype(F32))
            diag_ref[:lead, :] = flat(jnp.where(place >= RATE_C, below, have)).astype(BF)
        ext[pl.ds(at["out"], whole), :] = times(3)
        pre_ref[index, kept_rows, :] += ext[lead:whole, :]
        acc[:lead, :] += ext[their_rows, :]
        ext[pl.ds(at["out"], whole), :] = times(4)
        own = blocks(ext[lead:whole, :])
        rank = rank_of(own.shape, far)
        pre_ref[index, kept_rows, :] += flat(jnp.where(rank < SIDE - rate, turned_by(own, rate, 1 - far), 0.0))
        below = blocks(ext[their_rows, :])
        theirs = jnp.where(place < SIDE - rate, turned_by(below, rate, 1 - far), 0.0)
        row_ref[to_row, :] = (acc[:lead, :] + flat(theirs)).astype(BF)


def inner_parts(pos_ref, x_ref, part_ref, wp_ref, wa_ref, wb_ref, wc_ref, pre0_ref, pre_ref, acc, held, sems):
    low, far = pos_ref[2], pos_ref[3]
    whole = SIDE * SIDE
    copies = tap_copies(pos_ref, (wa_ref, wb_ref, wc_ref), INNER, held, sems)
    for copy in copies:
        copy.start()
    pre0_ref[...] = jnp.dot(x_ref[...], wp_ref[...], preferred_element_type=F32)
    for turn, (index, rate) in enumerate(((2, RATE_C), (1, RATE_B), (0, RATE_A))):
        lead = rate * SIDE
        inside = whole - lead
        at = row_marks(low, rate)
        from_rows = pl.ds(at["inward_from"], inside)
        to_rows = pl.ds(at["inner"], inside)

        def times(n, rows=slice(None)):
            copies[4 * turn + n].wait()
            return jnp.dot(x_ref[rows, :], held[4 * turn + n], preferred_element_type=F32)

        pre_ref[index] = part_ref[index] + times(0)
        pre_ref[index, to_rows, :] += times(1, from_rows)
        acc[...] = times(2)
        acc[to_rows, :] += times(3, from_rows)
        own = blocks(acc[...])
        rank = rank_of(own.shape, far)
        pre_ref[index] += flat(jnp.where(rank < SIDE - rate, turned_by(own, rate, 1 - far), 0.0))


def outer(pos, centre, w_rate_a, w_rate_b, w_rate_c):
    pixels, chans = centre.shape
    width = w_rate_a.shape[3]
    sends = (RATE_A + RATE_B + RATE_C) * SIDE
    shapes = [((3, pixels, width), F32), ((sends, width), BF), ((sends, width), BF), ((pixels, width), BF)]
    return call(
        outer_parts,
        [jax.ShapeDtypeStruct(*s) for s in shapes],
        1,
        1,
        2 * pixels * chans * width * 14,
        10 * MIB,
        28,
        [
            pltpu.VMEM(((SIDE + RATE_C) * SIDE, width), F32),
            pltpu.VMEM((RATE_C * SIDE, width), F32),
            pltpu.VMEM((len(OUTER), chans, width), BF),
            pltpu.SemaphoreType.DMA((len(OUTER),)),
        ],
        name="outer",
        n_any=3,
    )(pos, centre, w_rate_a, w_rate_b, w_rate_c)


def inner(pos, centre, part, w_point, w_rate_a, w_rate_b, w_rate_c):
    pixels, chans = centre.shape
    width = w_point.shape[1]
    return call(
        inner_parts,
        [jax.ShapeDtypeStruct((pixels, width), F32), jax.ShapeDtypeStruct((3, pixels, width), F32)],
        1,
        3,
        2 * pixels * chans * width * 10,
        10 * MIB,
        26,
        [
            pltpu.VMEM((pixels, width), F32),
            pltpu.VMEM((len(INNER), chans, width), BF),
            pltpu.SemaphoreType.DMA((len(INNER),)),
        ],
        name="inner",
        n_any=3,
    )(pos, centre, part, w_point, w_rate_a, w_rate_b, w_rate_c)


def merge_parts(
    pos_ref, pre0_ref, own_ref, row_ref, col_ref, diag_ref, cot_ref, wp_ref, joined_ref, g_ref, d0_ref, d3_ref, pre
):
    low = pos_ref[2]
    theirs = 1 - pos_ref[3]
    width = pre0_ref.shape[1]
    whole = SIDE * SIDE

    def rows_of(rate):
        return pl.multiple_of(jnp.where(low == 0, (SIDE - rate) * SIDE, 0), 16)

    pre[...] = own_ref[...]
    first = 0
    for index, rate in ((2, RATE_C), (1, RATE_B), (0, RATE_A)):
        lead = rate * SIDE
        pre[index, pl.ds(rows_of(rate), lead), :] += row_ref[first : first + lead, :].astype(F32)
        first += lead

    part = blocks(col_ref[:whole, :].astype(F32))
    rank = rank_of(part.shape, theirs)
    pre[2] += flat(jnp.where(rank < RATE_C, part, 0.0))
    pre[0] += flat(turned_by(jnp.where(rank >= RATE_C, part, 0.0), RATE_A, theirs))
    part = blocks(col_ref[whole:, :].astype(F32))
    rank = rank_of(part.shape, theirs)
    pre[1, : RATE_B * SIDE, :] += flat(jnp.where(rank < RATE_B, part, 0.0))
    pre[1, RATE_B * SIDE :, :] += flat(roll_cols(jnp.where(rank >= RATE_B, part, 0.0), RATE_B))

    part = blocks(diag_ref[: RATE_C * SIDE, :].astype(F32))
    rank = rank_of(part.shape, theirs)
    pre[2, pl.ds(rows_of(RATE_C), RATE_C * SIDE), :] += flat(jnp.where(rank < RATE_C, part, 0.0))
    few = part[:RATE_A]
    few = turned_by(jnp.where(rank[:RATE_A] >= RATE_C, few, 0.0), RATE_A, theirs)
    pre[0, pl.ds(rows_of(RATE_A), RATE_A * SIDE), :] += flat(few)
    part = blocks(diag_ref[RATE_C * SIDE :, :].astype(F32))
    rank = rank_of(part.shape, theirs)
    half = RATE_B // 2
    at = rows_of(RATE_B)
    pre[1, pl.ds(at, half * SIDE), :] += flat(jnp.where(rank < RATE_B, part, 0.0))
    last = pl.multiple_of(at + half * SIDE, 16)
    pre[1, pl.ds(last, half * SIDE), :] += flat(roll_cols(jnp.where(rank >= RATE_B, part, 0.0), RATE_B))

    slopes = {}
    for k in range(4):
        value = pre0_ref[...] if k == 0 else pre[k - 1]
        sig = jax.nn.sigmoid(value)
        joined_ref[:, k * width : (k + 1) * width] = (value * sig).astype(BF)
        if k in (0, 3):
            slopes[k] = sig * (1.0 + value * (1.0 - sig))
    proj_pre = jnp.dot(joined_ref[...], wp_ref[...], preferred_element_type=F32)
    g_proj = (cot_ref[...].astype(F32) * silu_slope(proj_pre)).astype(BF)
    g_ref[...] = g_proj
    for k, out in ((3, d3_ref), (0, d0_ref)):
        back = lax.dot_general(
            g_proj, wp_ref[k * width : (k + 1) * width, :], (((1,), (1,)), ((), ())), preferred_element_type=F32
        )
        out[...] = (back * slopes[k]).astype(BF)


def merge(pos, pre0, own, row, col, diag, cot, w_proj):
    pixels, width = pre0.shape
    block = jax.ShapeDtypeStruct((pixels, width), BF)
    return call(
        merge_parts,
        [jax.ShapeDtypeStruct((pixels, 4 * width), BF), block, block, block],
        1,
        7,
        2 * pixels * width * width * 6,
        6 * 1024 * 1024,
        18,
        [pltpu.VMEM((3, pixels, width), F32)],
        name="merge",
    )(pos, pre0, own, row, col, diag, cot, w_proj)


def pair_grads(pos_ref, joined_ref, g_ref, x_ref, d0_ref, keep_ref, *send_refs):
    core = pos_ref[4]
    over = (((0,), (0,)), ((), ()))
    grad_proj = lax.dot_general(joined_ref[...], g_ref[...], over, preferred_element_type=F32)
    grad_point = lax.dot_general(x_ref[...], d0_ref[...], over, preferred_element_type=F32)
    keep_ref[...] = jnp.where(core == 0, grad_proj, grad_point)
    half = send_refs[0].shape[0]
    for k, send_ref in enumerate(send_refs):
        part = slice(k * half, (k + 1) * half)
        send_ref[...] = jnp.where(core == 0, grad_point[part], grad_proj[part]).astype(BF)


def shards(features, cotangent, w_point, w_rate_a, w_rate_b, w_rate_c, w_proj, bucket_slot):
    image = features[0]
    rows_dev, cols_dev, chans = image.shape
    pixels = rows_dev * cols_dev
    width = w_point.shape[1]
    row, col, core = (lax.axis_index(n) for n in ("row", "col", "dp_2"))
    at_y, at_z = lax.axis_index("dp_0"), lax.axis_index("dp_1")
    pos = jnp.stack([2 * row + col, at_y, row, col, core, at_z]).astype(jnp.int32)
    replicas = lax.axis_size(DP)
    slot_count = replicas * (bucket_slot.shape[0] // replicas + 1)
    place = place_slots(bucket_slot, core, slot_count)
    centre = image.reshape(pixels, chans)
    weights = [pltpu.with_memory_space_constraint(w, pltpu.HBM) for w in (w_rate_a, w_rate_b, w_rate_c)]
    picked = pick(pos, centre)
    centre, *picked = lax.optimization_barrier((centre, *picked))
    got = [picked[0]] + [flip(picked[k], k) for k in (1, 2, 3)]
    part, *parts = outer(pos, centre, *weights)
    parts, got = lax.optimization_barrier((parts, got))
    to_row, to_col, to_diag = parts
    parts = [flip(to_row, 2), flip(to_col, 1), flip(to_diag, 3)]
    turned = turn(pos, got)
    pre0, own = inner(pos, centre, part, w_point, *weights)
    parts, pre0, own, turned = lax.optimization_barrier((parts, pre0, own, turned))
    joined, g_proj, delta0, delta3 = merge(
        pos, pre0, own, *parts, cotangent[0].reshape(pixels, width), w_proj
    )
    shared = [delta3] + [flip(delta3, k) for k in (1, 2, 3)]
    block = (4 * width, width)
    kept, *sent = call(
        pair_grads,
        [jax.ShapeDtypeStruct(block, F32)] + [jax.ShapeDtypeStruct((2 * width, width), BF)] * 2,
        1,
        4,
        4 * pixels * chans * width,
        4 * 1024 * 1024,
        16,
        name="pair",
    )(pos, joined, g_proj, centre, delta0)
    got = [swap_core(part) for part in sent]
    got, shared = lax.optimization_barrier((got, shared))
    by_owner = split_pair(pos, kept, got)
    by_owner, shared = lax.optimization_barrier((by_owner, shared))
    by_owner = [by_owner[0]] + [flip(by_owner[k], k) for k in (1, 2, 3)]
    kept, sent = tap_slots(pos, place, shared, turned, slot_count)
    sent, by_owner = lax.optimization_barrier((sent, by_owner))
    mine, other = sum_pair(by_owner)
    return reduce_slots(pos, place, kept, sent, mine, other)


def solution(mesh):
    torus = Mesh(
        mesh.devices.reshape(mesh.shape["row"], mesh.shape["col"], 4, 4, 2),
        ("row", "col", "dp_0", "dp_1", "dp_2"),
    )
    in_specs = (P(DP, "row", "col", None), P(DP, "row", "col", None), P(), P(), P(), P(), P(), P())
    out_specs = P(DP, ("row", "col"))
    return jax.shard_map(
        shards, mesh=torus, in_specs=in_specs, out_specs=out_specs, check_vma=False
    )
```

```python
import jax
import jax.numpy as jnp
from jax import lax
from jax.experimental import pallas as pl
from jax.experimental.pallas import tpu as pltpu
from jax.sharding import Mesh
from jax.sharding import PartitionSpec as P

RATE_A = 6
RATE_B = 12
RATE_C = 18
DP = ("dp_0", "dp_1", "dp_2")


BF = jnp.bfloat16
F32 = jnp.float32
MIB = 1024 * 1024


def flip(x, mask):
    if mask == 1:
        return lax.ppermute(x, "col", [(0, 1), (1, 0)])
    if mask == 2:
        return lax.ppermute(x, "row", [(0, 1), (1, 0)])
    return lax.ppermute(x, ("row", "col"), [(0, 3), (3, 0), (1, 2), (2, 1)])


def smem():
    return pl.BlockSpec(memory_space=pltpu.SMEM)


def vmem():
    return pl.BlockSpec(memory_space=pltpu.VMEM)


def call(body, outs, n_smem, n_vmem, flops, nbytes, limit, scratch=(), name=None, n_any=0):
    return pl.pallas_call(
        body,
        out_shape=outs,
        in_specs=[smem()] * n_smem + [vmem()] * n_vmem + [pl.BlockSpec(memory_space=pltpu.HBM)] * n_any,
        out_specs=jax.tree.map(lambda _: vmem(), outs),
        scratch_shapes=list(scratch),
        compiler_params=pltpu.CompilerParams(vmem_limit_bytes=limit * MIB),
        cost_estimate=pl.CostEstimate(flops=flops, bytes_accessed=nbytes, transcendentals=0),
        name=name,
    )


def select_channels(pos_ref, x_ref, *o_refs):
    chans = x_ref.shape[1]
    width = o_refs[0].shape[1]
    source = lax.broadcasted_iota(jnp.int32, (chans, width), 0)
    col = lax.broadcasted_iota(jnp.int32, (1, width), 1)
    wanted = 64 * (col // 16) + col % 16
    for k, o_ref in enumerate(o_refs):
        c = jnp.bitwise_xor(pos_ref[0], k)
        pick = jnp.where(source == wanted + 16 * c, 1.0, 0.0).astype(BF)
        o_ref[...] = jnp.dot(x_ref[...], pick, preferred_element_type=F32).astype(BF)


def turn_pixels(pos_ref, x0, x1, x2, x3, o_ref, held):
    pixels, width = x0.shape
    for k, x in enumerate((x0, x1, x2, x3)):
        s = jnp.bitwise_xor(pos_ref[0], k)
        held[s % 2, pl.ds((s // 2) * pixels, pixels), :] = x[...]
    eye = (
        lax.broadcasted_iota(jnp.int32, (width, width), 0)
        == lax.broadcasted_iota(jnp.int32, (width, width), 1)
    ).astype(F32).astype(BF)
    for g in range(2):
        o_ref[g] = lax.dot_general(
            eye, held[g], (((1,), (1,)), ((), ())), preferred_element_type=F32
        ).astype(BF)


def roll_cols(x, shift):
    return jnp.concatenate([x[:, x.shape[1] - shift :], x[:, : x.shape[1] - shift]], axis=1)


def tap_grads(pos_ref, place_ref, d0, d1, d2, d3, xt_ref, keep_ref, send_ref, held, padded, buf):
    side = RATE_C
    pixels, width = d0.shape
    cols = 24
    rows = pixels // cols
    for k, d in enumerate((d0, d1, d2, d3)):
        s = jnp.bitwise_xor(pos_ref[0], k)
        held[s % 2, pl.ds((s // 2) * pixels, pixels), :] = d[...]
    buf[...] = jnp.zeros_like(buf)
    tall = 2 * pixels
    lead = side * cols
    zeros = jnp.zeros((2, lead, width), BF)
    halves = [held[g].astype(F32).reshape(2 * rows, cols, width) for g in range(2)]
    at = lax.broadcasted_iota(jnp.int32, (2 * rows, cols, width), 1)
    rest = cols - side
    for across in (-1, 0, 1):
        padded[:, pl.ds(0, lead), :] = zeros
        padded[:, pl.ds(lead + tall, lead), :] = zeros
        if across == 0:
            shifted = halves
        elif across == 1:
            rolled = [roll_cols(h, side) for h in halves]
            shifted = [
                jnp.where(at >= side, rolled[0], 0.0),
                jnp.where(at < side, rolled[0], rolled[1]),
            ]
        else:
            rolled = [roll_cols(h, rest) for h in halves]
            shifted = [
                jnp.where(at < rest, rolled[0], rolled[1]),
                jnp.where(at < rest, rolled[1], 0.0),
            ]
        for g in range(2):
            padded[g, pl.ds(lead, tall), :] = shifted[g].reshape(tall, width).astype(BF)
        for above in (-1, 0, 1):
            first, last = {-1: (0, 32), 0: (0, 48), 1: (16, 48)}[above]
            base = first - side * above + side
            total = None
            for g in range(2):
                part = jnp.dot(
                    xt_ref[g, :, first * cols : last * cols],
                    padded[g, base * cols : (base + last - first) * cols, :],
                    preferred_element_type=F32,
                )
                total = part if total is None else total + part
            tap = 3 * (above + 1) + across + 1
            groups = total.reshape(width // 16, 16, width)
            for m in range(width // 16):
                buf[place_ref[32 + 16 * tap + m]] = groups[m]
    half = buf.shape[0] // 2
    keep_ref[...] = buf[:half]
    send_ref[...] = buf[half:].astype(BF)


def hand_out(total, me, outs):
    outs[0][...] = total[me]
    for s in range(1, len(outs)):
        outs[s][...] = total[lax.rem(me + s, len(outs))].astype(BF)


def join_owners(pos_ref, place_ref, keep_ref, got_ref, mine_ref, other_ref, *rest):
    *outs, total = rest
    count, each = total.shape[0], total.shape[1]
    total[...] = (keep_ref[...] + got_ref[...].astype(F32)).reshape(total.shape)
    core = pos_ref[4]
    for n in range(mine_ref.shape[0]):
        for ref, first in ((mine_ref, 16 * core), (other_ref, 16 * (1 - core))):
            at = place_ref[first + n]

            @pl.when(at < count * each)
            def _(ref=ref, at=at, n=n):
                total[at // each, at % each] = ref[n].astype(F32)

    hand_out(total, pos_ref[1], outs)


def fold_next(pos_ref, *refs):
    total = refs[-1]
    value = refs[0][...]
    for got in refs[1:4]:
        value = value + got[...].astype(F32)
    total[...] = value.reshape(total.shape)
    hand_out(total, pos_ref[5], refs[4:-1])


def fold_last(r0, r1, r2, r3, o_ref):
    total = r0[...] + r1[...].astype(F32) + r2[...].astype(F32) + r3[...].astype(F32)
    width = total.shape[2]
    for i in range(total.shape[1]):
        o_ref[:, i * width : (i + 1) * width] = total[:, i, :]


def share_rows(pos_ref, kept_ref, got0, got1, *rest):
    *outs, total = rest
    half, each = got0.shape[0], total.shape[0] // 2
    for n, got in enumerate((got0, got1)):
        value = kept_ref[n * half : (n + 1) * half, :] + got[...].astype(F32)
        total[n * each : (n + 1) * each] = value.reshape(each, *total.shape[1:])
    for k, out in enumerate(outs):
        out[...] = total[:, jnp.bitwise_xor(pos_ref[0], k)].astype(out.dtype)


def along(blocks, axis):
    count = lax.axis_size(axis)
    return [blocks[0]] + [
        lax.ppermute(blocks[s], axis, [(i, (i + s) % count) for i in range(count)]) for s in range(1, count)
    ]


def swap_core(x):
    return lax.ppermute(x, "dp_2", [(0, 1), (1, 0)])


def pick(pos, centre):
    pixels, chans = centre.shape
    block = jax.ShapeDtypeStruct((pixels, chans // 4), BF)
    return call(select_channels, [block] * 4, 1, 1, 2 * pixels * chans * chans, 4 * pixels * chans, 14, name="pick")(
        pos, centre
    )


def turn(pos, got):
    pixels, width = got[0].shape
    return call(
        turn_pixels,
        jax.ShapeDtypeStruct((2, width, 2 * pixels), BF),
        1,
        4,
        8 * pixels * width * width,
        16 * pixels * width,
        12,
        [pltpu.VMEM((2, 2 * pixels, width), BF)],
        name="turn",
    )(pos, *got)


def split_pair(pos, kept, got):
    width = kept.shape[1]
    slices = kept.shape[0] // 64
    shape = (slices, 16, width)
    return call(
        share_rows,
        [jax.ShapeDtypeStruct(shape, F32)] + [jax.ShapeDtypeStruct(shape, BF)] * 3,
        1,
        3,
        kept.size,
        8 * kept.size,
        10,
        [pltpu.VMEM((slices, 4, 16, width), F32)],
        name="rows",
    )(pos, kept, *got)


def sum_pair(blocks):
    mine = blocks[0] + sum(block.astype(F32) for block in blocks[1:])
    return mine, swap_core(mine.astype(BF))


def place_slots(bucket_slot, core, slot_count):
    replicas = lax.axis_size(DP)
    capacity = slot_count // replicas
    owner = bucket_slot // capacity
    other = jnp.bitwise_xor(owner % 2, core)
    return other * (slot_count // 2) + (owner // 2) * capacity + bucket_slot % capacity


def tap_slots(pos, place, deltas, turned, slot_count):
    pixels, width = deltas[0].shape
    half = slot_count // 2
    return call(
        tap_grads,
        [jax.ShapeDtypeStruct((half, 16, width), F32), jax.ShapeDtypeStruct((half, 16, width), BF)],
        2,
        5,
        2 * 7 * 4 * pixels * width * width,
        8 * 1024 * 1024,
        26,
        [
            pltpu.VMEM((2, 2 * pixels, width), BF),
            pltpu.VMEM((2, 2 * pixels + 2 * RATE_C * SIDE, width), BF),
            pltpu.VMEM((slot_count, 16, width), F32),
        ],
        name="taps",
    )(pos, place, *deltas, turned)


def reduce_slots(pos, place, kept, sent, mine, other):
    half, rows, width = kept.shape
    ys, zs = lax.axis_size("dp_0"), lax.axis_size("dp_1")
    each = half // ys
    last = each // zs

    def blocks(count, n):
        shape = (n, rows, width)
        return [jax.ShapeDtypeStruct(shape, F32)] + [jax.ShapeDtypeStruct(shape, BF)] * (count - 1)

    total = call(
        join_owners,
        blocks(ys, each),
        2,
        4,
        kept.size,
        8 * kept.size,
        12,
        [pltpu.VMEM((ys, each, rows, width), F32)],
        name="owners",
    )(pos, place, kept, swap_core(sent), mine, other)
    total = call(
        fold_next,
        blocks(zs, last),
        1,
        4,
        kept.size // 4,
        2 * kept.size,
        6,
        [pltpu.VMEM((zs, last, rows, width), F32)],
        name="fold",
    )(pos, *along(total, "dp_0"))
    return call(
        fold_last,
        jax.ShapeDtypeStruct((last, rows * width), F32),
        0,
        4,
        kept.size // 16,
        kept.size // 2,
        4,
        name="last",
    )(*along(total, "dp_1"))


def silu_slope(value):
    sig = jax.nn.sigmoid(value)
    return sig * (1.0 + value * (1.0 - sig))


RATES = (RATE_A, RATE_B, RATE_C)
SIDE = 24


def turned_by(x, shift, far):
    return jnp.where(far == 0, roll_cols(x, shift), roll_cols(x, SIDE - shift))


def rank_of(shape, far):
    at = lax.broadcasted_iota(jnp.int32, shape, 1)
    return jnp.where(far == 0, at, SIDE - 1 - at)


def row_marks(low, rate):
    lead = rate * SIDE
    whole = SIDE * SIDE

    def either(upper, lower):
        return pl.multiple_of(jnp.where(low == 0, upper, lower), 16)

    return dict(
        own=either(0, lead),
        out=either(lead, 0),
        theirs=either(whole, 0),
        inward_from=either(lead, 0),
        inward=either(0, 2 * lead),
        kept=either(lead, 0),
        inner=either(0, lead),
    )


def blocks(x):
    return x.reshape(x.shape[0] // SIDE, SIDE, x.shape[1])


def flat(x):
    return x.reshape(x.shape[0] * SIDE, x.shape[2])


def tap_copies(pos_ref, refs, jobs, held, sems):
    copies = []
    for branch, ref in enumerate(refs):
        for n, (above, across) in enumerate(jobs):
            a = 1 if above == 1 else jnp.where(pos_ref[2] == 0, above, 2 - above)
            b = 1 if across == 1 else jnp.where(pos_ref[3] == 0, across, 2 - across)
            width = ref.shape[3]
            to = held.at[branch, :, n * width : (n + 1) * width]
            copies.append(pltpu.make_async_copy(ref.at[a, b], to, sems.at[branch, n]))
    return copies


BRANCHES = ((2, RATE_C), (1, RATE_B), (0, RATE_A))
OUTER = ((0, 0), (1, 0), (0, 1), (0, 2), (2, 0))
INNER = ((1, 1), (1, 2), (2, 1), (2, 2))


def outer_parts(pos_ref, x_ref, wc_ref, wb_ref, wa_ref, pre_ref, row_ref, col_ref, diag_ref, ext, acc, y, held, sems):
    low, far = pos_ref[2], pos_ref[3]
    whole = SIDE * SIDE
    width = pre_ref.shape[2]
    copies = tap_copies(pos_ref, (wc_ref, wb_ref, wa_ref), OUTER, held, sems)
    for copy in copies:
        copy.start()
    first = 0
    for turn, (index, rate) in enumerate(BRANCHES):
        lead = rate * SIDE
        inside = whole - lead
        at = row_marks(low, rate)
        own_rows = pl.ds(at["own"], whole)
        their_rows = pl.ds(at["theirs"], lead)
        kept_rows = pl.ds(at["kept"], inside)
        to_row = slice(first, first + lead)
        first += lead
        count = len(OUTER)
        for copy in copies[turn * count : (turn + 1) * count]:
            copy.wait()
        y[...] = jnp.dot(x_ref[...], held[turn, :, : 4 * width], preferred_element_type=F32)
        ext[pl.ds(pl.multiple_of(whole - at["theirs"], 16), lead), :] = jnp.zeros((lead, width), F32)
        ext[pl.ds(at["out"], whole), :] = y[:, :width]
        ext[own_rows, :] += y[:, width : 2 * width]
        ext[pl.ds(at["inward"], inside), :] += jnp.dot(
            x_ref[pl.ds(at["inward_from"], inside), :], held[turn, :, 4 * width :], preferred_element_type=F32
        )
        own = blocks(ext[own_rows, :])
        ours = turned_by(own, rate, far)
        rank = rank_of(own.shape, far)
        pre_ref[index] = flat(jnp.where(rank >= rate, ours, 0.0))
        below = blocks(ext[their_rows, :])
        theirs = turned_by(below, rate, far)
        place = rank_of(below.shape, far)
        acc[:lead, :] = flat(jnp.where(place >= rate, theirs, 0.0))
        if rate == RATE_C:
            col_ref[:whole, :] = flat(jnp.where(rank < rate, ours, 0.0)).astype(BF)
            diag_ref[:lead, :] = flat(jnp.where(place < rate, theirs, 0.0)).astype(BF)
        elif rate == RATE_B:
            half = rate // 2
            col_ref[whole:, :] = flat(jnp.where(rank[:rate] < rate, ours[:rate], own[rate:])).astype(BF)
            part = place[:half] < rate
            diag_ref[RATE_C * SIDE :, :] = flat(jnp.where(part, theirs[:half], below[half:])).astype(BF)
        else:
            have = blocks(col_ref[:whole, :].astype(F32))
            col_ref[:whole, :] = flat(jnp.where(rank >= RATE_C, own, have)).astype(BF)
            have = blocks(diag_ref[:lead, :].astype(F32))
            diag_ref[:lead, :] = flat(jnp.where(place >= RATE_C, below, have)).astype(BF)
        next_from = pl.multiple_of(jnp.where(low == 0, inside, 0), 16)
        keep_from = pl.multiple_of(jnp.where(low == 0, 0, lead), 16)
        pre_ref[index, kept_rows, :] += y[pl.ds(keep_from, inside), 2 * width : 3 * width]
        own = blocks(y[pl.ds(keep_from, inside), 3 * width :])
        rank = rank_of(own.shape, far)
        pre_ref[index, kept_rows, :] += flat(jnp.where(rank < SIDE - rate, turned_by(own, rate, 1 - far), 0.0))
        below = blocks(y[pl.ds(next_from, lead), 3 * width :])
        theirs = flat(jnp.where(place < SIDE - rate, turned_by(below, rate, 1 - far), 0.0))
        row_ref[to_row, :] = (acc[:lead, :] + y[pl.ds(next_from, lead), 2 * width : 3 * width] + theirs).astype(BF)


def inner_parts(pos_ref, x_ref, part_ref, wp_ref, wc_ref, wb_ref, wa_ref, pre0_ref, pre_ref, y, z, held, sems):
    low, far = pos_ref[2], pos_ref[3]
    whole = SIDE * SIDE
    width = pre0_ref.shape[1]
    copies = tap_copies(pos_ref, (wc_ref, wb_ref, wa_ref), INNER, held, sems)
    for copy in copies:
        copy.start()
    pre0_ref[...] = jnp.dot(x_ref[...], wp_ref[...], preferred_element_type=F32)
    for turn, (index, rate) in enumerate(BRANCHES):
        lead = rate * SIDE
        inside = whole - lead
        at = row_marks(low, rate)
        from_rows = pl.ds(at["inward_from"], inside)
        to_rows = pl.ds(at["inner"], inside)
        count = len(INNER)
        for copy in copies[turn * count : (turn + 1) * count]:
            copy.wait()
        y[...] = jnp.dot(x_ref[...], held[turn, :, : 2 * width], preferred_element_type=F32)
        z[:inside, :] = jnp.dot(x_ref[from_rows, :], held[turn, :, 2 * width :], preferred_element_type=F32)
        y[to_rows, :] += z[:inside, :]
        own = blocks(y[:, width:])
        rank = rank_of(own.shape, far)
        moved = flat(jnp.where(rank < SIDE - rate, turned_by(own, rate, 1 - far), 0.0))
        pre_ref[index] = part_ref[index] + y[:, :width] + moved


def outer(pos, centre, w_rate_a, w_rate_b, w_rate_c):
    pixels, chans = centre.shape
    width = w_rate_a.shape[3]
    sends = (RATE_A + RATE_B + RATE_C) * SIDE
    shapes = [((3, pixels, width), F32), ((sends, width), BF), ((sends, width), BF), ((pixels, width), BF)]
    return call(
        outer_parts,
        [jax.ShapeDtypeStruct(*s) for s in shapes],
        1,
        1,
        2 * pixels * chans * width * 14,
        10 * MIB,
        28,
        [
            pltpu.VMEM(((SIDE + RATE_C) * SIDE, width), F32),
            pltpu.VMEM((RATE_C * SIDE, width), F32),
            pltpu.VMEM((pixels, 4 * width), F32),
            pltpu.VMEM((3, chans, len(OUTER) * width), BF),
            pltpu.SemaphoreType.DMA((3, len(OUTER))),
        ],
        name="outer",
        n_any=3,
    )(pos, centre, w_rate_c, w_rate_b, w_rate_a)


def inner(pos, centre, part, w_point, w_rate_a, w_rate_b, w_rate_c):
    pixels, chans = centre.shape
    width = w_point.shape[1]
    return call(
        inner_parts,
        [jax.ShapeDtypeStruct((pixels, width), F32), jax.ShapeDtypeStruct((3, pixels, width), F32)],
        1,
        3,
        2 * pixels * chans * width * 10,
        10 * MIB,
        26,
        [
            pltpu.VMEM((pixels, 2 * width), F32),
            pltpu.VMEM((pixels, 2 * width), F32),
            pltpu.VMEM((3, chans, len(INNER) * width), BF),
            pltpu.SemaphoreType.DMA((3, len(INNER))),
        ],
        name="inner",
        n_any=3,
    )(pos, centre, part, w_point, w_rate_c, w_rate_b, w_rate_a)


def merge_parts(
    pos_ref, pre0_ref, own_ref, row_ref, col_ref, diag_ref, cot_ref, wp_ref, joined_ref, g_ref, d0_ref, d3_ref, pre
):
    low = pos_ref[2]
    theirs = 1 - pos_ref[3]
    width = pre0_ref.shape[1]
    whole = SIDE * SIDE

    def rows_of(rate):
        return pl.multiple_of(jnp.where(low == 0, (SIDE - rate) * SIDE, 0), 16)

    pre[...] = own_ref[...]
    first = 0
    for index, rate in ((2, RATE_C), (1, RATE_B), (0, RATE_A)):
        lead = rate * SIDE
        pre[index, pl.ds(rows_of(rate), lead), :] += row_ref[first : first + lead, :].astype(F32)
        first += lead

    part = blocks(col_ref[:whole, :].astype(F32))
    rank = rank_of(part.shape, theirs)
    pre[2] += flat(jnp.where(rank < RATE_C, part, 0.0))
    pre[0] += flat(turned_by(jnp.where(rank >= RATE_C, part, 0.0), RATE_A, theirs))
    part = blocks(col_ref[whole:, :].astype(F32))
    rank = rank_of(part.shape, theirs)
    pre[1, : RATE_B * SIDE, :] += flat(jnp.where(rank < RATE_B, part, 0.0))
    pre[1, RATE_B * SIDE :, :] += flat(roll_cols(jnp.where(rank >= RATE_B, part, 0.0), RATE_B))

    part = blocks(diag_ref[: RATE_C * SIDE, :].astype(F32))
    rank = rank_of(part.shape, theirs)
    pre[2, pl.ds(rows_of(RATE_C), RATE_C * SIDE), :] += flat(jnp.where(rank < RATE_C, part, 0.0))
    few = part[:RATE_A]
    few = turned_by(jnp.where(rank[:RATE_A] >= RATE_C, few, 0.0), RATE_A, theirs)
    pre[0, pl.ds(rows_of(RATE_A), RATE_A * SIDE), :] += flat(few)
    part = blocks(diag_ref[RATE_C * SIDE :, :].astype(F32))
    rank = rank_of(part.shape, theirs)
    half = RATE_B // 2
    at = rows_of(RATE_B)
    pre[1, pl.ds(at, half * SIDE), :] += flat(jnp.where(rank < RATE_B, part, 0.0))
    last = pl.multiple_of(at + half * SIDE, 16)
    pre[1, pl.ds(last, half * SIDE), :] += flat(roll_cols(jnp.where(rank >= RATE_B, part, 0.0), RATE_B))

    slopes = {}
    for k in range(4):
        value = pre0_ref[...] if k == 0 else pre[k - 1]
        sig = jax.nn.sigmoid(value)
        joined_ref[:, k * width : (k + 1) * width] = (value * sig).astype(BF)
        if k in (0, 3):
            slopes[k] = sig * (1.0 + value * (1.0 - sig))
    proj_pre = jnp.dot(joined_ref[...], wp_ref[...], preferred_element_type=F32)
    g_proj = (cot_ref[...].astype(F32) * silu_slope(proj_pre)).astype(BF)
    g_ref[...] = g_proj
    for k, out in ((3, d3_ref), (0, d0_ref)):
        back = lax.dot_general(
            g_proj, wp_ref[k * width : (k + 1) * width, :], (((1,), (1,)), ((), ())), preferred_element_type=F32
        )
        out[...] = (back * slopes[k]).astype(BF)


def merge(pos, pre0, own, row, col, diag, cot, w_proj):
    pixels, width = pre0.shape
    block = jax.ShapeDtypeStruct((pixels, width), BF)
    return call(
        merge_parts,
        [jax.ShapeDtypeStruct((pixels, 4 * width), BF), block, block, block],
        1,
        7,
        2 * pixels * width * width * 6,
        6 * 1024 * 1024,
        18,
        [pltpu.VMEM((3, pixels, width), F32)],
        name="merge",
    )(pos, pre0, own, row, col, diag, cot, w_proj)


def pair_grads(pos_ref, joined_ref, g_ref, x_ref, d0_ref, keep_ref, *send_refs):
    core = pos_ref[4]
    over = (((0,), (0,)), ((), ()))
    grad_proj = lax.dot_general(joined_ref[...], g_ref[...], over, preferred_element_type=F32)
    grad_point = lax.dot_general(x_ref[...], d0_ref[...], over, preferred_element_type=F32)
    keep_ref[...] = jnp.where(core == 0, grad_proj, grad_point)
    half = send_refs[0].shape[0]
    for k, send_ref in enumerate(send_refs):
        part = slice(k * half, (k + 1) * half)
        send_ref[...] = jnp.where(core == 0, grad_point[part], grad_proj[part]).astype(BF)


def shards(features, cotangent, w_point, w_rate_a, w_rate_b, w_rate_c, w_proj, bucket_slot):
    image = features[0]
    rows_dev, cols_dev, chans = image.shape
    pixels = rows_dev * cols_dev
    width = w_point.shape[1]
    row, col, core = (lax.axis_index(n) for n in ("row", "col", "dp_2"))
    at_y, at_z = lax.axis_index("dp_0"), lax.axis_index("dp_1")
    pos = jnp.stack([2 * row + col, at_y, row, col, core, at_z]).astype(jnp.int32)
    replicas = lax.axis_size(DP)
    slot_count = replicas * (bucket_slot.shape[0] // replicas + 1)
    place = place_slots(bucket_slot, core, slot_count)
    centre = image.reshape(pixels, chans)
    weights = [pltpu.with_memory_space_constraint(w, pltpu.HBM) for w in (w_rate_a, w_rate_b, w_rate_c)]
    picked = pick(pos, centre)
    centre, *picked = lax.optimization_barrier((centre, *picked))
    got = [picked[0]] + [flip(picked[k], k) for k in (1, 2, 3)]
    part, *parts = outer(pos, centre, *weights)
    part, got = lax.optimization_barrier((part, got))
    to_row, to_col, to_diag = parts
    parts = [flip(to_row, 2), flip(to_col, 1), flip(to_diag, 3)]
    turned = turn(pos, got)
    pre0, own = inner(pos, centre, part, w_point, *weights)
    parts, pre0, own, turned = lax.optimization_barrier((parts, pre0, own, turned))
    joined, g_proj, delta0, delta3 = merge(
        pos, pre0, own, *parts, cotangent[0].reshape(pixels, width), w_proj
    )
    shared = [delta3] + [flip(delta3, k) for k in (1, 2, 3)]
    block = (4 * width, width)
    kept, *sent = call(
        pair_grads,
        [jax.ShapeDtypeStruct(block, F32)] + [jax.ShapeDtypeStruct((2 * width, width), BF)] * 2,
        1,
        4,
        4 * pixels * chans * width,
        4 * 1024 * 1024,
        16,
        name="pair",
    )(pos, joined, g_proj, centre, delta0)
    got = [swap_core(part) for part in sent]
    got, shared = lax.optimization_barrier((got, shared))
    by_owner = split_pair(pos, kept, got)
    by_owner, shared = lax.optimization_barrier((by_owner, shared))
    by_owner = [by_owner[0]] + [flip(by_owner[k], k) for k in (1, 2, 3)]
    kept, sent = tap_slots(pos, place, shared, turned, slot_count)
    sent, by_owner = lax.optimization_barrier((sent, by_owner))
    mine, other = sum_pair(by_owner)
    return reduce_slots(pos, place, kept, sent, mine, other)


def solution(mesh):
    torus = Mesh(
        mesh.devices.reshape(mesh.shape["row"], mesh.shape["col"], 4, 4, 2),
        ("row", "col", "dp_0", "dp_1", "dp_2"),
    )
    in_specs = (P(DP, "row", "col", None), P(DP, "row", "col", None), P(), P(), P(), P(), P(), P())
    out_specs = P(DP, ("row", "col"))
    return jax.shard_map(
        shards, mesh=torus, in_specs=in_specs, out_specs=out_specs, check_vma=False
    )
```

```python
import jax
import jax.numpy as jnp
from jax import lax
from jax.experimental import pallas as pl
from jax.experimental.pallas import tpu as pltpu
from jax.sharding import Mesh
from jax.sharding import PartitionSpec as P

RATE_A = 6
RATE_B = 12
RATE_C = 18
DP = ("dp_0", "dp_1", "dp_2")


BF = jnp.bfloat16
F32 = jnp.float32
MIB = 1024 * 1024


def flip(x, mask):
    if mask == 1:
        return lax.ppermute(x, "col", [(0, 1), (1, 0)])
    if mask == 2:
        return lax.ppermute(x, "row", [(0, 1), (1, 0)])
    return lax.ppermute(x, ("row", "col"), [(0, 3), (3, 0), (1, 2), (2, 1)])


def smem():
    return pl.BlockSpec(memory_space=pltpu.SMEM)


def vmem():
    return pl.BlockSpec(memory_space=pltpu.VMEM)


def call(body, outs, n_smem, n_vmem, flops, nbytes, limit, scratch=(), name=None, n_any=0):
    return pl.pallas_call(
        body,
        out_shape=outs,
        in_specs=[smem()] * n_smem + [vmem()] * n_vmem + [pl.BlockSpec(memory_space=pltpu.HBM)] * n_any,
        out_specs=jax.tree.map(lambda _: vmem(), outs),
        scratch_shapes=list(scratch),
        compiler_params=pltpu.CompilerParams(vmem_limit_bytes=limit * MIB),
        cost_estimate=pl.CostEstimate(flops=flops, bytes_accessed=nbytes, transcendentals=0),
        name=name,
    )


def select_channels(pos_ref, x_ref, *o_refs):
    chans = x_ref.shape[1]
    width = o_refs[0].shape[1]
    source = lax.broadcasted_iota(jnp.int32, (chans, width), 0)
    col = lax.broadcasted_iota(jnp.int32, (1, width), 1)
    wanted = 64 * (col // 16) + col % 16
    for k, o_ref in enumerate(o_refs):
        c = jnp.bitwise_xor(pos_ref[0], k)
        pick = jnp.where(source == wanted + 16 * c, 1.0, 0.0).astype(BF)
        o_ref[...] = jnp.dot(x_ref[...], pick, preferred_element_type=F32).astype(BF)


def turn_pixels(pos_ref, x0, x1, x2, x3, o_ref, held):
    pixels, width = x0.shape
    for k, x in enumerate((x0, x1, x2, x3)):
        s = jnp.bitwise_xor(pos_ref[0], k)
        held[s % 2, pl.ds((s // 2) * pixels, pixels), :] = x[...]
    eye = (
        lax.broadcasted_iota(jnp.int32, (width, width), 0)
        == lax.broadcasted_iota(jnp.int32, (width, width), 1)
    ).astype(F32).astype(BF)
    for g in range(2):
        o_ref[g] = lax.dot_general(
            eye, held[g], (((1,), (1,)), ((), ())), preferred_element_type=F32
        ).astype(BF)


def roll_cols(x, shift):
    return jnp.concatenate([x[:, x.shape[1] - shift :], x[:, : x.shape[1] - shift]], axis=1)


def tap_grads(pos_ref, place_ref, d0, d1, d2, d3, xt_ref, keep_ref, send_ref, held, padded, buf):
    side = RATE_C
    pixels, width = d0.shape
    cols = 24
    rows = pixels // cols
    for k, d in enumerate((d0, d1, d2, d3)):
        s = jnp.bitwise_xor(pos_ref[0], k)
        held[s % 2, pl.ds((s // 2) * pixels, pixels), :] = d[...]
    buf[...] = jnp.zeros_like(buf)
    tall = 2 * pixels
    lead = side * cols
    zeros = jnp.zeros((2, lead, width), BF)
    halves = [held[g].astype(F32).reshape(2 * rows, cols, width) for g in range(2)]
    at = lax.broadcasted_iota(jnp.int32, (2 * rows, cols, width), 1)
    rest = cols - side
    for across in (-1, 0, 1):
        padded[:, pl.ds(0, lead), :] = zeros
        padded[:, pl.ds(lead + tall, lead), :] = zeros
        if across == 0:
            shifted = halves
        elif across == 1:
            rolled = [roll_cols(h, side) for h in halves]
            shifted = [
                jnp.where(at >= side, rolled[0], 0.0),
                jnp.where(at < side, rolled[0], rolled[1]),
            ]
        else:
            rolled = [roll_cols(h, rest) for h in halves]
            shifted = [
                jnp.where(at < rest, rolled[0], rolled[1]),
                jnp.where(at < rest, rolled[1], 0.0),
            ]
        for g in range(2):
            padded[g, pl.ds(lead, tall), :] = shifted[g].reshape(tall, width).astype(BF)
        for above in (-1, 0, 1):
            first, last = {-1: (0, 32), 0: (0, 48), 1: (16, 48)}[above]
            base = first - side * above + side
            total = None
            for g in range(2):
                part = jnp.dot(
                    xt_ref[g, :, first * cols : last * cols],
                    padded[g, base * cols : (base + last - first) * cols, :],
                    preferred_element_type=F32,
                )
                total = part if total is None else total + part
            tap = 3 * (above + 1) + across + 1
            groups = total.reshape(width // 16, 16, width)
            for m in range(width // 16):
                buf[place_ref[32 + 16 * tap + m]] = groups[m]
    half = buf.shape[0] // 2
    keep_ref[...] = buf[:half]
    send_ref[...] = buf[half:].astype(BF)


def join_owners(pos_ref, place_ref, keep_ref, got_ref, mine_ref, other_ref, o_ref, total):
    total[...] = keep_ref[...] + got_ref[...].astype(F32)
    core = pos_ref[4]
    for n in range(mine_ref.shape[0]):
        for ref, first in ((mine_ref, 16 * core), (other_ref, 16 * (1 - core))):
            at = place_ref[first + n]

            @pl.when(at < total.shape[0])
            def _(ref=ref, at=at, n=n):
                total[at] = ref[n].astype(F32)

    o_ref[...] = total[...].astype(BF).reshape(o_ref.shape)


def fold_last(r_ref, o_ref, total):
    value = r_ref[0].astype(F32)
    for n in range(1, r_ref.shape[0]):
        value = value + r_ref[n].astype(F32)
    total[...] = value.reshape(total.shape)
    width = total.shape[2]
    for i in range(total.shape[1]):
        o_ref[:, i * width : (i + 1) * width] = total[:, i, :]


def share_rows(pos_ref, kept_ref, got0, got1, *rest):
    *outs, total = rest
    half, each = got0.shape[0], total.shape[0] // 2
    for n, got in enumerate((got0, got1)):
        value = kept_ref[n * half : (n + 1) * half, :] + got[...].astype(F32)
        total[n * each : (n + 1) * each] = value.reshape(each, *total.shape[1:])
    for k, out in enumerate(outs):
        out[...] = total[:, jnp.bitwise_xor(pos_ref[0], k)].astype(out.dtype)


def swap_core(x):
    return lax.ppermute(x, "dp_2", [(0, 1), (1, 0)])


def pick(pos, centre):
    pixels, chans = centre.shape
    block = jax.ShapeDtypeStruct((pixels, chans // 4), BF)
    return call(select_channels, [block] * 4, 1, 1, 2 * pixels * chans * chans, 4 * pixels * chans, 14, name="pick")(
        pos, centre
    )


def turn(pos, got):
    pixels, width = got[0].shape
    return call(
        turn_pixels,
        jax.ShapeDtypeStruct((2, width, 2 * pixels), BF),
        1,
        4,
        8 * pixels * width * width,
        16 * pixels * width,
        12,
        [pltpu.VMEM((2, 2 * pixels, width), BF)],
        name="turn",
    )(pos, *got)


def split_pair(pos, kept, got):
    width = kept.shape[1]
    slices = kept.shape[0] // 64
    shape = (slices, 16, width)
    return call(
        share_rows,
        [jax.ShapeDtypeStruct(shape, F32)] + [jax.ShapeDtypeStruct(shape, BF)] * 3,
        1,
        3,
        kept.size,
        8 * kept.size,
        10,
        [pltpu.VMEM((slices, 4, 16, width), F32)],
        name="rows",
    )(pos, kept, *got)


def sum_pair(blocks):
    mine = blocks[0] + sum(block.astype(F32) for block in blocks[1:])
    return mine, swap_core(mine.astype(BF))


def place_slots(bucket_slot, core, slot_count):
    replicas = lax.axis_size(DP)
    capacity = slot_count // replicas
    owner = bucket_slot // capacity
    other = jnp.bitwise_xor(owner % 2, core)
    return other * (slot_count // 2) + (owner // 2) * capacity + bucket_slot % capacity


def tap_slots(pos, place, deltas, turned, slot_count):
    pixels, width = deltas[0].shape
    half = slot_count // 2
    return call(
        tap_grads,
        [jax.ShapeDtypeStruct((half, 16, width), F32), jax.ShapeDtypeStruct((half, 16, width), BF)],
        2,
        5,
        2 * 7 * 4 * pixels * width * width,
        8 * 1024 * 1024,
        26,
        [
            pltpu.VMEM((2, 2 * pixels, width), BF),
            pltpu.VMEM((2, 2 * pixels + 2 * RATE_C * SIDE, width), BF),
            pltpu.VMEM((slot_count, 16, width), F32),
        ],
        name="taps",
    )(pos, place, *deltas, turned)


def reduce_slots(pos, place, kept, sent, mine, other):
    half, rows, width = kept.shape
    chips = lax.axis_size("dp_0") * lax.axis_size("dp_1")
    each = half // chips
    total = call(
        join_owners,
        jax.ShapeDtypeStruct((chips, each * rows, width), BF),
        2,
        4,
        kept.size,
        8 * kept.size,
        12,
        [pltpu.VMEM((half, rows, width), F32)],
        name="owners",
    )(pos, place, kept, swap_core(sent), mine, other)
    total = lax.all_to_all(total, ("dp_0", "dp_1"), 0, 0, tiled=True)
    return call(
        fold_last,
        jax.ShapeDtypeStruct((each, rows * width), F32),
        0,
        1,
        kept.size,
        2 * kept.size,
        8,
        [pltpu.VMEM((each, rows, width), F32)],
        name="last",
    )(total)


def silu_slope(value):
    sig = jax.nn.sigmoid(value)
    return sig * (1.0 + value * (1.0 - sig))


RATES = (RATE_A, RATE_B, RATE_C)
SIDE = 24


def turned_by(x, shift, far):
    return jnp.where(far == 0, roll_cols(x, shift), roll_cols(x, SIDE - shift))


def rank_of(shape, far):
    at = lax.broadcasted_iota(jnp.int32, shape, 1)
    return jnp.where(far == 0, at, SIDE - 1 - at)


def row_marks(low, rate):
    lead = rate * SIDE
    whole = SIDE * SIDE

    def either(upper, lower):
        return pl.multiple_of(jnp.where(low == 0, upper, lower), 16)

    return dict(
        own=either(0, lead),
        out=either(lead, 0),
        theirs=either(whole, 0),
        inward_from=either(lead, 0),
        inward=either(0, 2 * lead),
        kept=either(lead, 0),
        inner=either(0, lead),
    )


def blocks(x):
    return x.reshape(x.shape[0] // SIDE, SIDE, x.shape[1])


def flat(x):
    return x.reshape(x.shape[0] * SIDE, x.shape[2])


def tap_copies(pos_ref, refs, jobs, held, sems):
    copies = []
    for branch, ref in enumerate(refs):
        for n, (above, across) in enumerate(jobs):
            a = 1 if above == 1 else jnp.where(pos_ref[2] == 0, above, 2 - above)
            b = 1 if across == 1 else jnp.where(pos_ref[3] == 0, across, 2 - across)
            width = ref.shape[3]
            to = held.at[branch, :, n * width : (n + 1) * width]
            copies.append(pltpu.make_async_copy(ref.at[a, b], to, sems.at[branch, n]))
    return copies


BRANCHES = ((2, RATE_C), (1, RATE_B), (0, RATE_A))
OUTER = ((0, 0), (1, 0), (0, 1), (0, 2), (2, 0))
INNER = ((1, 1), (1, 2), (2, 1), (2, 2))


def outer_parts(pos_ref, x_ref, wc_ref, wb_ref, wa_ref, pre_ref, row_ref, col_ref, diag_ref, ext, acc, y, held, sems):
    low, far = pos_ref[2], pos_ref[3]
    whole = SIDE * SIDE
    width = pre_ref.shape[2]
    copies = tap_copies(pos_ref, (wc_ref, wb_ref, wa_ref), OUTER, held, sems)
    for copy in copies:
        copy.start()
    first = 0
    for turn, (index, rate) in enumerate(BRANCHES):
        lead = rate * SIDE
        inside = whole - lead
        at = row_marks(low, rate)
        own_rows = pl.ds(at["own"], whole)
        their_rows = pl.ds(at["theirs"], lead)
        kept_rows = pl.ds(at["kept"], inside)
        to_row = slice(first, first + lead)
        first += lead
        count = len(OUTER)
        for copy in copies[turn * count : (turn + 1) * count]:
            copy.wait()
        y[...] = jnp.dot(x_ref[...], held[turn, :, : 4 * width], preferred_element_type=F32)
        ext[pl.ds(pl.multiple_of(whole - at["theirs"], 16), lead), :] = jnp.zeros((lead, width), F32)
        ext[pl.ds(at["out"], whole), :] = y[:, :width]
        ext[own_rows, :] += y[:, width : 2 * width]
        ext[pl.ds(at["inward"], inside), :] += jnp.dot(
            x_ref[pl.ds(at["inward_from"], inside), :], held[turn, :, 4 * width :], preferred_element_type=F32
        )
        own = blocks(ext[own_rows, :])
        ours = turned_by(own, rate, far)
        rank = rank_of(own.shape, far)
        pre_ref[index] = flat(jnp.where(rank >= rate, ours, 0.0))
        below = blocks(ext[their_rows, :])
        theirs = turned_by(below, rate, far)
        place = rank_of(below.shape, far)
        acc[:lead, :] = flat(jnp.where(place >= rate, theirs, 0.0))
        if rate == RATE_C:
            col_ref[:whole, :] = flat(jnp.where(rank < rate, ours, 0.0)).astype(BF)
            diag_ref[:lead, :] = flat(jnp.where(place < rate, theirs, 0.0)).astype(BF)
        elif rate == RATE_B:
            half = rate // 2
            col_ref[whole:, :] = flat(jnp.where(rank[:rate] < rate, ours[:rate], own[rate:])).astype(BF)
            part = place[:half] < rate
            diag_ref[RATE_C * SIDE :, :] = flat(jnp.where(part, theirs[:half], below[half:])).astype(BF)
        else:
            have = blocks(col_ref[:whole, :].astype(F32))
            col_ref[:whole, :] = flat(jnp.where(rank >= RATE_C, own, have)).astype(BF)
            have = blocks(diag_ref[:lead, :].astype(F32))
            diag_ref[:lead, :] = flat(jnp.where(place >= RATE_C, below, have)).astype(BF)
        next_from = pl.multiple_of(jnp.where(low == 0, inside, 0), 16)
        keep_from = pl.multiple_of(jnp.where(low == 0, 0, lead), 16)
        pre_ref[index, kept_rows, :] += y[pl.ds(keep_from, inside), 2 * width : 3 * width]
        own = blocks(y[pl.ds(keep_from, inside), 3 * width :])
        rank = rank_of(own.shape, far)
        pre_ref[index, kept_rows, :] += flat(jnp.where(rank < SIDE - rate, turned_by(own, rate, 1 - far), 0.0))
        below = blocks(y[pl.ds(next_from, lead), 3 * width :])
        theirs = flat(jnp.where(place < SIDE - rate, turned_by(below, rate, 1 - far), 0.0))
        row_ref[to_row, :] = (acc[:lead, :] + y[pl.ds(next_from, lead), 2 * width : 3 * width] + theirs).astype(BF)


def inner_parts(pos_ref, x_ref, part_ref, wp_ref, wc_ref, wb_ref, wa_ref, pre0_ref, pre_ref, y, z, held, sems):
    low, far = pos_ref[2], pos_ref[3]
    whole = SIDE * SIDE
    width = pre0_ref.shape[1]
    copies = tap_copies(pos_ref, (wc_ref, wb_ref, wa_ref), INNER, held, sems)
    for copy in copies:
        copy.start()
    pre0_ref[...] = jnp.dot(x_ref[...], wp_ref[...], preferred_element_type=F32)
    for turn, (index, rate) in enumerate(BRANCHES):
        lead = rate * SIDE
        inside = whole - lead
        at = row_marks(low, rate)
        from_rows = pl.ds(at["inward_from"], inside)
        to_rows = pl.ds(at["inner"], inside)
        count = len(INNER)
        for copy in copies[turn * count : (turn + 1) * count]:
            copy.wait()
        y[...] = jnp.dot(x_ref[...], held[turn, :, : 2 * width], preferred_element_type=F32)
        z[:inside, :] = jnp.dot(x_ref[from_rows, :], held[turn, :, 2 * width :], preferred_element_type=F32)
        y[to_rows, :] += z[:inside, :]
        own = blocks(y[:, width:])
        rank = rank_of(own.shape, far)
        moved = flat(jnp.where(rank < SIDE - rate, turned_by(own, rate, 1 - far), 0.0))
        pre_ref[index] = part_ref[index] + y[:, :width] + moved


def outer(pos, centre, w_rate_a, w_rate_b, w_rate_c):
    pixels, chans = centre.shape
    width = w_rate_a.shape[3]
    sends = (RATE_A + RATE_B + RATE_C) * SIDE
    shapes = [((3, pixels, width), F32), ((sends, width), BF), ((sends, width), BF), ((pixels, width), BF)]
    return call(
        outer_parts,
        [jax.ShapeDtypeStruct(*s) for s in shapes],
        1,
        1,
        2 * pixels * chans * width * 14,
        10 * MIB,
        28,
        [
            pltpu.VMEM(((SIDE + RATE_C) * SIDE, width), F32),
            pltpu.VMEM((RATE_C * SIDE, width), F32),
            pltpu.VMEM((pixels, 4 * width), F32),
            pltpu.VMEM((3, chans, len(OUTER) * width), BF),
            pltpu.SemaphoreType.DMA((3, len(OUTER))),
        ],
        name="outer",
        n_any=3,
    )(pos, centre, w_rate_c, w_rate_b, w_rate_a)


def inner(pos, centre, part, w_point, w_rate_a, w_rate_b, w_rate_c):
    pixels, chans = centre.shape
    width = w_point.shape[1]
    return call(
        inner_parts,
        [jax.ShapeDtypeStruct((pixels, width), F32), jax.ShapeDtypeStruct((3, pixels, width), F32)],
        1,
        3,
        2 * pixels * chans * width * 10,
        10 * MIB,
        26,
        [
            pltpu.VMEM((pixels, 2 * width), F32),
            pltpu.VMEM((pixels, 2 * width), F32),
            pltpu.VMEM((3, chans, len(INNER) * width), BF),
            pltpu.SemaphoreType.DMA((3, len(INNER))),
        ],
        name="inner",
        n_any=3,
    )(pos, centre, part, w_point, w_rate_c, w_rate_b, w_rate_a)


def merge_parts(
    pos_ref, pre0_ref, own_ref, row_ref, col_ref, diag_ref, cot_ref, wp_ref, joined_ref, g_ref, d0_ref, d3_ref, pre
):
    low = pos_ref[2]
    theirs = 1 - pos_ref[3]
    width = pre0_ref.shape[1]
    whole = SIDE * SIDE

    def rows_of(rate):
        return pl.multiple_of(jnp.where(low == 0, (SIDE - rate) * SIDE, 0), 16)

    pre[...] = own_ref[...]
    first = 0
    for index, rate in ((2, RATE_C), (1, RATE_B), (0, RATE_A)):
        lead = rate * SIDE
        pre[index, pl.ds(rows_of(rate), lead), :] += row_ref[first : first + lead, :].astype(F32)
        first += lead

    part = blocks(col_ref[:whole, :].astype(F32))
    rank = rank_of(part.shape, theirs)
    pre[2] += flat(jnp.where(rank < RATE_C, part, 0.0))
    pre[0] += flat(turned_by(jnp.where(rank >= RATE_C, part, 0.0), RATE_A, theirs))
    part = blocks(col_ref[whole:, :].astype(F32))
    rank = rank_of(part.shape, theirs)
    pre[1, : RATE_B * SIDE, :] += flat(jnp.where(rank < RATE_B, part, 0.0))
    pre[1, RATE_B * SIDE :, :] += flat(roll_cols(jnp.where(rank >= RATE_B, part, 0.0), RATE_B))

    part = blocks(diag_ref[: RATE_C * SIDE, :].astype(F32))
    rank = rank_of(part.shape, theirs)
    pre[2, pl.ds(rows_of(RATE_C), RATE_C * SIDE), :] += flat(jnp.where(rank < RATE_C, part, 0.0))
    few = part[:RATE_A]
    few = turned_by(jnp.where(rank[:RATE_A] >= RATE_C, few, 0.0), RATE_A, theirs)
    pre[0, pl.ds(rows_of(RATE_A), RATE_A * SIDE), :] += flat(few)
    part = blocks(diag_ref[RATE_C * SIDE :, :].astype(F32))
    rank = rank_of(part.shape, theirs)
    half = RATE_B // 2
    at = rows_of(RATE_B)
    pre[1, pl.ds(at, half * SIDE), :] += flat(jnp.where(rank < RATE_B, part, 0.0))
    last = pl.multiple_of(at + half * SIDE, 16)
    pre[1, pl.ds(last, half * SIDE), :] += flat(roll_cols(jnp.where(rank >= RATE_B, part, 0.0), RATE_B))

    slopes = {}
    for k in range(4):
        value = pre0_ref[...] if k == 0 else pre[k - 1]
        sig = jax.nn.sigmoid(value)
        joined_ref[:, k * width : (k + 1) * width] = (value * sig).astype(BF)
        if k in (0, 3):
            slopes[k] = sig * (1.0 + value * (1.0 - sig))
    proj_pre = jnp.dot(joined_ref[...], wp_ref[...], preferred_element_type=F32)
    g_proj = (cot_ref[...].astype(F32) * silu_slope(proj_pre)).astype(BF)
    g_ref[...] = g_proj
    for k, out in ((3, d3_ref), (0, d0_ref)):
        back = lax.dot_general(
            g_proj, wp_ref[k * width : (k + 1) * width, :], (((1,), (1,)), ((), ())), preferred_element_type=F32
        )
        out[...] = (back * slopes[k]).astype(BF)


def merge(pos, pre0, own, row, col, diag, cot, w_proj):
    pixels, width = pre0.shape
    block = jax.ShapeDtypeStruct((pixels, width), BF)
    return call(
        merge_parts,
        [jax.ShapeDtypeStruct((pixels, 4 * width), BF), block, block, block],
        1,
        7,
        2 * pixels * width * width * 6,
        6 * 1024 * 1024,
        18,
        [pltpu.VMEM((3, pixels, width), F32)],
        name="merge",
    )(pos, pre0, own, row, col, diag, cot, w_proj)


def pair_grads(pos_ref, joined_ref, g_ref, x_ref, d0_ref, keep_ref, *send_refs):
    core = pos_ref[4]
    over = (((0,), (0,)), ((), ()))
    grad_proj = lax.dot_general(joined_ref[...], g_ref[...], over, preferred_element_type=F32)
    grad_point = lax.dot_general(x_ref[...], d0_ref[...], over, preferred_element_type=F32)
    keep_ref[...] = jnp.where(core == 0, grad_proj, grad_point)
    half = send_refs[0].shape[0]
    for k, send_ref in enumerate(send_refs):
        part = slice(k * half, (k + 1) * half)
        send_ref[...] = jnp.where(core == 0, grad_point[part], grad_proj[part]).astype(BF)


def shards(features, cotangent, w_point, w_rate_a, w_rate_b, w_rate_c, w_proj, bucket_slot):
    image = features[0]
    rows_dev, cols_dev, chans = image.shape
    pixels = rows_dev * cols_dev
    width = w_point.shape[1]
    row, col, core = (lax.axis_index(n) for n in ("row", "col", "dp_2"))
    at_y, at_z = lax.axis_index("dp_0"), lax.axis_index("dp_1")
    pos = jnp.stack([2 * row + col, at_y, row, col, core, at_z]).astype(jnp.int32)
    replicas = lax.axis_size(DP)
    slot_count = replicas * (bucket_slot.shape[0] // replicas + 1)
    place = place_slots(bucket_slot, core, slot_count)
    centre = image.reshape(pixels, chans)
    weights = [pltpu.with_memory_space_constraint(w, pltpu.HBM) for w in (w_rate_a, w_rate_b, w_rate_c)]
    picked = pick(pos, centre)
    centre, *picked = lax.optimization_barrier((centre, *picked))
    got = [picked[0]] + [flip(picked[k], k) for k in (1, 2, 3)]
    part, *parts = outer(pos, centre, *weights)
    part, got = lax.optimization_barrier((part, got))
    to_row, to_col, to_diag = parts
    parts = [flip(to_row, 2), flip(to_col, 1), flip(to_diag, 3)]
    turned = turn(pos, got)
    pre0, own = inner(pos, centre, part, w_point, *weights)
    parts, pre0, own, turned = lax.optimization_barrier((parts, pre0, own, turned))
    joined, g_proj, delta0, delta3 = merge(
        pos, pre0, own, *parts, cotangent[0].reshape(pixels, width), w_proj
    )
    shared = [delta3] + [flip(delta3, k) for k in (1, 2, 3)]
    block = (4 * width, width)
    kept, *sent = call(
        pair_grads,
        [jax.ShapeDtypeStruct(block, F32)] + [jax.ShapeDtypeStruct((2 * width, width), BF)] * 2,
        1,
        4,
        4 * pixels * chans * width,
        4 * 1024 * 1024,
        16,
        name="pair",
    )(pos, joined, g_proj, centre, delta0)
    got = [swap_core(part) for part in sent]
    got, shared = lax.optimization_barrier((got, shared))
    by_owner = split_pair(pos, kept, got)
    by_owner, shared = lax.optimization_barrier((by_owner, shared))
    by_owner = [by_owner[0]] + [flip(by_owner[k], k) for k in (1, 2, 3)]
    kept, sent = tap_slots(pos, place, shared, turned, slot_count)
    sent, by_owner = lax.optimization_barrier((sent, by_owner))
    mine, other = sum_pair(by_owner)
    return reduce_slots(pos, place, kept, sent, mine, other)


def solution(mesh):
    torus = Mesh(
        mesh.devices.reshape(mesh.shape["row"], mesh.shape["col"], 4, 4, 2),
        ("row", "col", "dp_0", "dp_1", "dp_2"),
    )
    in_specs = (P(DP, "row", "col", None), P(DP, "row", "col", None), P(), P(), P(), P(), P(), P())
    out_specs = P(DP, ("row", "col"))
    return jax.shard_map(
        shards, mesh=torus, in_specs=in_specs, out_specs=out_specs, check_vma=False
    )
```

```python
import jax
import jax.numpy as jnp
from jax import lax
from jax.experimental import pallas as pl
from jax.experimental.pallas import tpu as pltpu
from jax.sharding import Mesh
from jax.sharding import PartitionSpec as P

RATE_A = 6
RATE_B = 12
RATE_C = 18
DP = ("dp_0", "dp_1", "dp_2")


BF = jnp.bfloat16
F32 = jnp.float32
MIB = 1024 * 1024


def flip(x, mask):
    if mask == 1:
        return lax.ppermute(x, "col", [(0, 1), (1, 0)])
    if mask == 2:
        return lax.ppermute(x, "row", [(0, 1), (1, 0)])
    return lax.ppermute(x, ("row", "col"), [(0, 3), (3, 0), (1, 2), (2, 1)])


def smem():
    return pl.BlockSpec(memory_space=pltpu.SMEM)


def vmem():
    return pl.BlockSpec(memory_space=pltpu.VMEM)


def call(body, outs, n_smem, n_vmem, flops, nbytes, limit, scratch=(), name=None, n_any=0):
    return pl.pallas_call(
        body,
        out_shape=outs,
        in_specs=[smem()] * n_smem + [vmem()] * n_vmem + [pl.BlockSpec(memory_space=pltpu.HBM)] * n_any,
        out_specs=jax.tree.map(lambda _: vmem(), outs),
        scratch_shapes=list(scratch),
        compiler_params=pltpu.CompilerParams(vmem_limit_bytes=limit * MIB),
        cost_estimate=pl.CostEstimate(flops=flops, bytes_accessed=nbytes, transcendentals=0),
        name=name,
    )


def select_channels(pos_ref, x_ref, *rest):
    *o_refs, held, picks, sems = rest
    chans = x_ref.shape[1]
    width = o_refs[0].shape[1]
    pieces = sems.shape[0]
    each = x_ref.shape[0] // pieces
    copies = []
    for n in range(pieces):
        part = pl.ds(n * each, each)
        copies.append(pltpu.make_async_copy(x_ref.at[part, :], held.at[part, :], sems.at[n]))
        copies[n].start()
    source = lax.broadcasted_iota(jnp.int32, (chans, width), 0)
    col = lax.broadcasted_iota(jnp.int32, (1, width), 1)
    wanted = 64 * (col // 16) + col % 16
    for k in range(len(o_refs)):
        c = jnp.bitwise_xor(pos_ref[0], k)
        picks[:, k * width : (k + 1) * width] = jnp.where(source == wanted + 16 * c, 1.0, 0.0).astype(BF)
    for n in range(pieces):
        copies[n].wait()
        part = slice(n * each, (n + 1) * each)
        for k, o_ref in enumerate(o_refs):
            pick = picks[:, k * width : (k + 1) * width]
            o_ref[part, :] = jnp.dot(held[part, :], pick, preferred_element_type=F32).astype(BF)


def turn_pixels(pos_ref, x0, x1, x2, x3, o_ref, held):
    pixels, width = x0.shape
    for k, x in enumerate((x0, x1, x2, x3)):
        s = jnp.bitwise_xor(pos_ref[0], k)
        held[s % 2, pl.ds((s // 2) * pixels, pixels), :] = x[...]
    eye = (
        lax.broadcasted_iota(jnp.int32, (width, width), 0)
        == lax.broadcasted_iota(jnp.int32, (width, width), 1)
    ).astype(F32).astype(BF)
    for g in range(2):
        o_ref[g] = lax.dot_general(
            eye, held[g], (((1,), (1,)), ((), ())), preferred_element_type=F32
        ).astype(BF)


def roll_cols(x, shift):
    return jnp.concatenate([x[:, x.shape[1] - shift :], x[:, : x.shape[1] - shift]], axis=1)


def tap_grads(pos_ref, place_ref, d0, d1, d2, d3, xt_ref, keep_ref, send_ref, held, padded, buf):
    side = RATE_C
    pixels, width = d0.shape
    cols = 24
    rows = pixels // cols
    for k, d in enumerate((d0, d1, d2, d3)):
        s = jnp.bitwise_xor(pos_ref[0], k)
        held[s % 2, pl.ds((s // 2) * pixels, pixels), :] = d[...]
    buf[...] = jnp.zeros_like(buf)
    tall = 2 * pixels
    lead = side * cols
    zeros = jnp.zeros((2, lead, width), BF)
    halves = [held[g].astype(F32).reshape(2 * rows, cols, width) for g in range(2)]
    at = lax.broadcasted_iota(jnp.int32, (2 * rows, cols, width), 1)
    rest = cols - side
    for across in (-1, 0, 1):
        padded[:, pl.ds(0, lead), :] = zeros
        padded[:, pl.ds(lead + tall, lead), :] = zeros
        if across == 0:
            shifted = halves
        elif across == 1:
            rolled = [roll_cols(h, side) for h in halves]
            shifted = [
                jnp.where(at >= side, rolled[0], 0.0),
                jnp.where(at < side, rolled[0], rolled[1]),
            ]
        else:
            rolled = [roll_cols(h, rest) for h in halves]
            shifted = [
                jnp.where(at < rest, rolled[0], rolled[1]),
                jnp.where(at < rest, rolled[1], 0.0),
            ]
        for g in range(2):
            padded[g, pl.ds(lead, tall), :] = shifted[g].reshape(tall, width).astype(BF)
        for above in (-1, 0, 1):
            first, last = {-1: (0, 32), 0: (0, 48), 1: (16, 48)}[above]
            base = first - side * above + side
            total = None
            for g in range(2):
                part = jnp.dot(
                    xt_ref[g, :, first * cols : last * cols],
                    padded[g, base * cols : (base + last - first) * cols, :],
                    preferred_element_type=F32,
                )
                total = part if total is None else total + part
            tap = 3 * (above + 1) + across + 1
            groups = total.reshape(width // 16, 16, width)
            for m in range(width // 16):
                buf[place_ref[32 + 16 * tap + m]] = groups[m]
    half = buf.shape[0] // 2
    keep_ref[...] = buf[:half]
    send_ref[...] = buf[half:].astype(BF)


def join_owners(pos_ref, place_ref, keep_ref, got_ref, mine_ref, other_ref, o_ref, total):
    total[...] = keep_ref[...] + got_ref[...].astype(F32)
    core = pos_ref[4]
    for n in range(mine_ref.shape[0]):
        for ref, first in ((mine_ref, 16 * core), (other_ref, 16 * (1 - core))):
            at = place_ref[first + n]

            @pl.when(at < total.shape[0])
            def _(ref=ref, at=at, n=n):
                total[at] = ref[n].astype(F32)

    o_ref[...] = total[...].astype(BF).reshape(o_ref.shape)


def fold_last(r_ref, o_ref, total):
    value = r_ref[0].astype(F32)
    for n in range(1, r_ref.shape[0]):
        value = value + r_ref[n].astype(F32)
    total[...] = value.reshape(total.shape)
    width = total.shape[2]
    for i in range(total.shape[1]):
        o_ref[:, i * width : (i + 1) * width] = total[:, i, :]


def share_rows(pos_ref, kept_ref, got0, got1, *rest):
    *outs, total = rest
    half, each = got0.shape[0], total.shape[0] // 2
    for n, got in enumerate((got0, got1)):
        value = kept_ref[n * half : (n + 1) * half, :] + got[...].astype(F32)
        total[n * each : (n + 1) * each] = value.reshape(each, *total.shape[1:])
    for k, out in enumerate(outs):
        out[...] = total[:, jnp.bitwise_xor(pos_ref[0], k)].astype(out.dtype)


def swap_core(x):
    return lax.ppermute(x, "dp_2", [(0, 1), (1, 0)])


def pick(pos, centre):
    pixels, chans = centre.shape
    block = jax.ShapeDtypeStruct((pixels, chans // 4), BF)
    return call(
        select_channels,
        [block] * 4,
        1,
        0,
        2 * pixels * chans * chans,
        4 * pixels * chans,
        14,
        [
            pltpu.VMEM((pixels, chans), BF),
            pltpu.VMEM((chans, chans), BF),
            pltpu.SemaphoreType.DMA((2,)),
        ],
        name="pick",
        n_any=1,
    )(pos, pltpu.with_memory_space_constraint(centre, pltpu.HBM))


def turn(pos, got):
    pixels, width = got[0].shape
    return call(
        turn_pixels,
        jax.ShapeDtypeStruct((2, width, 2 * pixels), BF),
        1,
        4,
        8 * pixels * width * width,
        16 * pixels * width,
        12,
        [pltpu.VMEM((2, 2 * pixels, width), BF)],
        name="turn",
    )(pos, *got)


def split_pair(pos, kept, got):
    width = kept.shape[1]
    slices = kept.shape[0] // 64
    shape = (slices, 16, width)
    return call(
        share_rows,
        [jax.ShapeDtypeStruct(shape, F32)] + [jax.ShapeDtypeStruct(shape, BF)] * 3,
        1,
        3,
        kept.size,
        8 * kept.size,
        10,
        [pltpu.VMEM((slices, 4, 16, width), F32)],
        name="rows",
    )(pos, kept, *got)


def sum_pair(blocks):
    mine = blocks[0] + sum(block.astype(F32) for block in blocks[1:])
    return mine, swap_core(mine.astype(BF))


def place_slots(bucket_slot, core, slot_count):
    replicas = lax.axis_size(DP)
    capacity = slot_count // replicas
    owner = bucket_slot // capacity
    other = jnp.bitwise_xor(owner % 2, core)
    return other * (slot_count // 2) + (owner // 2) * capacity + bucket_slot % capacity


def tap_slots(pos, place, deltas, turned, slot_count):
    pixels, width = deltas[0].shape
    half = slot_count // 2
    return call(
        tap_grads,
        [jax.ShapeDtypeStruct((half, 16, width), F32), jax.ShapeDtypeStruct((half, 16, width), BF)],
        2,
        5,
        2 * 7 * 4 * pixels * width * width,
        8 * 1024 * 1024,
        26,
        [
            pltpu.VMEM((2, 2 * pixels, width), BF),
            pltpu.VMEM((2, 2 * pixels + 2 * RATE_C * SIDE, width), BF),
            pltpu.VMEM((slot_count, 16, width), F32),
        ],
        name="taps",
    )(pos, place, *deltas, turned)


def reduce_slots(pos, place, kept, sent, mine, other):
    half, rows, width = kept.shape
    chips = lax.axis_size("dp_0") * lax.axis_size("dp_1")
    each = half // chips
    total = call(
        join_owners,
        jax.ShapeDtypeStruct((chips, each * rows, width), BF),
        2,
        4,
        kept.size,
        8 * kept.size,
        12,
        [pltpu.VMEM((half, rows, width), F32)],
        name="owners",
    )(pos, place, kept, swap_core(sent), mine, other)
    total = lax.all_to_all(total, ("dp_0", "dp_1"), 0, 0, tiled=True)
    return call(
        fold_last,
        jax.ShapeDtypeStruct((each, rows * width), F32),
        0,
        1,
        kept.size,
        2 * kept.size,
        8,
        [pltpu.VMEM((each, rows, width), F32)],
        name="last",
    )(total)


def silu_slope(value):
    sig = jax.nn.sigmoid(value)
    return sig * (1.0 + value * (1.0 - sig))


RATES = (RATE_A, RATE_B, RATE_C)
SIDE = 24


def turned_by(x, shift, far):
    return roll_cols(x, shift if far == 0 else SIDE - shift)


def rank_of(shape, far):
    at = lax.broadcasted_iota(jnp.int32, shape, 1)
    return at if far == 0 else SIDE - 1 - at


def by_side(side, body):
    for far in range(2):

        @pl.when(side == far)
        def _(far=far):
            body(far)


def row_marks(low, rate):
    lead = rate * SIDE
    whole = SIDE * SIDE

    def either(upper, lower):
        return pl.multiple_of(jnp.where(low == 0, upper, lower), 16)

    return dict(
        own=either(0, lead),
        out=either(lead, 0),
        theirs=either(whole, 0),
        inward_from=either(lead, 0),
        inward=either(0, 2 * lead),
        kept=either(lead, 0),
        inner=either(0, lead),
    )


def blocks(x):
    return x.reshape(x.shape[0] // SIDE, SIDE, x.shape[1])


def flat(x):
    return x.reshape(x.shape[0] * SIDE, x.shape[2])


def tap_copies(pos_ref, refs, jobs, held, sems):
    copies = []
    for branch, ref in enumerate(refs):
        for n, (above, across) in enumerate(jobs):
            a = 1 if above == 1 else jnp.where(pos_ref[2] == 0, above, 2 - above)
            b = 1 if across == 1 else jnp.where(pos_ref[3] == 0, across, 2 - across)
            width = ref.shape[3]
            to = held.at[branch, :, n * width : (n + 1) * width]
            copies.append(pltpu.make_async_copy(ref.at[a, b], to, sems.at[branch, n]))
    return copies


BRANCHES = ((2, RATE_C), (1, RATE_B), (0, RATE_A))
OUTER = ((0, 0), (1, 0), (0, 1), (0, 2), (2, 0))
INNER = ((1, 1), (1, 2), (2, 1), (2, 2))


def outer_parts(pos_ref, x_ref, wc_ref, wb_ref, wa_ref, pre_ref, row_ref, col_ref, diag_ref, ext, acc, y, held, sems):
    low = pos_ref[2]
    whole = SIDE * SIDE
    width = pre_ref.shape[2]
    count = len(OUTER)
    copies = tap_copies(pos_ref, (wc_ref, wb_ref, wa_ref), OUTER, held, sems)
    for copy in copies:
        copy.start()

    def products(turn):
        rate = BRANCHES[turn][1]
        at = row_marks(low, rate)
        inside = whole - rate * SIDE
        for copy in copies[turn * count : (turn + 1) * count]:
            copy.wait()
        y[turn] = jnp.dot(x_ref[...], held[turn, :, : 4 * width], preferred_element_type=F32)
        acc[turn, :inside, :] = jnp.dot(
            x_ref[pl.ds(at["inward_from"], inside), :], held[turn, :, 4 * width :], preferred_element_type=F32
        )

    def sums(turn, far):
        index, rate = BRANCHES[turn]
        lead = rate * SIDE
        inside = whole - lead
        at = row_marks(low, rate)
        own_rows = pl.ds(at["own"], whole)
        their_rows = pl.ds(at["theirs"], lead)
        kept_rows = pl.ds(at["kept"], inside)
        first = sum(r for _, r in BRANCHES[:turn]) * SIDE
        ext[pl.ds(pl.multiple_of(whole - at["theirs"], 16), lead), :] = jnp.zeros((lead, width), F32)
        ext[pl.ds(at["out"], whole), :] = y[turn, :, :width]
        ext[own_rows, :] += y[turn, :, width : 2 * width]
        ext[pl.ds(at["inward"], inside), :] += acc[turn, :inside, :]
        own = blocks(ext[own_rows, :])
        ours = turned_by(own, rate, far)
        rank = rank_of(own.shape, far)
        pre_ref[index] = flat(jnp.where(rank >= rate, ours, 0.0))
        below = blocks(ext[their_rows, :])
        theirs = turned_by(below, rate, far)
        place = rank_of(below.shape, far)
        if rate == RATE_C:
            col_ref[:whole, :] = flat(jnp.where(rank < rate, ours, 0.0)).astype(BF)
            diag_ref[:lead, :] = flat(jnp.where(place < rate, theirs, 0.0)).astype(BF)
        elif rate == RATE_B:
            half = rate // 2
            col_ref[whole:, :] = flat(jnp.where(rank[:rate] < rate, ours[:rate], own[rate:])).astype(BF)
            part = place[:half] < rate
            diag_ref[RATE_C * SIDE :, :] = flat(jnp.where(part, theirs[:half], below[half:])).astype(BF)
        else:
            have = blocks(col_ref[:whole, :].astype(F32))
            col_ref[:whole, :] = flat(jnp.where(rank >= RATE_C, own, have)).astype(BF)
            have = blocks(diag_ref[:lead, :].astype(F32))
            diag_ref[:lead, :] = flat(jnp.where(place >= RATE_C, below, have)).astype(BF)
        next_rows = pl.ds(pl.multiple_of(jnp.where(low == 0, inside, 0), 16), lead)
        keep_rows = pl.ds(pl.multiple_of(jnp.where(low == 0, 0, lead), 16), inside)
        own = blocks(y[turn, keep_rows, 3 * width :])
        moved = flat(jnp.where(rank_of(own.shape, far) < SIDE - rate, turned_by(own, rate, 1 - far), 0.0))
        pre_ref[index, kept_rows, :] += y[turn, keep_rows, 2 * width : 3 * width] + moved
        below = blocks(y[turn, next_rows, 3 * width :])
        total = jnp.where(place < SIDE - rate, turned_by(below, rate, 1 - far), 0.0)
        total = flat(total + jnp.where(place >= rate, theirs, 0.0))
        row_ref[first : first + lead, :] = (total + y[turn, next_rows, 2 * width : 3 * width]).astype(BF)

    def body(far):
        products(0)
        products(1)
        sums(0, far)
        products(2)
        sums(1, far)
        sums(2, far)

    by_side(pos_ref[3], body)


def inner_parts(pos_ref, x_ref, part_ref, wp_ref, wc_ref, wb_ref, wa_ref, pre0_ref, pre_ref, y, z, held, sems):
    low = pos_ref[2]
    whole = SIDE * SIDE
    width = pre0_ref.shape[1]
    count = len(INNER)
    copies = tap_copies(pos_ref, (wc_ref, wb_ref, wa_ref), INNER, held, sems)
    for copy in copies:
        copy.start()
    pre0_ref[...] = jnp.dot(x_ref[...], wp_ref[...], preferred_element_type=F32)

    def body(far):
        for turn, (index, rate) in enumerate(BRANCHES):
            inside = whole - rate * SIDE
            at = row_marks(low, rate)
            from_rows = pl.ds(at["inward_from"], inside)
            to_rows = pl.ds(at["inner"], inside)
            for copy in copies[turn * count : (turn + 1) * count]:
                copy.wait()
            y[...] = jnp.dot(x_ref[...], held[turn, :, : 2 * width], preferred_element_type=F32)
            z[:inside, :] = jnp.dot(x_ref[from_rows, :], held[turn, :, 2 * width :], preferred_element_type=F32)
            y[to_rows, :] += z[:inside, :]
            own = blocks(y[:, width:])
            rank = rank_of(own.shape, far)
            moved = flat(jnp.where(rank < SIDE - rate, turned_by(own, rate, 1 - far), 0.0))
            pre_ref[index] = part_ref[index] + y[:, :width] + moved

    by_side(pos_ref[3], body)


def outer(pos, centre, w_rate_a, w_rate_b, w_rate_c):
    pixels, chans = centre.shape
    width = w_rate_a.shape[3]
    sends = (RATE_A + RATE_B + RATE_C) * SIDE
    shapes = [((3, pixels, width), F32), ((sends, width), BF), ((sends, width), BF), ((pixels, width), BF)]
    return call(
        outer_parts,
        [jax.ShapeDtypeStruct(*s) for s in shapes],
        1,
        1,
        2 * pixels * chans * width * 14,
        10 * MIB,
        36,
        [
            pltpu.VMEM(((SIDE + RATE_C) * SIDE, width), F32),
            pltpu.VMEM((3, pixels, width), F32),
            pltpu.VMEM((3, pixels, 4 * width), F32),
            pltpu.VMEM((3, chans, len(OUTER) * width), BF),
            pltpu.SemaphoreType.DMA((3, len(OUTER))),
        ],
        name="outer",
        n_any=3,
    )(pos, centre, w_rate_c, w_rate_b, w_rate_a)


def inner(pos, centre, part, w_point, w_rate_a, w_rate_b, w_rate_c):
    pixels, chans = centre.shape
    width = w_point.shape[1]
    return call(
        inner_parts,
        [jax.ShapeDtypeStruct((pixels, width), F32), jax.ShapeDtypeStruct((3, pixels, width), F32)],
        1,
        3,
        2 * pixels * chans * width * 10,
        10 * MIB,
        26,
        [
            pltpu.VMEM((pixels, 2 * width), F32),
            pltpu.VMEM((pixels, 2 * width), F32),
            pltpu.VMEM((3, chans, len(INNER) * width), BF),
            pltpu.SemaphoreType.DMA((3, len(INNER))),
        ],
        name="inner",
        n_any=3,
    )(pos, centre, part, w_point, w_rate_c, w_rate_b, w_rate_a)


def merge_parts(
    pos_ref, pre0_ref, own_ref, row_ref, col_ref, diag_ref, cot_ref, wp_ref, joined_ref, g_ref, d0_ref, d3_ref, pre
):
    low = pos_ref[2]
    width = pre0_ref.shape[1]
    whole = SIDE * SIDE

    def rows_of(rate):
        return pl.multiple_of(jnp.where(low == 0, (SIDE - rate) * SIDE, 0), 16)

    pre[...] = own_ref[...]
    first = 0
    for index, rate in ((2, RATE_C), (1, RATE_B), (0, RATE_A)):
        lead = rate * SIDE
        pre[index, pl.ds(rows_of(rate), lead), :] += row_ref[first : first + lead, :].astype(F32)
        first += lead

    def body(far):
        theirs = 1 - far
        part = blocks(col_ref[:whole, :].astype(F32))
        rank = rank_of(part.shape, theirs)
        pre[2] += flat(jnp.where(rank < RATE_C, part, 0.0))
        pre[0] += flat(turned_by(jnp.where(rank >= RATE_C, part, 0.0), RATE_A, theirs))
        part = blocks(col_ref[whole:, :].astype(F32))
        rank = rank_of(part.shape, theirs)
        pre[1, : RATE_B * SIDE, :] += flat(jnp.where(rank < RATE_B, part, 0.0))
        pre[1, RATE_B * SIDE :, :] += flat(roll_cols(jnp.where(rank >= RATE_B, part, 0.0), RATE_B))

        part = blocks(diag_ref[: RATE_C * SIDE, :].astype(F32))
        rank = rank_of(part.shape, theirs)
        pre[2, pl.ds(rows_of(RATE_C), RATE_C * SIDE), :] += flat(jnp.where(rank < RATE_C, part, 0.0))
        few = part[:RATE_A]
        few = turned_by(jnp.where(rank[:RATE_A] >= RATE_C, few, 0.0), RATE_A, theirs)
        pre[0, pl.ds(rows_of(RATE_A), RATE_A * SIDE), :] += flat(few)
        part = blocks(diag_ref[RATE_C * SIDE :, :].astype(F32))
        rank = rank_of(part.shape, theirs)
        half = RATE_B // 2
        at = rows_of(RATE_B)
        pre[1, pl.ds(at, half * SIDE), :] += flat(jnp.where(rank < RATE_B, part, 0.0))
        last = pl.multiple_of(at + half * SIDE, 16)
        pre[1, pl.ds(last, half * SIDE), :] += flat(roll_cols(jnp.where(rank >= RATE_B, part, 0.0), RATE_B))

    by_side(pos_ref[3], body)
    slopes = {}
    for k in range(4):
        value = pre0_ref[...] if k == 0 else pre[k - 1]
        sig = jax.nn.sigmoid(value)
        joined_ref[:, k * width : (k + 1) * width] = (value * sig).astype(BF)
        if k in (0, 3):
            slopes[k] = sig * (1.0 + value * (1.0 - sig))
    proj_pre = jnp.dot(joined_ref[...], wp_ref[...], preferred_element_type=F32)
    g_proj = (cot_ref[...].astype(F32) * silu_slope(proj_pre)).astype(BF)
    g_ref[...] = g_proj
    for k, out in ((3, d3_ref), (0, d0_ref)):
        back = lax.dot_general(
            g_proj, wp_ref[k * width : (k + 1) * width, :], (((1,), (1,)), ((), ())), preferred_element_type=F32
        )
        out[...] = (back * slopes[k]).astype(BF)


def merge(pos, pre0, own, row, col, diag, cot, w_proj):
    pixels, width = pre0.shape
    block = jax.ShapeDtypeStruct((pixels, width), BF)
    return call(
        merge_parts,
        [jax.ShapeDtypeStruct((pixels, 4 * width), BF), block, block, block],
        1,
        7,
        2 * pixels * width * width * 6,
        6 * 1024 * 1024,
        18,
        [pltpu.VMEM((3, pixels, width), F32)],
        name="merge",
    )(pos, pre0, own, row, col, diag, cot, w_proj)


def pair_grads(pos_ref, joined_ref, g_ref, x_ref, d0_ref, keep_ref, *send_refs):
    core = pos_ref[4]
    over = (((0,), (0,)), ((), ()))
    grad_proj = lax.dot_general(joined_ref[...], g_ref[...], over, preferred_element_type=F32)
    grad_point = lax.dot_general(x_ref[...], d0_ref[...], over, preferred_element_type=F32)
    keep_ref[...] = jnp.where(core == 0, grad_proj, grad_point)
    half = send_refs[0].shape[0]
    for k, send_ref in enumerate(send_refs):
        part = slice(k * half, (k + 1) * half)
        send_ref[...] = jnp.where(core == 0, grad_point[part], grad_proj[part]).astype(BF)


def shards(features, cotangent, w_point, w_rate_a, w_rate_b, w_rate_c, w_proj, bucket_slot):
    image = features[0]
    rows_dev, cols_dev, chans = image.shape
    pixels = rows_dev * cols_dev
    width = w_point.shape[1]
    row, col, core = (lax.axis_index(n) for n in ("row", "col", "dp_2"))
    at_y, at_z = lax.axis_index("dp_0"), lax.axis_index("dp_1")
    pos = jnp.stack([2 * row + col, at_y, row, col, core, at_z]).astype(jnp.int32)
    replicas = lax.axis_size(DP)
    slot_count = replicas * (bucket_slot.shape[0] // replicas + 1)
    place = place_slots(bucket_slot, core, slot_count)
    centre = image.reshape(pixels, chans)
    weights = [pltpu.with_memory_space_constraint(w, pltpu.HBM) for w in (w_rate_a, w_rate_b, w_rate_c)]
    picked = pick(pos, centre)
    centre, *picked = lax.optimization_barrier((centre, *picked))
    got = [picked[0]] + [flip(picked[k], k) for k in (1, 2, 3)]
    part, *parts = outer(pos, centre, *weights)
    part, got = lax.optimization_barrier((part, got))
    to_row, to_col, to_diag = parts
    parts = [flip(to_row, 2), flip(to_col, 1), flip(to_diag, 3)]
    turned = turn(pos, got)
    pre0, own = inner(pos, centre, part, w_point, *weights)
    parts, pre0, own, turned = lax.optimization_barrier((parts, pre0, own, turned))
    joined, g_proj, delta0, delta3 = merge(
        pos, pre0, own, *parts, cotangent[0].reshape(pixels, width), w_proj
    )
    shared = [delta3] + [flip(delta3, k) for k in (1, 2, 3)]
    block = (4 * width, width)
    kept, *sent = call(
        pair_grads,
        [jax.ShapeDtypeStruct(block, F32)] + [jax.ShapeDtypeStruct((2 * width, width), BF)] * 2,
        1,
        4,
        4 * pixels * chans * width,
        4 * 1024 * 1024,
        16,
        name="pair",
    )(pos, joined, g_proj, centre, delta0)
    got = [swap_core(part) for part in sent]
    got, shared = lax.optimization_barrier((got, shared))
    by_owner = split_pair(pos, kept, got)
    by_owner, shared = lax.optimization_barrier((by_owner, shared))
    by_owner = [by_owner[0]] + [flip(by_owner[k], k) for k in (1, 2, 3)]
    kept, sent = tap_slots(pos, place, shared, turned, slot_count)
    sent, by_owner = lax.optimization_barrier((sent, by_owner))
    mine, other = sum_pair(by_owner)
    return reduce_slots(pos, place, kept, sent, mine, other)


def solution(mesh):
    torus = Mesh(
        mesh.devices.reshape(mesh.shape["row"], mesh.shape["col"], 4, 4, 2),
        ("row", "col", "dp_0", "dp_1", "dp_2"),
    )
    in_specs = (P(DP, "row", "col", None), P(DP, "row", "col", None), P(), P(), P(), P(), P(), P())
    out_specs = P(DP, ("row", "col"))
    return jax.shard_map(
        shards, mesh=torus, in_specs=in_specs, out_specs=out_specs, check_vma=False
    )
```

```python
import functools

import jax
import jax.numpy as jnp
from jax import lax
from jax.experimental import pallas as pl
from jax.experimental.pallas import tpu as pltpu
from jax.sharding import Mesh
from jax.sharding import PartitionSpec as P

RATE_A = 6
RATE_B = 12
RATE_C = 18
DP = ("dp_0", "dp_1", "dp_2")


BF = jnp.bfloat16
F32 = jnp.float32
MIB = 1024 * 1024


def flip(x, mask):
    if mask == 1:
        return lax.ppermute(x, "col", [(0, 1), (1, 0)])
    if mask == 2:
        return lax.ppermute(x, "row", [(0, 1), (1, 0)])
    return lax.ppermute(x, ("row", "col"), [(0, 3), (3, 0), (1, 2), (2, 1)])


def smem():
    return pl.BlockSpec(memory_space=pltpu.SMEM)


def vmem():
    return pl.BlockSpec(memory_space=pltpu.VMEM)


def call(body, outs, n_smem, n_vmem, flops, nbytes, limit, scratch=(), name=None, n_any=0):
    return pl.pallas_call(
        body,
        out_shape=outs,
        in_specs=[smem()] * n_smem + [vmem()] * n_vmem + [pl.BlockSpec(memory_space=pltpu.HBM)] * n_any,
        out_specs=jax.tree.map(lambda _: vmem(), outs),
        scratch_shapes=list(scratch),
        compiler_params=pltpu.CompilerParams(vmem_limit_bytes=limit * MIB),
        cost_estimate=pl.CostEstimate(flops=flops, bytes_accessed=nbytes, transcendentals=0),
        name=name,
    )


def select_channels(pos_ref, x_ref, *rest):
    *o_refs, held, picks, sems = rest
    chans = x_ref.shape[1]
    width = o_refs[0].shape[1]
    pieces = sems.shape[0]
    each = x_ref.shape[0] // pieces
    copies = []
    for n in range(pieces):
        part = pl.ds(n * each, each)
        copies.append(pltpu.make_async_copy(x_ref.at[part, :], held.at[part, :], sems.at[n]))
        copies[n].start()
    source = lax.broadcasted_iota(jnp.int32, (chans, width), 0)
    col = lax.broadcasted_iota(jnp.int32, (1, width), 1)
    wanted = 64 * (col // 16) + col % 16
    for k in range(len(o_refs)):
        c = jnp.bitwise_xor(pos_ref[0], k)
        picks[:, k * width : (k + 1) * width] = jnp.where(source == wanted + 16 * c, 1.0, 0.0).astype(BF)
    for n in range(pieces):
        copies[n].wait()
        part = slice(n * each, (n + 1) * each)
        for k, o_ref in enumerate(o_refs):
            pick = picks[:, k * width : (k + 1) * width]
            o_ref[part, :] = jnp.dot(held[part, :], pick, preferred_element_type=F32).astype(BF)


def turn_pixels(pos_ref, x0, x1, x2, x3, o_ref, held):
    pixels, width = x0.shape
    for k, x in enumerate((x0, x1, x2, x3)):
        s = jnp.bitwise_xor(pos_ref[0], k)
        held[s % 2, pl.ds((s // 2) * pixels, pixels), :] = x[...]
    eye = (
        lax.broadcasted_iota(jnp.int32, (width, width), 0)
        == lax.broadcasted_iota(jnp.int32, (width, width), 1)
    ).astype(F32).astype(BF)
    for g in range(2):
        o_ref[g] = lax.dot_general(
            eye, held[g], (((1,), (1,)), ((), ())), preferred_element_type=F32
        ).astype(BF)


def roll_cols(x, shift):
    return jnp.concatenate([x[:, x.shape[1] - shift :], x[:, : x.shape[1] - shift]], axis=1)


def tap_grads(pos_ref, place_ref, *refs):
    deltas, (xt_ref, keep_ref, send_ref, held, padded, buf) = refs[:8], refs[8:]
    side = RATE_C
    half, width = deltas[0].shape
    pixels = 2 * half
    cols = SIDE
    rows = pixels // cols
    for k in range(4):
        s = jnp.bitwise_xor(pos_ref[0], k)
        upper = s // 2
        for first, d in ((3 * upper, deltas[k]), (1 + upper, deltas[4 + k])):
            held[s % 2, pl.ds(pl.multiple_of(first * half, 16), half), :] = d[...]
    buf[...] = jnp.zeros_like(buf)
    tall = 2 * pixels
    lead = side * cols
    zeros = jnp.zeros((2, lead, width), BF)
    halves = [held[g].astype(F32).reshape(2 * rows, cols, width) for g in range(2)]
    at = lax.broadcasted_iota(jnp.int32, (2 * rows, cols, width), 1)
    rest = cols - side
    for across in (-1, 0, 1):
        padded[:, pl.ds(0, lead), :] = zeros
        padded[:, pl.ds(lead + tall, lead), :] = zeros
        if across == 0:
            shifted = halves
        elif across == 1:
            rolled = [roll_cols(h, side) for h in halves]
            shifted = [
                jnp.where(at >= side, rolled[0], 0.0),
                jnp.where(at < side, rolled[0], rolled[1]),
            ]
        else:
            rolled = [roll_cols(h, rest) for h in halves]
            shifted = [
                jnp.where(at < rest, rolled[0], rolled[1]),
                jnp.where(at < rest, rolled[1], 0.0),
            ]
        for g in range(2):
            padded[g, pl.ds(lead, tall), :] = shifted[g].reshape(tall, width).astype(BF)
        for above in (-1, 0, 1):
            first, last = {-1: (0, 32), 0: (0, 48), 1: (16, 48)}[above]
            base = first - side * above + side
            total = None
            for g in range(2):
                part = jnp.dot(
                    xt_ref[g, :, first * cols : last * cols],
                    padded[g, base * cols : (base + last - first) * cols, :],
                    preferred_element_type=F32,
                )
                total = part if total is None else total + part
            tap = 3 * (above + 1) + across + 1
            groups = total.reshape(width // 16, 16, width)
            for m in range(width // 16):
                buf[place_ref[32 + 16 * tap + m]] = groups[m]
    half = buf.shape[0] // 2
    keep_ref[...] = buf[:half]
    send_ref[...] = buf[half:].astype(BF)


def join_owners(pos_ref, place_ref, keep_ref, got_ref, mine_ref, other_ref, o_ref, total):
    total[...] = keep_ref[...] + got_ref[...].astype(F32)
    core = pos_ref[4]
    for n in range(mine_ref.shape[0]):
        for ref, first in ((mine_ref, 16 * core), (other_ref, 16 * (1 - core))):
            at = place_ref[first + n]

            @pl.when(at < total.shape[0])
            def _(ref=ref, at=at, n=n):
                total[at] = ref[n].astype(F32)

    o_ref[...] = total[...].astype(BF).reshape(o_ref.shape)


def fold_last(r_ref, o_ref, total):
    value = r_ref[0].astype(F32)
    for n in range(1, r_ref.shape[0]):
        value = value + r_ref[n].astype(F32)
    total[...] = value.reshape(total.shape)
    width = total.shape[2]
    for i in range(total.shape[1]):
        o_ref[:, i * width : (i + 1) * width] = total[:, i, :]


def share_rows(pos_ref, kept_ref, got0, got1, *rest):
    *outs, total = rest
    half, each = got0.shape[0], total.shape[0] // 2
    for n, got in enumerate((got0, got1)):
        value = kept_ref[n * half : (n + 1) * half, :] + got[...].astype(F32)
        total[n * each : (n + 1) * each] = value.reshape(each, *total.shape[1:])
    for k, out in enumerate(outs):
        out[...] = total[:, jnp.bitwise_xor(pos_ref[0], k)].astype(out.dtype)


def swap_core(x):
    return lax.ppermute(x, "dp_2", [(0, 1), (1, 0)])


def pick(pos, centre):
    pixels, chans = centre.shape
    block = jax.ShapeDtypeStruct((pixels, chans // 4), BF)
    return call(
        select_channels,
        [block] * 4,
        1,
        0,
        2 * pixels * chans * chans,
        4 * pixels * chans,
        14,
        [
            pltpu.VMEM((pixels, chans), BF),
            pltpu.VMEM((chans, chans), BF),
            pltpu.SemaphoreType.DMA((2,)),
        ],
        name="pick",
        n_any=1,
    )(pos, pltpu.with_memory_space_constraint(centre, pltpu.HBM))


def turn(pos, got):
    pixels, width = got[0].shape
    return call(
        turn_pixels,
        jax.ShapeDtypeStruct((2, width, 2 * pixels), BF),
        1,
        4,
        8 * pixels * width * width,
        16 * pixels * width,
        12,
        [pltpu.VMEM((2, 2 * pixels, width), BF)],
        name="turn",
    )(pos, *got)


def split_pair(pos, kept, got):
    width = kept.shape[1]
    slices = kept.shape[0] // 64
    shape = (slices, 16, width)
    return call(
        share_rows,
        [jax.ShapeDtypeStruct(shape, F32)] + [jax.ShapeDtypeStruct(shape, BF)] * 3,
        1,
        3,
        kept.size,
        8 * kept.size,
        10,
        [pltpu.VMEM((slices, 4, 16, width), F32)],
        name="rows",
    )(pos, kept, *got)


def sum_pair(blocks):
    mine = blocks[0] + sum(block.astype(F32) for block in blocks[1:])
    return mine, swap_core(mine.astype(BF))


def place_slots(bucket_slot, core, slot_count):
    replicas = lax.axis_size(DP)
    capacity = slot_count // replicas
    owner = bucket_slot // capacity
    other = jnp.bitwise_xor(owner % 2, core)
    return other * (slot_count // 2) + (owner // 2) * capacity + bucket_slot % capacity


def tap_slots(pos, place, deltas, turned, slot_count):
    width = deltas[0].shape[1]
    pixels = 2 * deltas[0].shape[0]
    half = slot_count // 2
    return call(
        tap_grads,
        [jax.ShapeDtypeStruct((half, 16, width), F32), jax.ShapeDtypeStruct((half, 16, width), BF)],
        2,
        9,
        2 * 7 * 4 * pixels * width * width,
        8 * 1024 * 1024,
        26,
        [
            pltpu.VMEM((2, 2 * pixels, width), BF),
            pltpu.VMEM((2, 2 * pixels + 2 * RATE_C * SIDE, width), BF),
            pltpu.VMEM((slot_count, 16, width), F32),
        ],
        name="taps",
    )(pos, place, *deltas, turned)


def reduce_slots(pos, place, kept, sent, mine, other):
    half, rows, width = kept.shape
    chips = lax.axis_size("dp_0") * lax.axis_size("dp_1")
    each = half // chips
    total = call(
        join_owners,
        jax.ShapeDtypeStruct((chips, each * rows, width), BF),
        2,
        4,
        kept.size,
        8 * kept.size,
        12,
        [pltpu.VMEM((half, rows, width), F32)],
        name="owners",
    )(pos, place, kept, swap_core(sent), mine, other)
    total = lax.all_to_all(total, ("dp_0", "dp_1"), 0, 0, tiled=True)
    return call(
        fold_last,
        jax.ShapeDtypeStruct((each, rows * width), F32),
        0,
        1,
        kept.size,
        2 * kept.size,
        8,
        [pltpu.VMEM((each, rows, width), F32)],
        name="last",
    )(total)


def silu_slope(value):
    sig = jax.nn.sigmoid(value)
    return sig * (1.0 + value * (1.0 - sig))


RATES = (RATE_A, RATE_B, RATE_C)
SIDE = 24


def turned_by(x, shift, far):
    return roll_cols(x, shift if far == 0 else SIDE - shift)


def rank_of(shape, far):
    at = lax.broadcasted_iota(jnp.int32, shape, 1)
    return at if far == 0 else SIDE - 1 - at


def by_side(side, body):
    for far in range(2):

        @pl.when(side == far)
        def _(far=far):
            body(far)


def row_marks(low, rate):
    lead = rate * SIDE
    whole = SIDE * SIDE

    def either(upper, lower):
        return pl.multiple_of(jnp.where(low == 0, upper, lower), 16)

    return dict(
        own=either(0, lead),
        out=either(lead, 0),
        theirs=either(whole, 0),
        inward_from=either(lead, 0),
        inward=either(0, 2 * lead),
        kept=either(lead, 0),
        inner=either(0, lead),
    )


def blocks(x):
    return x.reshape(x.shape[0] // SIDE, SIDE, x.shape[1])


def flat(x):
    return x.reshape(x.shape[0] * SIDE, x.shape[2])


def tap_copies(pos_ref, refs, jobs, held, sems):
    copies = []
    for branch, ref in enumerate(refs):
        for n, (above, across) in enumerate(jobs):
            a = 1 if above == 1 else jnp.where(pos_ref[2] == 0, above, 2 - above)
            b = 1 if across == 1 else jnp.where(pos_ref[3] == 0, across, 2 - across)
            width = ref.shape[3]
            to = held.at[branch, :, n * width : (n + 1) * width]
            copies.append(pltpu.make_async_copy(ref.at[a, b], to, sems.at[branch, n]))
    return copies


BRANCHES = ((2, RATE_C), (1, RATE_B), (0, RATE_A))
OUTER = ((0, 0), (1, 0), (0, 1), (0, 2), (2, 0))
INNER = ((1, 1), (1, 2), (2, 1), (2, 2))


def outer_parts(
    pos_ref, x_ref, wc_ref, wb_ref, wa_ref, pre_ref, rf_ref, cf_ref, df_ref, rn_ref, cn_ref, dn_ref, ext, acc, y, part, held, sems
):
    low = pos_ref[2]
    whole = SIDE * SIDE
    width = pre_ref.shape[2]
    count = len(OUTER)
    copies = tap_copies(pos_ref, (wc_ref, wb_ref, wa_ref), OUTER, held, sems)
    for copy in copies:
        copy.start()

    def products(turn):
        rate = BRANCHES[turn][1]
        at = row_marks(low, rate)
        inside = whole - rate * SIDE
        for copy in copies[turn * count : (turn + 1) * count]:
            copy.wait()
        y[turn] = jnp.dot(x_ref[...], held[turn, :, : 4 * width], preferred_element_type=F32)
        acc[turn, :inside, :] = jnp.dot(
            x_ref[pl.ds(at["inward_from"], inside), :], held[turn, :, 4 * width :], preferred_element_type=F32
        )

    def sums(turn, far):
        index, rate = BRANCHES[turn]
        lead = rate * SIDE
        inside = whole - lead
        at = row_marks(low, rate)
        own_rows = pl.ds(at["own"], whole)
        their_rows = pl.ds(at["theirs"], lead)
        kept_rows = pl.ds(at["kept"], inside)
        ext[pl.ds(pl.multiple_of(whole - at["theirs"], 16), lead), :] = jnp.zeros((lead, width), F32)
        ext[pl.ds(at["out"], whole), :] = y[turn, :, :width]
        ext[own_rows, :] += y[turn, :, width : 2 * width]
        ext[pl.ds(at["inward"], inside), :] += acc[turn, :inside, :]
        own = blocks(ext[own_rows, :])
        ours = turned_by(own, rate, far)
        rank = rank_of(own.shape, far)
        pre_ref[index] = flat(jnp.where(rank >= rate, ours, 0.0))
        below = blocks(ext[their_rows, :])
        theirs = turned_by(below, rate, far)
        place = rank_of(below.shape, far)
        if rate == RATE_C:
            part[0, :whole, :] = flat(jnp.where(rank < rate, ours, 0.0))
            part[1, :lead, :] = flat(jnp.where(place < rate, theirs, 0.0))
        elif rate == RATE_B:
            half = rate // 2
            for n in range(2):
                top = 2 * half * n
                pair = jnp.where(rank[:half] < rate, ours[top : top + half], own[top + half : top + 2 * half])
                part[0, whole + half * n * SIDE : whole + half * (n + 1) * SIDE, :] = flat(pair)
            few = place[:half] < rate
            dn_ref[RATE_B * SIDE :, :] = flat(jnp.where(few, theirs[:half], below[half:])).astype(BF)
        else:
            have = blocks(part[0, :whole, :])
            part[0, :whole, :] = flat(jnp.where(rank >= RATE_C, own, have))
            mid = whole // 2
            quarter = RATE_A * SIDE
            for away, to in ((True, cf_ref), (False, cn_ref)):
                lower = jnp.where(low == 0, 0, 1) if away else jnp.where(low == 0, 1, 0)
                at_a = pl.multiple_of(lower * mid, 16)
                at_b = pl.multiple_of(whole + lower * quarter, 16)
                to[:mid, :] = part[0, pl.ds(at_a, mid), :].astype(BF)
                to[mid:, :] = part[0, pl.ds(at_b, quarter), :].astype(BF)
            away_at = pl.multiple_of(jnp.where(low == 0, 2 * quarter, 0), 16)
            near_at = pl.multiple_of(jnp.where(low == 0, 0, quarter), 16)
            df_ref[...] = part[1, pl.ds(away_at, quarter), :].astype(BF)
            near = blocks(part[1, pl.ds(near_at, 2 * quarter), :])
            dn_ref[:quarter, :] = flat(jnp.where(place >= RATE_C, below, near[:RATE_A])).astype(BF)
            dn_ref[quarter : 2 * quarter, :] = flat(near[RATE_A:]).astype(BF)
            rf_ref[...] = part[2, pl.ds(away_at, quarter), :].astype(BF)
            rn_ref[: 2 * quarter, :] = part[2, pl.ds(near_at, 2 * quarter), :].astype(BF)
        next_rows = pl.ds(pl.multiple_of(jnp.where(low == 0, inside, 0), 16), lead)
        keep_rows = pl.ds(pl.multiple_of(jnp.where(low == 0, 0, lead), 16), inside)
        own = blocks(y[turn, keep_rows, 3 * width :])
        moved = flat(jnp.where(rank_of(own.shape, far) < SIDE - rate, turned_by(own, rate, 1 - far), 0.0))
        pre_ref[index, kept_rows, :] += y[turn, keep_rows, 2 * width : 3 * width] + moved
        below = blocks(y[turn, next_rows, 3 * width :])
        total = jnp.where(place < SIDE - rate, turned_by(below, rate, 1 - far), 0.0)
        total = flat(total + jnp.where(place >= rate, theirs, 0.0))
        total = total + y[turn, next_rows, 2 * width : 3 * width]
        if rate == RATE_C:
            part[2, :lead, :] = total
        elif rate == RATE_B:
            rn_ref[RATE_B * SIDE : 2 * RATE_B * SIDE, :] = total.astype(BF)
        else:
            rn_ref[2 * RATE_B * SIDE :, :] = total.astype(BF)

    def body(far):
        products(0)
        products(1)
        sums(0, far)
        products(2)
        sums(1, far)
        sums(2, far)

    by_side(pos_ref[3], body)


def inner_parts(pos_ref, x_ref, part_ref, wp_ref, wc_ref, wb_ref, wa_ref, pre0_ref, pre_ref, y, z, held, sems):
    low = pos_ref[2]
    whole = SIDE * SIDE
    width = pre0_ref.shape[1]
    count = len(INNER)
    copies = tap_copies(pos_ref, (wc_ref, wb_ref, wa_ref), INNER, held, sems)
    for copy in copies:
        copy.start()
    pre0_ref[...] = jnp.dot(x_ref[...], wp_ref[...], preferred_element_type=F32)

    def body(far):
        for turn, (index, rate) in enumerate(BRANCHES):
            inside = whole - rate * SIDE
            at = row_marks(low, rate)
            from_rows = pl.ds(at["inward_from"], inside)
            to_rows = pl.ds(at["inner"], inside)
            for copy in copies[turn * count : (turn + 1) * count]:
                copy.wait()
            y[...] = jnp.dot(x_ref[...], held[turn, :, : 2 * width], preferred_element_type=F32)
            z[:inside, :] = jnp.dot(x_ref[from_rows, :], held[turn, :, 2 * width :], preferred_element_type=F32)
            y[to_rows, :] += z[:inside, :]
            own = blocks(y[:, width:])
            rank = rank_of(own.shape, far)
            moved = flat(jnp.where(rank < SIDE - rate, turned_by(own, rate, 1 - far), 0.0))
            pre_ref[index] = part_ref[index] + y[:, :width] + moved

    by_side(pos_ref[3], body)


def outer(pos, centre, w_rate_a, w_rate_b, w_rate_c):
    pixels, chans = centre.shape
    width = w_rate_a.shape[3]
    away, near = (RATE_A, 18, RATE_A), (30, 18, 18)
    shapes = [((3, pixels, width), F32)] + [((n * SIDE, width), BF) for n in away + near]
    return call(
        outer_parts,
        [jax.ShapeDtypeStruct(*s) for s in shapes],
        1,
        1,
        2 * pixels * chans * width * 14,
        10 * MIB,
        40,
        [
            pltpu.VMEM(((SIDE + RATE_C) * SIDE, width), F32),
            pltpu.VMEM((3, pixels, width), F32),
            pltpu.VMEM((3, pixels, 4 * width), F32),
            pltpu.VMEM((3, (SIDE + RATE_B) * SIDE, width), F32),
            pltpu.VMEM((3, chans, len(OUTER) * width), BF),
            pltpu.SemaphoreType.DMA((3, len(OUTER))),
        ],
        name="outer",
        n_any=3,
    )(pos, centre, w_rate_c, w_rate_b, w_rate_a)


def inner(pos, centre, part, w_point, w_rate_a, w_rate_b, w_rate_c):
    pixels, chans = centre.shape
    width = w_point.shape[1]
    return call(
        inner_parts,
        [jax.ShapeDtypeStruct((pixels, width), F32), jax.ShapeDtypeStruct((3, pixels, width), F32)],
        1,
        3,
        2 * pixels * chans * width * 10,
        10 * MIB,
        26,
        [
            pltpu.VMEM((pixels, 2 * width), F32),
            pltpu.VMEM((pixels, 2 * width), F32),
            pltpu.VMEM((3, chans, len(INNER) * width), BF),
            pltpu.SemaphoreType.DMA((3, len(INNER))),
        ],
        name="inner",
        n_any=3,
    )(pos, centre, part, w_point, w_rate_c, w_rate_b, w_rate_a)


def merge_parts(
    away, pos_ref, pre0_ref, own_ref, row_ref, col_ref, diag_ref, cot_ref, wp_ref, joined_ref, g_ref, d0_ref, d3_ref, pre
):
    low = pos_ref[2]
    width = pre0_ref.shape[1]
    half = SIDE * SIDE // 2
    quarter = half // 2
    lower = low if away else 1 - low
    mine = pl.ds(pl.multiple_of(lower * half, 16), half)
    touched = pl.multiple_of(jnp.where(low == 0, quarter, 0), 16)
    pre[...] = own_ref[:, mine, :]

    def body(far):
        theirs = 1 - far
        part = blocks(col_ref[:half, :].astype(F32))
        rank = rank_of(part.shape, theirs)
        pre[2] += flat(jnp.where(rank < RATE_C, part, 0.0))
        pre[0] += flat(turned_by(jnp.where(rank >= RATE_C, part, 0.0), RATE_A, theirs))
        part = blocks(col_ref[half:, :].astype(F32))
        rank = rank[: part.shape[0]]
        pre[1, :quarter, :] += flat(jnp.where(rank < RATE_B, part, 0.0))
        pre[1, quarter:, :] += flat(roll_cols(jnp.where(rank >= RATE_B, part, 0.0), RATE_B))
        if away:
            some = pl.ds(touched, quarter)
            part = blocks(diag_ref[...].astype(F32))
            part = flat(jnp.where(rank < RATE_C, part, 0.0))
            pre[2, some, :] += row_ref[...].astype(F32) + part
        else:
            some = pl.ds(touched, quarter)
            part = blocks(diag_ref[:half, :].astype(F32))
            wide = rank_of(part.shape, theirs)
            pre[2] += row_ref[:half, :].astype(F32) + flat(jnp.where(wide < RATE_C, part, 0.0))
            pre[1] += row_ref[half : 2 * half, :].astype(F32)
            few = turned_by(jnp.where(rank >= RATE_C, part[:RATE_A], 0.0), RATE_A, theirs)
            pre[0, some, :] += row_ref[2 * half :, :].astype(F32) + flat(few)
            part = blocks(diag_ref[half:, :].astype(F32))
            pre[1, :quarter, :] += flat(jnp.where(rank < RATE_B, part, 0.0))
            pre[1, quarter:, :] += flat(roll_cols(jnp.where(rank >= RATE_B, part, 0.0), RATE_B))

    by_side(pos_ref[3], body)
    slopes = {}
    for k in range(4):
        value = pre0_ref[mine, :] if k == 0 else pre[k - 1]
        sig = jax.nn.sigmoid(value)
        joined_ref[:, k * width : (k + 1) * width] = (value * sig).astype(BF)
        if k in (0, 3):
            slopes[k] = sig * (1.0 + value * (1.0 - sig))
    proj_pre = jnp.dot(joined_ref[...], wp_ref[...], preferred_element_type=F32)
    g_proj = (cot_ref[mine, :].astype(F32) * silu_slope(proj_pre)).astype(BF)
    g_ref[...] = g_proj
    for k, out in ((3, d3_ref), (0, d0_ref)):
        back = lax.dot_general(
            g_proj, wp_ref[k * width : (k + 1) * width, :], (((1,), (1,)), ((), ())), preferred_element_type=F32
        )
        out[...] = (back * slopes[k]).astype(BF)


def merge(away, pos, pre0, own, row, col, diag, cot, w_proj):
    pixels, width = pre0.shape
    half = pixels // 2
    block = jax.ShapeDtypeStruct((half, width), BF)
    return call(
        functools.partial(merge_parts, away),
        [jax.ShapeDtypeStruct((half, 4 * width), BF), block, block, block],
        1,
        7,
        2 * half * width * width * 6,
        3 * MIB,
        14,
        [pltpu.VMEM((3, half, width), F32)],
        name="merge",
    )(pos, pre0, own, row, col, diag, cot, w_proj)


def pair_grads(pos_ref, ja_ref, ga_ref, da_ref, jn_ref, gn_ref, dn_ref, x_ref, keep_ref, *send_refs):
    core = pos_ref[4]
    over = (((0,), (0,)), ((), ()))
    rows = ja_ref.shape[0]
    grad_proj = grad_point = None
    for lower, (j, g, d) in ((pos_ref[2], (ja_ref, ga_ref, da_ref)), (1 - pos_ref[2], (jn_ref, gn_ref, dn_ref))):
        x = x_ref[pl.ds(pl.multiple_of(lower * rows, 16), rows), :]
        one = lax.dot_general(j[...], g[...], over, preferred_element_type=F32)
        two = lax.dot_general(x, d[...], over, preferred_element_type=F32)
        grad_proj = one if grad_proj is None else grad_proj + one
        grad_point = two if grad_point is None else grad_point + two
    keep_ref[...] = jnp.where(core == 0, grad_proj, grad_point)
    half = send_refs[0].shape[0]
    for k, send_ref in enumerate(send_refs):
        part = slice(k * half, (k + 1) * half)
        send_ref[...] = jnp.where(core == 0, grad_point[part], grad_proj[part]).astype(BF)


def shards(features, cotangent, w_point, w_rate_a, w_rate_b, w_rate_c, w_proj, bucket_slot):
    image = features[0]
    rows_dev, cols_dev, chans = image.shape
    pixels = rows_dev * cols_dev
    width = w_point.shape[1]
    row, col, core = (lax.axis_index(n) for n in ("row", "col", "dp_2"))
    at_y, at_z = lax.axis_index("dp_0"), lax.axis_index("dp_1")
    pos = jnp.stack([2 * row + col, at_y, row, col, core, at_z]).astype(jnp.int32)
    replicas = lax.axis_size(DP)
    slot_count = replicas * (bucket_slot.shape[0] // replicas + 1)
    place = place_slots(bucket_slot, core, slot_count)
    centre = image.reshape(pixels, chans)
    weights = [pltpu.with_memory_space_constraint(w, pltpu.HBM) for w in (w_rate_a, w_rate_b, w_rate_c)]
    picked = pick(pos, centre)
    centre, *picked = lax.optimization_barrier((centre, *picked))
    got = [picked[0]] + [flip(picked[k], k) for k in (1, 2, 3)]
    part, *parts = outer(pos, centre, *weights)
    part, got = lax.optimization_barrier((part, got))
    parts = [flip(p, k) for p, k in zip(parts, (2, 1, 3, 2, 1, 3))]
    turned = turn(pos, got)
    pre0, own = inner(pos, centre, part, w_point, *weights)
    parts[:3], pre0, own, turned = lax.optimization_barrier((parts[:3], pre0, own, turned))
    cot = cotangent[0].reshape(pixels, width)
    *first, delta_a = merge(True, pos, pre0, own, *parts[:3], cot, w_proj)
    shared = [delta_a] + [flip(delta_a, k) for k in (1, 2, 3)]
    *last, delta_n = merge(False, pos, pre0, own, *parts[3:], cot, w_proj)
    shared = shared + [delta_n] + [flip(delta_n, k) for k in (1, 2, 3)]
    block = (4 * width, width)
    kept, *sent = call(
        pair_grads,
        [jax.ShapeDtypeStruct(block, F32)] + [jax.ShapeDtypeStruct((2 * width, width), BF)] * 2,
        1,
        7,
        4 * pixels * chans * width,
        4 * 1024 * 1024,
        16,
        name="pair",
    )(pos, *first, *last, centre)
    got = [swap_core(part) for part in sent]
    got, shared = lax.optimization_barrier((got, shared))
    by_owner = split_pair(pos, kept, got)
    by_owner, shared = lax.optimization_barrier((by_owner, shared))
    by_owner = [by_owner[0]] + [flip(by_owner[k], k) for k in (1, 2, 3)]
    kept, sent = tap_slots(pos, place, shared, turned, slot_count)
    sent, by_owner = lax.optimization_barrier((sent, by_owner))
    mine, other = sum_pair(by_owner)
    return reduce_slots(pos, place, kept, sent, mine, other)


def solution(mesh):
    torus = Mesh(
        mesh.devices.reshape(mesh.shape["row"], mesh.shape["col"], 4, 4, 2),
        ("row", "col", "dp_0", "dp_1", "dp_2"),
    )
    in_specs = (P(DP, "row", "col", None), P(DP, "row", "col", None), P(), P(), P(), P(), P(), P())
    out_specs = P(DP, ("row", "col"))
    return jax.shard_map(
        shards, mesh=torus, in_specs=in_specs, out_specs=out_specs, check_vma=False
    )
```

```python
import jax
import jax.numpy as jnp
from jax import lax
from jax.experimental import pallas as pl
from jax.experimental.pallas import tpu as pltpu
from jax.sharding import Mesh
from jax.sharding import PartitionSpec as P

RATE_A = 6
RATE_B = 12
RATE_C = 18
DP = ("dp_0", "dp_1", "dp_2")


BF = jnp.bfloat16
F32 = jnp.float32
MIB = 1024 * 1024


def flip(x, mask):
    if mask == 1:
        return lax.ppermute(x, "col", [(0, 1), (1, 0)])
    if mask == 2:
        return lax.ppermute(x, "row", [(0, 1), (1, 0)])
    return lax.ppermute(x, ("row", "col"), [(0, 3), (3, 0), (1, 2), (2, 1)])


def smem():
    return pl.BlockSpec(memory_space=pltpu.SMEM)


def vmem():
    return pl.BlockSpec(memory_space=pltpu.VMEM)


def call(body, outs, n_smem, n_vmem, flops, nbytes, limit, scratch=(), name=None, n_any=0):
    return pl.pallas_call(
        body,
        out_shape=outs,
        in_specs=[smem()] * n_smem + [vmem()] * n_vmem + [pl.BlockSpec(memory_space=pltpu.HBM)] * n_any,
        out_specs=jax.tree.map(lambda _: vmem(), outs),
        scratch_shapes=list(scratch),
        compiler_params=pltpu.CompilerParams(vmem_limit_bytes=limit * MIB),
        cost_estimate=pl.CostEstimate(flops=flops, bytes_accessed=nbytes, transcendentals=0),
        name=name,
    )


def select_channels(pos_ref, x_ref, *rest):
    *o_refs, held, sems = rest
    lanes = 128
    group = lanes * len(o_refs)
    pieces = sems.shape[0]
    each = x_ref.shape[0] // pieces
    copies = []
    for n in range(pieces):
        part = pl.ds(n * each, each)
        copies.append(pltpu.make_async_copy(x_ref.at[part, :], held.at[part, :], sems.at[n]))
        copies[n].start()
    source = lax.broadcasted_iota(jnp.int32, (group, group), 0)
    col = lax.broadcasted_iota(jnp.int32, (1, group), 1)
    owner = jnp.bitwise_xor(pos_ref[0], col // lanes)
    wanted = 64 * ((col % lanes) // 16) + 16 * owner + col % 16
    picks = jnp.where(source == wanted, 1.0, 0.0).astype(BF)
    for n in range(pieces):
        copies[n].wait()
        rows = slice(n * each, (n + 1) * each)
        for p in range(x_ref.shape[1] // group):
            taken = jnp.dot(held[rows, p * group : (p + 1) * group], picks, preferred_element_type=F32).astype(BF)
            for k, o_ref in enumerate(o_refs):
                o_ref[rows, p * lanes : (p + 1) * lanes] = taken[:, k * lanes : (k + 1) * lanes]


def turn_pixels(pos_ref, x0, x1, x2, x3, o_ref, held):
    pixels, width = x0.shape
    for k, x in enumerate((x0, x1, x2, x3)):
        s = jnp.bitwise_xor(pos_ref[0], k)
        held[s % 2, pl.ds((s // 2) * pixels, pixels), :] = x[...]
    eye = (
        lax.broadcasted_iota(jnp.int32, (width, width), 0)
        == lax.broadcasted_iota(jnp.int32, (width, width), 1)
    ).astype(F32).astype(BF)
    for g in range(2):
        o_ref[g] = lax.dot_general(
            eye, held[g], (((1,), (1,)), ((), ())), preferred_element_type=F32
        ).astype(BF)


def roll_cols(x, shift):
    return jnp.concatenate([x[:, x.shape[1] - shift :], x[:, : x.shape[1] - shift]], axis=1)


def tap_grads(pos_ref, place_ref, d0, d1, d2, d3, xt_ref, keep_ref, send_ref, held, padded, buf):
    side = RATE_C
    pixels, width = d0.shape
    cols = 24
    rows = pixels // cols
    for k, d in enumerate((d0, d1, d2, d3)):
        s = jnp.bitwise_xor(pos_ref[0], k)
        held[s % 2, pl.ds((s // 2) * pixels, pixels), :] = d[...]
    buf[...] = jnp.zeros_like(buf)
    tall = 2 * pixels
    lead = side * cols
    zeros = jnp.zeros((2, lead, width), BF)
    halves = [held[g].astype(F32).reshape(2 * rows, cols, width) for g in range(2)]
    at = lax.broadcasted_iota(jnp.int32, (2 * rows, cols, width), 1)
    rest = cols - side
    for across in (-1, 0, 1):
        padded[:, pl.ds(0, lead), :] = zeros
        padded[:, pl.ds(lead + tall, lead), :] = zeros
        if across == 0:
            shifted = halves
        elif across == 1:
            rolled = [roll_cols(h, side) for h in halves]
            shifted = [
                jnp.where(at >= side, rolled[0], 0.0),
                jnp.where(at < side, rolled[0], rolled[1]),
            ]
        else:
            rolled = [roll_cols(h, rest) for h in halves]
            shifted = [
                jnp.where(at < rest, rolled[0], rolled[1]),
                jnp.where(at < rest, rolled[1], 0.0),
            ]
        for g in range(2):
            padded[g, pl.ds(lead, tall), :] = shifted[g].reshape(tall, width).astype(BF)
        for above in (-1, 0, 1):
            first, last = {-1: (0, 32), 0: (0, 48), 1: (16, 48)}[above]
            base = first - side * above + side
            total = None
            for g in range(2):
                part = jnp.dot(
                    xt_ref[g, :, first * cols : last * cols],
                    padded[g, base * cols : (base + last - first) * cols, :],
                    preferred_element_type=F32,
                )
                total = part if total is None else total + part
            tap = 3 * (above + 1) + across + 1
            groups = total.reshape(width // 16, 16, width)
            for m in range(width // 16):
                buf[place_ref[32 + 16 * tap + m]] = groups[m]
    half = buf.shape[0] // 2
    keep_ref[...] = buf[:half]
    send_ref[...] = buf[half:].astype(BF)


def join_owners(pos_ref, place_ref, keep_ref, got_ref, mine_ref, other_ref, o_ref, total):
    total[...] = keep_ref[...] + got_ref[...].astype(F32)
    core = pos_ref[4]
    for n in range(mine_ref.shape[0]):
        for ref, first in ((mine_ref, 16 * core), (other_ref, 16 * (1 - core))):
            at = place_ref[first + n]

            @pl.when(at < total.shape[0])
            def _(ref=ref, at=at, n=n):
                total[at] = ref[n].astype(F32)

    o_ref[...] = total[...].astype(BF).reshape(o_ref.shape)


def fold_last(r_ref, o_ref, total):
    value = r_ref[0].astype(F32)
    for n in range(1, r_ref.shape[0]):
        value = value + r_ref[n].astype(F32)
    total[...] = value.reshape(total.shape)
    width = total.shape[2]
    for i in range(total.shape[1]):
        o_ref[:, i * width : (i + 1) * width] = total[:, i, :]


def share_rows(pos_ref, kept_ref, got0, got1, *rest):
    *outs, total = rest
    half, each = got0.shape[0], total.shape[0] // 2
    for n, got in enumerate((got0, got1)):
        value = kept_ref[n * half : (n + 1) * half, :] + got[...].astype(F32)
        total[n * each : (n + 1) * each] = value.reshape(each, *total.shape[1:])
    for k, out in enumerate(outs):
        out[...] = total[:, jnp.bitwise_xor(pos_ref[0], k)].astype(out.dtype)


def swap_core(x):
    return lax.ppermute(x, "dp_2", [(0, 1), (1, 0)])


def pick(pos, centre):
    pixels, chans = centre.shape
    block = jax.ShapeDtypeStruct((pixels, chans // 4), BF)
    return call(
        select_channels,
        [block] * 4,
        1,
        0,
        pixels * chans * chans,
        4 * pixels * chans,
        12,
        [pltpu.VMEM((pixels, chans), BF), pltpu.SemaphoreType.DMA((2,))],
        name="pick",
        n_any=1,
    )(pos, pltpu.with_memory_space_constraint(centre, pltpu.HBM))


def turn(pos, got):
    pixels, width = got[0].shape
    return call(
        turn_pixels,
        jax.ShapeDtypeStruct((2, width, 2 * pixels), BF),
        1,
        4,
        8 * pixels * width * width,
        16 * pixels * width,
        12,
        [pltpu.VMEM((2, 2 * pixels, width), BF)],
        name="turn",
    )(pos, *got)


def split_pair(pos, kept, got):
    width = kept.shape[1]
    slices = kept.shape[0] // 64
    shape = (slices, 16, width)
    return call(
        share_rows,
        [jax.ShapeDtypeStruct(shape, F32)] + [jax.ShapeDtypeStruct(shape, BF)] * 3,
        1,
        3,
        kept.size,
        8 * kept.size,
        10,
        [pltpu.VMEM((slices, 4, 16, width), F32)],
        name="rows",
    )(pos, kept, *got)


def sum_pair(blocks):
    mine = blocks[0] + sum(block.astype(F32) for block in blocks[1:])
    return mine, swap_core(mine.astype(BF))


def place_slots(bucket_slot, core, slot_count):
    replicas = lax.axis_size(DP)
    capacity = slot_count // replicas
    owner = bucket_slot // capacity
    other = jnp.bitwise_xor(owner % 2, core)
    return other * (slot_count // 2) + (owner // 2) * capacity + bucket_slot % capacity


def tap_slots(pos, place, deltas, turned, slot_count):
    pixels, width = deltas[0].shape
    half = slot_count // 2
    return call(
        tap_grads,
        [jax.ShapeDtypeStruct((half, 16, width), F32), jax.ShapeDtypeStruct((half, 16, width), BF)],
        2,
        5,
        2 * 7 * 4 * pixels * width * width,
        8 * 1024 * 1024,
        26,
        [
            pltpu.VMEM((2, 2 * pixels, width), BF),
            pltpu.VMEM((2, 2 * pixels + 2 * RATE_C * SIDE, width), BF),
            pltpu.VMEM((slot_count, 16, width), F32),
        ],
        name="taps",
    )(pos, place, *deltas, turned)


def reduce_slots(pos, place, kept, sent, mine, other):
    half, rows, width = kept.shape
    chips = lax.axis_size("dp_0") * lax.axis_size("dp_1")
    each = half // chips
    total = call(
        join_owners,
        jax.ShapeDtypeStruct((chips, each * rows, width), BF),
        2,
        4,
        kept.size,
        8 * kept.size,
        12,
        [pltpu.VMEM((half, rows, width), F32)],
        name="owners",
    )(pos, place, kept, swap_core(sent), mine, other)
    total = lax.all_to_all(total, ("dp_0", "dp_1"), 0, 0, tiled=True)
    return call(
        fold_last,
        jax.ShapeDtypeStruct((each, rows * width), F32),
        0,
        1,
        kept.size,
        2 * kept.size,
        8,
        [pltpu.VMEM((each, rows, width), F32)],
        name="last",
    )(total)


def sigmoid(value):
    return 0.5 + 0.5 * jnp.tanh(0.5 * value)


def silu_slope(value):
    sig = sigmoid(value)
    return sig * (1.0 + value * (1.0 - sig))


RATES = (RATE_A, RATE_B, RATE_C)
SIDE = 24


def turned_by(x, shift, far):
    return jnp.where(far == 0, roll_cols(x, shift), roll_cols(x, SIDE - shift))


def rank_of(shape, far):
    at = lax.broadcasted_iota(jnp.int32, shape, 1)
    return jnp.where(far == 0, at, SIDE - 1 - at)


def row_marks(low, rate):
    lead = rate * SIDE
    whole = SIDE * SIDE

    def either(upper, lower):
        return pl.multiple_of(jnp.where(low == 0, upper, lower), 16)

    return dict(
        own=either(0, lead),
        out=either(lead, 0),
        theirs=either(whole, 0),
        inward_from=either(lead, 0),
        inward=either(0, 2 * lead),
        kept=either(lead, 0),
        inner=either(0, lead),
    )


def blocks(x):
    return x.reshape(x.shape[0] // SIDE, SIDE, x.shape[1])


def flat(x):
    return x.reshape(x.shape[0] * SIDE, x.shape[2])


def tap_copies(pos_ref, refs, jobs, held, sems):
    copies = []
    for branch, ref in enumerate(refs):
        for n, (above, across) in enumerate(jobs):
            a = 1 if above == 1 else jnp.where(pos_ref[2] == 0, above, 2 - above)
            b = 1 if across == 1 else jnp.where(pos_ref[3] == 0, across, 2 - across)
            width = ref.shape[3]
            to = held.at[branch, :, n * width : (n + 1) * width]
            copies.append(pltpu.make_async_copy(ref.at[a, b], to, sems.at[branch, n]))
    return copies


BRANCHES = ((2, RATE_C), (1, RATE_B), (0, RATE_A))
OUTER = ((0, 0), (1, 0), (0, 1), (0, 2), (2, 0))
INNER = ((1, 1), (1, 2), (2, 1), (2, 2))


def outer_parts(pos_ref, x_ref, wc_ref, wb_ref, wa_ref, pre_ref, row_ref, col_ref, diag_ref, ext, acc, y, held, sems):
    low, far = pos_ref[2], pos_ref[3]
    whole = SIDE * SIDE
    width = pre_ref.shape[2]
    copies = tap_copies(pos_ref, (wc_ref, wb_ref, wa_ref), OUTER, held, sems)
    for copy in copies:
        copy.start()
    first = 0
    for turn, (index, rate) in enumerate(BRANCHES):
        lead = rate * SIDE
        inside = whole - lead
        at = row_marks(low, rate)
        own_rows = pl.ds(at["own"], whole)
        their_rows = pl.ds(at["theirs"], lead)
        kept_rows = pl.ds(at["kept"], inside)
        to_row = slice(first, first + lead)
        first += lead
        count = len(OUTER)
        for copy in copies[turn * count : (turn + 1) * count]:
            copy.wait()
        y[...] = jnp.dot(x_ref[...], held[turn, :, : 4 * width], preferred_element_type=F32)
        ext[pl.ds(pl.multiple_of(whole - at["theirs"], 16), lead), :] = jnp.zeros((lead, width), F32)
        ext[pl.ds(at["out"], whole), :] = y[:, :width]
        ext[own_rows, :] += y[:, width : 2 * width]
        ext[pl.ds(at["inward"], inside), :] += jnp.dot(
            x_ref[pl.ds(at["inward_from"], inside), :], held[turn, :, 4 * width :], preferred_element_type=F32
        )
        own = blocks(ext[own_rows, :])
        ours = turned_by(own, rate, far)
        rank = rank_of(own.shape, far)
        pre_ref[index] = flat(jnp.where(rank >= rate, ours, 0.0))
        below = blocks(ext[their_rows, :])
        theirs = turned_by(below, rate, far)
        place = rank_of(below.shape, far)
        acc[:lead, :] = flat(jnp.where(place >= rate, theirs, 0.0))
        if rate == RATE_C:
            col_ref[:whole, :] = flat(jnp.where(rank < rate, ours, 0.0)).astype(BF)
            diag_ref[:lead, :] = flat(jnp.where(place < rate, theirs, 0.0)).astype(BF)
        elif rate == RATE_B:
            half = rate // 2
            col_ref[whole:, :] = flat(jnp.where(rank[:rate] < rate, ours[:rate], own[rate:])).astype(BF)
            part = place[:half] < rate
            diag_ref[RATE_C * SIDE :, :] = flat(jnp.where(part, theirs[:half], below[half:])).astype(BF)
        else:
            have = blocks(col_ref[:whole, :].astype(F32))
            col_ref[:whole, :] = flat(jnp.where(rank >= RATE_C, own, have)).astype(BF)
            have = blocks(diag_ref[:lead, :].astype(F32))
            diag_ref[:lead, :] = flat(jnp.where(place >= RATE_C, below, have)).astype(BF)
        next_from = pl.multiple_of(jnp.where(low == 0, inside, 0), 16)
        keep_from = pl.multiple_of(jnp.where(low == 0, 0, lead), 16)
        pre_ref[index, kept_rows, :] += y[pl.ds(keep_from, inside), 2 * width : 3 * width]
        own = blocks(y[pl.ds(keep_from, inside), 3 * width :])
        rank = rank_of(own.shape, far)
        pre_ref[index, kept_rows, :] += flat(jnp.where(rank < SIDE - rate, turned_by(own, rate, 1 - far), 0.0))
        below = blocks(y[pl.ds(next_from, lead), 3 * width :])
        theirs = flat(jnp.where(place < SIDE - rate, turned_by(below, rate, 1 - far), 0.0))
        row_ref[to_row, :] = (acc[:lead, :] + y[pl.ds(next_from, lead), 2 * width : 3 * width] + theirs).astype(BF)


def inner_parts(pos_ref, x_ref, part_ref, wp_ref, wc_ref, wb_ref, wa_ref, pre0_ref, pre_ref, y, z, held, sems):
    low, far = pos_ref[2], pos_ref[3]
    whole = SIDE * SIDE
    width = pre0_ref.shape[1]
    copies = tap_copies(pos_ref, (wc_ref, wb_ref, wa_ref), INNER, held, sems)
    for copy in copies:
        copy.start()
    pre0_ref[...] = jnp.dot(x_ref[...], wp_ref[...], preferred_element_type=F32)
    for turn, (index, rate) in enumerate(BRANCHES):
        lead = rate * SIDE
        inside = whole - lead
        at = row_marks(low, rate)
        from_rows = pl.ds(at["inward_from"], inside)
        to_rows = pl.ds(at["inner"], inside)
        count = len(INNER)
        for copy in copies[turn * count : (turn + 1) * count]:
            copy.wait()
        y[...] = jnp.dot(x_ref[...], held[turn, :, : 2 * width], preferred_element_type=F32)
        z[:inside, :] = jnp.dot(x_ref[from_rows, :], held[turn, :, 2 * width :], preferred_element_type=F32)
        y[to_rows, :] += z[:inside, :]
        own = blocks(y[:, width:])
        rank = rank_of(own.shape, far)
        moved = flat(jnp.where(rank < SIDE - rate, turned_by(own, rate, 1 - far), 0.0))
        pre_ref[index] = part_ref[index] + y[:, :width] + moved


def outer(pos, centre, w_rate_a, w_rate_b, w_rate_c):
    pixels, chans = centre.shape
    width = w_rate_a.shape[3]
    sends = (RATE_A + RATE_B + RATE_C) * SIDE
    shapes = [((3, pixels, width), F32), ((sends, width), BF), ((sends, width), BF), ((pixels, width), BF)]
    return call(
        outer_parts,
        [jax.ShapeDtypeStruct(*s) for s in shapes],
        1,
        1,
        2 * pixels * chans * width * 14,
        10 * MIB,
        28,
        [
            pltpu.VMEM(((SIDE + RATE_C) * SIDE, width), F32),
            pltpu.VMEM((RATE_C * SIDE, width), F32),
            pltpu.VMEM((pixels, 4 * width), F32),
            pltpu.VMEM((3, chans, len(OUTER) * width), BF),
            pltpu.SemaphoreType.DMA((3, len(OUTER))),
        ],
        name="outer",
        n_any=3,
    )(pos, centre, w_rate_c, w_rate_b, w_rate_a)


def inner(pos, centre, part, w_point, w_rate_a, w_rate_b, w_rate_c):
    pixels, chans = centre.shape
    width = w_point.shape[1]
    return call(
        inner_parts,
        [jax.ShapeDtypeStruct((pixels, width), F32), jax.ShapeDtypeStruct((3, pixels, width), F32)],
        1,
        3,
        2 * pixels * chans * width * 10,
        10 * MIB,
        26,
        [
            pltpu.VMEM((pixels, 2 * width), F32),
            pltpu.VMEM((pixels, 2 * width), F32),
            pltpu.VMEM((3, chans, len(INNER) * width), BF),
            pltpu.SemaphoreType.DMA((3, len(INNER))),
        ],
        name="inner",
        n_any=3,
    )(pos, centre, part, w_point, w_rate_c, w_rate_b, w_rate_a)


def merge_parts(
    pos_ref, pre0_ref, own_ref, row_ref, col_ref, diag_ref, cot_ref, wp_ref, joined_ref, g_ref, d0_ref, d3_ref, pre
):
    low = pos_ref[2]
    theirs = 1 - pos_ref[3]
    width = pre0_ref.shape[1]
    whole = SIDE * SIDE

    def rows_of(rate):
        return pl.multiple_of(jnp.where(low == 0, (SIDE - rate) * SIDE, 0), 16)

    pre[...] = own_ref[...]
    first = 0
    for index, rate in ((2, RATE_C), (1, RATE_B), (0, RATE_A)):
        lead = rate * SIDE
        pre[index, pl.ds(rows_of(rate), lead), :] += row_ref[first : first + lead, :].astype(F32)
        first += lead

    part = blocks(col_ref[:whole, :].astype(F32))
    rank = rank_of(part.shape, theirs)
    pre[2] += flat(jnp.where(rank < RATE_C, part, 0.0))
    pre[0] += flat(turned_by(jnp.where(rank >= RATE_C, part, 0.0), RATE_A, theirs))
    part = blocks(col_ref[whole:, :].astype(F32))
    rank = rank_of(part.shape, theirs)
    pre[1, : RATE_B * SIDE, :] += flat(jnp.where(rank < RATE_B, part, 0.0))
    pre[1, RATE_B * SIDE :, :] += flat(roll_cols(jnp.where(rank >= RATE_B, part, 0.0), RATE_B))

    part = blocks(diag_ref[: RATE_C * SIDE, :].astype(F32))
    rank = rank_of(part.shape, theirs)
    pre[2, pl.ds(rows_of(RATE_C), RATE_C * SIDE), :] += flat(jnp.where(rank < RATE_C, part, 0.0))
    few = part[:RATE_A]
    few = turned_by(jnp.where(rank[:RATE_A] >= RATE_C, few, 0.0), RATE_A, theirs)
    pre[0, pl.ds(rows_of(RATE_A), RATE_A * SIDE), :] += flat(few)
    part = blocks(diag_ref[RATE_C * SIDE :, :].astype(F32))
    rank = rank_of(part.shape, theirs)
    half = RATE_B // 2
    at = rows_of(RATE_B)
    pre[1, pl.ds(at, half * SIDE), :] += flat(jnp.where(rank < RATE_B, part, 0.0))
    last = pl.multiple_of(at + half * SIDE, 16)
    pre[1, pl.ds(last, half * SIDE), :] += flat(roll_cols(jnp.where(rank >= RATE_B, part, 0.0), RATE_B))

    slopes = {}
    for k in range(4):
        value = pre0_ref[...] if k == 0 else pre[k - 1]
        sig = sigmoid(value)
        joined_ref[:, k * width : (k + 1) * width] = (value * sig).astype(BF)
        if k in (0, 3):
            slopes[k] = sig * (1.0 + value * (1.0 - sig))
    proj_pre = jnp.dot(joined_ref[...], wp_ref[...], preferred_element_type=F32)
    g_proj = (cot_ref[...].astype(F32) * silu_slope(proj_pre)).astype(BF)
    g_ref[...] = g_proj
    for k, out in ((3, d3_ref), (0, d0_ref)):
        back = lax.dot_general(
            g_proj, wp_ref[k * width : (k + 1) * width, :], (((1,), (1,)), ((), ())), preferred_element_type=F32
        )
        out[...] = (back * slopes[k]).astype(BF)


def merge(pos, pre0, own, row, col, diag, cot, w_proj):
    pixels, width = pre0.shape
    block = jax.ShapeDtypeStruct((pixels, width), BF)
    return call(
        merge_parts,
        [jax.ShapeDtypeStruct((pixels, 4 * width), BF), block, block, block],
        1,
        7,
        2 * pixels * width * width * 6,
        6 * 1024 * 1024,
        18,
        [pltpu.VMEM((3, pixels, width), F32)],
        name="merge",
    )(pos, pre0, own, row, col, diag, cot, w_proj)


def pair_grads(pos_ref, joined_ref, g_ref, x_ref, d0_ref, keep_ref, *send_refs):
    core = pos_ref[4]
    over = (((0,), (0,)), ((), ()))
    grad_proj = lax.dot_general(joined_ref[...], g_ref[...], over, preferred_element_type=F32)
    grad_point = lax.dot_general(x_ref[...], d0_ref[...], over, preferred_element_type=F32)
    keep_ref[...] = jnp.where(core == 0, grad_proj, grad_point)
    half = send_refs[0].shape[0]
    for k, send_ref in enumerate(send_refs):
        part = slice(k * half, (k + 1) * half)
        send_ref[...] = jnp.where(core == 0, grad_point[part], grad_proj[part]).astype(BF)


def shards(features, cotangent, w_point, w_rate_a, w_rate_b, w_rate_c, w_proj, bucket_slot):
    image = features[0]
    rows_dev, cols_dev, chans = image.shape
    pixels = rows_dev * cols_dev
    width = w_point.shape[1]
    row, col, core = (lax.axis_index(n) for n in ("row", "col", "dp_2"))
    at_y, at_z = lax.axis_index("dp_0"), lax.axis_index("dp_1")
    pos = jnp.stack([2 * row + col, at_y, row, col, core, at_z]).astype(jnp.int32)
    replicas = lax.axis_size(DP)
    slot_count = replicas * (bucket_slot.shape[0] // replicas + 1)
    place = place_slots(bucket_slot, core, slot_count)
    centre = image.reshape(pixels, chans)
    weights = [pltpu.with_memory_space_constraint(w, pltpu.HBM) for w in (w_rate_a, w_rate_b, w_rate_c)]
    picked = pick(pos, centre)
    centre, *picked = lax.optimization_barrier((centre, *picked))
    got = [picked[0]] + [flip(picked[k], k) for k in (1, 2, 3)]
    part, *parts = outer(pos, centre, *weights)
    part, got = lax.optimization_barrier((part, got))
    to_row, to_col, to_diag = parts
    parts = [flip(to_row, 2), flip(to_col, 1), flip(to_diag, 3)]
    turned = turn(pos, got)
    pre0, own = inner(pos, centre, part, w_point, *weights)
    parts, pre0, own, turned = lax.optimization_barrier((parts, pre0, own, turned))
    joined, g_proj, delta0, delta3 = merge(
        pos, pre0, own, *parts, cotangent[0].reshape(pixels, width), w_proj
    )
    shared = [delta3] + [flip(delta3, k) for k in (1, 2, 3)]
    block = (4 * width, width)
    kept, *sent = call(
        pair_grads,
        [jax.ShapeDtypeStruct(block, F32)] + [jax.ShapeDtypeStruct((2 * width, width), BF)] * 2,
        1,
        4,
        4 * pixels * chans * width,
        4 * 1024 * 1024,
        16,
        name="pair",
    )(pos, joined, g_proj, centre, delta0)
    got = [swap_core(part) for part in sent]
    got, shared = lax.optimization_barrier((got, shared))
    by_owner = split_pair(pos, kept, got)
    by_owner, shared = lax.optimization_barrier((by_owner, shared))
    by_owner = [by_owner[0]] + [flip(by_owner[k], k) for k in (1, 2, 3)]
    kept, sent = tap_slots(pos, place, shared, turned, slot_count)
    sent, by_owner = lax.optimization_barrier((sent, by_owner))
    mine, other = sum_pair(by_owner)
    return reduce_slots(pos, place, kept, sent, mine, other)


def solution(mesh):
    torus = Mesh(
        mesh.devices.reshape(mesh.shape["row"], mesh.shape["col"], 4, 4, 2),
        ("row", "col", "dp_0", "dp_1", "dp_2"),
    )
    in_specs = (P(DP, "row", "col", None), P(DP, "row", "col", None), P(), P(), P(), P(), P(), P())
    out_specs = P(DP, ("row", "col"))
    return jax.shard_map(
        shards, mesh=torus, in_specs=in_specs, out_specs=out_specs, check_vma=False
    )
```

```python
import jax
import jax.numpy as jnp
from jax import lax
from jax.experimental import pallas as pl
from jax.experimental.pallas import tpu as pltpu
from jax.sharding import Mesh
from jax.sharding import PartitionSpec as P

RATE_A = 6
RATE_B = 12
RATE_C = 18
DP = ("dp_0", "dp_1", "dp_2")


BF = jnp.bfloat16
F32 = jnp.float32
MIB = 1024 * 1024


def flip(x, mask):
    if mask == 1:
        return lax.ppermute(x, "col", [(0, 1), (1, 0)])
    if mask == 2:
        return lax.ppermute(x, "row", [(0, 1), (1, 0)])
    return lax.ppermute(x, ("row", "col"), [(0, 3), (3, 0), (1, 2), (2, 1)])


def smem():
    return pl.BlockSpec(memory_space=pltpu.SMEM)


def vmem():
    return pl.BlockSpec(memory_space=pltpu.VMEM)


def call(body, outs, n_smem, n_vmem, flops, nbytes, limit, scratch=(), name=None, n_any=0):
    return pl.pallas_call(
        body,
        out_shape=outs,
        in_specs=[smem()] * n_smem + [vmem()] * n_vmem + [pl.BlockSpec(memory_space=pltpu.HBM)] * n_any,
        out_specs=jax.tree.map(lambda _: vmem(), outs),
        scratch_shapes=list(scratch),
        compiler_params=pltpu.CompilerParams(vmem_limit_bytes=limit * MIB),
        cost_estimate=pl.CostEstimate(flops=flops, bytes_accessed=nbytes, transcendentals=0),
        name=name,
    )


def select_channels(pos_ref, x_ref, *rest):
    *o_refs, held, sems = rest
    lanes = 128
    group = lanes * len(o_refs)
    pieces = sems.shape[0]
    each = x_ref.shape[0] // pieces
    copies = []
    for n in range(pieces):
        part = pl.ds(n * each, each)
        copies.append(pltpu.make_async_copy(x_ref.at[part, :], held.at[part, :], sems.at[n]))
        copies[n].start()
    source = lax.broadcasted_iota(jnp.int32, (group, group), 0)
    col = lax.broadcasted_iota(jnp.int32, (1, group), 1)
    owner = jnp.bitwise_xor(pos_ref[0], col // lanes)
    wanted = 64 * ((col % lanes) // 16) + 16 * owner + col % 16
    picks = jnp.where(source == wanted, 1.0, 0.0).astype(BF)
    for n in range(pieces):
        copies[n].wait()
        rows = slice(n * each, (n + 1) * each)
        for p in range(x_ref.shape[1] // group):
            taken = jnp.dot(held[rows, p * group : (p + 1) * group], picks, preferred_element_type=F32).astype(BF)
            for k, o_ref in enumerate(o_refs):
                o_ref[rows, p * lanes : (p + 1) * lanes] = taken[:, k * lanes : (k + 1) * lanes]


def turn_pixels(pos_ref, x0, x1, x2, x3, o_ref, held):
    pixels, width = x0.shape
    for k, x in enumerate((x0, x1, x2, x3)):
        s = jnp.bitwise_xor(pos_ref[0], k)
        held[s % 2, pl.ds((s // 2) * pixels, pixels), :] = x[...]
    eye = (
        lax.broadcasted_iota(jnp.int32, (width, width), 0)
        == lax.broadcasted_iota(jnp.int32, (width, width), 1)
    ).astype(F32).astype(BF)
    for g in range(2):
        o_ref[g] = lax.dot_general(
            eye, held[g], (((1,), (1,)), ((), ())), preferred_element_type=F32
        ).astype(BF)


def roll_cols(x, shift):
    return jnp.concatenate([x[:, x.shape[1] - shift :], x[:, : x.shape[1] - shift]], axis=1)


def tap_grads(pos_ref, place_ref, d0, d1, d2, d3, xt_ref, keep_ref, send_ref, held, padded, buf):
    side = RATE_C
    pixels, width = d0.shape
    cols = 24
    rows = pixels // cols
    for k, d in enumerate((d0, d1, d2, d3)):
        s = jnp.bitwise_xor(pos_ref[0], k)
        held[s % 2, pl.ds((s // 2) * pixels, pixels), :] = d[...]
    buf[...] = jnp.zeros_like(buf)
    tall = 2 * pixels
    lead = side * cols
    zeros = jnp.zeros((2, lead, width), BF)
    halves = [held[g].astype(F32).reshape(2 * rows, cols, width) for g in range(2)]
    at = lax.broadcasted_iota(jnp.int32, (2 * rows, cols, width), 1)
    rest = cols - side
    for across in (-1, 0, 1):
        padded[:, pl.ds(0, lead), :] = zeros
        padded[:, pl.ds(lead + tall, lead), :] = zeros
        if across == 0:
            shifted = halves
        elif across == 1:
            rolled = [roll_cols(h, side) for h in halves]
            shifted = [
                jnp.where(at >= side, rolled[0], 0.0),
                jnp.where(at < side, rolled[0], rolled[1]),
            ]
        else:
            rolled = [roll_cols(h, rest) for h in halves]
            shifted = [
                jnp.where(at < rest, rolled[0], rolled[1]),
                jnp.where(at < rest, rolled[1], 0.0),
            ]
        for g in range(2):
            padded[g, pl.ds(lead, tall), :] = shifted[g].reshape(tall, width).astype(BF)
        for above in (-1, 0, 1):
            first, last = {-1: (0, 32), 0: (0, 48), 1: (16, 48)}[above]
            base = first - side * above + side
            total = None
            for g in range(2):
                part = jnp.dot(
                    xt_ref[g, :, first * cols : last * cols],
                    padded[g, base * cols : (base + last - first) * cols, :],
                    preferred_element_type=F32,
                )
                total = part if total is None else total + part
            tap = 3 * (above + 1) + across + 1
            groups = total.reshape(width // 16, 16, width)
            for m in range(width // 16):
                buf[place_ref[32 + 16 * tap + m]] = groups[m]
    half = buf.shape[0] // 2
    keep_ref[...] = buf[:half]
    send_ref[...] = buf[half:].astype(BF)


def join_owners(pos_ref, place_ref, keep_ref, got_ref, mine_ref, other_ref, o_ref, total):
    total[...] = keep_ref[...] + got_ref[...].astype(F32)
    core = pos_ref[4]
    for n in range(mine_ref.shape[0]):
        for ref, first in ((mine_ref, 16 * core), (other_ref, 16 * (1 - core))):
            at = place_ref[first + n]

            @pl.when(at < total.shape[0])
            def _(ref=ref, at=at, n=n):
                total[at] = ref[n].astype(F32)

    o_ref[...] = total[...].astype(BF).reshape(o_ref.shape)


def fold_last(r_ref, o_ref, total):
    value = r_ref[0].astype(F32)
    for n in range(1, r_ref.shape[0]):
        value = value + r_ref[n].astype(F32)
    total[...] = value.reshape(total.shape)
    width = total.shape[2]
    for i in range(total.shape[1]):
        o_ref[:, i * width : (i + 1) * width] = total[:, i, :]


def share_rows(pos_ref, kept_ref, got0, got1, *rest):
    *outs, total = rest
    half, each = got0.shape[0], total.shape[0] // 2
    for n, got in enumerate((got0, got1)):
        value = kept_ref[n * half : (n + 1) * half, :] + got[...].astype(F32)
        total[n * each : (n + 1) * each] = value.reshape(each, *total.shape[1:])
    for k, out in enumerate(outs):
        out[...] = total[:, jnp.bitwise_xor(pos_ref[0], k)].astype(out.dtype)


def swap_core(x):
    return lax.ppermute(x, "dp_2", [(0, 1), (1, 0)])


def pick(pos, centre):
    pixels, chans = centre.shape
    block = jax.ShapeDtypeStruct((pixels, chans // 4), BF)
    return call(
        select_channels,
        [block] * 4,
        1,
        0,
        pixels * chans * chans,
        4 * pixels * chans,
        12,
        [pltpu.VMEM((pixels, chans), BF), pltpu.SemaphoreType.DMA((2,))],
        name="pick",
        n_any=1,
    )(pos, pltpu.with_memory_space_constraint(centre, pltpu.HBM))


def turn(pos, got):
    pixels, width = got[0].shape
    return call(
        turn_pixels,
        jax.ShapeDtypeStruct((2, width, 2 * pixels), BF),
        1,
        4,
        8 * pixels * width * width,
        16 * pixels * width,
        12,
        [pltpu.VMEM((2, 2 * pixels, width), BF)],
        name="turn",
    )(pos, *got)


def split_pair(pos, kept, got):
    width = kept.shape[1]
    slices = kept.shape[0] // 64
    shape = (slices, 16, width)
    return call(
        share_rows,
        [jax.ShapeDtypeStruct(shape, F32)] + [jax.ShapeDtypeStruct(shape, BF)] * 3,
        1,
        3,
        kept.size,
        8 * kept.size,
        10,
        [pltpu.VMEM((slices, 4, 16, width), F32)],
        name="rows",
    )(pos, kept, *got)


def sum_pair(blocks):
    mine = blocks[0] + sum(block.astype(F32) for block in blocks[1:])
    return mine, swap_core(mine.astype(BF))


def place_slots(bucket_slot, core, slot_count):
    replicas = lax.axis_size(DP)
    capacity = slot_count // replicas
    owner = bucket_slot // capacity
    other = jnp.bitwise_xor(owner % 2, core)
    return other * (slot_count // 2) + (owner // 2) * capacity + bucket_slot % capacity


def tap_slots(pos, place, deltas, turned, slot_count):
    pixels, width = deltas[0].shape
    half = slot_count // 2
    return call(
        tap_grads,
        [jax.ShapeDtypeStruct((half, 16, width), F32), jax.ShapeDtypeStruct((half, 16, width), BF)],
        2,
        5,
        2 * 7 * 4 * pixels * width * width,
        8 * 1024 * 1024,
        26,
        [
            pltpu.VMEM((2, 2 * pixels, width), BF),
            pltpu.VMEM((2, 2 * pixels + 2 * RATE_C * SIDE, width), BF),
            pltpu.VMEM((slot_count, 16, width), F32),
        ],
        name="taps",
    )(pos, place, *deltas, turned)


def reduce_slots(pos, place, kept, sent, mine, other):
    half, rows, width = kept.shape
    chips = lax.axis_size("dp_0") * lax.axis_size("dp_1")
    each = half // chips
    total = call(
        join_owners,
        jax.ShapeDtypeStruct((chips, each * rows, width), BF),
        2,
        4,
        kept.size,
        8 * kept.size,
        12,
        [pltpu.VMEM((half, rows, width), F32)],
        name="owners",
    )(pos, place, kept, swap_core(sent), mine, other)
    total = lax.all_to_all(total, ("dp_0", "dp_1"), 0, 0, tiled=True)
    return call(
        fold_last,
        jax.ShapeDtypeStruct((each, rows * width), F32),
        0,
        1,
        kept.size,
        2 * kept.size,
        8,
        [pltpu.VMEM((each, rows, width), F32)],
        name="last",
    )(total)


def sigmoid(value):
    return 0.5 + 0.5 * jnp.tanh(0.5 * value)


def silu_slope(value):
    sig = sigmoid(value)
    return sig * (1.0 + value * (1.0 - sig))


RATES = (RATE_A, RATE_B, RATE_C)
SIDE = 24


def turned_by(x, shift, far):
    return jnp.where(far == 0, roll_cols(x, shift), roll_cols(x, SIDE - shift))


def rank_of(shape, far):
    at = lax.broadcasted_iota(jnp.int32, shape, 1)
    return jnp.where(far == 0, at, SIDE - 1 - at)


def row_marks(low, rate):
    lead = rate * SIDE
    whole = SIDE * SIDE

    def either(upper, lower):
        return pl.multiple_of(jnp.where(low == 0, upper, lower), 16)

    return dict(
        own=either(0, lead),
        out=either(lead, 0),
        theirs=either(whole, 0),
        inward_from=either(lead, 0),
        inward=either(0, 2 * lead),
        kept=either(lead, 0),
        inner=either(0, lead),
    )


def blocks(x):
    return x.reshape(x.shape[0] // SIDE, SIDE, x.shape[1])


def flat(x):
    return x.reshape(x.shape[0] * SIDE, x.shape[2])


def tap_copies(pos_ref, refs, jobs, held, sems):
    copies = []
    for branch, ref in enumerate(refs):
        for n, (above, across) in enumerate(jobs):
            a = 1 if above == 1 else jnp.where(pos_ref[2] == 0, above, 2 - above)
            b = 1 if across == 1 else jnp.where(pos_ref[3] == 0, across, 2 - across)
            width = ref.shape[3]
            to = held.at[branch, :, n * width : (n + 1) * width]
            copies.append(pltpu.make_async_copy(ref.at[a, b], to, sems.at[branch, n]))
    return copies


BRANCHES = ((2, RATE_C), (1, RATE_B), (0, RATE_A))
OUTER = ((0, 0), (1, 0), (0, 1), (0, 2), (2, 0))
INNER = ((1, 1), (1, 2), (2, 1), (2, 2))


def outer_parts(pos_ref, x_ref, wc_ref, wb_ref, wa_ref, pre_ref, row_ref, col_ref, diag_ref, ext, acc, y, held, sems):
    low, far = pos_ref[2], pos_ref[3]
    whole = SIDE * SIDE
    width = pre_ref.shape[2]
    copies = tap_copies(pos_ref, (wc_ref, wb_ref, wa_ref), OUTER, held, sems)
    for copy in copies:
        copy.start()
    first = 0
    for turn, (index, rate) in enumerate(BRANCHES):
        lead = rate * SIDE
        inside = whole - lead
        at = row_marks(low, rate)
        own_rows = pl.ds(at["own"], whole)
        their_rows = pl.ds(at["theirs"], lead)
        kept_rows = pl.ds(at["kept"], inside)
        to_row = slice(first, first + lead)
        first += lead
        count = len(OUTER)
        for copy in copies[turn * count : (turn + 1) * count]:
            copy.wait()
        y[...] = jnp.dot(x_ref[...], held[turn, :, : 4 * width], preferred_element_type=F32)
        ext[pl.ds(pl.multiple_of(whole - at["theirs"], 16), lead), :] = jnp.zeros((lead, width), F32)
        ext[pl.ds(at["out"], whole), :] = y[:, :width]
        ext[own_rows, :] += y[:, width : 2 * width]
        ext[pl.ds(at["inward"], inside), :] += jnp.dot(
            x_ref[pl.ds(at["inward_from"], inside), :], held[turn, :, 4 * width :], preferred_element_type=F32
        )
        own = blocks(ext[own_rows, :])
        ours = turned_by(own, rate, far)
        rank = rank_of(own.shape, far)
        pre_ref[index] = flat(jnp.where(rank >= rate, ours, 0.0))
        below = blocks(ext[their_rows, :])
        theirs = turned_by(below, rate, far)
        place = rank_of(below.shape, far)
        acc[:lead, :] = flat(jnp.where(place >= rate, theirs, 0.0))
        if rate == RATE_C:
            col_ref[:whole, :] = flat(jnp.where(rank < rate, ours, 0.0)).astype(BF)
            diag_ref[:lead, :] = flat(jnp.where(place < rate, theirs, 0.0)).astype(BF)
        elif rate == RATE_B:
            half = rate // 2
            col_ref[whole:, :] = flat(jnp.where(rank[:rate] < rate, ours[:rate], own[rate:])).astype(BF)
            part = place[:half] < rate
            diag_ref[RATE_C * SIDE :, :] = flat(jnp.where(part, theirs[:half], below[half:])).astype(BF)
        else:
            have = blocks(col_ref[:whole, :].astype(F32))
            col_ref[:whole, :] = flat(jnp.where(rank >= RATE_C, own, have)).astype(BF)
            have = blocks(diag_ref[:lead, :].astype(F32))
            diag_ref[:lead, :] = flat(jnp.where(place >= RATE_C, below, have)).astype(BF)
        next_from = pl.multiple_of(jnp.where(low == 0, inside, 0), 16)
        keep_from = pl.multiple_of(jnp.where(low == 0, 0, lead), 16)
        pre_ref[index, kept_rows, :] += y[pl.ds(keep_from, inside), 2 * width : 3 * width]
        own = blocks(y[pl.ds(keep_from, inside), 3 * width :])
        rank = rank_of(own.shape, far)
        pre_ref[index, kept_rows, :] += flat(jnp.where(rank < SIDE - rate, turned_by(own, rate, 1 - far), 0.0))
        below = blocks(y[pl.ds(next_from, lead), 3 * width :])
        theirs = flat(jnp.where(place < SIDE - rate, turned_by(below, rate, 1 - far), 0.0))
        row_ref[to_row, :] = (acc[:lead, :] + y[pl.ds(next_from, lead), 2 * width : 3 * width] + theirs).astype(BF)


def inner_parts(pos_ref, x_ref, part_ref, wp_ref, wc_ref, wb_ref, wa_ref, pre0_ref, pre_ref, y, z, held, sems):
    low, far = pos_ref[2], pos_ref[3]
    whole = SIDE * SIDE
    width = pre0_ref.shape[1]
    copies = tap_copies(pos_ref, (wc_ref, wb_ref, wa_ref), INNER, held, sems)
    for copy in copies:
        copy.start()
    pre0_ref[...] = jnp.dot(x_ref[...], wp_ref[...], preferred_element_type=F32)
    for turn, (index, rate) in enumerate(BRANCHES):
        lead = rate * SIDE
        inside = whole - lead
        at = row_marks(low, rate)
        from_rows = pl.ds(at["inward_from"], inside)
        to_rows = pl.ds(at["inner"], inside)
        count = len(INNER)
        for copy in copies[turn * count : (turn + 1) * count]:
            copy.wait()
        y[...] = jnp.dot(x_ref[...], held[turn, :, : 2 * width], preferred_element_type=F32)
        z[:inside, :] = jnp.dot(x_ref[from_rows, :], held[turn, :, 2 * width :], preferred_element_type=F32)
        y[to_rows, :] += z[:inside, :]
        own = blocks(y[:, width:])
        rank = rank_of(own.shape, far)
        moved = flat(jnp.where(rank < SIDE - rate, turned_by(own, rate, 1 - far), 0.0))
        pre_ref[index] = part_ref[index] + y[:, :width] + moved


def outer(pos, centre, w_rate_a, w_rate_b, w_rate_c):
    pixels, chans = centre.shape
    width = w_rate_a.shape[3]
    sends = (RATE_A + RATE_B + RATE_C) * SIDE
    shapes = [((3, pixels, width), F32), ((sends, width), BF), ((sends, width), BF), ((pixels, width), BF)]
    return call(
        outer_parts,
        [jax.ShapeDtypeStruct(*s) for s in shapes],
        1,
        1,
        2 * pixels * chans * width * 14,
        10 * MIB,
        28,
        [
            pltpu.VMEM(((SIDE + RATE_C) * SIDE, width), F32),
            pltpu.VMEM((RATE_C * SIDE, width), F32),
            pltpu.VMEM((pixels, 4 * width), F32),
            pltpu.VMEM((3, chans, len(OUTER) * width), BF),
            pltpu.SemaphoreType.DMA((3, len(OUTER))),
        ],
        name="outer",
        n_any=3,
    )(pos, centre, w_rate_c, w_rate_b, w_rate_a)


def inner(pos, centre, part, w_point, w_rate_a, w_rate_b, w_rate_c):
    pixels, chans = centre.shape
    width = w_point.shape[1]
    return call(
        inner_parts,
        [jax.ShapeDtypeStruct((pixels, width), F32), jax.ShapeDtypeStruct((3, pixels, width), F32)],
        1,
        3,
        2 * pixels * chans * width * 10,
        10 * MIB,
        26,
        [
            pltpu.VMEM((pixels, 2 * width), F32),
            pltpu.VMEM((pixels, 2 * width), F32),
            pltpu.VMEM((3, chans, len(INNER) * width), BF),
            pltpu.SemaphoreType.DMA((3, len(INNER))),
        ],
        name="inner",
        n_any=3,
    )(pos, centre, part, w_point, w_rate_c, w_rate_b, w_rate_a)


def merge_parts(
    pos_ref, pre0_ref, own_ref, row_ref, col_ref, diag_ref, cot_ref, wp_ref, joined_ref, g_ref, d0_ref, d3_ref, pre
):
    low = pos_ref[2]
    theirs = 1 - pos_ref[3]
    width = pre0_ref.shape[1]
    whole = SIDE * SIDE

    def rows_of(rate):
        return pl.multiple_of(jnp.where(low == 0, (SIDE - rate) * SIDE, 0), 16)

    pre[...] = own_ref[...]
    first = 0
    for index, rate in ((2, RATE_C), (1, RATE_B), (0, RATE_A)):
        lead = rate * SIDE
        pre[index, pl.ds(rows_of(rate), lead), :] += row_ref[first : first + lead, :].astype(F32)
        first += lead

    part = blocks(col_ref[:whole, :].astype(F32))
    rank = rank_of(part.shape, theirs)
    pre[2] += flat(jnp.where(rank < RATE_C, part, 0.0))
    pre[0] += flat(turned_by(jnp.where(rank >= RATE_C, part, 0.0), RATE_A, theirs))
    part = blocks(col_ref[whole:, :].astype(F32))
    rank = rank_of(part.shape, theirs)
    pre[1, : RATE_B * SIDE, :] += flat(jnp.where(rank < RATE_B, part, 0.0))
    pre[1, RATE_B * SIDE :, :] += flat(roll_cols(jnp.where(rank >= RATE_B, part, 0.0), RATE_B))

    part = blocks(diag_ref[: RATE_C * SIDE, :].astype(F32))
    rank = rank_of(part.shape, theirs)
    pre[2, pl.ds(rows_of(RATE_C), RATE_C * SIDE), :] += flat(jnp.where(rank < RATE_C, part, 0.0))
    few = part[:RATE_A]
    few = turned_by(jnp.where(rank[:RATE_A] >= RATE_C, few, 0.0), RATE_A, theirs)
    pre[0, pl.ds(rows_of(RATE_A), RATE_A * SIDE), :] += flat(few)
    part = blocks(diag_ref[RATE_C * SIDE :, :].astype(F32))
    rank = rank_of(part.shape, theirs)
    half = RATE_B // 2
    at = rows_of(RATE_B)
    pre[1, pl.ds(at, half * SIDE), :] += flat(jnp.where(rank < RATE_B, part, 0.0))
    last = pl.multiple_of(at + half * SIDE, 16)
    pre[1, pl.ds(last, half * SIDE), :] += flat(roll_cols(jnp.where(rank >= RATE_B, part, 0.0), RATE_B))

    slopes = {}
    for k in range(4):
        value = pre0_ref[...] if k == 0 else pre[k - 1]
        sig = sigmoid(value)
        joined_ref[:, k * width : (k + 1) * width] = (value * sig).astype(BF)
        if k in (0, 3):
            slopes[k] = sig * (1.0 + value * (1.0 - sig))
    proj_pre = jnp.dot(joined_ref[...], wp_ref[...], preferred_element_type=F32)
    g_proj = (cot_ref[...].astype(F32) * silu_slope(proj_pre)).astype(BF)
    g_ref[...] = g_proj
    for k, out in ((3, d3_ref), (0, d0_ref)):
        back = lax.dot_general(
            g_proj, wp_ref[k * width : (k + 1) * width, :], (((1,), (1,)), ((), ())), preferred_element_type=F32
        )
        out[...] = (back * slopes[k]).astype(BF)


def merge(pos, pre0, own, row, col, diag, cot, w_proj):
    pixels, width = pre0.shape
    block = jax.ShapeDtypeStruct((pixels, width), BF)
    return call(
        merge_parts,
        [jax.ShapeDtypeStruct((pixels, 4 * width), BF), block, block, block],
        1,
        7,
        2 * pixels * width * width * 6,
        6 * 1024 * 1024,
        18,
        [pltpu.VMEM((3, pixels, width), F32)],
        name="merge",
    )(pos, pre0, own, row, col, diag, cot, w_proj)


def pair_grads(pos_ref, joined_ref, g_ref, x_ref, d0_ref, keep_ref, *send_refs):
    core = pos_ref[4]
    over = (((0,), (0,)), ((), ()))
    grad_proj = lax.dot_general(joined_ref[...], g_ref[...], over, preferred_element_type=F32)
    grad_point = lax.dot_general(x_ref[...], d0_ref[...], over, preferred_element_type=F32)
    keep_ref[...] = jnp.where(core == 0, grad_proj, grad_point)
    half = send_refs[0].shape[0]
    for k, send_ref in enumerate(send_refs):
        part = slice(k * half, (k + 1) * half)
        send_ref[...] = jnp.where(core == 0, grad_point[part], grad_proj[part]).astype(BF)


def shards(features, cotangent, w_point, w_rate_a, w_rate_b, w_rate_c, w_proj, bucket_slot):
    image = features[0]
    rows_dev, cols_dev, chans = image.shape
    pixels = rows_dev * cols_dev
    width = w_point.shape[1]
    row, col, core = (lax.axis_index(n) for n in ("row", "col", "dp_2"))
    at_y, at_z = lax.axis_index("dp_0"), lax.axis_index("dp_1")
    pos = jnp.stack([2 * row + col, at_y, row, col, core, at_z]).astype(jnp.int32)
    replicas = lax.axis_size(DP)
    slot_count = replicas * (bucket_slot.shape[0] // replicas + 1)
    place = place_slots(bucket_slot, core, slot_count)
    centre = image.reshape(pixels, chans)
    weights = [pltpu.with_memory_space_constraint(w, pltpu.HBM) for w in (w_rate_a, w_rate_b, w_rate_c)]
    picked = pick(pos, centre)
    centre, *picked = lax.optimization_barrier((centre, *picked))
    got = [picked[0]] + [flip(picked[k], k) for k in (1, 2, 3)]
    part, *parts = outer(pos, centre, *weights)
    part, got = lax.optimization_barrier((part, got))
    to_row, to_col, to_diag = parts
    parts = [flip(to_row, 2), flip(to_col, 1), flip(to_diag, 3)]
    turned = turn(pos, got)
    pre0, own = inner(pos, centre, part, w_point, *weights)
    parts, pre0, own, turned = lax.optimization_barrier((parts, pre0, own, turned))
    joined, g_proj, delta0, delta3 = merge(
        pos, pre0, own, *parts, cotangent[0].reshape(pixels, width), w_proj
    )
    shared = [delta3] + [flip(delta3, k) for k in (1, 2, 3)]
    block = (4 * width, width)
    kept, *sent = call(
        pair_grads,
        [jax.ShapeDtypeStruct(block, F32)] + [jax.ShapeDtypeStruct((2 * width, width), BF)] * 2,
        1,
        4,
        4 * pixels * chans * width,
        4 * 1024 * 1024,
        16,
        name="pair",
    )(pos, joined, g_proj, centre, delta0)
    got = [swap_core(part) for part in sent]
    by_owner = split_pair(pos, kept, got)
    early = [flip(by_owner[k], k) for k in (1, 2)]
    late, early, shared = lax.optimization_barrier((by_owner[3], early, shared))
    by_owner = [by_owner[0], *early, flip(late, 3)]
    kept, sent = tap_slots(pos, place, shared, turned, slot_count)
    sent, by_owner = lax.optimization_barrier((sent, by_owner))
    mine, other = sum_pair(by_owner)
    return reduce_slots(pos, place, kept, sent, mine, other)


def solution(mesh):
    torus = Mesh(
        mesh.devices.reshape(mesh.shape["row"], mesh.shape["col"], 4, 4, 2),
        ("row", "col", "dp_0", "dp_1", "dp_2"),
    )
    in_specs = (P(DP, "row", "col", None), P(DP, "row", "col", None), P(), P(), P(), P(), P(), P())
    out_specs = P(DP, ("row", "col"))
    return jax.shard_map(
        shards, mesh=torus, in_specs=in_specs, out_specs=out_specs, check_vma=False
    )
```

```python
import jax
import jax.numpy as jnp
from jax import lax
from jax.experimental import pallas as pl
from jax.experimental.pallas import tpu as pltpu
from jax.sharding import Mesh
from jax.sharding import PartitionSpec as P

RATE_A = 6
RATE_B = 12
RATE_C = 18
DP = ("dp_0", "dp_1", "dp_2")


BF = jnp.bfloat16
F32 = jnp.float32
MIB = 1024 * 1024


def flip(x, mask):
    if mask == 1:
        return lax.ppermute(x, "col", [(0, 1), (1, 0)])
    if mask == 2:
        return lax.ppermute(x, "row", [(0, 1), (1, 0)])
    return lax.ppermute(x, ("row", "col"), [(0, 3), (3, 0), (1, 2), (2, 1)])


def smem():
    return pl.BlockSpec(memory_space=pltpu.SMEM)


def vmem():
    return pl.BlockSpec(memory_space=pltpu.VMEM)


def call(body, outs, n_smem, n_vmem, flops, nbytes, limit, scratch=(), name=None, n_any=0):
    return pl.pallas_call(
        body,
        out_shape=outs,
        in_specs=[smem()] * n_smem + [vmem()] * n_vmem + [pl.BlockSpec(memory_space=pltpu.HBM)] * n_any,
        out_specs=jax.tree.map(lambda _: vmem(), outs),
        scratch_shapes=list(scratch),
        compiler_params=pltpu.CompilerParams(vmem_limit_bytes=limit * MIB),
        cost_estimate=pl.CostEstimate(flops=flops, bytes_accessed=nbytes, transcendentals=0),
        name=name,
    )


def select_channels(pos_ref, x_ref, *rest):
    *o_refs, held, sems = rest
    lanes = 128
    group = lanes * len(o_refs)
    pieces = sems.shape[0]
    each = x_ref.shape[0] // pieces
    copies = []
    for n in range(pieces):
        part = pl.ds(n * each, each)
        copies.append(pltpu.make_async_copy(x_ref.at[part, :], held.at[part, :], sems.at[n]))
        copies[n].start()
    source = lax.broadcasted_iota(jnp.int32, (group, group), 0)
    col = lax.broadcasted_iota(jnp.int32, (1, group), 1)
    owner = jnp.bitwise_xor(pos_ref[0], col // lanes)
    wanted = 64 * ((col % lanes) // 16) + 16 * owner + col % 16
    picks = jnp.where(source == wanted, 1.0, 0.0).astype(BF)
    for n in range(pieces):
        copies[n].wait()
        rows = slice(n * each, (n + 1) * each)
        for p in range(x_ref.shape[1] // group):
            taken = jnp.dot(held[rows, p * group : (p + 1) * group], picks, preferred_element_type=F32).astype(BF)
            for k, o_ref in enumerate(o_refs):
                o_ref[rows, p * lanes : (p + 1) * lanes] = taken[:, k * lanes : (k + 1) * lanes]


def turn_pixels(pos_ref, x0, x1, x2, x3, o_ref, held):
    pixels, width = x0.shape
    for k, x in enumerate((x0, x1, x2, x3)):
        s = jnp.bitwise_xor(pos_ref[0], k)
        held[s % 2, pl.ds((s // 2) * pixels, pixels), :] = x[...]
    eye = (
        lax.broadcasted_iota(jnp.int32, (width, width), 0)
        == lax.broadcasted_iota(jnp.int32, (width, width), 1)
    ).astype(F32).astype(BF)
    for g in range(2):
        o_ref[g] = lax.dot_general(
            eye, held[g], (((1,), (1,)), ((), ())), preferred_element_type=F32
        ).astype(BF)


def roll_cols(x, shift):
    return jnp.concatenate([x[:, x.shape[1] - shift :], x[:, : x.shape[1] - shift]], axis=1)


def tap_grads(pos_ref, place_ref, d0, d1, d2, d3, xt_ref, keep_ref, send_ref, held, padded, buf):
    side = RATE_C
    pixels, width = d0.shape
    cols = 24
    rows = pixels // cols
    for k, d in enumerate((d0, d1, d2, d3)):
        s = jnp.bitwise_xor(pos_ref[0], k)
        held[s % 2, pl.ds((s // 2) * pixels, pixels), :] = d[...]
    buf[...] = jnp.zeros_like(buf)
    tall = 2 * pixels
    lead = side * cols
    zeros = jnp.zeros((2, lead, width), BF)
    halves = [held[g].astype(F32).reshape(2 * rows, cols, width) for g in range(2)]
    at = lax.broadcasted_iota(jnp.int32, (2 * rows, cols, width), 1)
    rest = cols - side
    for across in (0, 1, -1):
        turn = across + 1
        padded[turn, :, pl.ds(0, lead), :] = zeros
        padded[turn, :, pl.ds(lead + tall, lead), :] = zeros
        if across == 0:
            shifted = halves
        elif across == 1:
            rolled = [roll_cols(h, side) for h in halves]
            shifted = [
                jnp.where(at >= side, rolled[0], 0.0),
                jnp.where(at < side, rolled[0], rolled[1]),
            ]
        else:
            rolled = [roll_cols(h, rest) for h in halves]
            shifted = [
                jnp.where(at < rest, rolled[0], rolled[1]),
                jnp.where(at < rest, rolled[1], 0.0),
            ]
        for g in range(2):
            padded[turn, g, pl.ds(lead, tall), :] = shifted[g].reshape(tall, width).astype(BF)
        for above in (-1, 0, 1):
            first, last = {-1: (0, 32), 0: (0, 48), 1: (16, 48)}[above]
            base = first - side * above + side
            total = None
            for g in range(2):
                part = jnp.dot(
                    xt_ref[g, :, first * cols : last * cols],
                    padded[turn, g, base * cols : (base + last - first) * cols, :],
                    preferred_element_type=F32,
                )
                total = part if total is None else total + part
            tap = 3 * (above + 1) + across + 1
            groups = total.reshape(width // 16, 16, width)
            for m in range(width // 16):
                buf[place_ref[32 + 16 * tap + m]] = groups[m]
    half = buf.shape[0] // 2
    keep_ref[...] = buf[:half]
    send_ref[...] = buf[half:].astype(BF)


def join_owners(pos_ref, place_ref, keep_ref, got_ref, mine_ref, other_ref, o_ref, total):
    total[...] = keep_ref[...] + got_ref[...].astype(F32)
    core = pos_ref[4]
    for n in range(mine_ref.shape[0]):
        for ref, first in ((mine_ref, 16 * core), (other_ref, 16 * (1 - core))):
            at = place_ref[first + n]

            @pl.when(at < total.shape[0])
            def _(ref=ref, at=at, n=n):
                total[at] = ref[n].astype(F32)

    o_ref[...] = total[...].astype(BF).reshape(o_ref.shape)


def fold_last(r_ref, o_ref, total):
    value = r_ref[0].astype(F32)
    for n in range(1, r_ref.shape[0]):
        value = value + r_ref[n].astype(F32)
    total[...] = value.reshape(total.shape)
    width = total.shape[2]
    for i in range(total.shape[1]):
        o_ref[:, i * width : (i + 1) * width] = total[:, i, :]


def share_rows(pos_ref, kept_ref, got0, got1, *rest):
    *outs, total = rest
    half, each = got0.shape[0], total.shape[0] // 2
    for n, got in enumerate((got0, got1)):
        value = kept_ref[n * half : (n + 1) * half, :] + got[...].astype(F32)
        total[n * each : (n + 1) * each] = value.reshape(each, *total.shape[1:])
    for k, out in enumerate(outs):
        out[...] = total[:, jnp.bitwise_xor(pos_ref[0], k)].astype(out.dtype)


def swap_core(x):
    return lax.ppermute(x, "dp_2", [(0, 1), (1, 0)])


def pick(pos, centre):
    pixels, chans = centre.shape
    block = jax.ShapeDtypeStruct((pixels, chans // 4), BF)
    return call(
        select_channels,
        [block] * 4,
        1,
        0,
        pixels * chans * chans,
        4 * pixels * chans,
        12,
        [pltpu.VMEM((pixels, chans), BF), pltpu.SemaphoreType.DMA((2,))],
        name="pick",
        n_any=1,
    )(pos, pltpu.with_memory_space_constraint(centre, pltpu.HBM))


def turn(pos, got):
    pixels, width = got[0].shape
    return call(
        turn_pixels,
        jax.ShapeDtypeStruct((2, width, 2 * pixels), BF),
        1,
        4,
        8 * pixels * width * width,
        16 * pixels * width,
        12,
        [pltpu.VMEM((2, 2 * pixels, width), BF)],
        name="turn",
    )(pos, *got)


def split_pair(pos, kept, got):
    width = kept.shape[1]
    slices = kept.shape[0] // 64
    shape = (slices, 16, width)
    return call(
        share_rows,
        [jax.ShapeDtypeStruct(shape, F32)] + [jax.ShapeDtypeStruct(shape, BF)] * 3,
        1,
        3,
        0,
        0,
        10,
        [pltpu.VMEM((slices, 4, 16, width), F32)],
        name="rows",
    )(pos, kept, *got)


def sum_pair(blocks):
    mine = blocks[0] + sum(block.astype(F32) for block in blocks[1:])
    return mine, swap_core(mine.astype(BF))


def place_slots(bucket_slot, core, slot_count):
    replicas = lax.axis_size(DP)
    capacity = slot_count // replicas
    owner = bucket_slot // capacity
    other = jnp.bitwise_xor(owner % 2, core)
    return other * (slot_count // 2) + (owner // 2) * capacity + bucket_slot % capacity


def tap_slots(pos, place, deltas, turned, slot_count):
    pixels, width = deltas[0].shape
    half = slot_count // 2
    return call(
        tap_grads,
        [jax.ShapeDtypeStruct((half, 16, width), F32), jax.ShapeDtypeStruct((half, 16, width), BF)],
        2,
        5,
        2 * 7 * 4 * pixels * width * width,
        8 * 1024 * 1024,
        26,
        [
            pltpu.VMEM((2, 2 * pixels, width), BF),
            pltpu.VMEM((3, 2, 2 * pixels + 2 * RATE_C * SIDE, width), BF),
            pltpu.VMEM((slot_count, 16, width), F32),
        ],
        name="taps",
    )(pos, place, *deltas, turned)


def reduce_slots(pos, place, kept, sent, mine, other):
    half, rows, width = kept.shape
    chips = lax.axis_size("dp_0") * lax.axis_size("dp_1")
    each = half // chips
    total = call(
        join_owners,
        jax.ShapeDtypeStruct((chips, each * rows, width), BF),
        2,
        4,
        kept.size,
        8 * kept.size,
        12,
        [pltpu.VMEM((half, rows, width), F32)],
        name="owners",
    )(pos, place, kept, swap_core(sent), mine, other)
    total = lax.all_to_all(total, ("dp_0", "dp_1"), 0, 0, tiled=True)
    return call(
        fold_last,
        jax.ShapeDtypeStruct((each, rows * width), F32),
        0,
        1,
        kept.size,
        2 * kept.size,
        8,
        [pltpu.VMEM((each, rows, width), F32)],
        name="last",
    )(total)


def sigmoid(value):
    return 0.5 + 0.5 * jnp.tanh(0.5 * value)


def silu_slope(value):
    sig = sigmoid(value)
    return sig * (1.0 + value * (1.0 - sig))


RATES = (RATE_A, RATE_B, RATE_C)
SIDE = 24


def turned_by(x, shift, far):
    return jnp.where(far == 0, roll_cols(x, shift), roll_cols(x, SIDE - shift))


def rank_of(shape, far):
    at = lax.broadcasted_iota(jnp.int32, shape, 1)
    return jnp.where(far == 0, at, SIDE - 1 - at)


def row_marks(low, rate):
    lead = rate * SIDE
    whole = SIDE * SIDE

    def either(upper, lower):
        return pl.multiple_of(jnp.where(low == 0, upper, lower), 16)

    return dict(
        own=either(0, lead),
        out=either(lead, 0),
        theirs=either(whole, 0),
        inward_from=either(lead, 0),
        inward=either(0, 2 * lead),
        kept=either(lead, 0),
        inner=either(0, lead),
    )


def blocks(x):
    return x.reshape(x.shape[0] // SIDE, SIDE, x.shape[1])


def flat(x):
    return x.reshape(x.shape[0] * SIDE, x.shape[2])


def tap_copies(pos_ref, refs, jobs, held, sems):
    copies = []
    for branch, ref in enumerate(refs):
        for n, (above, across) in enumerate(jobs):
            a = 1 if above == 1 else jnp.where(pos_ref[2] == 0, above, 2 - above)
            b = 1 if across == 1 else jnp.where(pos_ref[3] == 0, across, 2 - across)
            width = ref.shape[3]
            to = held.at[branch, :, n * width : (n + 1) * width]
            copies.append(pltpu.make_async_copy(ref.at[a, b], to, sems.at[branch, n]))
    return copies


BRANCHES = ((2, RATE_C), (1, RATE_B), (0, RATE_A))
OUTER = ((0, 0), (1, 0), (0, 1), (0, 2), (2, 0))
INNER = ((1, 1), (1, 2), (2, 1), (2, 2))


def outer_parts(pos_ref, x_ref, wc_ref, wb_ref, wa_ref, pre_ref, row_ref, col_ref, diag_ref, ext, acc, y, held, sems):
    low, far = pos_ref[2], pos_ref[3]
    whole = SIDE * SIDE
    width = pre_ref.shape[2]
    copies = tap_copies(pos_ref, (wc_ref, wb_ref, wa_ref), OUTER, held, sems)
    for copy in copies:
        copy.start()
    first = 0
    for turn, (index, rate) in enumerate(BRANCHES):
        lead = rate * SIDE
        inside = whole - lead
        at = row_marks(low, rate)
        own_rows = pl.ds(at["own"], whole)
        their_rows = pl.ds(at["theirs"], lead)
        kept_rows = pl.ds(at["kept"], inside)
        to_row = slice(first, first + lead)
        first += lead
        count = len(OUTER)
        for copy in copies[turn * count : (turn + 1) * count]:
            copy.wait()
        y[...] = jnp.dot(x_ref[...], held[turn, :, : 4 * width], preferred_element_type=F32)
        ext[pl.ds(pl.multiple_of(whole - at["theirs"], 16), lead), :] = jnp.zeros((lead, width), F32)
        ext[pl.ds(at["out"], whole), :] = y[:, :width]
        ext[own_rows, :] += y[:, width : 2 * width]
        ext[pl.ds(at["inward"], inside), :] += jnp.dot(
            x_ref[pl.ds(at["inward_from"], inside), :], held[turn, :, 4 * width :], preferred_element_type=F32
        )
        own = blocks(ext[own_rows, :])
        ours = turned_by(own, rate, far)
        rank = rank_of(own.shape, far)
        pre_ref[index] = flat(jnp.where(rank >= rate, ours, 0.0))
        below = blocks(ext[their_rows, :])
        theirs = turned_by(below, rate, far)
        place = rank_of(below.shape, far)
        acc[:lead, :] = flat(jnp.where(place >= rate, theirs, 0.0))
        if rate == RATE_C:
            col_ref[:whole, :] = flat(jnp.where(rank < rate, ours, 0.0)).astype(BF)
            diag_ref[:lead, :] = flat(jnp.where(place < rate, theirs, 0.0)).astype(BF)
        elif rate == RATE_B:
            half = rate // 2
            col_ref[whole:, :] = flat(jnp.where(rank[:rate] < rate, ours[:rate], own[rate:])).astype(BF)
            part = place[:half] < rate
            diag_ref[RATE_C * SIDE :, :] = flat(jnp.where(part, theirs[:half], below[half:])).astype(BF)
        else:
            have = blocks(col_ref[:whole, :].astype(F32))
            col_ref[:whole, :] = flat(jnp.where(rank >= RATE_C, own, have)).astype(BF)
            have = blocks(diag_ref[:lead, :].astype(F32))
            diag_ref[:lead, :] = flat(jnp.where(place >= RATE_C, below, have)).astype(BF)
        next_from = pl.multiple_of(jnp.where(low == 0, inside, 0), 16)
        keep_from = pl.multiple_of(jnp.where(low == 0, 0, lead), 16)
        pre_ref[index, kept_rows, :] += y[pl.ds(keep_from, inside), 2 * width : 3 * width]
        own = blocks(y[pl.ds(keep_from, inside), 3 * width :])
        rank = rank_of(own.shape, far)
        pre_ref[index, kept_rows, :] += flat(jnp.where(rank < SIDE - rate, turned_by(own, rate, 1 - far), 0.0))
        below = blocks(y[pl.ds(next_from, lead), 3 * width :])
        theirs = flat(jnp.where(place < SIDE - rate, turned_by(below, rate, 1 - far), 0.0))
        row_ref[to_row, :] = (acc[:lead, :] + y[pl.ds(next_from, lead), 2 * width : 3 * width] + theirs).astype(BF)


def inner_parts(pos_ref, x_ref, part_ref, wp_ref, wc_ref, wb_ref, wa_ref, pre0_ref, pre_ref, y, z, held, sems):
    low, far = pos_ref[2], pos_ref[3]
    whole = SIDE * SIDE
    width = pre0_ref.shape[1]
    copies = tap_copies(pos_ref, (wc_ref, wb_ref, wa_ref), INNER, held, sems)
    for copy in copies:
        copy.start()
    pre0_ref[...] = jnp.dot(x_ref[...], wp_ref[...], preferred_element_type=F32)
    for turn, (index, rate) in enumerate(BRANCHES):
        lead = rate * SIDE
        inside = whole - lead
        at = row_marks(low, rate)
        from_rows = pl.ds(at["inward_from"], inside)
        to_rows = pl.ds(at["inner"], inside)
        count = len(INNER)
        for copy in copies[turn * count : (turn + 1) * count]:
            copy.wait()
        y[...] = jnp.dot(x_ref[...], held[turn, :, : 2 * width], preferred_element_type=F32)
        z[:inside, :] = jnp.dot(x_ref[from_rows, :], held[turn, :, 2 * width :], preferred_element_type=F32)
        y[to_rows, :] += z[:inside, :]
        own = blocks(y[:, width:])
        rank = rank_of(own.shape, far)
        moved = flat(jnp.where(rank < SIDE - rate, turned_by(own, rate, 1 - far), 0.0))
        pre_ref[index] = part_ref[index] + y[:, :width] + moved


def outer(pos, centre, w_rate_a, w_rate_b, w_rate_c):
    pixels, chans = centre.shape
    width = w_rate_a.shape[3]
    sends = (RATE_A + RATE_B + RATE_C) * SIDE
    shapes = [((3, pixels, width), F32), ((sends, width), BF), ((sends, width), BF), ((pixels, width), BF)]
    return call(
        outer_parts,
        [jax.ShapeDtypeStruct(*s) for s in shapes],
        1,
        1,
        2 * pixels * chans * width * 14,
        10 * MIB,
        28,
        [
            pltpu.VMEM(((SIDE + RATE_C) * SIDE, width), F32),
            pltpu.VMEM((RATE_C * SIDE, width), F32),
            pltpu.VMEM((pixels, 4 * width), F32),
            pltpu.VMEM((3, chans, len(OUTER) * width), BF),
            pltpu.SemaphoreType.DMA((3, len(OUTER))),
        ],
        name="outer",
        n_any=3,
    )(pos, centre, w_rate_c, w_rate_b, w_rate_a)


def inner(pos, centre, part, w_point, w_rate_a, w_rate_b, w_rate_c):
    pixels, chans = centre.shape
    width = w_point.shape[1]
    return call(
        inner_parts,
        [jax.ShapeDtypeStruct((pixels, width), F32), jax.ShapeDtypeStruct((3, pixels, width), F32)],
        1,
        3,
        2 * pixels * chans * width * 10,
        10 * MIB,
        26,
        [
            pltpu.VMEM((pixels, 2 * width), F32),
            pltpu.VMEM((pixels, 2 * width), F32),
            pltpu.VMEM((3, chans, len(INNER) * width), BF),
            pltpu.SemaphoreType.DMA((3, len(INNER))),
        ],
        name="inner",
        n_any=3,
    )(pos, centre, part, w_point, w_rate_c, w_rate_b, w_rate_a)


def merge_parts(
    pos_ref, pre0_ref, own_ref, row_ref, col_ref, diag_ref, cot_ref, wp_ref, joined_ref, g_ref, d0_ref, d3_ref, pre
):
    low = pos_ref[2]
    theirs = 1 - pos_ref[3]
    width = pre0_ref.shape[1]
    whole = SIDE * SIDE

    def rows_of(rate):
        return pl.multiple_of(jnp.where(low == 0, (SIDE - rate) * SIDE, 0), 16)

    pre[...] = own_ref[...]
    first = 0
    for index, rate in ((2, RATE_C), (1, RATE_B), (0, RATE_A)):
        lead = rate * SIDE
        pre[index, pl.ds(rows_of(rate), lead), :] += row_ref[first : first + lead, :].astype(F32)
        first += lead

    part = blocks(col_ref[:whole, :].astype(F32))
    rank = rank_of(part.shape, theirs)
    pre[2] += flat(jnp.where(rank < RATE_C, part, 0.0))
    pre[0] += flat(turned_by(jnp.where(rank >= RATE_C, part, 0.0), RATE_A, theirs))
    part = blocks(col_ref[whole:, :].astype(F32))
    rank = rank_of(part.shape, theirs)
    pre[1, : RATE_B * SIDE, :] += flat(jnp.where(rank < RATE_B, part, 0.0))
    pre[1, RATE_B * SIDE :, :] += flat(roll_cols(jnp.where(rank >= RATE_B, part, 0.0), RATE_B))

    part = blocks(diag_ref[: RATE_C * SIDE, :].astype(F32))
    rank = rank_of(part.shape, theirs)
    pre[2, pl.ds(rows_of(RATE_C), RATE_C * SIDE), :] += flat(jnp.where(rank < RATE_C, part, 0.0))
    few = part[:RATE_A]
    few = turned_by(jnp.where(rank[:RATE_A] >= RATE_C, few, 0.0), RATE_A, theirs)
    pre[0, pl.ds(rows_of(RATE_A), RATE_A * SIDE), :] += flat(few)
    part = blocks(diag_ref[RATE_C * SIDE :, :].astype(F32))
    rank = rank_of(part.shape, theirs)
    half = RATE_B // 2
    at = rows_of(RATE_B)
    pre[1, pl.ds(at, half * SIDE), :] += flat(jnp.where(rank < RATE_B, part, 0.0))
    last = pl.multiple_of(at + half * SIDE, 16)
    pre[1, pl.ds(last, half * SIDE), :] += flat(roll_cols(jnp.where(rank >= RATE_B, part, 0.0), RATE_B))

    slopes = {}
    for k in range(4):
        value = pre0_ref[...] if k == 0 else pre[k - 1]
        sig = sigmoid(value)
        joined_ref[:, k * width : (k + 1) * width] = (value * sig).astype(BF)
        if k in (0, 3):
            slopes[k] = sig * (1.0 + value * (1.0 - sig))
    proj_pre = jnp.dot(joined_ref[...], wp_ref[...], preferred_element_type=F32)
    g_proj = (cot_ref[...].astype(F32) * silu_slope(proj_pre)).astype(BF)
    g_ref[...] = g_proj
    for k, out in ((3, d3_ref), (0, d0_ref)):
        back = lax.dot_general(
            g_proj, wp_ref[k * width : (k + 1) * width, :], (((1,), (1,)), ((), ())), preferred_element_type=F32
        )
        out[...] = (back * slopes[k]).astype(BF)


def merge(pos, pre0, own, row, col, diag, cot, w_proj):
    pixels, width = pre0.shape
    block = jax.ShapeDtypeStruct((pixels, width), BF)
    return call(
        merge_parts,
        [jax.ShapeDtypeStruct((pixels, 4 * width), BF), block, block, block],
        1,
        7,
        2 * pixels * width * width * 6,
        6 * 1024 * 1024,
        18,
        [pltpu.VMEM((3, pixels, width), F32)],
        name="merge",
    )(pos, pre0, own, row, col, diag, cot, w_proj)


def pair_grads(pos_ref, joined_ref, g_ref, x_ref, d0_ref, keep_ref, *send_refs):
    core = pos_ref[4]
    over = (((0,), (0,)), ((), ()))
    grad_proj = lax.dot_general(joined_ref[...], g_ref[...], over, preferred_element_type=F32)
    grad_point = lax.dot_general(x_ref[...], d0_ref[...], over, preferred_element_type=F32)
    keep_ref[...] = jnp.where(core == 0, grad_proj, grad_point)
    half = send_refs[0].shape[0]
    for k, send_ref in enumerate(send_refs):
        part = slice(k * half, (k + 1) * half)
        send_ref[...] = jnp.where(core == 0, grad_point[part], grad_proj[part]).astype(BF)


def shards(features, cotangent, w_point, w_rate_a, w_rate_b, w_rate_c, w_proj, bucket_slot):
    image = features[0]
    rows_dev, cols_dev, chans = image.shape
    pixels = rows_dev * cols_dev
    width = w_point.shape[1]
    row, col, core = (lax.axis_index(n) for n in ("row", "col", "dp_2"))
    at_y, at_z = lax.axis_index("dp_0"), lax.axis_index("dp_1")
    pos = jnp.stack([2 * row + col, at_y, row, col, core, at_z]).astype(jnp.int32)
    replicas = lax.axis_size(DP)
    slot_count = replicas * (bucket_slot.shape[0] // replicas + 1)
    place = place_slots(bucket_slot, core, slot_count)
    centre = image.reshape(pixels, chans)
    weights = [pltpu.with_memory_space_constraint(w, pltpu.HBM) for w in (w_rate_a, w_rate_b, w_rate_c)]
    picked = pick(pos, centre)
    centre, *picked = lax.optimization_barrier((centre, *picked))
    got = [picked[0]] + [flip(picked[k], k) for k in (1, 2, 3)]
    part, *parts = outer(pos, centre, *weights)
    part, got = lax.optimization_barrier((part, got))
    to_row, to_col, to_diag = parts
    parts = [flip(to_row, 2), flip(to_col, 1), flip(to_diag, 3)]
    turned = turn(pos, got)
    pre0, own = inner(pos, centre, part, w_point, *weights)
    parts, pre0, own, turned = lax.optimization_barrier((parts, pre0, own, turned))
    joined, g_proj, delta0, delta3 = merge(
        pos, pre0, own, *parts, cotangent[0].reshape(pixels, width), w_proj
    )
    shared = [delta3] + [flip(delta3, k) for k in (1, 2, 3)]
    block = (4 * width, width)
    kept, *sent = call(
        pair_grads,
        [jax.ShapeDtypeStruct(block, F32)] + [jax.ShapeDtypeStruct((2 * width, width), BF)] * 2,
        1,
        4,
        4 * pixels * chans * width,
        4 * 1024 * 1024,
        16,
        name="pair",
    )(pos, joined, g_proj, centre, delta0)
    got = [swap_core(part) for part in sent]
    by_owner = split_pair(pos, kept, got)
    by_owner, shared = lax.optimization_barrier((by_owner, shared))
    by_owner = [by_owner[0]] + [flip(by_owner[k], k) for k in (1, 2, 3)]
    kept, sent = tap_slots(pos, place, shared, turned, slot_count)
    sent, by_owner = lax.optimization_barrier((sent, by_owner))
    mine, other = sum_pair(by_owner)
    return reduce_slots(pos, place, kept, sent, mine, other)


def solution(mesh):
    torus = Mesh(
        mesh.devices.reshape(mesh.shape["row"], mesh.shape["col"], 4, 4, 2),
        ("row", "col", "dp_0", "dp_1", "dp_2"),
    )
    in_specs = (P(DP, "row", "col", None), P(DP, "row", "col", None), P(), P(), P(), P(), P(), P())
    out_specs = P(DP, ("row", "col"))
    return jax.shard_map(
        shards, mesh=torus, in_specs=in_specs, out_specs=out_specs, check_vma=False
    )
```

```python
import jax
import jax.numpy as jnp
from jax import lax
from jax.experimental import pallas as pl
from jax.experimental.pallas import tpu as pltpu
from jax.sharding import Mesh
from jax.sharding import PartitionSpec as P

RATE_A = 6
RATE_B = 12
RATE_C = 18
DP = ("dp_0", "dp_1", "dp_2")


BF = jnp.bfloat16
F32 = jnp.float32
MIB = 1024 * 1024


def flip(x, mask):
    if mask == 1:
        return lax.ppermute(x, "col", [(0, 1), (1, 0)])
    if mask == 2:
        return lax.ppermute(x, "row", [(0, 1), (1, 0)])
    return lax.ppermute(x, ("row", "col"), [(0, 3), (3, 0), (1, 2), (2, 1)])


def smem():
    return pl.BlockSpec(memory_space=pltpu.SMEM)


def vmem():
    return pl.BlockSpec(memory_space=pltpu.VMEM)


def call(body, outs, n_smem, n_vmem, flops, nbytes, limit, scratch=(), name=None, n_any=0):
    return pl.pallas_call(
        body,
        out_shape=outs,
        in_specs=[smem()] * n_smem + [vmem()] * n_vmem + [pl.BlockSpec(memory_space=pltpu.HBM)] * n_any,
        out_specs=jax.tree.map(lambda _: vmem(), outs),
        scratch_shapes=list(scratch),
        compiler_params=pltpu.CompilerParams(vmem_limit_bytes=limit * MIB),
        cost_estimate=pl.CostEstimate(flops=flops, bytes_accessed=nbytes, transcendentals=0),
        name=name,
    )


def select_channels(pos_ref, x_ref, *rest):
    *o_refs, held, sems = rest
    lanes = 128
    group = lanes * len(o_refs)
    pieces = sems.shape[0]
    each = x_ref.shape[0] // pieces
    copies = []
    for n in range(pieces):
        part = pl.ds(n * each, each)
        copies.append(pltpu.make_async_copy(x_ref.at[part, :], held.at[part, :], sems.at[n]))
        copies[n].start()
    source = lax.broadcasted_iota(jnp.int32, (group, group), 0)
    col = lax.broadcasted_iota(jnp.int32, (1, group), 1)
    owner = jnp.bitwise_xor(pos_ref[0], col // lanes)
    wanted = 64 * ((col % lanes) // 16) + 16 * owner + col % 16
    picks = jnp.where(source == wanted, 1.0, 0.0).astype(BF)
    for n in range(pieces):
        copies[n].wait()
        rows = slice(n * each, (n + 1) * each)
        for p in range(x_ref.shape[1] // group):
            taken = jnp.dot(held[rows, p * group : (p + 1) * group], picks, preferred_element_type=F32).astype(BF)
            for k, o_ref in enumerate(o_refs):
                o_ref[rows, p * lanes : (p + 1) * lanes] = taken[:, k * lanes : (k + 1) * lanes]


def turn_pixels(pos_ref, x0, x1, x2, x3, o_ref, held):
    pixels, width = x0.shape
    for k, x in enumerate((x0, x1, x2, x3)):
        s = jnp.bitwise_xor(pos_ref[0], k)
        held[s % 2, pl.ds((s // 2) * pixels, pixels), :] = x[...]
    eye = (
        lax.broadcasted_iota(jnp.int32, (width, width), 0)
        == lax.broadcasted_iota(jnp.int32, (width, width), 1)
    ).astype(F32).astype(BF)
    for g in range(2):
        o_ref[g] = lax.dot_general(
            eye, held[g], (((1,), (1,)), ((), ())), preferred_element_type=F32
        ).astype(BF)


def roll_cols(x, shift):
    return jnp.concatenate([x[:, x.shape[1] - shift :], x[:, : x.shape[1] - shift]], axis=1)


def tap_grads(pos_ref, place_ref, d0, d1, d2, d3, xt_ref, keep_ref, send_ref, held, padded, buf):
    side = RATE_C
    pixels, width = d0.shape
    cols = 24
    rows = pixels // cols
    for k, d in enumerate((d0, d1, d2, d3)):
        s = jnp.bitwise_xor(pos_ref[0], k)
        held[s % 2, pl.ds((s // 2) * pixels, pixels), :] = d[...]
    buf[...] = jnp.zeros_like(buf)
    tall = 2 * pixels
    lead = side * cols
    zeros = jnp.zeros((2, lead, width), BF)
    halves = [held[g].astype(F32).reshape(2 * rows, cols, width) for g in range(2)]
    at = lax.broadcasted_iota(jnp.int32, (2 * rows, cols, width), 1)
    rest = cols - side
    for across in (0, 1, -1):
        turn = across + 1
        padded[turn, :, pl.ds(0, lead), :] = zeros
        padded[turn, :, pl.ds(lead + tall, lead), :] = zeros
        if across == 0:
            shifted = halves
        elif across == 1:
            rolled = [roll_cols(h, side) for h in halves]
            shifted = [
                jnp.where(at >= side, rolled[0], 0.0),
                jnp.where(at < side, rolled[0], rolled[1]),
            ]
        else:
            rolled = [roll_cols(h, rest) for h in halves]
            shifted = [
                jnp.where(at < rest, rolled[0], rolled[1]),
                jnp.where(at < rest, rolled[1], 0.0),
            ]
        for g in range(2):
            padded[turn, g, pl.ds(lead, tall), :] = shifted[g].reshape(tall, width).astype(BF)
        for above in (-1, 0, 1):
            first, last = {-1: (0, 32), 0: (0, 48), 1: (16, 48)}[above]
            base = first - side * above + side
            total = None
            for g in range(2):
                part = jnp.dot(
                    xt_ref[g, :, first * cols : last * cols],
                    padded[turn, g, base * cols : (base + last - first) * cols, :],
                    preferred_element_type=F32,
                )
                total = part if total is None else total + part
            tap = 3 * (above + 1) + across + 1
            groups = total.reshape(width // 16, 16, width)
            for m in range(width // 16):
                buf[place_ref[32 + 16 * tap + m]] = groups[m]
    half = buf.shape[0] // 2
    keep_ref[...] = buf[:half]
    send_ref[...] = buf[half:].astype(BF)


def join_owners(pos_ref, place_ref, keep_ref, got_ref, mine_ref, other_ref, o_ref, total):
    total[...] = keep_ref[...] + got_ref[...].astype(F32)
    core = pos_ref[4]
    for n in range(mine_ref.shape[0]):
        for ref, first in ((mine_ref, 16 * core), (other_ref, 16 * (1 - core))):
            at = place_ref[first + n]

            @pl.when(at < total.shape[0])
            def _(ref=ref, at=at, n=n):
                total[at] = ref[n].astype(F32)

    o_ref[...] = total[...].astype(BF).reshape(o_ref.shape)


def fold_last(r_ref, o_ref, total):
    value = r_ref[0].astype(F32)
    for n in range(1, r_ref.shape[0]):
        value = value + r_ref[n].astype(F32)
    total[...] = value.reshape(total.shape)
    width = total.shape[2]
    for i in range(total.shape[1]):
        o_ref[:, i * width : (i + 1) * width] = total[:, i, :]


def share_rows(pos_ref, kept_ref, got0, got1, *rest):
    *outs, total = rest
    half, each = got0.shape[0], total.shape[0] // 2
    for n, got in enumerate((got0, got1)):
        value = kept_ref[n * half : (n + 1) * half, :] + got[...].astype(F32)
        total[n * each : (n + 1) * each] = value.reshape(each, *total.shape[1:])
    for k, out in enumerate(outs):
        out[...] = total[:, jnp.bitwise_xor(pos_ref[0], k)].astype(out.dtype)


def swap_core(x):
    return lax.ppermute(x, "dp_2", [(0, 1), (1, 0)])


def pick(pos, centre):
    pixels, chans = centre.shape
    block = jax.ShapeDtypeStruct((pixels, chans // 4), BF)
    return call(
        select_channels,
        [block] * 4,
        1,
        0,
        pixels * chans * chans,
        4 * pixels * chans,
        12,
        [pltpu.VMEM((pixels, chans), BF), pltpu.SemaphoreType.DMA((2,))],
        name="pick",
        n_any=1,
    )(pos, pltpu.with_memory_space_constraint(centre, pltpu.HBM))


def turn(pos, got):
    pixels, width = got[0].shape
    return call(
        turn_pixels,
        jax.ShapeDtypeStruct((2, width, 2 * pixels), BF),
        1,
        4,
        8 * pixels * width * width,
        16 * pixels * width,
        12,
        [pltpu.VMEM((2, 2 * pixels, width), BF)],
        name="turn",
    )(pos, *got)


def split_pair(pos, kept, got):
    width = kept.shape[1]
    slices = kept.shape[0] // 64
    shape = (slices, 16, width)
    return call(
        share_rows,
        [jax.ShapeDtypeStruct(shape, F32)] + [jax.ShapeDtypeStruct(shape, BF)] * 3,
        1,
        3,
        0,
        0,
        10,
        [pltpu.VMEM((slices, 4, 16, width), F32)],
        name="rows",
    )(pos, kept, *got)


def sum_pair(blocks):
    mine = blocks[0] + sum(block.astype(F32) for block in blocks[1:])
    return mine, swap_core(mine.astype(BF))


def place_slots(bucket_slot, core, slot_count):
    replicas = lax.axis_size(DP)
    capacity = slot_count // replicas
    owner = bucket_slot // capacity
    other = jnp.bitwise_xor(owner % 2, core)
    return other * (slot_count // 2) + (owner // 2) * capacity + bucket_slot % capacity


def tap_slots(pos, place, deltas, turned, slot_count):
    pixels, width = deltas[0].shape
    half = slot_count // 2
    return call(
        tap_grads,
        [jax.ShapeDtypeStruct((half, 16, width), F32), jax.ShapeDtypeStruct((half, 16, width), BF)],
        2,
        5,
        2 * 7 * 4 * pixels * width * width,
        8 * 1024 * 1024,
        26,
        [
            pltpu.VMEM((2, 2 * pixels, width), BF),
            pltpu.VMEM((3, 2, 2 * pixels + 2 * RATE_C * SIDE, width), BF),
            pltpu.VMEM((slot_count, 16, width), F32),
        ],
        name="taps",
    )(pos, place, *deltas, turned)


def reduce_slots(pos, place, kept, sent, mine, other):
    half, rows, width = kept.shape
    chips = lax.axis_size("dp_0") * lax.axis_size("dp_1")
    each = half // chips
    total = call(
        join_owners,
        jax.ShapeDtypeStruct((chips, each * rows, width), BF),
        2,
        4,
        kept.size,
        8 * kept.size,
        12,
        [pltpu.VMEM((half, rows, width), F32)],
        name="owners",
    )(pos, place, kept, swap_core(sent), mine, other)
    total = lax.all_to_all(total, ("dp_0", "dp_1"), 0, 0, tiled=True)
    return call(
        fold_last,
        jax.ShapeDtypeStruct((each, rows * width), F32),
        0,
        1,
        kept.size,
        2 * kept.size,
        8,
        [pltpu.VMEM((each, rows, width), F32)],
        name="last",
    )(total)


def sigmoid(value):
    return 0.5 + 0.5 * jnp.tanh(0.5 * value)


def silu_slope(value):
    sig = sigmoid(value)
    return sig * (1.0 + value * (1.0 - sig))


RATES = (RATE_A, RATE_B, RATE_C)
SIDE = 24


def turned_by(x, shift, far):
    return jnp.where(far == 0, roll_cols(x, shift), roll_cols(x, SIDE - shift))


def rank_of(shape, far):
    at = lax.broadcasted_iota(jnp.int32, shape, 1)
    return jnp.where(far == 0, at, SIDE - 1 - at)


def row_marks(low, rate):
    lead = rate * SIDE
    whole = SIDE * SIDE

    def either(upper, lower):
        return pl.multiple_of(jnp.where(low == 0, upper, lower), 16)

    return dict(
        own=either(0, lead),
        out=either(lead, 0),
        theirs=either(whole, 0),
        inward_from=either(lead, 0),
        inward=either(0, 2 * lead),
        kept=either(lead, 0),
        inner=either(0, lead),
    )


def blocks(x):
    return x.reshape(x.shape[0] // SIDE, SIDE, x.shape[1])


def flat(x):
    return x.reshape(x.shape[0] * SIDE, x.shape[2])


def tap_copies(pos_ref, refs, jobs, held, sems):
    copies = []
    for branch, ref in enumerate(refs):
        for n, (above, across) in enumerate(jobs):
            a = 1 if above == 1 else jnp.where(pos_ref[2] == 0, above, 2 - above)
            b = 1 if across == 1 else jnp.where(pos_ref[3] == 0, across, 2 - across)
            width = ref.shape[3]
            to = held.at[branch, :, n * width : (n + 1) * width]
            copies.append(pltpu.make_async_copy(ref.at[a, b], to, sems.at[branch, n]))
    return copies


BRANCHES = ((2, RATE_C), (1, RATE_B), (0, RATE_A))
OUTER = ((0, 0), (1, 0), (0, 1), (0, 2), (2, 0))
INNER = ((1, 1), (1, 2), (2, 1), (2, 2))


def outer_parts(pos_ref, x_ref, wc_ref, wb_ref, wa_ref, pre_ref, row_ref, col_ref, diag_ref, ext, acc, y, held, sems):
    low, far = pos_ref[2], pos_ref[3]
    whole = SIDE * SIDE
    width = pre_ref.shape[2]
    copies = tap_copies(pos_ref, (wc_ref, wb_ref, wa_ref), OUTER, held, sems)
    for copy in copies:
        copy.start()
    first = 0
    for turn, (index, rate) in enumerate(BRANCHES):
        lead = rate * SIDE
        inside = whole - lead
        at = row_marks(low, rate)
        own_rows = pl.ds(at["own"], whole)
        their_rows = pl.ds(at["theirs"], lead)
        kept_rows = pl.ds(at["kept"], inside)
        to_row = slice(first, first + lead)
        first += lead
        count = len(OUTER)
        for copy in copies[turn * count : (turn + 1) * count]:
            copy.wait()
        y[...] = jnp.dot(x_ref[...], held[turn, :, : 4 * width], preferred_element_type=F32)
        ext[pl.ds(pl.multiple_of(whole - at["theirs"], 16), lead), :] = jnp.zeros((lead, width), F32)
        ext[pl.ds(at["out"], whole), :] = y[:, :width]
        ext[own_rows, :] += y[:, width : 2 * width]
        ext[pl.ds(at["inward"], inside), :] += jnp.dot(
            x_ref[pl.ds(at["inward_from"], inside), :], held[turn, :, 4 * width :], preferred_element_type=F32
        )
        own = blocks(ext[own_rows, :])
        ours = turned_by(own, rate, far)
        rank = rank_of(own.shape, far)
        pre_ref[index] = flat(jnp.where(rank >= rate, ours, 0.0))
        below = blocks(ext[their_rows, :])
        theirs = turned_by(below, rate, far)
        place = rank_of(below.shape, far)
        acc[:lead, :] = flat(jnp.where(place >= rate, theirs, 0.0))
        if rate == RATE_C:
            col_ref[:whole, :] = flat(jnp.where(rank < rate, ours, 0.0)).astype(BF)
            diag_ref[:lead, :] = flat(jnp.where(place < rate, theirs, 0.0)).astype(BF)
        elif rate == RATE_B:
            half = rate // 2
            col_ref[whole:, :] = flat(jnp.where(rank[:rate] < rate, ours[:rate], own[rate:])).astype(BF)
            part = place[:half] < rate
            diag_ref[RATE_C * SIDE :, :] = flat(jnp.where(part, theirs[:half], below[half:])).astype(BF)
        else:
            have = blocks(col_ref[:whole, :].astype(F32))
            col_ref[:whole, :] = flat(jnp.where(rank >= RATE_C, own, have)).astype(BF)
            have = blocks(diag_ref[:lead, :].astype(F32))
            diag_ref[:lead, :] = flat(jnp.where(place >= RATE_C, below, have)).astype(BF)
        next_from = pl.multiple_of(jnp.where(low == 0, inside, 0), 16)
        keep_from = pl.multiple_of(jnp.where(low == 0, 0, lead), 16)
        pre_ref[index, kept_rows, :] += y[pl.ds(keep_from, inside), 2 * width : 3 * width]
        own = blocks(y[pl.ds(keep_from, inside), 3 * width :])
        rank = rank_of(own.shape, far)
        pre_ref[index, kept_rows, :] += flat(jnp.where(rank < SIDE - rate, turned_by(own, rate, 1 - far), 0.0))
        below = blocks(y[pl.ds(next_from, lead), 3 * width :])
        theirs = flat(jnp.where(place < SIDE - rate, turned_by(below, rate, 1 - far), 0.0))
        row_ref[to_row, :] = (acc[:lead, :] + y[pl.ds(next_from, lead), 2 * width : 3 * width] + theirs).astype(BF)


def inner_parts(pos_ref, x_ref, part_ref, wp_ref, wc_ref, wb_ref, wa_ref, pre0_ref, pre_ref, y, z, held, sems):
    low, far = pos_ref[2], pos_ref[3]
    whole = SIDE * SIDE
    width = pre0_ref.shape[1]
    copies = tap_copies(pos_ref, (wc_ref, wb_ref, wa_ref), INNER, held, sems)
    for copy in copies:
        copy.start()
    pre0_ref[...] = jnp.dot(x_ref[...], wp_ref[...], preferred_element_type=F32)
    for turn, (index, rate) in enumerate(BRANCHES):
        lead = rate * SIDE
        inside = whole - lead
        at = row_marks(low, rate)
        from_rows = pl.ds(at["inward_from"], inside)
        to_rows = pl.ds(at["inner"], inside)
        count = len(INNER)
        for copy in copies[turn * count : (turn + 1) * count]:
            copy.wait()
        y[...] = jnp.dot(x_ref[...], held[turn, :, : 2 * width], preferred_element_type=F32)
        z[:inside, :] = jnp.dot(x_ref[from_rows, :], held[turn, :, 2 * width :], preferred_element_type=F32)
        y[to_rows, :] += z[:inside, :]
        own = blocks(y[:, width:])
        rank = rank_of(own.shape, far)
        moved = flat(jnp.where(rank < SIDE - rate, turned_by(own, rate, 1 - far), 0.0))
        pre_ref[index] = part_ref[index] + y[:, :width] + moved


def outer(pos, centre, w_rate_a, w_rate_b, w_rate_c):
    pixels, chans = centre.shape
    width = w_rate_a.shape[3]
    sends = (RATE_A + RATE_B + RATE_C) * SIDE
    shapes = [((3, pixels, width), F32), ((sends, width), BF), ((sends, width), BF), ((pixels, width), BF)]
    return call(
        outer_parts,
        [jax.ShapeDtypeStruct(*s) for s in shapes],
        1,
        1,
        2 * pixels * chans * width * 14,
        10 * MIB,
        28,
        [
            pltpu.VMEM(((SIDE + RATE_C) * SIDE, width), F32),
            pltpu.VMEM((RATE_C * SIDE, width), F32),
            pltpu.VMEM((pixels, 4 * width), F32),
            pltpu.VMEM((3, chans, len(OUTER) * width), BF),
            pltpu.SemaphoreType.DMA((3, len(OUTER))),
        ],
        name="outer",
        n_any=3,
    )(pos, centre, w_rate_c, w_rate_b, w_rate_a)


def inner(pos, centre, part, w_point, w_rate_a, w_rate_b, w_rate_c):
    pixels, chans = centre.shape
    width = w_point.shape[1]
    return call(
        inner_parts,
        [jax.ShapeDtypeStruct((pixels, width), F32), jax.ShapeDtypeStruct((3, pixels, width), F32)],
        1,
        3,
        2 * pixels * chans * width * 10,
        10 * MIB,
        26,
        [
            pltpu.VMEM((pixels, 2 * width), F32),
            pltpu.VMEM((pixels, 2 * width), F32),
            pltpu.VMEM((3, chans, len(INNER) * width), BF),
            pltpu.SemaphoreType.DMA((3, len(INNER))),
        ],
        name="inner",
        n_any=3,
    )(pos, centre, part, w_point, w_rate_c, w_rate_b, w_rate_a)


def merge_parts(
    pos_ref, pre0_ref, own_ref, row_ref, col_ref, diag_ref, cot_ref, wp_ref, joined_ref, g_ref, d0_ref, d3_ref, pre
):
    low = pos_ref[2]
    theirs = 1 - pos_ref[3]
    width = pre0_ref.shape[1]
    whole = SIDE * SIDE

    def rows_of(rate):
        return pl.multiple_of(jnp.where(low == 0, (SIDE - rate) * SIDE, 0), 16)

    pre[...] = own_ref[...]
    first = 0
    for index, rate in ((2, RATE_C), (1, RATE_B), (0, RATE_A)):
        lead = rate * SIDE
        pre[index, pl.ds(rows_of(rate), lead), :] += row_ref[first : first + lead, :].astype(F32)
        first += lead

    part = blocks(col_ref[:whole, :].astype(F32))
    rank = rank_of(part.shape, theirs)
    pre[2] += flat(jnp.where(rank < RATE_C, part, 0.0))
    pre[0] += flat(turned_by(jnp.where(rank >= RATE_C, part, 0.0), RATE_A, theirs))
    part = blocks(col_ref[whole:, :].astype(F32))
    rank = rank_of(part.shape, theirs)
    pre[1, : RATE_B * SIDE, :] += flat(jnp.where(rank < RATE_B, part, 0.0))
    pre[1, RATE_B * SIDE :, :] += flat(roll_cols(jnp.where(rank >= RATE_B, part, 0.0), RATE_B))

    part = blocks(diag_ref[: RATE_C * SIDE, :].astype(F32))
    rank = rank_of(part.shape, theirs)
    pre[2, pl.ds(rows_of(RATE_C), RATE_C * SIDE), :] += flat(jnp.where(rank < RATE_C, part, 0.0))
    few = part[:RATE_A]
    few = turned_by(jnp.where(rank[:RATE_A] >= RATE_C, few, 0.0), RATE_A, theirs)
    pre[0, pl.ds(rows_of(RATE_A), RATE_A * SIDE), :] += flat(few)
    part = blocks(diag_ref[RATE_C * SIDE :, :].astype(F32))
    rank = rank_of(part.shape, theirs)
    half = RATE_B // 2
    at = rows_of(RATE_B)
    pre[1, pl.ds(at, half * SIDE), :] += flat(jnp.where(rank < RATE_B, part, 0.0))
    last = pl.multiple_of(at + half * SIDE, 16)
    pre[1, pl.ds(last, half * SIDE), :] += flat(roll_cols(jnp.where(rank >= RATE_B, part, 0.0), RATE_B))

    slopes = {}
    for k in range(4):
        value = pre0_ref[...] if k == 0 else pre[k - 1]
        sig = sigmoid(value)
        joined_ref[:, k * width : (k + 1) * width] = (value * sig).astype(BF)
        if k in (0, 3):
            slopes[k] = sig * (1.0 + value * (1.0 - sig))
    proj_pre = jnp.dot(joined_ref[...], wp_ref[...], preferred_element_type=F32)
    g_proj = (cot_ref[...].astype(F32) * silu_slope(proj_pre)).astype(BF)
    g_ref[...] = g_proj
    for k, out in ((3, d3_ref), (0, d0_ref)):
        back = lax.dot_general(
            g_proj, wp_ref[k * width : (k + 1) * width, :], (((1,), (1,)), ((), ())), preferred_element_type=F32
        )
        out[...] = (back * slopes[k]).astype(BF)


def merge(pos, pre0, own, row, col, diag, cot, w_proj):
    pixels, width = pre0.shape
    block = jax.ShapeDtypeStruct((pixels, width), BF)
    return call(
        merge_parts,
        [jax.ShapeDtypeStruct((pixels, 4 * width), BF), block, block, block],
        1,
        7,
        2 * pixels * width * width * 6,
        6 * 1024 * 1024,
        18,
        [pltpu.VMEM((3, pixels, width), F32)],
        name="merge",
    )(pos, pre0, own, row, col, diag, cot, w_proj)


def pair_grads(pos_ref, joined_ref, g_ref, x_ref, d0_ref, keep_ref, *send_refs):
    core = pos_ref[4]
    over = (((0,), (0,)), ((), ()))
    grad_proj = lax.dot_general(joined_ref[...], g_ref[...], over, preferred_element_type=F32)
    grad_point = lax.dot_general(x_ref[...], d0_ref[...], over, preferred_element_type=F32)
    keep_ref[...] = jnp.where(core == 0, grad_proj, grad_point)
    half = send_refs[0].shape[0]
    for k, send_ref in enumerate(send_refs):
        part = slice(k * half, (k + 1) * half)
        send_ref[...] = jnp.where(core == 0, grad_point[part], grad_proj[part]).astype(BF)


def shards(features, cotangent, w_point, w_rate_a, w_rate_b, w_rate_c, w_proj, bucket_slot):
    image = features[0]
    rows_dev, cols_dev, chans = image.shape
    pixels = rows_dev * cols_dev
    width = w_point.shape[1]
    row, col, core = (lax.axis_index(n) for n in ("row", "col", "dp_2"))
    at_y, at_z = lax.axis_index("dp_0"), lax.axis_index("dp_1")
    pos = jnp.stack([2 * row + col, at_y, row, col, core, at_z]).astype(jnp.int32)
    replicas = lax.axis_size(DP)
    slot_count = replicas * (bucket_slot.shape[0] // replicas + 1)
    place = place_slots(bucket_slot, core, slot_count)
    centre = image.reshape(pixels, chans)
    weights = [pltpu.with_memory_space_constraint(w, pltpu.HBM) for w in (w_rate_a, w_rate_b, w_rate_c)]
    picked = pick(pos, centre)
    centre, *picked = lax.optimization_barrier((centre, *picked))
    got = [picked[0]] + [flip(picked[k], k) for k in (1, 2, 3)]
    part, *parts = outer(pos, centre, *weights)
    part, got = lax.optimization_barrier((part, got))
    to_row, to_col, to_diag = parts
    parts = [flip(to_row, 2), flip(to_col, 1), flip(to_diag, 3)]
    turned = turn(pos, got)
    pre0, own = inner(pos, centre, part, w_point, *weights)
    parts, pre0, own, turned = lax.optimization_barrier((parts, pre0, own, turned))
    joined, g_proj, delta0, delta3 = merge(
        pos, pre0, own, *parts, cotangent[0].reshape(pixels, width), w_proj
    )
    shared = [delta3] + [flip(delta3, k) for k in (1, 2, 3)]
    block = (4 * width, width)
    kept, *sent = call(
        pair_grads,
        [jax.ShapeDtypeStruct(block, F32)] + [jax.ShapeDtypeStruct((2 * width, width), BF)] * 2,
        1,
        4,
        4 * pixels * chans * width,
        4 * 1024 * 1024,
        16,
        name="pair",
    )(pos, joined, g_proj, centre, delta0)
    got = [swap_core(part) for part in sent]
    by_owner = split_pair(pos, kept, got)
    across = flip(by_owner[1], 1)
    late, shared = lax.optimization_barrier((by_owner[2:], shared))
    by_owner = [by_owner[0], across, flip(late[0], 2), flip(late[1], 3)]
    kept, sent = tap_slots(pos, place, shared, turned, slot_count)
    sent, by_owner = lax.optimization_barrier((sent, by_owner))
    mine, other = sum_pair(by_owner)
    return reduce_slots(pos, place, kept, sent, mine, other)


def solution(mesh):
    torus = Mesh(
        mesh.devices.reshape(mesh.shape["row"], mesh.shape["col"], 4, 4, 2),
        ("row", "col", "dp_0", "dp_1", "dp_2"),
    )
    in_specs = (P(DP, "row", "col", None), P(DP, "row", "col", None), P(), P(), P(), P(), P(), P())
    out_specs = P(DP, ("row", "col"))
    return jax.shard_map(
        shards, mesh=torus, in_specs=in_specs, out_specs=out_specs, check_vma=False
    )
```

```python
import jax
import jax.numpy as jnp
from jax import lax
from jax.experimental import pallas as pl
from jax.experimental.pallas import tpu as pltpu
from jax.sharding import Mesh
from jax.sharding import PartitionSpec as P

RATE_A = 6
RATE_B = 12
RATE_C = 18
DP = ("dp_0", "dp_1", "dp_2")


BF = jnp.bfloat16
F32 = jnp.float32
MIB = 1024 * 1024
EDGE = 8


def flip(x, mask):
    if mask == 1:
        return lax.ppermute(x, "col", [(0, 1), (1, 0)])
    if mask == 2:
        return lax.ppermute(x, "row", [(0, 1), (1, 0)])
    return lax.ppermute(x, ("row", "col"), [(0, 3), (3, 0), (1, 2), (2, 1)])


def smem():
    return pl.BlockSpec(memory_space=pltpu.SMEM)


def vmem():
    return pl.BlockSpec(memory_space=pltpu.VMEM)


def call(body, outs, n_smem, n_vmem, flops, nbytes, limit, scratch=(), name=None, n_any=0):
    return pl.pallas_call(
        body,
        out_shape=outs,
        in_specs=[smem()] * n_smem + [vmem()] * n_vmem + [pl.BlockSpec(memory_space=pltpu.HBM)] * n_any,
        out_specs=jax.tree.map(lambda _: vmem(), outs),
        scratch_shapes=list(scratch),
        compiler_params=pltpu.CompilerParams(vmem_limit_bytes=limit * MIB),
        cost_estimate=pl.CostEstimate(flops=flops, bytes_accessed=nbytes, transcendentals=0),
        name=name,
    )


def select_channels(pos_ref, x_ref, *rest):
    *o_refs, held, sems = rest
    lanes = 128
    group = lanes * len(o_refs)
    pieces = sems.shape[0]
    each = x_ref.shape[0] // pieces
    copies = []
    for n in range(pieces):
        part = pl.ds(n * each, each)
        copies.append(pltpu.make_async_copy(x_ref.at[part, :], held.at[part, :], sems.at[n]))
        copies[n].start()
    source = lax.broadcasted_iota(jnp.int32, (group, group), 0)
    col = lax.broadcasted_iota(jnp.int32, (1, group), 1)
    owner = jnp.bitwise_xor(pos_ref[0], col // lanes)
    wanted = 64 * ((col % lanes) // 16) + 16 * owner + col % 16
    picks = jnp.where(source == wanted, 1.0, 0.0).astype(BF)
    for n in range(pieces):
        copies[n].wait()
        rows = slice(n * each, (n + 1) * each)
        for p in range(x_ref.shape[1] // group):
            taken = jnp.dot(held[rows, p * group : (p + 1) * group], picks, preferred_element_type=F32).astype(BF)
            for k, o_ref in enumerate(o_refs):
                o_ref[rows, p * lanes : (p + 1) * lanes] = taken[:, k * lanes : (k + 1) * lanes]


def turn_pixels(pos_ref, x0, x1, x2, x3, o_ref, edge_ref, held):
    pixels, width = x0.shape
    for k, x in enumerate((x0, x1, x2, x3)):
        s = jnp.bitwise_xor(pos_ref[0], k)
        held[s % 2, pl.ds((s // 2) * pixels, pixels), :] = x[...]
    eye = (
        lax.broadcasted_iota(jnp.int32, (width, width), 0)
        == lax.broadcasted_iota(jnp.int32, (width, width), 1)
    ).astype(F32).astype(BF)
    for g in range(2):
        o_ref[g] = lax.dot_general(
            eye, held[g], (((1,), (1,)), ((), ())), preferred_element_type=F32
        ).astype(BF)
        wide = held[g].astype(F32).reshape(-1, SIDE, width)
        near = wide[:, SIDE - EDGE :] if g == 0 else wide[:, :EDGE]
        edge_ref[g] = lax.dot_general(
            eye, near.reshape(-1, width).astype(BF), (((1,), (1,)), ((), ())), preferred_element_type=F32
        ).astype(BF)


def roll_cols(x, shift):
    return jnp.concatenate([x[:, x.shape[1] - shift :], x[:, : x.shape[1] - shift]], axis=1)


def tap_grads(pos_ref, place_ref, d0, d1, d2, d3, xt_ref, xe_ref, keep_ref, send_ref, held, padded, edge, buf):
    side = RATE_C
    pixels, width = d0.shape
    cols = 24
    rows = pixels // cols
    for k, d in enumerate((d0, d1, d2, d3)):
        s = jnp.bitwise_xor(pos_ref[0], k)
        held[s % 2, pl.ds((s // 2) * pixels, pixels), :] = d[...]
    buf[...] = jnp.zeros_like(buf)
    tall = 2 * pixels
    lead = side * cols
    zeros = jnp.zeros((2, lead, width), BF)
    halves = [held[g].astype(F32).reshape(2 * rows, cols, width) for g in range(2)]
    at = lax.broadcasted_iota(jnp.int32, (2 * rows, cols, width), 1)
    rest = cols - side
    for across in (0, 1, -1):
        turn = across + 1
        padded[turn, :, pl.ds(0, lead), :] = zeros
        padded[turn, :, pl.ds(lead + tall, lead), :] = zeros
        if across == 0:
            shifted = halves
        elif across == 1:
            rolled = [roll_cols(h, side) for h in halves]
            shifted = [
                jnp.where(at >= side, rolled[0], 0.0),
                jnp.where(at < side, rolled[0], rolled[1]),
            ]
        else:
            rolled = [roll_cols(h, rest) for h in halves]
            shifted = [
                jnp.where(at < rest, rolled[0], rolled[1]),
                jnp.where(at < rest, rolled[1], 0.0),
            ]
        thin = {1: 0, -1: 1}.get(across)
        for g in range(2):
            if g == thin:
                near = shifted[g][:, SIDE - EDGE :] if g == 0 else shifted[g][:, :EDGE]
                short = side * EDGE
                edge[g, pl.ds(0, short), :] = jnp.zeros((short, width), BF)
                edge[g, pl.ds(short, 2 * rows * EDGE), :] = near.reshape(2 * rows * EDGE, width).astype(BF)
                edge[g, pl.ds(short + 2 * rows * EDGE, short), :] = jnp.zeros((short, width), BF)
            else:
                padded[turn, g, pl.ds(lead, tall), :] = shifted[g].reshape(tall, width).astype(BF)
        for above in (-1, 0, 1):
            first, last = {-1: (0, 32), 0: (0, 48), 1: (16, 48)}[above]
            base = first - side * above + side
            total = None
            for g in range(2):
                left, right, each = (xe_ref, edge.at[g], EDGE) if g == thin else (xt_ref, padded.at[turn, g], cols)
                part = jnp.dot(
                    left[g, :, first * each : last * each],
                    right[base * each : (base + last - first) * each, :],
                    preferred_element_type=F32,
                )
                total = part if total is None else total + part
            tap = 3 * (above + 1) + across + 1
            groups = total.reshape(width // 16, 16, width)
            for m in range(width // 16):
                buf[place_ref[32 + 16 * tap + m]] = groups[m]
    half = buf.shape[0] // 2
    keep_ref[...] = buf[:half]
    send_ref[...] = buf[half:].astype(BF)


def join_owners(pos_ref, place_ref, keep_ref, got_ref, mine_ref, other_ref, o_ref, total):
    total[...] = keep_ref[...] + got_ref[...].astype(F32)
    core = pos_ref[4]
    for n in range(mine_ref.shape[0]):
        for ref, first in ((mine_ref, 16 * core), (other_ref, 16 * (1 - core))):
            at = place_ref[first + n]

            @pl.when(at < total.shape[0])
            def _(ref=ref, at=at, n=n):
                total[at] = ref[n].astype(F32)

    o_ref[...] = total[...].astype(BF).reshape(o_ref.shape)


def fold_last(r_ref, o_ref, total):
    value = r_ref[0].astype(F32)
    for n in range(1, r_ref.shape[0]):
        value = value + r_ref[n].astype(F32)
    total[...] = value.reshape(total.shape)
    width = total.shape[2]
    for i in range(total.shape[1]):
        o_ref[:, i * width : (i + 1) * width] = total[:, i, :]


def share_rows(pos_ref, kept_ref, got0, got1, *rest):
    *outs, total = rest
    half, each = got0.shape[0], total.shape[0] // 2
    for n, got in enumerate((got0, got1)):
        value = kept_ref[n * half : (n + 1) * half, :] + got[...].astype(F32)
        total[n * each : (n + 1) * each] = value.reshape(each, *total.shape[1:])
    for k, out in enumerate(outs):
        out[...] = total[:, jnp.bitwise_xor(pos_ref[0], k)].astype(out.dtype)


def swap_core(x):
    return lax.ppermute(x, "dp_2", [(0, 1), (1, 0)])


def pick(pos, centre):
    pixels, chans = centre.shape
    block = jax.ShapeDtypeStruct((pixels, chans // 4), BF)
    return call(
        select_channels,
        [block] * 4,
        1,
        0,
        pixels * chans * chans,
        4 * pixels * chans,
        12,
        [pltpu.VMEM((pixels, chans), BF), pltpu.SemaphoreType.DMA((2,))],
        name="pick",
        n_any=1,
    )(pos, pltpu.with_memory_space_constraint(centre, pltpu.HBM))


def turn(pos, got):
    pixels, width = got[0].shape
    return call(
        turn_pixels,
        [
            jax.ShapeDtypeStruct((2, width, 2 * pixels), BF),
            jax.ShapeDtypeStruct((2, width, 2 * pixels // SIDE * EDGE), BF),
        ],
        1,
        4,
        8 * pixels * width * width,
        16 * pixels * width,
        12,
        [pltpu.VMEM((2, 2 * pixels, width), BF)],
        name="turn",
    )(pos, *got)


def split_pair(pos, kept, got):
    width = kept.shape[1]
    slices = kept.shape[0] // 64
    shape = (slices, 16, width)
    return call(
        share_rows,
        [jax.ShapeDtypeStruct(shape, F32)] + [jax.ShapeDtypeStruct(shape, BF)] * 3,
        1,
        3,
        0,
        0,
        10,
        [pltpu.VMEM((slices, 4, 16, width), F32)],
        name="rows",
    )(pos, kept, *got)


def sum_pair(blocks):
    mine = blocks[0] + sum(block.astype(F32) for block in blocks[1:])
    return mine, swap_core(mine.astype(BF))


def place_slots(bucket_slot, core, slot_count):
    replicas = lax.axis_size(DP)
    capacity = slot_count // replicas
    owner = bucket_slot // capacity
    other = jnp.bitwise_xor(owner % 2, core)
    return other * (slot_count // 2) + (owner // 2) * capacity + bucket_slot % capacity


def tap_slots(pos, place, deltas, turned, slot_count):
    pixels, width = deltas[0].shape
    half = slot_count // 2
    return call(
        tap_grads,
        [jax.ShapeDtypeStruct((half, 16, width), F32), jax.ShapeDtypeStruct((half, 16, width), BF)],
        2,
        6,
        2 * 7 * 4 * pixels * width * width,
        8 * 1024 * 1024,
        26,
        [
            pltpu.VMEM((2, 2 * pixels, width), BF),
            pltpu.VMEM((3, 2, 2 * pixels + 2 * RATE_C * SIDE, width), BF),
            pltpu.VMEM((2, (2 * SIDE + 2 * RATE_C) * EDGE, width), BF),
            pltpu.VMEM((slot_count, 16, width), F32),
        ],
        name="taps",
    )(pos, place, *deltas, *turned)


def reduce_slots(pos, place, kept, sent, mine, other):
    half, rows, width = kept.shape
    chips = lax.axis_size("dp_0") * lax.axis_size("dp_1")
    each = half // chips
    total = call(
        join_owners,
        jax.ShapeDtypeStruct((chips, each * rows, width), BF),
        2,
        4,
        kept.size,
        8 * kept.size,
        12,
        [pltpu.VMEM((half, rows, width), F32)],
        name="owners",
    )(pos, place, kept, swap_core(sent), mine, other)
    total = lax.all_to_all(total, ("dp_0", "dp_1"), 0, 0, tiled=True)
    return call(
        fold_last,
        jax.ShapeDtypeStruct((each, rows * width), F32),
        0,
        1,
        kept.size,
        2 * kept.size,
        8,
        [pltpu.VMEM((each, rows, width), F32)],
        name="last",
    )(total)


def sigmoid(value):
    return 0.5 + 0.5 * jnp.tanh(0.5 * value)


def silu_slope(value):
    sig = sigmoid(value)
    return sig * (1.0 + value * (1.0 - sig))


RATES = (RATE_A, RATE_B, RATE_C)
SIDE = 24


def turned_by(x, shift, far):
    return jnp.where(far == 0, roll_cols(x, shift), roll_cols(x, SIDE - shift))


def rank_of(shape, far):
    at = lax.broadcasted_iota(jnp.int32, shape, 1)
    return jnp.where(far == 0, at, SIDE - 1 - at)


def row_marks(low, rate):
    lead = rate * SIDE
    whole = SIDE * SIDE

    def either(upper, lower):
        return pl.multiple_of(jnp.where(low == 0, upper, lower), 16)

    return dict(
        own=either(0, lead),
        out=either(lead, 0),
        theirs=either(whole, 0),
        inward_from=either(lead, 0),
        inward=either(0, 2 * lead),
        kept=either(lead, 0),
        inner=either(0, lead),
    )


def blocks(x):
    return x.reshape(x.shape[0] // SIDE, SIDE, x.shape[1])


def flat(x):
    return x.reshape(x.shape[0] * SIDE, x.shape[2])


def tap_copies(pos_ref, refs, jobs, held, sems):
    copies = []
    for branch, ref in enumerate(refs):
        for n, (above, across) in enumerate(jobs):
            a = 1 if above == 1 else jnp.where(pos_ref[2] == 0, above, 2 - above)
            b = 1 if across == 1 else jnp.where(pos_ref[3] == 0, across, 2 - across)
            width = ref.shape[3]
            to = held.at[branch, :, n * width : (n + 1) * width]
            copies.append(pltpu.make_async_copy(ref.at[a, b], to, sems.at[branch, n]))
    return copies


BRANCHES = ((2, RATE_C), (1, RATE_B), (0, RATE_A))
OUTER = ((0, 0), (1, 0), (0, 1), (0, 2), (2, 0))
INNER = ((1, 1), (1, 2), (2, 1), (2, 2))


def outer_parts(pos_ref, x_ref, wc_ref, wb_ref, wa_ref, pre_ref, row_ref, col_ref, diag_ref, ext, acc, y, held, sems):
    low, far = pos_ref[2], pos_ref[3]
    whole = SIDE * SIDE
    width = pre_ref.shape[2]
    copies = tap_copies(pos_ref, (wc_ref, wb_ref, wa_ref), OUTER, held, sems)
    for copy in copies:
        copy.start()
    first = 0
    for turn, (index, rate) in enumerate(BRANCHES):
        lead = rate * SIDE
        inside = whole - lead
        at = row_marks(low, rate)
        own_rows = pl.ds(at["own"], whole)
        their_rows = pl.ds(at["theirs"], lead)
        kept_rows = pl.ds(at["kept"], inside)
        to_row = slice(first, first + lead)
        first += lead
        count = len(OUTER)
        for copy in copies[turn * count : (turn + 1) * count]:
            copy.wait()
        y[...] = jnp.dot(x_ref[...], held[turn, :, : 4 * width], preferred_element_type=F32)
        ext[pl.ds(pl.multiple_of(whole - at["theirs"], 16), lead), :] = jnp.zeros((lead, width), F32)
        ext[pl.ds(at["out"], whole), :] = y[:, :width]
        ext[own_rows, :] += y[:, width : 2 * width]
        ext[pl.ds(at["inward"], inside), :] += jnp.dot(
            x_ref[pl.ds(at["inward_from"], inside), :], held[turn, :, 4 * width :], preferred_element_type=F32
        )
        own = blocks(ext[own_rows, :])
        ours = turned_by(own, rate, far)
        rank = rank_of(own.shape, far)
        pre_ref[index] = flat(jnp.where(rank >= rate, ours, 0.0))
        below = blocks(ext[their_rows, :])
        theirs = turned_by(below, rate, far)
        place = rank_of(below.shape, far)
        acc[:lead, :] = flat(jnp.where(place >= rate, theirs, 0.0))
        if rate == RATE_C:
            col_ref[:whole, :] = flat(jnp.where(rank < rate, ours, 0.0)).astype(BF)
            diag_ref[:lead, :] = flat(jnp.where(place < rate, theirs, 0.0)).astype(BF)
        elif rate == RATE_B:
            half = rate // 2
            col_ref[whole:, :] = flat(jnp.where(rank[:rate] < rate, ours[:rate], own[rate:])).astype(BF)
            part = place[:half] < rate
            diag_ref[RATE_C * SIDE :, :] = flat(jnp.where(part, theirs[:half], below[half:])).astype(BF)
        else:
            have = blocks(col_ref[:whole, :].astype(F32))
            col_ref[:whole, :] = flat(jnp.where(rank >= RATE_C, own, have)).astype(BF)
            have = blocks(diag_ref[:lead, :].astype(F32))
            diag_ref[:lead, :] = flat(jnp.where(place >= RATE_C, below, have)).astype(BF)
        next_from = pl.multiple_of(jnp.where(low == 0, inside, 0), 16)
        keep_from = pl.multiple_of(jnp.where(low == 0, 0, lead), 16)
        pre_ref[index, kept_rows, :] += y[pl.ds(keep_from, inside), 2 * width : 3 * width]
        own = blocks(y[pl.ds(keep_from, inside), 3 * width :])
        rank = rank_of(own.shape, far)
        pre_ref[index, kept_rows, :] += flat(jnp.where(rank < SIDE - rate, turned_by(own, rate, 1 - far), 0.0))
        below = blocks(y[pl.ds(next_from, lead), 3 * width :])
        theirs = flat(jnp.where(place < SIDE - rate, turned_by(below, rate, 1 - far), 0.0))
        row_ref[to_row, :] = (acc[:lead, :] + y[pl.ds(next_from, lead), 2 * width : 3 * width] + theirs).astype(BF)


def inner_parts(pos_ref, x_ref, part_ref, wp_ref, wc_ref, wb_ref, wa_ref, joined_ref, slope_ref, pre_ref, y, z, held, sems):
    low, far = pos_ref[2], pos_ref[3]
    whole = SIDE * SIDE
    width = joined_ref.shape[1]
    copies = tap_copies(pos_ref, (wc_ref, wb_ref, wa_ref), INNER, held, sems)
    for copy in copies:
        copy.start()
    value = jnp.dot(x_ref[...], wp_ref[...], preferred_element_type=F32)
    sig = sigmoid(value)
    joined_ref[...] = (value * sig).astype(BF)
    slope_ref[...] = sig * (1.0 + value * (1.0 - sig))
    for turn, (index, rate) in enumerate(BRANCHES):
        lead = rate * SIDE
        inside = whole - lead
        at = row_marks(low, rate)
        from_rows = pl.ds(at["inward_from"], inside)
        to_rows = pl.ds(at["inner"], inside)
        count = len(INNER)
        for copy in copies[turn * count : (turn + 1) * count]:
            copy.wait()
        y[...] = jnp.dot(x_ref[...], held[turn, :, : 2 * width], preferred_element_type=F32)
        z[:inside, :] = jnp.dot(x_ref[from_rows, :], held[turn, :, 2 * width :], preferred_element_type=F32)
        y[to_rows, :] += z[:inside, :]
        own = blocks(y[:, width:])
        rank = rank_of(own.shape, far)
        moved = flat(jnp.where(rank < SIDE - rate, turned_by(own, rate, 1 - far), 0.0))
        pre_ref[index] = part_ref[index] + y[:, :width] + moved


def outer(pos, centre, w_rate_a, w_rate_b, w_rate_c):
    pixels, chans = centre.shape
    width = w_rate_a.shape[3]
    sends = (RATE_A + RATE_B + RATE_C) * SIDE
    shapes = [((3, pixels, width), F32), ((sends, width), BF), ((sends, width), BF), ((pixels, width), BF)]
    return call(
        outer_parts,
        [jax.ShapeDtypeStruct(*s) for s in shapes],
        1,
        1,
        2 * pixels * chans * width * 14,
        10 * MIB,
        28,
        [
            pltpu.VMEM(((SIDE + RATE_C) * SIDE, width), F32),
            pltpu.VMEM((RATE_C * SIDE, width), F32),
            pltpu.VMEM((pixels, 4 * width), F32),
            pltpu.VMEM((3, chans, len(OUTER) * width), BF),
            pltpu.SemaphoreType.DMA((3, len(OUTER))),
        ],
        name="outer",
        n_any=3,
    )(pos, centre, w_rate_c, w_rate_b, w_rate_a)


def inner(pos, centre, part, w_point, w_rate_a, w_rate_b, w_rate_c):
    pixels, chans = centre.shape
    width = w_point.shape[1]
    return call(
        inner_parts,
        [
            jax.ShapeDtypeStruct((pixels, width), BF),
            jax.ShapeDtypeStruct((pixels, width), F32),
            jax.ShapeDtypeStruct((3, pixels, width), F32),
        ],
        1,
        3,
        2 * pixels * chans * width * 10,
        10 * MIB,
        26,
        [
            pltpu.VMEM((pixels, 2 * width), F32),
            pltpu.VMEM((pixels, 2 * width), F32),
            pltpu.VMEM((3, chans, len(INNER) * width), BF),
            pltpu.SemaphoreType.DMA((3, len(INNER))),
        ],
        name="inner",
        n_any=3,
    )(pos, centre, part, w_point, w_rate_c, w_rate_b, w_rate_a)


def merge_parts(
    pos_ref, joined0_ref, own_ref, row_ref, col_ref, diag_ref, cot_ref, wp_ref, joined_ref, g_ref, d3_ref, pre
):
    low = pos_ref[2]
    theirs = 1 - pos_ref[3]
    width = joined0_ref.shape[1]
    whole = SIDE * SIDE

    def rows_of(rate):
        return pl.multiple_of(jnp.where(low == 0, (SIDE - rate) * SIDE, 0), 16)

    pre[...] = own_ref[...]
    first = 0
    for index, rate in ((2, RATE_C), (1, RATE_B), (0, RATE_A)):
        lead = rate * SIDE
        pre[index, pl.ds(rows_of(rate), lead), :] += row_ref[first : first + lead, :].astype(F32)
        first += lead

    part = blocks(col_ref[:whole, :].astype(F32))
    rank = rank_of(part.shape, theirs)
    pre[2] += flat(jnp.where(rank < RATE_C, part, 0.0))
    pre[0] += flat(turned_by(jnp.where(rank >= RATE_C, part, 0.0), RATE_A, theirs))
    part = blocks(col_ref[whole:, :].astype(F32))
    rank = rank_of(part.shape, theirs)
    pre[1, : RATE_B * SIDE, :] += flat(jnp.where(rank < RATE_B, part, 0.0))
    pre[1, RATE_B * SIDE :, :] += flat(roll_cols(jnp.where(rank >= RATE_B, part, 0.0), RATE_B))

    part = blocks(diag_ref[: RATE_C * SIDE, :].astype(F32))
    rank = rank_of(part.shape, theirs)
    pre[2, pl.ds(rows_of(RATE_C), RATE_C * SIDE), :] += flat(jnp.where(rank < RATE_C, part, 0.0))
    few = part[:RATE_A]
    few = turned_by(jnp.where(rank[:RATE_A] >= RATE_C, few, 0.0), RATE_A, theirs)
    pre[0, pl.ds(rows_of(RATE_A), RATE_A * SIDE), :] += flat(few)
    part = blocks(diag_ref[RATE_C * SIDE :, :].astype(F32))
    rank = rank_of(part.shape, theirs)
    half = RATE_B // 2
    at = rows_of(RATE_B)
    pre[1, pl.ds(at, half * SIDE), :] += flat(jnp.where(rank < RATE_B, part, 0.0))
    last = pl.multiple_of(at + half * SIDE, 16)
    pre[1, pl.ds(last, half * SIDE), :] += flat(roll_cols(jnp.where(rank >= RATE_B, part, 0.0), RATE_B))

    joined_ref[:, :width] = joined0_ref[...]
    for k in range(1, 4):
        value = pre[k - 1]
        sig = sigmoid(value)
        joined_ref[:, k * width : (k + 1) * width] = (value * sig).astype(BF)
    slope = sig * (1.0 + value * (1.0 - sig))
    proj_pre = jnp.dot(joined_ref[...], wp_ref[...], preferred_element_type=F32)
    g_proj = (cot_ref[...].astype(F32) * silu_slope(proj_pre)).astype(BF)
    g_ref[...] = g_proj
    d3_ref[...] = (back_through(g_proj, wp_ref, 3) * slope).astype(BF)


def back_through(g_proj, wp_ref, k):
    width = g_proj.shape[1]
    return lax.dot_general(
        g_proj, wp_ref[k * width : (k + 1) * width, :], (((1,), (1,)), ((), ())), preferred_element_type=F32
    )


def merge(pos, joined0, own, row, col, diag, cot, w_proj):
    pixels, width = joined0.shape
    block = jax.ShapeDtypeStruct((pixels, width), BF)
    return call(
        merge_parts,
        [jax.ShapeDtypeStruct((pixels, 4 * width), BF), block, block],
        1,
        7,
        2 * pixels * width * width * 6,
        6 * 1024 * 1024,
        18,
        [pltpu.VMEM((3, pixels, width), F32)],
        name="merge",
    )(pos, joined0, own, row, col, diag, cot, w_proj)


def pair_grads(pos_ref, joined_ref, g_ref, x_ref, slope_ref, wp_ref, keep_ref, *send_refs):
    core = pos_ref[4]
    over = (((0,), (0,)), ((), ()))
    grad_proj = lax.dot_general(joined_ref[...], g_ref[...], over, preferred_element_type=F32)
    delta = (back_through(g_ref[...], wp_ref, 0) * slope_ref[...]).astype(BF)
    grad_point = lax.dot_general(x_ref[...], delta, over, preferred_element_type=F32)
    keep_ref[...] = jnp.where(core == 0, grad_proj, grad_point)
    half = send_refs[0].shape[0]
    for k, send_ref in enumerate(send_refs):
        part = slice(k * half, (k + 1) * half)
        send_ref[...] = jnp.where(core == 0, grad_point[part], grad_proj[part]).astype(BF)


def shards(features, cotangent, w_point, w_rate_a, w_rate_b, w_rate_c, w_proj, bucket_slot):
    image = features[0]
    rows_dev, cols_dev, chans = image.shape
    pixels = rows_dev * cols_dev
    width = w_point.shape[1]
    row, col, core = (lax.axis_index(n) for n in ("row", "col", "dp_2"))
    at_y, at_z = lax.axis_index("dp_0"), lax.axis_index("dp_1")
    pos = jnp.stack([2 * row + col, at_y, row, col, core, at_z]).astype(jnp.int32)
    replicas = lax.axis_size(DP)
    slot_count = replicas * (bucket_slot.shape[0] // replicas + 1)
    place = place_slots(bucket_slot, core, slot_count)
    centre = image.reshape(pixels, chans)
    weights = [pltpu.with_memory_space_constraint(w, pltpu.HBM) for w in (w_rate_a, w_rate_b, w_rate_c)]
    picked = pick(pos, centre)
    centre, *picked = lax.optimization_barrier((centre, *picked))
    got = [picked[0]] + [flip(picked[k], k) for k in (1, 2, 3)]
    part, *parts = outer(pos, centre, *weights)
    part, got = lax.optimization_barrier((part, got))
    to_row, to_col, to_diag = parts
    parts = [flip(to_row, 2), flip(to_col, 1), flip(to_diag, 3)]
    turned = turn(pos, got)
    joined0, slope0, own = inner(pos, centre, part, w_point, *weights)
    parts, joined0, own, turned = lax.optimization_barrier((parts, joined0, own, turned))
    joined, g_proj, delta3 = merge(
        pos, joined0, own, *parts, cotangent[0].reshape(pixels, width), w_proj
    )
    shared = [delta3] + [flip(delta3, k) for k in (1, 2, 3)]
    block = (4 * width, width)
    kept, *sent = call(
        pair_grads,
        [jax.ShapeDtypeStruct(block, F32)] + [jax.ShapeDtypeStruct((2 * width, width), BF)] * 2,
        1,
        5,
        4 * pixels * chans * width,
        4 * 1024 * 1024,
        16,
        name="pair",
    )(pos, joined, g_proj, centre, slope0, w_proj)
    got = [swap_core(part) for part in sent]
    by_owner = split_pair(pos, kept, got)
    by_owner, shared = lax.optimization_barrier((by_owner, shared))
    by_owner = [by_owner[0]] + [flip(by_owner[k], k) for k in (1, 2, 3)]
    kept, sent = tap_slots(pos, place, shared, turned, slot_count)
    sent, by_owner = lax.optimization_barrier((sent, by_owner))
    mine, other = sum_pair(by_owner)
    return reduce_slots(pos, place, kept, sent, mine, other)


def solution(mesh):
    torus = Mesh(
        mesh.devices.reshape(mesh.shape["row"], mesh.shape["col"], 4, 4, 2),
        ("row", "col", "dp_0", "dp_1", "dp_2"),
    )
    in_specs = (P(DP, "row", "col", None), P(DP, "row", "col", None), P(), P(), P(), P(), P(), P())
    out_specs = P(DP, ("row", "col"))
    return jax.shard_map(
        shards, mesh=torus, in_specs=in_specs, out_specs=out_specs, check_vma=False
    )
```

```python
import jax
import jax.numpy as jnp
from jax import lax
from jax.experimental import pallas as pl
from jax.experimental.pallas import tpu as pltpu
from jax.sharding import Mesh
from jax.sharding import PartitionSpec as P

RATE_A = 6
RATE_B = 12
RATE_C = 18
DP = ("dp_0", "dp_1", "dp_2")


BF = jnp.bfloat16
F32 = jnp.float32
MIB = 1024 * 1024
EDGE = 8


def flip(x, mask):
    if mask == 1:
        return lax.ppermute(x, "col", [(0, 1), (1, 0)])
    if mask == 2:
        return lax.ppermute(x, "row", [(0, 1), (1, 0)])
    return lax.ppermute(x, ("row", "col"), [(0, 3), (3, 0), (1, 2), (2, 1)])


def smem():
    return pl.BlockSpec(memory_space=pltpu.SMEM)


def vmem():
    return pl.BlockSpec(memory_space=pltpu.VMEM)


def call(body, outs, n_smem, n_vmem, flops, nbytes, limit, scratch=(), name=None, n_any=0):
    return pl.pallas_call(
        body,
        out_shape=outs,
        in_specs=[smem()] * n_smem + [vmem()] * n_vmem + [pl.BlockSpec(memory_space=pltpu.HBM)] * n_any,
        out_specs=jax.tree.map(lambda _: vmem(), outs),
        scratch_shapes=list(scratch),
        compiler_params=pltpu.CompilerParams(vmem_limit_bytes=limit * MIB),
        cost_estimate=pl.CostEstimate(flops=flops, bytes_accessed=nbytes, transcendentals=0),
        name=name,
    )


LANES = 128


def pick_matrix(me, first, count):
    shape = (4 * LANES, count * LANES)
    source = lax.broadcasted_iota(jnp.int32, shape, 0)
    col = lax.broadcasted_iota(jnp.int32, (1, shape[1]), 1)
    owner = jnp.bitwise_xor(me, col // LANES + first)
    wanted = 64 * ((col % LANES) // 16) + 16 * owner + col % 16
    return jnp.where(source == wanted, 1.0, 0.0).astype(BF)


def select_channels(pos_ref, x_ref, *rest):
    *o_refs, held, sems = rest
    group = 4 * LANES
    pieces = sems.shape[0]
    each = x_ref.shape[0] // pieces
    copies = []
    for n in range(pieces):
        part = pl.ds(n * each, each)
        copies.append(pltpu.make_async_copy(x_ref.at[part, :], held.at[part, :], sems.at[n]))
        copies[n].start()
    picks = pick_matrix(pos_ref[0], 1, len(o_refs))
    for n in range(pieces):
        copies[n].wait()
        rows = slice(n * each, (n + 1) * each)
        for p in range(x_ref.shape[1] // group):
            taken = jnp.dot(held[rows, p * group : (p + 1) * group], picks, preferred_element_type=F32).astype(BF)
            for k, o_ref in enumerate(o_refs):
                o_ref[rows, p * LANES : (p + 1) * LANES] = taken[:, k * LANES : (k + 1) * LANES]


def turn_pixels(pos_ref, x_ref, x1, x2, x3, o_ref, edge_ref, held):
    pixels, width = x1.shape
    mine = pl.multiple_of((pos_ref[0] // 2) * pixels, 16)
    group = 4 * LANES
    picks = pick_matrix(pos_ref[0], 0, 1)
    for p in range(width // LANES):
        taken = jnp.dot(x_ref[:, p * group : (p + 1) * group], picks, preferred_element_type=F32).astype(BF)
        held[pos_ref[0] % 2, pl.ds(mine, pixels), p * LANES : (p + 1) * LANES] = taken
    for k, x in ((1, x1), (2, x2), (3, x3)):
        s = jnp.bitwise_xor(pos_ref[0], k)
        held[s % 2, pl.ds(pl.multiple_of((s // 2) * pixels, 16), pixels), :] = x[...]
    eye = (
        lax.broadcasted_iota(jnp.int32, (width, width), 0)
        == lax.broadcasted_iota(jnp.int32, (width, width), 1)
    ).astype(F32).astype(BF)
    for g in range(2):
        o_ref[g] = lax.dot_general(
            eye, held[g], (((1,), (1,)), ((), ())), preferred_element_type=F32
        ).astype(BF)
        wide = held[g].astype(F32).reshape(-1, SIDE, width)
        near = wide[:, SIDE - EDGE :] if g == 0 else wide[:, :EDGE]
        edge_ref[g] = lax.dot_general(
            eye, near.reshape(-1, width).astype(BF), (((1,), (1,)), ((), ())), preferred_element_type=F32
        ).astype(BF)


def roll_cols(x, shift):
    return jnp.concatenate([x[:, x.shape[1] - shift :], x[:, : x.shape[1] - shift]], axis=1)


def tap_grads(pos_ref, place_ref, d0, d1, d2, d3, xt_ref, xe_ref, keep_ref, send_ref, held, padded, edge, buf):
    side = RATE_C
    pixels, width = d0.shape
    cols = 24
    rows = pixels // cols
    for k, d in enumerate((d0, d1, d2, d3)):
        s = jnp.bitwise_xor(pos_ref[0], k)
        held[s % 2, pl.ds((s // 2) * pixels, pixels), :] = d[...]
    buf[...] = jnp.zeros_like(buf)
    tall = 2 * pixels
    lead = side * cols
    zeros = jnp.zeros((2, lead, width), BF)
    halves = [held[g].astype(F32).reshape(2 * rows, cols, width) for g in range(2)]
    at = lax.broadcasted_iota(jnp.int32, (2 * rows, cols, width), 1)
    rest = cols - side
    for across in (0, 1, -1):
        turn = across + 1
        padded[turn, :, pl.ds(0, lead), :] = zeros
        padded[turn, :, pl.ds(lead + tall, lead), :] = zeros
        if across == 0:
            shifted = halves
        elif across == 1:
            rolled = [roll_cols(h, side) for h in halves]
            shifted = [
                jnp.where(at >= side, rolled[0], 0.0),
                jnp.where(at < side, rolled[0], rolled[1]),
            ]
        else:
            rolled = [roll_cols(h, rest) for h in halves]
            shifted = [
                jnp.where(at < rest, rolled[0], rolled[1]),
                jnp.where(at < rest, rolled[1], 0.0),
            ]
        thin = {1: 0, -1: 1}.get(across)
        for g in range(2):
            if g == thin:
                near = shifted[g][:, SIDE - EDGE :] if g == 0 else shifted[g][:, :EDGE]
                short = side * EDGE
                edge[g, pl.ds(0, short), :] = jnp.zeros((short, width), BF)
                edge[g, pl.ds(short, 2 * rows * EDGE), :] = near.reshape(2 * rows * EDGE, width).astype(BF)
                edge[g, pl.ds(short + 2 * rows * EDGE, short), :] = jnp.zeros((short, width), BF)
            else:
                padded[turn, g, pl.ds(lead, tall), :] = shifted[g].reshape(tall, width).astype(BF)
        for above in (-1, 0, 1):
            first, last = {-1: (0, 32), 0: (0, 48), 1: (16, 48)}[above]
            base = first - side * above + side
            total = None
            for g in range(2):
                left, right, each = (xe_ref, edge.at[g], EDGE) if g == thin else (xt_ref, padded.at[turn, g], cols)
                part = jnp.dot(
                    left[g, :, first * each : last * each],
                    right[base * each : (base + last - first) * each, :],
                    preferred_element_type=F32,
                )
                total = part if total is None else total + part
            tap = 3 * (above + 1) + across + 1
            groups = total.reshape(width // 16, 16, width)
            for m in range(width // 16):
                buf[place_ref[32 + 16 * tap + m]] = groups[m]
    half = buf.shape[0] // 2
    keep_ref[...] = buf[:half]
    send_ref[...] = buf[half:].astype(BF)


def join_owners(pos_ref, place_ref, keep_ref, got_ref, mine_ref, other_ref, o_ref, total):
    total[...] = keep_ref[...] + got_ref[...].astype(F32)
    core = pos_ref[4]
    for n in range(mine_ref.shape[0]):
        for ref, first in ((mine_ref, 16 * core), (other_ref, 16 * (1 - core))):
            at = place_ref[first + n]

            @pl.when(at < total.shape[0])
            def _(ref=ref, at=at, n=n):
                total[at] = ref[n].astype(F32)

    o_ref[...] = total[...].astype(BF).reshape(o_ref.shape)


def fold_last(r_ref, o_ref, total):
    value = r_ref[0].astype(F32)
    for n in range(1, r_ref.shape[0]):
        value = value + r_ref[n].astype(F32)
    total[...] = value.reshape(total.shape)
    width = total.shape[2]
    for i in range(total.shape[1]):
        o_ref[:, i * width : (i + 1) * width] = total[:, i, :]


def share_rows(pos_ref, kept_ref, got0, got1, *rest):
    *outs, total = rest
    half, each = got0.shape[0], total.shape[0] // 2
    for n, got in enumerate((got0, got1)):
        value = kept_ref[n * half : (n + 1) * half, :] + got[...].astype(F32)
        total[n * each : (n + 1) * each] = value.reshape(each, *total.shape[1:])
    for k, out in enumerate(outs):
        out[...] = total[:, jnp.bitwise_xor(pos_ref[0], k)].astype(out.dtype)


def swap_core(x):
    return lax.ppermute(x, "dp_2", [(0, 1), (1, 0)])


def pick(pos, centre):
    pixels, chans = centre.shape
    block = jax.ShapeDtypeStruct((pixels, chans // 4), BF)
    return call(
        select_channels,
        [block] * 3,
        1,
        0,
        pixels * chans * chans,
        4 * pixels * chans,
        12,
        [pltpu.VMEM((pixels, chans), BF), pltpu.SemaphoreType.DMA((2,))],
        name="pick",
        n_any=1,
    )(pos, pltpu.with_memory_space_constraint(centre, pltpu.HBM))


def turn(pos, centre, got):
    pixels, width = got[0].shape
    return call(
        turn_pixels,
        [
            jax.ShapeDtypeStruct((2, width, 2 * pixels), BF),
            jax.ShapeDtypeStruct((2, width, 2 * pixels // SIDE * EDGE), BF),
        ],
        1,
        4,
        8 * pixels * width * width,
        16 * pixels * width,
        12,
        [pltpu.VMEM((2, 2 * pixels, width), BF)],
        name="turn",
    )(pos, centre, *got)


def split_pair(pos, kept, got):
    width = kept.shape[1]
    slices = kept.shape[0] // 64
    shape = (slices, 16, width)
    return call(
        share_rows,
        [jax.ShapeDtypeStruct(shape, F32)] + [jax.ShapeDtypeStruct(shape, BF)] * 3,
        1,
        3,
        0,
        0,
        10,
        [pltpu.VMEM((slices, 4, 16, width), F32)],
        name="rows",
    )(pos, kept, *got)


def sum_pair(blocks):
    mine = blocks[0] + sum(block.astype(F32) for block in blocks[1:])
    return mine, swap_core(mine.astype(BF))


def place_slots(bucket_slot, core, slot_count):
    replicas = lax.axis_size(DP)
    capacity = slot_count // replicas
    owner = bucket_slot // capacity
    other = jnp.bitwise_xor(owner % 2, core)
    return other * (slot_count // 2) + (owner // 2) * capacity + bucket_slot % capacity


def tap_slots(pos, place, deltas, turned, slot_count):
    pixels, width = deltas[0].shape
    half = slot_count // 2
    return call(
        tap_grads,
        [jax.ShapeDtypeStruct((half, 16, width), F32), jax.ShapeDtypeStruct((half, 16, width), BF)],
        2,
        6,
        2 * 7 * 4 * pixels * width * width,
        8 * 1024 * 1024,
        26,
        [
            pltpu.VMEM((2, 2 * pixels, width), BF),
            pltpu.VMEM((3, 2, 2 * pixels + 2 * RATE_C * SIDE, width), BF),
            pltpu.VMEM((2, (2 * SIDE + 2 * RATE_C) * EDGE, width), BF),
            pltpu.VMEM((slot_count, 16, width), F32),
        ],
        name="taps",
    )(pos, place, *deltas, *turned)


def reduce_slots(pos, place, kept, sent, mine, other):
    half, rows, width = kept.shape
    chips = lax.axis_size("dp_0") * lax.axis_size("dp_1")
    each = half // chips
    total = call(
        join_owners,
        jax.ShapeDtypeStruct((chips, each * rows, width), BF),
        2,
        4,
        kept.size,
        8 * kept.size,
        12,
        [pltpu.VMEM((half, rows, width), F32)],
        name="owners",
    )(pos, place, kept, swap_core(sent), mine, other)
    total = lax.all_to_all(total, ("dp_0", "dp_1"), 0, 0, tiled=True)
    return call(
        fold_last,
        jax.ShapeDtypeStruct((each, rows * width), F32),
        0,
        1,
        kept.size,
        2 * kept.size,
        8,
        [pltpu.VMEM((each, rows, width), F32)],
        name="last",
    )(total)


def sigmoid(value):
    return 0.5 + 0.5 * jnp.tanh(0.5 * value)


def silu_slope(value):
    sig = sigmoid(value)
    return sig * (1.0 + value * (1.0 - sig))


RATES = (RATE_A, RATE_B, RATE_C)
SIDE = 24


def turned_by(x, shift, far):
    return jnp.where(far == 0, roll_cols(x, shift), roll_cols(x, SIDE - shift))


def rank_of(shape, far):
    at = lax.broadcasted_iota(jnp.int32, shape, 1)
    return jnp.where(far == 0, at, SIDE - 1 - at)


def row_marks(low, rate):
    lead = rate * SIDE
    whole = SIDE * SIDE

    def either(upper, lower):
        return pl.multiple_of(jnp.where(low == 0, upper, lower), 16)

    return dict(
        own=either(0, lead),
        out=either(lead, 0),
        theirs=either(whole, 0),
        inward_from=either(lead, 0),
        inward=either(0, 2 * lead),
        kept=either(lead, 0),
        inner=either(0, lead),
    )


def blocks(x):
    return x.reshape(x.shape[0] // SIDE, SIDE, x.shape[1])


def flat(x):
    return x.reshape(x.shape[0] * SIDE, x.shape[2])


def tap_copies(pos_ref, refs, jobs, held, sems):
    copies = []
    for branch, ref in enumerate(refs):
        for n, (above, across) in enumerate(jobs):
            a = 1 if above == 1 else jnp.where(pos_ref[2] == 0, above, 2 - above)
            b = 1 if across == 1 else jnp.where(pos_ref[3] == 0, across, 2 - across)
            width = ref.shape[3]
            to = held.at[branch, :, n * width : (n + 1) * width]
            copies.append(pltpu.make_async_copy(ref.at[a, b], to, sems.at[branch, n]))
    return copies


BRANCHES = ((2, RATE_C), (1, RATE_B), (0, RATE_A))
OUTER = ((0, 0), (1, 0), (0, 1), (0, 2), (2, 0))
INNER = ((1, 1), (1, 2), (2, 1), (2, 2))


def outer_parts(pos_ref, x_ref, wc_ref, wb_ref, wa_ref, pre_ref, row_ref, col_ref, diag_ref, ext, acc, y, held, sems):
    low, far = pos_ref[2], pos_ref[3]
    whole = SIDE * SIDE
    width = pre_ref.shape[2]
    copies = tap_copies(pos_ref, (wc_ref, wb_ref, wa_ref), OUTER, held, sems)
    for copy in copies:
        copy.start()
    first = 0
    for turn, (index, rate) in enumerate(BRANCHES):
        lead = rate * SIDE
        inside = whole - lead
        at = row_marks(low, rate)
        own_rows = pl.ds(at["own"], whole)
        their_rows = pl.ds(at["theirs"], lead)
        kept_rows = pl.ds(at["kept"], inside)
        to_row = slice(first, first + lead)
        first += lead
        count = len(OUTER)
        for copy in copies[turn * count : (turn + 1) * count]:
            copy.wait()
        y[...] = jnp.dot(x_ref[...], held[turn, :, : 4 * width], preferred_element_type=F32)
        ext[pl.ds(pl.multiple_of(whole - at["theirs"], 16), lead), :] = jnp.zeros((lead, width), F32)
        ext[pl.ds(at["out"], whole), :] = y[:, :width]
        ext[own_rows, :] += y[:, width : 2 * width]
        ext[pl.ds(at["inward"], inside), :] += jnp.dot(
            x_ref[pl.ds(at["inward_from"], inside), :], held[turn, :, 4 * width :], preferred_element_type=F32
        )
        own = blocks(ext[own_rows, :])
        ours = turned_by(own, rate, far)
        rank = rank_of(own.shape, far)
        pre_ref[index] = flat(jnp.where(rank >= rate, ours, 0.0))
        below = blocks(ext[their_rows, :])
        theirs = turned_by(below, rate, far)
        place = rank_of(below.shape, far)
        acc[:lead, :] = flat(jnp.where(place >= rate, theirs, 0.0))
        if rate == RATE_C:
            col_ref[:whole, :] = flat(jnp.where(rank < rate, ours, 0.0)).astype(BF)
            diag_ref[:lead, :] = flat(jnp.where(place < rate, theirs, 0.0)).astype(BF)
        elif rate == RATE_B:
            half = rate // 2
            col_ref[whole:, :] = flat(jnp.where(rank[:rate] < rate, ours[:rate], own[rate:])).astype(BF)
            part = place[:half] < rate
            diag_ref[RATE_C * SIDE :, :] = flat(jnp.where(part, theirs[:half], below[half:])).astype(BF)
        else:
            have = blocks(col_ref[:whole, :].astype(F32))
            col_ref[:whole, :] = flat(jnp.where(rank >= RATE_C, own, have)).astype(BF)
            have = blocks(diag_ref[:lead, :].astype(F32))
            diag_ref[:lead, :] = flat(jnp.where(place >= RATE_C, below, have)).astype(BF)
        next_from = pl.multiple_of(jnp.where(low == 0, inside, 0), 16)
        keep_from = pl.multiple_of(jnp.where(low == 0, 0, lead), 16)
        pre_ref[index, kept_rows, :] += y[pl.ds(keep_from, inside), 2 * width : 3 * width]
        own = blocks(y[pl.ds(keep_from, inside), 3 * width :])
        rank = rank_of(own.shape, far)
        pre_ref[index, kept_rows, :] += flat(jnp.where(rank < SIDE - rate, turned_by(own, rate, 1 - far), 0.0))
        below = blocks(y[pl.ds(next_from, lead), 3 * width :])
        theirs = flat(jnp.where(place < SIDE - rate, turned_by(below, rate, 1 - far), 0.0))
        row_ref[to_row, :] = (acc[:lead, :] + y[pl.ds(next_from, lead), 2 * width : 3 * width] + theirs).astype(BF)


def inner_parts(pos_ref, x_ref, part_ref, wp_ref, wc_ref, wb_ref, wa_ref, joined_ref, slope_ref, pre_ref, y, z, held, sems):
    low, far = pos_ref[2], pos_ref[3]
    whole = SIDE * SIDE
    width = joined_ref.shape[1]
    copies = tap_copies(pos_ref, (wc_ref, wb_ref, wa_ref), INNER, held, sems)
    for copy in copies:
        copy.start()
    value = jnp.dot(x_ref[...], wp_ref[...], preferred_element_type=F32)
    sig = sigmoid(value)
    joined_ref[...] = (value * sig).astype(BF)
    slope_ref[...] = sig * (1.0 + value * (1.0 - sig))
    for turn, (index, rate) in enumerate(BRANCHES):
        lead = rate * SIDE
        inside = whole - lead
        at = row_marks(low, rate)
        from_rows = pl.ds(at["inward_from"], inside)
        to_rows = pl.ds(at["inner"], inside)
        count = len(INNER)
        for copy in copies[turn * count : (turn + 1) * count]:
            copy.wait()
        y[...] = jnp.dot(x_ref[...], held[turn, :, : 2 * width], preferred_element_type=F32)
        z[:inside, :] = jnp.dot(x_ref[from_rows, :], held[turn, :, 2 * width :], preferred_element_type=F32)
        y[to_rows, :] += z[:inside, :]
        own = blocks(y[:, width:])
        rank = rank_of(own.shape, far)
        moved = flat(jnp.where(rank < SIDE - rate, turned_by(own, rate, 1 - far), 0.0))
        pre_ref[index] = part_ref[index] + y[:, :width] + moved


def outer(pos, centre, w_rate_a, w_rate_b, w_rate_c):
    pixels, chans = centre.shape
    width = w_rate_a.shape[3]
    sends = (RATE_A + RATE_B + RATE_C) * SIDE
    shapes = [((3, pixels, width), F32), ((sends, width), BF), ((sends, width), BF), ((pixels, width), BF)]
    return call(
        outer_parts,
        [jax.ShapeDtypeStruct(*s) for s in shapes],
        1,
        1,
        2 * pixels * chans * width * 14,
        10 * MIB,
        28,
        [
            pltpu.VMEM(((SIDE + RATE_C) * SIDE, width), F32),
            pltpu.VMEM((RATE_C * SIDE, width), F32),
            pltpu.VMEM((pixels, 4 * width), F32),
            pltpu.VMEM((3, chans, len(OUTER) * width), BF),
            pltpu.SemaphoreType.DMA((3, len(OUTER))),
        ],
        name="outer",
        n_any=3,
    )(pos, centre, w_rate_c, w_rate_b, w_rate_a)


def inner(pos, centre, part, w_point, w_rate_a, w_rate_b, w_rate_c):
    pixels, chans = centre.shape
    width = w_point.shape[1]
    return call(
        inner_parts,
        [
            jax.ShapeDtypeStruct((pixels, width), BF),
            jax.ShapeDtypeStruct((pixels, width), F32),
            jax.ShapeDtypeStruct((3, pixels, width), F32),
        ],
        1,
        3,
        2 * pixels * chans * width * 10,
        10 * MIB,
        26,
        [
            pltpu.VMEM((pixels, 2 * width), F32),
            pltpu.VMEM((pixels, 2 * width), F32),
            pltpu.VMEM((3, chans, len(INNER) * width), BF),
            pltpu.SemaphoreType.DMA((3, len(INNER))),
        ],
        name="inner",
        n_any=3,
    )(pos, centre, part, w_point, w_rate_c, w_rate_b, w_rate_a)


def merge_parts(
    pos_ref, joined0_ref, own_ref, row_ref, col_ref, diag_ref, cot_ref, wp_ref, joined_ref, g_ref, d3_ref, pre
):
    low = pos_ref[2]
    theirs = 1 - pos_ref[3]
    width = joined0_ref.shape[1]
    whole = SIDE * SIDE

    def rows_of(rate):
        return pl.multiple_of(jnp.where(low == 0, (SIDE - rate) * SIDE, 0), 16)

    part = blocks(col_ref[:whole, :].astype(F32))
    rank = rank_of(part.shape, theirs)
    pre[2] = own_ref[2] + flat(jnp.where(rank < RATE_C, part, 0.0))
    pre[0] = own_ref[0] + flat(turned_by(jnp.where(rank >= RATE_C, part, 0.0), RATE_A, theirs))
    part = blocks(col_ref[whole:, :].astype(F32))
    rank = rank_of(part.shape, theirs)
    half = RATE_B * SIDE
    pre[1, :half, :] = own_ref[1, :half, :] + flat(jnp.where(rank < RATE_B, part, 0.0))
    pre[1, half:, :] = own_ref[1, half:, :] + flat(roll_cols(jnp.where(rank >= RATE_B, part, 0.0), RATE_B))
    first = 0
    for index, rate in ((2, RATE_C), (1, RATE_B), (0, RATE_A)):
        lead = rate * SIDE
        pre[index, pl.ds(rows_of(rate), lead), :] += row_ref[first : first + lead, :].astype(F32)
        first += lead

    part = blocks(diag_ref[: RATE_C * SIDE, :].astype(F32))
    rank = rank_of(part.shape, theirs)
    pre[2, pl.ds(rows_of(RATE_C), RATE_C * SIDE), :] += flat(jnp.where(rank < RATE_C, part, 0.0))
    few = part[:RATE_A]
    few = turned_by(jnp.where(rank[:RATE_A] >= RATE_C, few, 0.0), RATE_A, theirs)
    pre[0, pl.ds(rows_of(RATE_A), RATE_A * SIDE), :] += flat(few)
    part = blocks(diag_ref[RATE_C * SIDE :, :].astype(F32))
    rank = rank_of(part.shape, theirs)
    half = RATE_B // 2
    at = rows_of(RATE_B)
    pre[1, pl.ds(at, half * SIDE), :] += flat(jnp.where(rank < RATE_B, part, 0.0))
    last = pl.multiple_of(at + half * SIDE, 16)
    pre[1, pl.ds(last, half * SIDE), :] += flat(roll_cols(jnp.where(rank >= RATE_B, part, 0.0), RATE_B))

    joined_ref[:, :width] = joined0_ref[...]
    for k in range(1, 4):
        value = pre[k - 1]
        sig = sigmoid(value)
        joined_ref[:, k * width : (k + 1) * width] = (value * sig).astype(BF)
    slope = sig * (1.0 + value * (1.0 - sig))
    proj_pre = jnp.dot(joined_ref[...], wp_ref[...], preferred_element_type=F32)
    g_proj = (cot_ref[...].astype(F32) * silu_slope(proj_pre)).astype(BF)
    g_ref[...] = g_proj
    d3_ref[...] = (back_through(g_proj, wp_ref, 3) * slope).astype(BF)


def back_through(g_proj, wp_ref, k):
    width = g_proj.shape[1]
    return lax.dot_general(
        g_proj, wp_ref[k * width : (k + 1) * width, :], (((1,), (1,)), ((), ())), preferred_element_type=F32
    )


def merge(pos, joined0, own, row, col, diag, cot, w_proj):
    pixels, width = joined0.shape
    block = jax.ShapeDtypeStruct((pixels, width), BF)
    return call(
        merge_parts,
        [jax.ShapeDtypeStruct((pixels, 4 * width), BF), block, block],
        1,
        7,
        2 * pixels * width * width * 6,
        6 * 1024 * 1024,
        18,
        [pltpu.VMEM((3, pixels, width), F32)],
        name="merge",
    )(pos, joined0, own, row, col, diag, cot, w_proj)


def pair_grads(pos_ref, joined_ref, g_ref, x_ref, slope_ref, wp_ref, keep_ref, *send_refs):
    core = pos_ref[4]
    over = (((0,), (0,)), ((), ()))
    grad_proj = lax.dot_general(joined_ref[...], g_ref[...], over, preferred_element_type=F32)
    delta = (back_through(g_ref[...], wp_ref, 0) * slope_ref[...]).astype(BF)
    grad_point = lax.dot_general(x_ref[...], delta, over, preferred_element_type=F32)
    keep_ref[...] = jnp.where(core == 0, grad_proj, grad_point)
    half = send_refs[0].shape[0]
    for k, send_ref in enumerate(send_refs):
        part = slice(k * half, (k + 1) * half)
        send_ref[...] = jnp.where(core == 0, grad_point[part], grad_proj[part]).astype(BF)


def shards(features, cotangent, w_point, w_rate_a, w_rate_b, w_rate_c, w_proj, bucket_slot):
    image = features[0]
    rows_dev, cols_dev, chans = image.shape
    pixels = rows_dev * cols_dev
    width = w_point.shape[1]
    row, col, core = (lax.axis_index(n) for n in ("row", "col", "dp_2"))
    at_y, at_z = lax.axis_index("dp_0"), lax.axis_index("dp_1")
    pos = jnp.stack([2 * row + col, at_y, row, col, core, at_z]).astype(jnp.int32)
    replicas = lax.axis_size(DP)
    slot_count = replicas * (bucket_slot.shape[0] // replicas + 1)
    place = place_slots(bucket_slot, core, slot_count)
    centre = image.reshape(pixels, chans)
    weights = [pltpu.with_memory_space_constraint(w, pltpu.HBM) for w in (w_rate_a, w_rate_b, w_rate_c)]
    picked = pick(pos, centre)
    centre, *picked = lax.optimization_barrier((centre, *picked))
    got = [flip(picked[k - 1], k) for k in (1, 2, 3)]
    part, *parts = outer(pos, centre, *weights)
    part, got = lax.optimization_barrier((part, got))
    to_row, to_col, to_diag = parts
    parts = [flip(to_row, 2), flip(to_col, 1), flip(to_diag, 3)]
    turned = turn(pos, centre, got)
    joined0, slope0, own = inner(pos, centre, part, w_point, *weights)
    parts, joined0, own, turned = lax.optimization_barrier((parts, joined0, own, turned))
    joined, g_proj, delta3 = merge(
        pos, joined0, own, *parts, cotangent[0].reshape(pixels, width), w_proj
    )
    shared = [delta3] + [flip(delta3, k) for k in (1, 2, 3)]
    block = (4 * width, width)
    kept, *sent = call(
        pair_grads,
        [jax.ShapeDtypeStruct(block, F32)] + [jax.ShapeDtypeStruct((2 * width, width), BF)] * 2,
        1,
        5,
        4 * pixels * chans * width,
        4 * 1024 * 1024,
        16,
        name="pair",
    )(pos, joined, g_proj, centre, slope0, w_proj)
    got = [swap_core(part) for part in sent]
    by_owner = split_pair(pos, kept, got)
    by_owner, shared = lax.optimization_barrier((by_owner, shared))
    by_owner = [by_owner[0]] + [flip(by_owner[k], k) for k in (1, 2, 3)]
    kept, sent = tap_slots(pos, place, shared, turned, slot_count)
    sent, by_owner = lax.optimization_barrier((sent, by_owner))
    mine, other = sum_pair(by_owner)
    return reduce_slots(pos, place, kept, sent, mine, other)


def solution(mesh):
    torus = Mesh(
        mesh.devices.reshape(mesh.shape["row"], mesh.shape["col"], 4, 4, 2),
        ("row", "col", "dp_0", "dp_1", "dp_2"),
    )
    in_specs = (P(DP, "row", "col", None), P(DP, "row", "col", None), P(), P(), P(), P(), P(), P())
    out_specs = P(DP, ("row", "col"))
    return jax.shard_map(
        shards, mesh=torus, in_specs=in_specs, out_specs=out_specs, check_vma=False
    )
```

```python
import jax
import jax.numpy as jnp
from jax import lax
from jax.experimental import pallas as pl
from jax.experimental.pallas import tpu as pltpu
from jax.sharding import Mesh
from jax.sharding import PartitionSpec as P

RATE_A = 6
RATE_B = 12
RATE_C = 18
DP = ("dp_0", "dp_1", "dp_2")


BF = jnp.bfloat16
F32 = jnp.float32
MIB = 1024 * 1024
EDGE = 8


def flip(x, mask):
    if mask == 1:
        return lax.ppermute(x, "col", [(0, 1), (1, 0)])
    if mask == 2:
        return lax.ppermute(x, "row", [(0, 1), (1, 0)])
    return lax.ppermute(x, ("row", "col"), [(0, 3), (3, 0), (1, 2), (2, 1)])


def smem():
    return pl.BlockSpec(memory_space=pltpu.SMEM)


def vmem():
    return pl.BlockSpec(memory_space=pltpu.VMEM)


def call(body, outs, n_smem, n_vmem, flops, nbytes, limit, scratch=(), name=None, n_any=0):
    return pl.pallas_call(
        body,
        out_shape=outs,
        in_specs=[smem()] * n_smem + [vmem()] * n_vmem + [pl.BlockSpec(memory_space=pltpu.HBM)] * n_any,
        out_specs=jax.tree.map(lambda _: vmem(), outs),
        scratch_shapes=list(scratch),
        compiler_params=pltpu.CompilerParams(vmem_limit_bytes=limit * MIB),
        cost_estimate=pl.CostEstimate(flops=flops, bytes_accessed=nbytes, transcendentals=0),
        name=name,
    )


LANES = 128


def pick_matrix(me, first, count):
    shape = (4 * LANES, count * LANES)
    source = lax.broadcasted_iota(jnp.int32, shape, 0)
    col = lax.broadcasted_iota(jnp.int32, (1, shape[1]), 1)
    owner = jnp.bitwise_xor(me, col // LANES + first)
    wanted = 64 * ((col % LANES) // 16) + 16 * owner + col % 16
    return jnp.where(source == wanted, 1.0, 0.0).astype(BF)


def select_channels(pos_ref, x_ref, *rest):
    held, *o_refs, sems = rest
    group = 4 * LANES
    pieces = sems.shape[0]
    each = x_ref.shape[0] // pieces
    copies = []
    for n in range(pieces):
        part = pl.ds(n * each, each)
        copies.append(pltpu.make_async_copy(x_ref.at[part, :], held.at[part, :], sems.at[n]))
        copies[n].start()
    picks = pick_matrix(pos_ref[0], 1, len(o_refs))
    for n in range(pieces):
        copies[n].wait()
        rows = slice(n * each, (n + 1) * each)
        for p in range(x_ref.shape[1] // group):
            taken = jnp.dot(held[rows, p * group : (p + 1) * group], picks, preferred_element_type=F32).astype(BF)
            for k, o_ref in enumerate(o_refs):
                o_ref[rows, p * LANES : (p + 1) * LANES] = taken[:, k * LANES : (k + 1) * LANES]


def turn_pixels(pos_ref, x_ref, x1, x2, x3, o_ref, edge_ref, held):
    pixels, width = x1.shape
    mine = pl.multiple_of((pos_ref[0] // 2) * pixels, 16)
    group = 4 * LANES
    picks = pick_matrix(pos_ref[0], 0, 1)
    for p in range(width // LANES):
        taken = jnp.dot(x_ref[:, p * group : (p + 1) * group], picks, preferred_element_type=F32).astype(BF)
        held[pos_ref[0] % 2, pl.ds(mine, pixels), p * LANES : (p + 1) * LANES] = taken
    for k, x in ((1, x1), (2, x2), (3, x3)):
        s = jnp.bitwise_xor(pos_ref[0], k)
        held[s % 2, pl.ds(pl.multiple_of((s // 2) * pixels, 16), pixels), :] = x[...]
    eye = (
        lax.broadcasted_iota(jnp.int32, (width, width), 0)
        == lax.broadcasted_iota(jnp.int32, (width, width), 1)
    ).astype(F32).astype(BF)
    for g in range(2):
        o_ref[g] = lax.dot_general(
            eye, held[g], (((1,), (1,)), ((), ())), preferred_element_type=F32
        ).astype(BF)
        wide = held[g].astype(F32).reshape(-1, SIDE, width)
        near = wide[:, SIDE - EDGE :] if g == 0 else wide[:, :EDGE]
        edge_ref[g] = lax.dot_general(
            eye, near.reshape(-1, width).astype(BF), (((1,), (1,)), ((), ())), preferred_element_type=F32
        ).astype(BF)


def roll_cols(x, shift):
    return jnp.concatenate([x[:, x.shape[1] - shift :], x[:, : x.shape[1] - shift]], axis=1)


def tap_grads(pos_ref, place_ref, d0, d1, d2, d3, xt_ref, xe_ref, keep_ref, send_ref, held, padded, edge, buf):
    side = RATE_C
    pixels, width = d0.shape
    cols = 24
    rows = pixels // cols
    for k, d in enumerate((d0, d1, d2, d3)):
        s = jnp.bitwise_xor(pos_ref[0], k)
        held[s % 2, pl.ds((s // 2) * pixels, pixels), :] = d[...]
    buf[...] = jnp.zeros_like(buf)
    tall = 2 * pixels
    lead = side * cols
    zeros = jnp.zeros((2, lead, width), BF)
    halves = [held[g].astype(F32).reshape(2 * rows, cols, width) for g in range(2)]
    at = lax.broadcasted_iota(jnp.int32, (2 * rows, cols, width), 1)
    rest = cols - side
    for across in (0, 1, -1):
        turn = across + 1
        padded[turn, :, pl.ds(0, lead), :] = zeros
        padded[turn, :, pl.ds(lead + tall, lead), :] = zeros
        if across == 0:
            shifted = halves
        elif across == 1:
            rolled = [roll_cols(h, side) for h in halves]
            shifted = [
                jnp.where(at >= side, rolled[0], 0.0),
                jnp.where(at < side, rolled[0], rolled[1]),
            ]
        else:
            rolled = [roll_cols(h, rest) for h in halves]
            shifted = [
                jnp.where(at < rest, rolled[0], rolled[1]),
                jnp.where(at < rest, rolled[1], 0.0),
            ]
        thin = {1: 0, -1: 1}.get(across)
        for g in range(2):
            if g == thin:
                near = shifted[g][:, SIDE - EDGE :] if g == 0 else shifted[g][:, :EDGE]
                short = side * EDGE
                edge[g, pl.ds(0, short), :] = jnp.zeros((short, width), BF)
                edge[g, pl.ds(short, 2 * rows * EDGE), :] = near.reshape(2 * rows * EDGE, width).astype(BF)
                edge[g, pl.ds(short + 2 * rows * EDGE, short), :] = jnp.zeros((short, width), BF)
            else:
                padded[turn, g, pl.ds(lead, tall), :] = shifted[g].reshape(tall, width).astype(BF)
        for above in (-1, 0, 1):
            first, last = {-1: (0, 32), 0: (0, 48), 1: (16, 48)}[above]
            base = first - side * above + side
            total = None
            for g in range(2):
                left, right, each = (xe_ref, edge.at[g], EDGE) if g == thin else (xt_ref, padded.at[turn, g], cols)
                part = jnp.dot(
                    left[g, :, first * each : last * each],
                    right[base * each : (base + last - first) * each, :],
                    preferred_element_type=F32,
                )
                total = part if total is None else total + part
            tap = 3 * (above + 1) + across + 1
            groups = total.reshape(width // 16, 16, width)
            for m in range(width // 16):
                buf[place_ref[32 + 16 * tap + m]] = groups[m]
    half = buf.shape[0] // 2
    keep_ref[...] = buf[:half]
    send_ref[...] = buf[half:].astype(BF)


def join_owners(pos_ref, place_ref, keep_ref, got_ref, mine_ref, other_ref, o_ref, total):
    total[...] = keep_ref[...] + got_ref[...].astype(F32)
    core = pos_ref[4]
    for n in range(mine_ref.shape[0]):
        for ref, first in ((mine_ref, 16 * core), (other_ref, 16 * (1 - core))):
            at = place_ref[first + n]

            @pl.when(at < total.shape[0])
            def _(ref=ref, at=at, n=n):
                total[at] = ref[n].astype(F32)

    o_ref[...] = total[...].astype(BF).reshape(o_ref.shape)


def fold_last(r_ref, o_ref, total):
    value = r_ref[0].astype(F32)
    for n in range(1, r_ref.shape[0]):
        value = value + r_ref[n].astype(F32)
    total[...] = value.reshape(total.shape)
    width = total.shape[2]
    for i in range(total.shape[1]):
        o_ref[:, i * width : (i + 1) * width] = total[:, i, :]


def share_rows(pos_ref, kept_ref, got0, got1, *rest):
    *outs, total = rest
    half, each = got0.shape[0], total.shape[0] // 2
    for n, got in enumerate((got0, got1)):
        value = kept_ref[n * half : (n + 1) * half, :] + got[...].astype(F32)
        total[n * each : (n + 1) * each] = value.reshape(each, *total.shape[1:])
    for k, out in enumerate(outs):
        out[...] = total[:, jnp.bitwise_xor(pos_ref[0], k)].astype(out.dtype)


def swap_core(x):
    return lax.ppermute(x, "dp_2", [(0, 1), (1, 0)])


def pick(pos, centre):
    pixels, chans = centre.shape
    block = jax.ShapeDtypeStruct((pixels, chans // 4), BF)
    return call(
        select_channels,
        [jax.ShapeDtypeStruct((pixels, chans), BF)] + [block] * 3,
        1,
        0,
        pixels * chans * chans,
        4 * pixels * chans,
        12,
        [pltpu.SemaphoreType.DMA((3,))],
        name="pick",
        n_any=1,
    )(pos, pltpu.with_memory_space_constraint(centre, pltpu.HBM))


def turn(pos, centre, got):
    pixels, width = got[0].shape
    return call(
        turn_pixels,
        [
            jax.ShapeDtypeStruct((2, width, 2 * pixels), BF),
            jax.ShapeDtypeStruct((2, width, 2 * pixels // SIDE * EDGE), BF),
        ],
        1,
        4,
        8 * pixels * width * width,
        16 * pixels * width,
        12,
        [pltpu.VMEM((2, 2 * pixels, width), BF)],
        name="turn",
    )(pos, centre, *got)


def split_pair(pos, kept, got):
    width = kept.shape[1]
    slices = kept.shape[0] // 64
    shape = (slices, 16, width)
    return call(
        share_rows,
        [jax.ShapeDtypeStruct(shape, F32)] + [jax.ShapeDtypeStruct(shape, BF)] * 3,
        1,
        3,
        0,
        0,
        10,
        [pltpu.VMEM((slices, 4, 16, width), F32)],
        name="rows",
    )(pos, kept, *got)


def sum_pair(blocks):
    mine = blocks[0] + sum(block.astype(F32) for block in blocks[1:])
    return mine, swap_core(mine.astype(BF))


def place_slots(bucket_slot, core, slot_count):
    replicas = lax.axis_size(DP)
    capacity = slot_count // replicas
    owner = bucket_slot // capacity
    other = jnp.bitwise_xor(owner % 2, core)
    return other * (slot_count // 2) + (owner // 2) * capacity + bucket_slot % capacity


def tap_slots(pos, place, deltas, turned, slot_count):
    pixels, width = deltas[0].shape
    half = slot_count // 2
    return call(
        tap_grads,
        [jax.ShapeDtypeStruct((half, 16, width), F32), jax.ShapeDtypeStruct((half, 16, width), BF)],
        2,
        6,
        2 * 7 * 4 * pixels * width * width,
        8 * 1024 * 1024,
        26,
        [
            pltpu.VMEM((2, 2 * pixels, width), BF),
            pltpu.VMEM((3, 2, 2 * pixels + 2 * RATE_C * SIDE, width), BF),
            pltpu.VMEM((2, (2 * SIDE + 2 * RATE_C) * EDGE, width), BF),
            pltpu.VMEM((slot_count, 16, width), F32),
        ],
        name="taps",
    )(pos, place, *deltas, *turned)


def reduce_slots(pos, place, kept, sent, mine, other):
    half, rows, width = kept.shape
    chips = lax.axis_size("dp_0") * lax.axis_size("dp_1")
    each = half // chips
    total = call(
        join_owners,
        jax.ShapeDtypeStruct((chips, each * rows, width), BF),
        2,
        4,
        kept.size,
        8 * kept.size,
        12,
        [pltpu.VMEM((half, rows, width), F32)],
        name="owners",
    )(pos, place, kept, swap_core(sent), mine, other)
    total = lax.all_to_all(total, ("dp_0", "dp_1"), 0, 0, tiled=True)
    return call(
        fold_last,
        jax.ShapeDtypeStruct((each, rows * width), F32),
        0,
        1,
        kept.size,
        2 * kept.size,
        8,
        [pltpu.VMEM((each, rows, width), F32)],
        name="last",
    )(total)


def sigmoid(value):
    return 0.5 + 0.5 * jnp.tanh(0.5 * value)


def silu_slope(value):
    sig = sigmoid(value)
    return sig * (1.0 + value * (1.0 - sig))


RATES = (RATE_A, RATE_B, RATE_C)
SIDE = 24


def turned_by(x, shift, far):
    return jnp.where(far == 0, roll_cols(x, shift), roll_cols(x, SIDE - shift))


def rank_of(shape, far):
    at = lax.broadcasted_iota(jnp.int32, shape, 1)
    return jnp.where(far == 0, at, SIDE - 1 - at)


def row_marks(low, rate):
    lead = rate * SIDE
    whole = SIDE * SIDE

    def either(upper, lower):
        return pl.multiple_of(jnp.where(low == 0, upper, lower), 16)

    return dict(
        own=either(0, lead),
        out=either(lead, 0),
        theirs=either(whole, 0),
        inward_from=either(lead, 0),
        inward=either(0, 2 * lead),
        kept=either(lead, 0),
        inner=either(0, lead),
    )


def blocks(x):
    return x.reshape(x.shape[0] // SIDE, SIDE, x.shape[1])


def flat(x):
    return x.reshape(x.shape[0] * SIDE, x.shape[2])


def tap_copies(pos_ref, refs, jobs, held, sems):
    copies = []
    for branch, ref in enumerate(refs):
        for n, (above, across) in enumerate(jobs):
            a = 1 if above == 1 else jnp.where(pos_ref[2] == 0, above, 2 - above)
            b = 1 if across == 1 else jnp.where(pos_ref[3] == 0, across, 2 - across)
            width = ref.shape[3]
            to = held.at[branch, :, n * width : (n + 1) * width]
            copies.append(pltpu.make_async_copy(ref.at[a, b], to, sems.at[branch, n]))
    return copies


BRANCHES = ((2, RATE_C), (1, RATE_B), (0, RATE_A))
OUTER = ((0, 0), (1, 0), (0, 1), (0, 2), (2, 0))
INNER = ((1, 1), (1, 2), (2, 1), (2, 2))


def outer_parts(pos_ref, x_ref, wc_ref, wb_ref, wa_ref, pre_ref, row_ref, col_ref, diag_ref, ext, acc, y, held, sems):
    low, far = pos_ref[2], pos_ref[3]
    whole = SIDE * SIDE
    width = pre_ref.shape[2]
    copies = tap_copies(pos_ref, (wc_ref, wb_ref, wa_ref), OUTER, held, sems)
    for copy in copies:
        copy.start()
    first = 0
    for turn, (index, rate) in enumerate(BRANCHES):
        lead = rate * SIDE
        inside = whole - lead
        at = row_marks(low, rate)
        own_rows = pl.ds(at["own"], whole)
        their_rows = pl.ds(at["theirs"], lead)
        kept_rows = pl.ds(at["kept"], inside)
        to_row = slice(first, first + lead)
        first += lead
        count = len(OUTER)
        for copy in copies[turn * count : (turn + 1) * count]:
            copy.wait()
        y[...] = jnp.dot(x_ref[...], held[turn, :, : 4 * width], preferred_element_type=F32)
        ext[pl.ds(pl.multiple_of(whole - at["theirs"], 16), lead), :] = jnp.zeros((lead, width), F32)
        ext[pl.ds(at["out"], whole), :] = y[:, :width]
        ext[own_rows, :] += y[:, width : 2 * width]
        ext[pl.ds(at["inward"], inside), :] += jnp.dot(
            x_ref[pl.ds(at["inward_from"], inside), :], held[turn, :, 4 * width :], preferred_element_type=F32
        )
        own = blocks(ext[own_rows, :])
        ours = turned_by(own, rate, far)
        rank = rank_of(own.shape, far)
        pre_ref[index] = flat(jnp.where(rank >= rate, ours, 0.0))
        below = blocks(ext[their_rows, :])
        theirs = turned_by(below, rate, far)
        place = rank_of(below.shape, far)
        acc[:lead, :] = flat(jnp.where(place >= rate, theirs, 0.0))
        if rate == RATE_C:
            col_ref[:whole, :] = flat(jnp.where(rank < rate, ours, 0.0)).astype(BF)
            diag_ref[:lead, :] = flat(jnp.where(place < rate, theirs, 0.0)).astype(BF)
        elif rate == RATE_B:
            half = rate // 2
            col_ref[whole:, :] = flat(jnp.where(rank[:rate] < rate, ours[:rate], own[rate:])).astype(BF)
            part = place[:half] < rate
            diag_ref[RATE_C * SIDE :, :] = flat(jnp.where(part, theirs[:half], below[half:])).astype(BF)
        else:
            have = blocks(col_ref[:whole, :].astype(F32))
            col_ref[:whole, :] = flat(jnp.where(rank >= RATE_C, own, have)).astype(BF)
            have = blocks(diag_ref[:lead, :].astype(F32))
            diag_ref[:lead, :] = flat(jnp.where(place >= RATE_C, below, have)).astype(BF)
        next_from = pl.multiple_of(jnp.where(low == 0, inside, 0), 16)
        keep_from = pl.multiple_of(jnp.where(low == 0, 0, lead), 16)
        pre_ref[index, kept_rows, :] += y[pl.ds(keep_from, inside), 2 * width : 3 * width]
        own = blocks(y[pl.ds(keep_from, inside), 3 * width :])
        rank = rank_of(own.shape, far)
        pre_ref[index, kept_rows, :] += flat(jnp.where(rank < SIDE - rate, turned_by(own, rate, 1 - far), 0.0))
        below = blocks(y[pl.ds(next_from, lead), 3 * width :])
        theirs = flat(jnp.where(place < SIDE - rate, turned_by(below, rate, 1 - far), 0.0))
        row_ref[to_row, :] = (acc[:lead, :] + y[pl.ds(next_from, lead), 2 * width : 3 * width] + theirs).astype(BF)


def inner_parts(pos_ref, x_ref, part_ref, wp_ref, wc_ref, wb_ref, wa_ref, joined_ref, slope_ref, pre_ref, y, z, held, sems):
    low, far = pos_ref[2], pos_ref[3]
    whole = SIDE * SIDE
    width = joined_ref.shape[1]
    copies = tap_copies(pos_ref, (wc_ref, wb_ref, wa_ref), INNER, held, sems)
    for copy in copies:
        copy.start()
    value = jnp.dot(x_ref[...], wp_ref[...], preferred_element_type=F32)
    sig = sigmoid(value)
    joined_ref[...] = (value * sig).astype(BF)
    slope_ref[...] = sig * (1.0 + value * (1.0 - sig))
    for turn, (index, rate) in enumerate(BRANCHES):
        lead = rate * SIDE
        inside = whole - lead
        at = row_marks(low, rate)
        from_rows = pl.ds(at["inward_from"], inside)
        to_rows = pl.ds(at["inner"], inside)
        count = len(INNER)
        for copy in copies[turn * count : (turn + 1) * count]:
            copy.wait()
        y[...] = jnp.dot(x_ref[...], held[turn, :, : 2 * width], preferred_element_type=F32)
        z[:inside, :] = jnp.dot(x_ref[from_rows, :], held[turn, :, 2 * width :], preferred_element_type=F32)
        y[to_rows, :] += z[:inside, :]
        own = blocks(y[:, width:])
        rank = rank_of(own.shape, far)
        moved = flat(jnp.where(rank < SIDE - rate, turned_by(own, rate, 1 - far), 0.0))
        pre_ref[index] = part_ref[index] + y[:, :width] + moved


def outer(pos, centre, w_rate_a, w_rate_b, w_rate_c):
    pixels, chans = centre.shape
    width = w_rate_a.shape[3]
    sends = (RATE_A + RATE_B + RATE_C) * SIDE
    shapes = [((3, pixels, width), F32), ((sends, width), BF), ((sends, width), BF), ((pixels, width), BF)]
    return call(
        outer_parts,
        [jax.ShapeDtypeStruct(*s) for s in shapes],
        1,
        1,
        2 * pixels * chans * width * 14,
        10 * MIB,
        28,
        [
            pltpu.VMEM(((SIDE + RATE_C) * SIDE, width), F32),
            pltpu.VMEM((RATE_C * SIDE, width), F32),
            pltpu.VMEM((pixels, 4 * width), F32),
            pltpu.VMEM((3, chans, len(OUTER) * width), BF),
            pltpu.SemaphoreType.DMA((3, len(OUTER))),
        ],
        name="outer",
        n_any=3,
    )(pos, centre, w_rate_c, w_rate_b, w_rate_a)


def inner(pos, centre, part, w_point, w_rate_a, w_rate_b, w_rate_c):
    pixels, chans = centre.shape
    width = w_point.shape[1]
    return call(
        inner_parts,
        [
            jax.ShapeDtypeStruct((pixels, width), BF),
            jax.ShapeDtypeStruct((pixels, width), F32),
            jax.ShapeDtypeStruct((3, pixels, width), F32),
        ],
        1,
        3,
        2 * pixels * chans * width * 10,
        10 * MIB,
        26,
        [
            pltpu.VMEM((pixels, 2 * width), F32),
            pltpu.VMEM((pixels, 2 * width), F32),
            pltpu.VMEM((3, chans, len(INNER) * width), BF),
            pltpu.SemaphoreType.DMA((3, len(INNER))),
        ],
        name="inner",
        n_any=3,
    )(pos, centre, part, w_point, w_rate_c, w_rate_b, w_rate_a)


def merge_parts(
    pos_ref, joined0_ref, own_ref, row_ref, col_ref, diag_ref, cot_ref, wp_ref, joined_ref, g_ref, d3_ref, pre
):
    low = pos_ref[2]
    theirs = 1 - pos_ref[3]
    width = joined0_ref.shape[1]
    whole = SIDE * SIDE

    def rows_of(rate):
        return pl.multiple_of(jnp.where(low == 0, (SIDE - rate) * SIDE, 0), 16)

    part = blocks(col_ref[:whole, :].astype(F32))
    rank = rank_of(part.shape, theirs)
    pre[2] = own_ref[2] + flat(jnp.where(rank < RATE_C, part, 0.0))
    pre[0] = own_ref[0] + flat(turned_by(jnp.where(rank >= RATE_C, part, 0.0), RATE_A, theirs))
    part = blocks(col_ref[whole:, :].astype(F32))
    rank = rank_of(part.shape, theirs)
    half = RATE_B * SIDE
    pre[1, :half, :] = own_ref[1, :half, :] + flat(jnp.where(rank < RATE_B, part, 0.0))
    pre[1, half:, :] = own_ref[1, half:, :] + flat(roll_cols(jnp.where(rank >= RATE_B, part, 0.0), RATE_B))
    first = 0
    for index, rate in ((2, RATE_C), (1, RATE_B), (0, RATE_A)):
        lead = rate * SIDE
        pre[index, pl.ds(rows_of(rate), lead), :] += row_ref[first : first + lead, :].astype(F32)
        first += lead

    part = blocks(diag_ref[: RATE_C * SIDE, :].astype(F32))
    rank = rank_of(part.shape, theirs)
    pre[2, pl.ds(rows_of(RATE_C), RATE_C * SIDE), :] += flat(jnp.where(rank < RATE_C, part, 0.0))
    few = part[:RATE_A]
    few = turned_by(jnp.where(rank[:RATE_A] >= RATE_C, few, 0.0), RATE_A, theirs)
    pre[0, pl.ds(rows_of(RATE_A), RATE_A * SIDE), :] += flat(few)
    part = blocks(diag_ref[RATE_C * SIDE :, :].astype(F32))
    rank = rank_of(part.shape, theirs)
    half = RATE_B // 2
    at = rows_of(RATE_B)
    pre[1, pl.ds(at, half * SIDE), :] += flat(jnp.where(rank < RATE_B, part, 0.0))
    last = pl.multiple_of(at + half * SIDE, 16)
    pre[1, pl.ds(last, half * SIDE), :] += flat(roll_cols(jnp.where(rank >= RATE_B, part, 0.0), RATE_B))

    joined_ref[:, :width] = joined0_ref[...]
    for k in range(1, 4):
        value = pre[k - 1]
        sig = sigmoid(value)
        joined_ref[:, k * width : (k + 1) * width] = (value * sig).astype(BF)
    slope = sig * (1.0 + value * (1.0 - sig))
    proj_pre = jnp.dot(joined_ref[...], wp_ref[...], preferred_element_type=F32)
    g_proj = (cot_ref[...].astype(F32) * silu_slope(proj_pre)).astype(BF)
    g_ref[...] = g_proj
    d3_ref[...] = (back_through(g_proj, wp_ref, 3) * slope).astype(BF)


def back_through(g_proj, wp_ref, k):
    width = g_proj.shape[1]
    return lax.dot_general(
        g_proj, wp_ref[k * width : (k + 1) * width, :], (((1,), (1,)), ((), ())), preferred_element_type=F32
    )


def merge(pos, joined0, own, row, col, diag, cot, w_proj):
    pixels, width = joined0.shape
    block = jax.ShapeDtypeStruct((pixels, width), BF)
    return call(
        merge_parts,
        [jax.ShapeDtypeStruct((pixels, 4 * width), BF), block, block],
        1,
        7,
        2 * pixels * width * width * 6,
        6 * 1024 * 1024,
        18,
        [pltpu.VMEM((3, pixels, width), F32)],
        name="merge",
    )(pos, joined0, own, row, col, diag, cot, w_proj)


def pair_grads(pos_ref, joined_ref, g_ref, x_ref, slope_ref, wp_ref, keep_ref, *send_refs):
    core = pos_ref[4]
    over = (((0,), (0,)), ((), ()))
    grad_proj = lax.dot_general(joined_ref[...], g_ref[...], over, preferred_element_type=F32)
    delta = (back_through(g_ref[...], wp_ref, 0) * slope_ref[...]).astype(BF)
    grad_point = lax.dot_general(x_ref[...], delta, over, preferred_element_type=F32)
    keep_ref[...] = jnp.where(core == 0, grad_proj, grad_point)
    half = send_refs[0].shape[0]
    for k, send_ref in enumerate(send_refs):
        part = slice(k * half, (k + 1) * half)
        send_ref[...] = jnp.where(core == 0, grad_point[part], grad_proj[part]).astype(BF)


def shards(features, cotangent, w_point, w_rate_a, w_rate_b, w_rate_c, w_proj, bucket_slot):
    image = features[0]
    rows_dev, cols_dev, chans = image.shape
    pixels = rows_dev * cols_dev
    width = w_point.shape[1]
    row, col, core = (lax.axis_index(n) for n in ("row", "col", "dp_2"))
    at_y, at_z = lax.axis_index("dp_0"), lax.axis_index("dp_1")
    pos = jnp.stack([2 * row + col, at_y, row, col, core, at_z]).astype(jnp.int32)
    replicas = lax.axis_size(DP)
    slot_count = replicas * (bucket_slot.shape[0] // replicas + 1)
    place = place_slots(bucket_slot, core, slot_count)
    centre = image.reshape(pixels, chans)
    weights = [pltpu.with_memory_space_constraint(w, pltpu.HBM) for w in (w_rate_a, w_rate_b, w_rate_c)]
    centre, *picked = pick(pos, centre)
    got = [flip(picked[k - 1], k) for k in (1, 2, 3)]
    part, *parts = outer(pos, centre, *weights)
    part, got = lax.optimization_barrier((part, got))
    to_row, to_col, to_diag = parts
    parts = [flip(to_row, 2), flip(to_col, 1), flip(to_diag, 3)]
    turned = turn(pos, centre, got)
    joined0, slope0, own = inner(pos, centre, part, w_point, *weights)
    parts, joined0, own, turned = lax.optimization_barrier((parts, joined0, own, turned))
    joined, g_proj, delta3 = merge(
        pos, joined0, own, *parts, cotangent[0].reshape(pixels, width), w_proj
    )
    shared = [delta3] + [flip(delta3, k) for k in (1, 2, 3)]
    block = (4 * width, width)
    kept, *sent = call(
        pair_grads,
        [jax.ShapeDtypeStruct(block, F32)] + [jax.ShapeDtypeStruct((2 * width, width), BF)] * 2,
        1,
        5,
        4 * pixels * chans * width,
        4 * 1024 * 1024,
        16,
        name="pair",
    )(pos, joined, g_proj, centre, slope0, w_proj)
    got = [swap_core(part) for part in sent]
    by_owner = split_pair(pos, kept, got)
    by_owner, shared = lax.optimization_barrier((by_owner, shared))
    by_owner = [by_owner[0]] + [flip(by_owner[k], k) for k in (1, 2, 3)]
    kept, sent = tap_slots(pos, place, shared, turned, slot_count)
    sent, by_owner = lax.optimization_barrier((sent, by_owner))
    mine, other = sum_pair(by_owner)
    return reduce_slots(pos, place, kept, sent, mine, other)


def solution(mesh):
    torus = Mesh(
        mesh.devices.reshape(mesh.shape["row"], mesh.shape["col"], 4, 4, 2),
        ("row", "col", "dp_0", "dp_1", "dp_2"),
    )
    in_specs = (P(DP, "row", "col", None), P(DP, "row", "col", None), P(), P(), P(), P(), P(), P())
    out_specs = P(DP, ("row", "col"))
    return jax.shard_map(
        shards, mesh=torus, in_specs=in_specs, out_specs=out_specs, check_vma=False
    )
```

```python
import jax
import jax.numpy as jnp
from jax import lax
from jax.experimental import pallas as pl
from jax.experimental.pallas import tpu as pltpu
from jax.sharding import Mesh
from jax.sharding import PartitionSpec as P

RATE_A = 6
RATE_B = 12
RATE_C = 18
DP = ("dp_0", "dp_1", "dp_2")


BF = jnp.bfloat16
F32 = jnp.float32
MIB = 1024 * 1024
EDGE = 8


def flip(x, mask):
    if mask == 1:
        return lax.ppermute(x, "col", [(0, 1), (1, 0)])
    if mask == 2:
        return lax.ppermute(x, "row", [(0, 1), (1, 0)])
    return lax.ppermute(x, ("row", "col"), [(0, 3), (3, 0), (1, 2), (2, 1)])


def smem():
    return pl.BlockSpec(memory_space=pltpu.SMEM)


def vmem():
    return pl.BlockSpec(memory_space=pltpu.VMEM)


def call(body, outs, n_smem, n_vmem, flops, nbytes, limit, scratch=(), name=None, n_any=0):
    return pl.pallas_call(
        body,
        out_shape=outs,
        in_specs=[smem()] * n_smem + [vmem()] * n_vmem + [pl.BlockSpec(memory_space=pltpu.HBM)] * n_any,
        out_specs=jax.tree.map(lambda _: vmem(), outs),
        scratch_shapes=list(scratch),
        compiler_params=pltpu.CompilerParams(vmem_limit_bytes=limit * MIB),
        cost_estimate=pl.CostEstimate(flops=flops, bytes_accessed=nbytes, transcendentals=0),
        name=name,
    )


def select_channels(pos_ref, x_ref, *rest):
    *o_refs, held, sems = rest
    lanes = 128
    group = lanes * len(o_refs)
    pieces = sems.shape[0]
    each = x_ref.shape[0] // pieces
    copies = []
    for n in range(pieces):
        part = pl.ds(n * each, each)
        copies.append(pltpu.make_async_copy(x_ref.at[part, :], held.at[part, :], sems.at[n]))
        copies[n].start()
    source = lax.broadcasted_iota(jnp.int32, (group, group), 0)
    col = lax.broadcasted_iota(jnp.int32, (1, group), 1)
    owner = jnp.bitwise_xor(pos_ref[0], col // lanes)
    wanted = 64 * ((col % lanes) // 16) + 16 * owner + col % 16
    picks = jnp.where(source == wanted, 1.0, 0.0).astype(BF)
    for n in range(pieces):
        copies[n].wait()
        rows = slice(n * each, (n + 1) * each)
        for p in range(x_ref.shape[1] // group):
            taken = jnp.dot(held[rows, p * group : (p + 1) * group], picks, preferred_element_type=F32).astype(BF)
            for k, o_ref in enumerate(o_refs):
                o_ref[rows, p * lanes : (p + 1) * lanes] = taken[:, k * lanes : (k + 1) * lanes]


def turn_pixels(pos_ref, x0, x1, x2, x3, o_ref, edge_ref, held):
    pixels, width = x0.shape
    for k, x in enumerate((x0, x1, x2, x3)):
        s = jnp.bitwise_xor(pos_ref[0], k)
        held[s % 2, pl.ds((s // 2) * pixels, pixels), :] = x[...]
    eye = (
        lax.broadcasted_iota(jnp.int32, (width, width), 0)
        == lax.broadcasted_iota(jnp.int32, (width, width), 1)
    ).astype(F32).astype(BF)
    for g in range(2):
        o_ref[g] = lax.dot_general(
            eye, held[g], (((1,), (1,)), ((), ())), preferred_element_type=F32
        ).astype(BF)
        wide = held[g].astype(F32).reshape(-1, SIDE, width)
        near = wide[:, SIDE - EDGE :] if g == 0 else wide[:, :EDGE]
        edge_ref[g] = lax.dot_general(
            eye, near.reshape(-1, width).astype(BF), (((1,), (1,)), ((), ())), preferred_element_type=F32
        ).astype(BF)


def roll_cols(x, shift):
    return jnp.concatenate([x[:, x.shape[1] - shift :], x[:, : x.shape[1] - shift]], axis=1)


def tap_grads(pos_ref, place_ref, d0, d1, d2, d3, xt_ref, xe_ref, keep_ref, send_ref, held, padded, edge, buf):
    side = RATE_C
    pixels, width = d0.shape
    cols = 24
    rows = pixels // cols
    for k, d in enumerate((d0, d1, d2, d3)):
        s = jnp.bitwise_xor(pos_ref[0], k)
        held[s % 2, pl.ds((s // 2) * pixels, pixels), :] = d[...]
    buf[...] = jnp.zeros_like(buf)
    tall = 2 * pixels
    lead = side * cols
    zeros = jnp.zeros((2, lead, width), BF)
    halves = [held[g].astype(F32).reshape(2 * rows, cols, width) for g in range(2)]
    at = lax.broadcasted_iota(jnp.int32, (2 * rows, cols, width), 1)
    rest = cols - side
    for across in (0, 1, -1):
        turn = across + 1
        padded[turn, :, pl.ds(0, lead), :] = zeros
        padded[turn, :, pl.ds(lead + tall, lead), :] = zeros
        if across == 0:
            shifted = halves
        elif across == 1:
            rolled = [roll_cols(h, side) for h in halves]
            shifted = [
                jnp.where(at >= side, rolled[0], 0.0),
                jnp.where(at < side, rolled[0], rolled[1]),
            ]
        else:
            rolled = [roll_cols(h, rest) for h in halves]
            shifted = [
                jnp.where(at < rest, rolled[0], rolled[1]),
                jnp.where(at < rest, rolled[1], 0.0),
            ]
        thin = {1: 0, -1: 1}.get(across)
        for g in range(2):
            if g == thin:
                near = shifted[g][:, SIDE - EDGE :] if g == 0 else shifted[g][:, :EDGE]
                short = side * EDGE
                edge[g, pl.ds(0, short), :] = jnp.zeros((short, width), BF)
                edge[g, pl.ds(short, 2 * rows * EDGE), :] = near.reshape(2 * rows * EDGE, width).astype(BF)
                edge[g, pl.ds(short + 2 * rows * EDGE, short), :] = jnp.zeros((short, width), BF)
            else:
                padded[turn, g, pl.ds(lead, tall), :] = shifted[g].reshape(tall, width).astype(BF)
        for above in (-1, 0, 1):
            first, last = {-1: (0, 32), 0: (0, 48), 1: (16, 48)}[above]
            base = first - side * above + side
            total = None
            for g in range(2):
                left, right, each = (xe_ref, edge.at[g], EDGE) if g == thin else (xt_ref, padded.at[turn, g], cols)
                part = jnp.dot(
                    left[g, :, first * each : last * each],
                    right[base * each : (base + last - first) * each, :],
                    preferred_element_type=F32,
                )
                total = part if total is None else total + part
            tap = 3 * (above + 1) + across + 1
            groups = total.reshape(width // 16, 16, width)
            for m in range(width // 16):
                buf[place_ref[32 + 16 * tap + m]] = groups[m]
    half = buf.shape[0] // 2
    keep_ref[...] = buf[:half]
    send_ref[...] = buf[half:].astype(BF)


def join_owners(pos_ref, place_ref, keep_ref, got_ref, mine_ref, other_ref, o_ref):
    o_ref[...] = (keep_ref[...] + got_ref[...].astype(F32)).astype(BF).reshape(o_ref.shape)
    each = o_ref.shape[1] // 16
    core = pos_ref[4]
    for n in range(mine_ref.shape[0]):
        for ref, first in ((mine_ref, 16 * core), (other_ref, 16 * (1 - core))):
            at = place_ref[first + n]

            @pl.when(at < o_ref.shape[0] * each)
            def _(ref=ref, at=at, n=n):
                rows = pl.ds(pl.multiple_of((at % each) * 16, 16), 16)
                o_ref[at // each, rows, :] = ref[n].astype(BF)


def fold_last(r_ref, o_ref, total):
    value = r_ref[0].astype(F32)
    for n in range(1, r_ref.shape[0]):
        value = value + r_ref[n].astype(F32)
    total[...] = value.reshape(total.shape)
    width = total.shape[2]
    for i in range(total.shape[1]):
        o_ref[:, i * width : (i + 1) * width] = total[:, i, :]


def share_rows(pos_ref, kept_ref, got0, got1, *rest):
    *outs, total = rest
    half, each = got0.shape[0], total.shape[0] // 2
    for n, got in enumerate((got0, got1)):
        value = kept_ref[n * half : (n + 1) * half, :] + got[...].astype(F32)
        total[n * each : (n + 1) * each] = value.reshape(each, *total.shape[1:])
    for k, out in enumerate(outs):
        out[...] = total[:, jnp.bitwise_xor(pos_ref[0], k)].astype(out.dtype)


def swap_core(x):
    return lax.ppermute(x, "dp_2", [(0, 1), (1, 0)])


def pick(pos, centre):
    pixels, chans = centre.shape
    block = jax.ShapeDtypeStruct((pixels, chans // 4), BF)
    return call(
        select_channels,
        [block] * 4,
        1,
        0,
        pixels * chans * chans,
        4 * pixels * chans,
        12,
        [pltpu.VMEM((pixels, chans), BF), pltpu.SemaphoreType.DMA((2,))],
        name="pick",
        n_any=1,
    )(pos, pltpu.with_memory_space_constraint(centre, pltpu.HBM))


def turn(pos, got):
    pixels, width = got[0].shape
    return call(
        turn_pixels,
        [
            jax.ShapeDtypeStruct((2, width, 2 * pixels), BF),
            jax.ShapeDtypeStruct((2, width, 2 * pixels // SIDE * EDGE), BF),
        ],
        1,
        4,
        8 * pixels * width * width,
        16 * pixels * width,
        12,
        [pltpu.VMEM((2, 2 * pixels, width), BF)],
        name="turn",
    )(pos, *got)


def split_pair(pos, kept, got):
    width = kept.shape[1]
    slices = kept.shape[0] // 64
    shape = (slices, 16, width)
    return call(
        share_rows,
        [jax.ShapeDtypeStruct(shape, F32)] + [jax.ShapeDtypeStruct(shape, BF)] * 3,
        1,
        3,
        0,
        0,
        10,
        [pltpu.VMEM((slices, 4, 16, width), F32)],
        name="rows",
    )(pos, kept, *got)


def sum_pair(blocks):
    mine = blocks[0] + sum(block.astype(F32) for block in blocks[1:])
    return mine, swap_core(mine.astype(BF))


def place_slots(bucket_slot, core, slot_count):
    replicas = lax.axis_size(DP)
    capacity = slot_count // replicas
    owner = bucket_slot // capacity
    other = jnp.bitwise_xor(owner % 2, core)
    return other * (slot_count // 2) + (owner // 2) * capacity + bucket_slot % capacity


def tap_slots(pos, place, deltas, turned, slot_count):
    pixels, width = deltas[0].shape
    half = slot_count // 2
    return call(
        tap_grads,
        [jax.ShapeDtypeStruct((half, 16, width), F32), jax.ShapeDtypeStruct((half, 16, width), BF)],
        2,
        6,
        2 * 7 * 4 * pixels * width * width,
        8 * 1024 * 1024,
        26,
        [
            pltpu.VMEM((2, 2 * pixels, width), BF),
            pltpu.VMEM((3, 2, 2 * pixels + 2 * RATE_C * SIDE, width), BF),
            pltpu.VMEM((2, (2 * SIDE + 2 * RATE_C) * EDGE, width), BF),
            pltpu.VMEM((slot_count, 16, width), F32),
        ],
        name="taps",
    )(pos, place, *deltas, *turned)


def reduce_slots(pos, place, kept, sent, mine, other):
    half, rows, width = kept.shape
    chips = lax.axis_size("dp_0") * lax.axis_size("dp_1")
    each = half // chips
    total = call(
        join_owners,
        jax.ShapeDtypeStruct((chips, each * rows, width), BF),
        2,
        4,
        kept.size,
        8 * kept.size,
        8,
        name="owners",
    )(pos, place, kept, swap_core(sent), mine, other)
    total = lax.all_to_all(total, ("dp_0", "dp_1"), 0, 0, tiled=True)
    return call(
        fold_last,
        jax.ShapeDtypeStruct((each, rows * width), F32),
        0,
        1,
        kept.size,
        2 * kept.size,
        8,
        [pltpu.VMEM((each, rows, width), F32)],
        name="last",
    )(total)


def sigmoid(value):
    return 0.5 + 0.5 * jnp.tanh(0.5 * value)


def silu_slope(value):
    sig = sigmoid(value)
    return sig * (1.0 + value * (1.0 - sig))


RATES = (RATE_A, RATE_B, RATE_C)
SIDE = 24


def turned_by(x, shift, far):
    return jnp.where(far == 0, roll_cols(x, shift), roll_cols(x, SIDE - shift))


def rank_of(shape, far):
    at = lax.broadcasted_iota(jnp.int32, shape, 1)
    return jnp.where(far == 0, at, SIDE - 1 - at)


def row_marks(low, rate):
    lead = rate * SIDE
    whole = SIDE * SIDE

    def either(upper, lower):
        return pl.multiple_of(jnp.where(low == 0, upper, lower), 16)

    return dict(
        own=either(0, lead),
        out=either(lead, 0),
        theirs=either(whole, 0),
        inward_from=either(lead, 0),
        inward=either(0, 2 * lead),
        kept=either(lead, 0),
        inner=either(0, lead),
    )


def blocks(x):
    return x.reshape(x.shape[0] // SIDE, SIDE, x.shape[1])


def flat(x):
    return x.reshape(x.shape[0] * SIDE, x.shape[2])


def tap_copies(pos_ref, refs, jobs, held, sems):
    copies = []
    for branch, ref in enumerate(refs):
        for n, (above, across) in enumerate(jobs):
            a = 1 if above == 1 else jnp.where(pos_ref[2] == 0, above, 2 - above)
            b = 1 if across == 1 else jnp.where(pos_ref[3] == 0, across, 2 - across)
            width = ref.shape[3]
            to = held.at[branch, :, n * width : (n + 1) * width]
            copies.append(pltpu.make_async_copy(ref.at[a, b], to, sems.at[branch, n]))
    return copies


BRANCHES = ((2, RATE_C), (1, RATE_B), (0, RATE_A))
OUTER = ((0, 0), (1, 0), (0, 1), (0, 2), (2, 0))
INNER = ((1, 1), (1, 2), (2, 1), (2, 2))


def outer_parts(pos_ref, x_ref, wc_ref, wb_ref, wa_ref, pre_ref, row_ref, col_ref, diag_ref, ext, acc, y, held, sems):
    low, far = pos_ref[2], pos_ref[3]
    whole = SIDE * SIDE
    width = pre_ref.shape[2]
    copies = tap_copies(pos_ref, (wc_ref, wb_ref, wa_ref), OUTER, held, sems)
    for copy in copies:
        copy.start()
    first = 0
    for turn, (index, rate) in enumerate(BRANCHES):
        lead = rate * SIDE
        inside = whole - lead
        at = row_marks(low, rate)
        own_rows = pl.ds(at["own"], whole)
        their_rows = pl.ds(at["theirs"], lead)
        kept_rows = pl.ds(at["kept"], inside)
        to_row = slice(first, first + lead)
        first += lead
        count = len(OUTER)
        for copy in copies[turn * count : (turn + 1) * count]:
            copy.wait()
        y[...] = jnp.dot(x_ref[...], held[turn, :, : 4 * width], preferred_element_type=F32)
        ext[pl.ds(pl.multiple_of(whole - at["theirs"], 16), lead), :] = jnp.zeros((lead, width), F32)
        ext[pl.ds(at["out"], whole), :] = y[:, :width]
        ext[own_rows, :] += y[:, width : 2 * width]
        ext[pl.ds(at["inward"], inside), :] += jnp.dot(
            x_ref[pl.ds(at["inward_from"], inside), :], held[turn, :, 4 * width :], preferred_element_type=F32
        )
        own = blocks(ext[own_rows, :])
        ours = turned_by(own, rate, far)
        rank = rank_of(own.shape, far)
        pre_ref[index] = flat(jnp.where(rank >= rate, ours, 0.0))
        below = blocks(ext[their_rows, :])
        theirs = turned_by(below, rate, far)
        place = rank_of(below.shape, far)
        acc[:lead, :] = flat(jnp.where(place >= rate, theirs, 0.0))
        if rate == RATE_C:
            col_ref[:whole, :] = flat(jnp.where(rank < rate, ours, 0.0)).astype(BF)
            diag_ref[:lead, :] = flat(jnp.where(place < rate, theirs, 0.0)).astype(BF)
        elif rate == RATE_B:
            half = rate // 2
            col_ref[whole:, :] = flat(jnp.where(rank[:rate] < rate, ours[:rate], own[rate:])).astype(BF)
            part = place[:half] < rate
            diag_ref[RATE_C * SIDE :, :] = flat(jnp.where(part, theirs[:half], below[half:])).astype(BF)
        else:
            have = blocks(col_ref[:whole, :].astype(F32))
            col_ref[:whole, :] = flat(jnp.where(rank >= RATE_C, own, have)).astype(BF)
            have = blocks(diag_ref[:lead, :].astype(F32))
            diag_ref[:lead, :] = flat(jnp.where(place >= RATE_C, below, have)).astype(BF)
        next_from = pl.multiple_of(jnp.where(low == 0, inside, 0), 16)
        keep_from = pl.multiple_of(jnp.where(low == 0, 0, lead), 16)
        pre_ref[index, kept_rows, :] += y[pl.ds(keep_from, inside), 2 * width : 3 * width]
        own = blocks(y[pl.ds(keep_from, inside), 3 * width :])
        rank = rank_of(own.shape, far)
        pre_ref[index, kept_rows, :] += flat(jnp.where(rank < SIDE - rate, turned_by(own, rate, 1 - far), 0.0))
        below = blocks(y[pl.ds(next_from, lead), 3 * width :])
        theirs = flat(jnp.where(place < SIDE - rate, turned_by(below, rate, 1 - far), 0.0))
        row_ref[to_row, :] = (acc[:lead, :] + y[pl.ds(next_from, lead), 2 * width : 3 * width] + theirs).astype(BF)


def inner_parts(pos_ref, x_ref, part_ref, wp_ref, wc_ref, wb_ref, wa_ref, joined_ref, slope_ref, pre_ref, y, z, held, sems):
    low, far = pos_ref[2], pos_ref[3]
    whole = SIDE * SIDE
    width = joined_ref.shape[1]
    copies = tap_copies(pos_ref, (wc_ref, wb_ref, wa_ref), INNER, held, sems)
    for copy in copies:
        copy.start()
    value = jnp.dot(x_ref[...], wp_ref[...], preferred_element_type=F32)
    sig = sigmoid(value)
    joined_ref[...] = (value * sig).astype(BF)
    slope_ref[...] = sig * (1.0 + value * (1.0 - sig))
    for turn, (index, rate) in enumerate(BRANCHES):
        lead = rate * SIDE
        inside = whole - lead
        at = row_marks(low, rate)
        from_rows = pl.ds(at["inward_from"], inside)
        to_rows = pl.ds(at["inner"], inside)
        count = len(INNER)
        for copy in copies[turn * count : (turn + 1) * count]:
            copy.wait()
        y[...] = jnp.dot(x_ref[...], held[turn, :, : 2 * width], preferred_element_type=F32)
        z[:inside, :] = jnp.dot(x_ref[from_rows, :], held[turn, :, 2 * width :], preferred_element_type=F32)
        y[to_rows, :] += z[:inside, :]
        own = blocks(y[:, width:])
        rank = rank_of(own.shape, far)
        moved = flat(jnp.where(rank < SIDE - rate, turned_by(own, rate, 1 - far), 0.0))
        pre_ref[index] = part_ref[index] + y[:, :width] + moved


def outer(pos, centre, w_rate_a, w_rate_b, w_rate_c):
    pixels, chans = centre.shape
    width = w_rate_a.shape[3]
    sends = (RATE_A + RATE_B + RATE_C) * SIDE
    shapes = [((3, pixels, width), F32), ((sends, width), BF), ((sends, width), BF), ((pixels, width), BF)]
    return call(
        outer_parts,
        [jax.ShapeDtypeStruct(*s) for s in shapes],
        1,
        1,
        2 * pixels * chans * width * 14,
        10 * MIB,
        28,
        [
            pltpu.VMEM(((SIDE + RATE_C) * SIDE, width), F32),
            pltpu.VMEM((RATE_C * SIDE, width), F32),
            pltpu.VMEM((pixels, 4 * width), F32),
            pltpu.VMEM((3, chans, len(OUTER) * width), BF),
            pltpu.SemaphoreType.DMA((3, len(OUTER))),
        ],
        name="outer",
        n_any=3,
    )(pos, centre, w_rate_c, w_rate_b, w_rate_a)


def inner(pos, centre, part, w_point, w_rate_a, w_rate_b, w_rate_c):
    pixels, chans = centre.shape
    width = w_point.shape[1]
    return call(
        inner_parts,
        [
            jax.ShapeDtypeStruct((pixels, width), BF),
            jax.ShapeDtypeStruct((pixels, width), F32),
            jax.ShapeDtypeStruct((3, pixels, width), F32),
        ],
        1,
        3,
        2 * pixels * chans * width * 10,
        10 * MIB,
        26,
        [
            pltpu.VMEM((pixels, 2 * width), F32),
            pltpu.VMEM((pixels, 2 * width), F32),
            pltpu.VMEM((3, chans, len(INNER) * width), BF),
            pltpu.SemaphoreType.DMA((3, len(INNER))),
        ],
        name="inner",
        n_any=3,
    )(pos, centre, part, w_point, w_rate_c, w_rate_b, w_rate_a)


def merge_parts(
    pos_ref, joined0_ref, own_ref, row_ref, col_ref, diag_ref, cot_ref, wp_ref, joined_ref, g_ref, d3_ref, pre
):
    low = pos_ref[2]
    theirs = 1 - pos_ref[3]
    width = joined0_ref.shape[1]
    whole = SIDE * SIDE

    def rows_of(rate):
        return pl.multiple_of(jnp.where(low == 0, (SIDE - rate) * SIDE, 0), 16)

    pre[...] = own_ref[...]
    first = 0
    for index, rate in ((2, RATE_C), (1, RATE_B), (0, RATE_A)):
        lead = rate * SIDE
        pre[index, pl.ds(rows_of(rate), lead), :] += row_ref[first : first + lead, :].astype(F32)
        first += lead

    part = blocks(col_ref[:whole, :].astype(F32))
    rank = rank_of(part.shape, theirs)
    pre[2] += flat(jnp.where(rank < RATE_C, part, 0.0))
    pre[0] += flat(turned_by(jnp.where(rank >= RATE_C, part, 0.0), RATE_A, theirs))
    part = blocks(col_ref[whole:, :].astype(F32))
    rank = rank_of(part.shape, theirs)
    pre[1, : RATE_B * SIDE, :] += flat(jnp.where(rank < RATE_B, part, 0.0))
    pre[1, RATE_B * SIDE :, :] += flat(roll_cols(jnp.where(rank >= RATE_B, part, 0.0), RATE_B))

    part = blocks(diag_ref[: RATE_C * SIDE, :].astype(F32))
    rank = rank_of(part.shape, theirs)
    pre[2, pl.ds(rows_of(RATE_C), RATE_C * SIDE), :] += flat(jnp.where(rank < RATE_C, part, 0.0))
    few = part[:RATE_A]
    few = turned_by(jnp.where(rank[:RATE_A] >= RATE_C, few, 0.0), RATE_A, theirs)
    pre[0, pl.ds(rows_of(RATE_A), RATE_A * SIDE), :] += flat(few)
    part = blocks(diag_ref[RATE_C * SIDE :, :].astype(F32))
    rank = rank_of(part.shape, theirs)
    half = RATE_B // 2
    at = rows_of(RATE_B)
    pre[1, pl.ds(at, half * SIDE), :] += flat(jnp.where(rank < RATE_B, part, 0.0))
    last = pl.multiple_of(at + half * SIDE, 16)
    pre[1, pl.ds(last, half * SIDE), :] += flat(roll_cols(jnp.where(rank >= RATE_B, part, 0.0), RATE_B))

    joined_ref[:, :width] = joined0_ref[...]
    for k in range(1, 4):
        value = pre[k - 1]
        sig = sigmoid(value)
        joined_ref[:, k * width : (k + 1) * width] = (value * sig).astype(BF)
    slope = sig * (1.0 + value * (1.0 - sig))
    proj_pre = jnp.dot(joined_ref[...], wp_ref[...], preferred_element_type=F32)
    g_proj = (cot_ref[...].astype(F32) * silu_slope(proj_pre)).astype(BF)
    g_ref[...] = g_proj
    d3_ref[...] = (back_through(g_proj, wp_ref, 3) * slope).astype(BF)


def back_through(g_proj, wp_ref, k):
    width = g_proj.shape[1]
    return lax.dot_general(
        g_proj, wp_ref[k * width : (k + 1) * width, :], (((1,), (1,)), ((), ())), preferred_element_type=F32
    )


def merge(pos, joined0, own, row, col, diag, cot, w_proj):
    pixels, width = joined0.shape
    block = jax.ShapeDtypeStruct((pixels, width), BF)
    return call(
        merge_parts,
        [jax.ShapeDtypeStruct((pixels, 4 * width), BF), block, block],
        1,
        7,
        2 * pixels * width * width * 6,
        6 * 1024 * 1024,
        18,
        [pltpu.VMEM((3, pixels, width), F32)],
        name="merge",
    )(pos, joined0, own, row, col, diag, cot, w_proj)


def pair_grads(pos_ref, joined_ref, g_ref, x_ref, slope_ref, wp_ref, keep_ref, *send_refs):
    core = pos_ref[4]
    over = (((0,), (0,)), ((), ()))
    grad_proj = lax.dot_general(joined_ref[...], g_ref[...], over, preferred_element_type=F32)
    delta = (back_through(g_ref[...], wp_ref, 0) * slope_ref[...]).astype(BF)
    grad_point = lax.dot_general(x_ref[...], delta, over, preferred_element_type=F32)
    keep_ref[...] = jnp.where(core == 0, grad_proj, grad_point)
    half = send_refs[0].shape[0]
    for k, send_ref in enumerate(send_refs):
        part = slice(k * half, (k + 1) * half)
        send_ref[...] = jnp.where(core == 0, grad_point[part], grad_proj[part]).astype(BF)


def shards(features, cotangent, w_point, w_rate_a, w_rate_b, w_rate_c, w_proj, bucket_slot):
    image = features[0]
    rows_dev, cols_dev, chans = image.shape
    pixels = rows_dev * cols_dev
    width = w_point.shape[1]
    row, col, core = (lax.axis_index(n) for n in ("row", "col", "dp_2"))
    at_y, at_z = lax.axis_index("dp_0"), lax.axis_index("dp_1")
    pos = jnp.stack([2 * row + col, at_y, row, col, core, at_z]).astype(jnp.int32)
    replicas = lax.axis_size(DP)
    slot_count = replicas * (bucket_slot.shape[0] // replicas + 1)
    place = place_slots(bucket_slot, core, slot_count)
    centre = image.reshape(pixels, chans)
    weights = [pltpu.with_memory_space_constraint(w, pltpu.HBM) for w in (w_rate_a, w_rate_b, w_rate_c)]
    picked = pick(pos, centre)
    centre, *picked = lax.optimization_barrier((centre, *picked))
    got = [picked[0]] + [flip(picked[k], k) for k in (1, 2, 3)]
    part, *parts = outer(pos, centre, *weights)
    part, got = lax.optimization_barrier((part, got))
    to_row, to_col, to_diag = parts
    parts = [flip(to_row, 2), flip(to_col, 1), flip(to_diag, 3)]
    turned = turn(pos, got)
    joined0, slope0, own = inner(pos, centre, part, w_point, *weights)
    parts, joined0, own, turned = lax.optimization_barrier((parts, joined0, own, turned))
    joined, g_proj, delta3 = merge(
        pos, joined0, own, *parts, cotangent[0].reshape(pixels, width), w_proj
    )
    shared = [delta3] + [flip(delta3, k) for k in (1, 2, 3)]
    block = (4 * width, width)
    kept, *sent = call(
        pair_grads,
        [jax.ShapeDtypeStruct(block, F32)] + [jax.ShapeDtypeStruct((2 * width, width), BF)] * 2,
        1,
        5,
        4 * pixels * chans * width,
        4 * 1024 * 1024,
        16,
        name="pair",
    )(pos, joined, g_proj, centre, slope0, w_proj)
    got = [swap_core(part) for part in sent]
    by_owner = split_pair(pos, kept, got)
    by_owner, shared = lax.optimization_barrier((by_owner, shared))
    by_owner = [by_owner[0]] + [flip(by_owner[k], k) for k in (1, 2, 3)]
    kept, sent = tap_slots(pos, place, shared, turned, slot_count)
    sent, by_owner = lax.optimization_barrier((sent, by_owner))
    mine, other = sum_pair(by_owner)
    return reduce_slots(pos, place, kept, sent, mine, other)


def solution(mesh):
    torus = Mesh(
        mesh.devices.reshape(mesh.shape["row"], mesh.shape["col"], 4, 4, 2),
        ("row", "col", "dp_0", "dp_1", "dp_2"),
    )
    in_specs = (P(DP, "row", "col", None), P(DP, "row", "col", None), P(), P(), P(), P(), P(), P())
    out_specs = P(DP, ("row", "col"))
    return jax.shard_map(
        shards, mesh=torus, in_specs=in_specs, out_specs=out_specs, check_vma=False
    )
```

```python
import jax
import jax.numpy as jnp
from jax import lax
from jax.experimental import pallas as pl
from jax.experimental.pallas import tpu as pltpu
from jax.sharding import Mesh
from jax.sharding import PartitionSpec as P

RATE_A = 6
RATE_B = 12
RATE_C = 18
DP = ("dp_0", "dp_1", "dp_2")


BF = jnp.bfloat16
F32 = jnp.float32
MIB = 1024 * 1024
EDGE = 8


def flip(x, mask):
    if mask == 1:
        return lax.ppermute(x, "col", [(0, 1), (1, 0)])
    if mask == 2:
        return lax.ppermute(x, "row", [(0, 1), (1, 0)])
    return lax.ppermute(x, ("row", "col"), [(0, 3), (3, 0), (1, 2), (2, 1)])


def smem():
    return pl.BlockSpec(memory_space=pltpu.SMEM)


def vmem():
    return pl.BlockSpec(memory_space=pltpu.VMEM)


def call(body, outs, n_smem, n_vmem, flops, nbytes, limit, scratch=(), name=None, n_any=0):
    return pl.pallas_call(
        body,
        out_shape=outs,
        in_specs=[smem()] * n_smem + [vmem()] * n_vmem + [pl.BlockSpec(memory_space=pltpu.HBM)] * n_any,
        out_specs=jax.tree.map(lambda _: vmem(), outs),
        scratch_shapes=list(scratch),
        compiler_params=pltpu.CompilerParams(vmem_limit_bytes=limit * MIB),
        cost_estimate=pl.CostEstimate(flops=flops, bytes_accessed=nbytes, transcendentals=0),
        name=name,
    )


LANES = 128


def pick_matrix(me, first, count):
    shape = (4 * LANES, count * LANES)
    source = lax.broadcasted_iota(jnp.int32, shape, 0)
    col = lax.broadcasted_iota(jnp.int32, (1, shape[1]), 1)
    owner = jnp.bitwise_xor(me, col // LANES + first)
    wanted = 64 * ((col % LANES) // 16) + 16 * owner + col % 16
    return jnp.where(source == wanted, 1.0, 0.0).astype(BF)


def select_channels(pos_ref, x_ref, *rest):
    held, *o_refs, sems = rest
    group = 4 * LANES
    pieces = sems.shape[0]
    each = x_ref.shape[0] // pieces
    copies = []
    for n in range(pieces):
        part = pl.ds(n * each, each)
        copies.append(pltpu.make_async_copy(x_ref.at[part, :], held.at[part, :], sems.at[n]))
        copies[n].start()
    picks = pick_matrix(pos_ref[0], 1, len(o_refs))
    for n in range(pieces):
        copies[n].wait()
        rows = slice(n * each, (n + 1) * each)
        for p in range(x_ref.shape[1] // group):
            taken = jnp.dot(held[rows, p * group : (p + 1) * group], picks, preferred_element_type=F32).astype(BF)
            for k, o_ref in enumerate(o_refs):
                o_ref[rows, p * LANES : (p + 1) * LANES] = taken[:, k * LANES : (k + 1) * LANES]


def turn_pixels(pos_ref, x_ref, x1, x2, x3, o_ref, edge_ref, held):
    pixels, width = x1.shape
    mine = pl.multiple_of((pos_ref[0] // 2) * pixels, 16)
    group = 4 * LANES
    picks = pick_matrix(pos_ref[0], 0, 1)
    for p in range(width // LANES):
        taken = jnp.dot(x_ref[:, p * group : (p + 1) * group], picks, preferred_element_type=F32).astype(BF)
        held[pos_ref[0] % 2, pl.ds(mine, pixels), p * LANES : (p + 1) * LANES] = taken
    for k, x in ((1, x1), (2, x2), (3, x3)):
        s = jnp.bitwise_xor(pos_ref[0], k)
        held[s % 2, pl.ds(pl.multiple_of((s // 2) * pixels, 16), pixels), :] = x[...]
    eye = (
        lax.broadcasted_iota(jnp.int32, (width, width), 0)
        == lax.broadcasted_iota(jnp.int32, (width, width), 1)
    ).astype(F32).astype(BF)
    for g in range(2):
        o_ref[g] = lax.dot_general(
            eye, held[g], (((1,), (1,)), ((), ())), preferred_element_type=F32
        ).astype(BF)
        wide = held[g].astype(F32).reshape(-1, SIDE, width)
        near = wide[:, SIDE - EDGE :] if g == 0 else wide[:, :EDGE]
        edge_ref[g] = lax.dot_general(
            eye, near.reshape(-1, width).astype(BF), (((1,), (1,)), ((), ())), preferred_element_type=F32
        ).astype(BF)


def roll_cols(x, shift):
    return jnp.concatenate([x[:, x.shape[1] - shift :], x[:, : x.shape[1] - shift]], axis=1)


def tap_grads(pos_ref, place_ref, d0, d1, d2, d3, xt_ref, xe_ref, keep_ref, send_ref, held, padded, edge, buf):
    side = RATE_C
    pixels, width = d0.shape
    cols = 24
    rows = pixels // cols
    for k, d in enumerate((d0, d1, d2, d3)):
        s = jnp.bitwise_xor(pos_ref[0], k)
        held[s % 2, pl.ds((s // 2) * pixels, pixels), :] = d[...]
    buf[...] = jnp.zeros_like(buf)
    tall = 2 * pixels
    lead = side * cols
    zeros = jnp.zeros((2, lead, width), BF)
    halves = [held[g].astype(F32).reshape(2 * rows, cols, width) for g in range(2)]
    at = lax.broadcasted_iota(jnp.int32, (2 * rows, cols, width), 1)
    rest = cols - side
    for across in (0, 1, -1):
        turn = across + 1
        padded[turn, :, pl.ds(0, lead), :] = zeros
        padded[turn, :, pl.ds(lead + tall, lead), :] = zeros
        if across == 0:
            shifted = halves
        elif across == 1:
            rolled = [roll_cols(h, side) for h in halves]
            shifted = [
                jnp.where(at >= side, rolled[0], 0.0),
                jnp.where(at < side, rolled[0], rolled[1]),
            ]
        else:
            rolled = [roll_cols(h, rest) for h in halves]
            shifted = [
                jnp.where(at < rest, rolled[0], rolled[1]),
                jnp.where(at < rest, rolled[1], 0.0),
            ]
        thin = {1: 0, -1: 1}.get(across)
        for g in range(2):
            if g == thin:
                near = shifted[g][:, SIDE - EDGE :] if g == 0 else shifted[g][:, :EDGE]
                short = side * EDGE
                edge[g, pl.ds(0, short), :] = jnp.zeros((short, width), BF)
                edge[g, pl.ds(short, 2 * rows * EDGE), :] = near.reshape(2 * rows * EDGE, width).astype(BF)
                edge[g, pl.ds(short + 2 * rows * EDGE, short), :] = jnp.zeros((short, width), BF)
            else:
                padded[turn, g, pl.ds(lead, tall), :] = shifted[g].reshape(tall, width).astype(BF)
        for above in (-1, 0, 1):
            first, last = {-1: (0, 32), 0: (0, 48), 1: (16, 48)}[above]
            base = first - side * above + side
            total = None
            for g in range(2):
                left, right, each = (xe_ref, edge.at[g], EDGE) if g == thin else (xt_ref, padded.at[turn, g], cols)
                part = jnp.dot(
                    left[g, :, first * each : last * each],
                    right[base * each : (base + last - first) * each, :],
                    preferred_element_type=F32,
                )
                total = part if total is None else total + part
            tap = 3 * (above + 1) + across + 1
            groups = total.reshape(width // 16, 16, width)
            for m in range(width // 16):
                buf[place_ref[32 + 16 * tap + m]] = groups[m]
    half = buf.shape[0] // 2
    keep_ref[...] = buf[:half]
    send_ref[...] = buf[half:].astype(BF)


def join_owners(pos_ref, place_ref, keep_ref, got_ref, mine_ref, other_ref, o_ref):
    o_ref[...] = (keep_ref[...] + got_ref[...].astype(F32)).astype(BF).reshape(o_ref.shape)
    each = o_ref.shape[1] // 16
    core = pos_ref[4]
    for n in range(mine_ref.shape[0]):
        for ref, first in ((mine_ref, 16 * core), (other_ref, 16 * (1 - core))):
            at = place_ref[first + n]

            @pl.when(at < o_ref.shape[0] * each)
            def _(ref=ref, at=at, n=n):
                rows = pl.ds(pl.multiple_of((at % each) * 16, 16), 16)
                o_ref[at // each, rows, :] = ref[n].astype(BF)


def fold_last(r_ref, o_ref, total):
    value = r_ref[0].astype(F32)
    for n in range(1, r_ref.shape[0]):
        value = value + r_ref[n].astype(F32)
    total[...] = value.reshape(total.shape)
    width = total.shape[2]
    for i in range(total.shape[1]):
        o_ref[:, i * width : (i + 1) * width] = total[:, i, :]


def share_rows(pos_ref, kept_ref, got0, got1, *rest):
    *outs, total = rest
    half, each = got0.shape[0], total.shape[0] // 2
    for n, got in enumerate((got0, got1)):
        value = kept_ref[n * half : (n + 1) * half, :] + got[...].astype(F32)
        total[n * each : (n + 1) * each] = value.reshape(each, *total.shape[1:])
    for k, out in enumerate(outs):
        out[...] = total[:, jnp.bitwise_xor(pos_ref[0], k)].astype(out.dtype)


def swap_core(x):
    return lax.ppermute(x, "dp_2", [(0, 1), (1, 0)])


def pick(pos, centre):
    pixels, chans = centre.shape
    block = jax.ShapeDtypeStruct((pixels, chans // 4), BF)
    return call(
        select_channels,
        [jax.ShapeDtypeStruct((pixels, chans), BF)] + [block] * 3,
        1,
        0,
        pixels * chans * chans,
        4 * pixels * chans,
        12,
        [pltpu.SemaphoreType.DMA((3,))],
        name="pick",
        n_any=1,
    )(pos, pltpu.with_memory_space_constraint(centre, pltpu.HBM))


def turn(pos, centre, got):
    pixels, width = got[0].shape
    return call(
        turn_pixels,
        [
            jax.ShapeDtypeStruct((2, width, 2 * pixels), BF),
            jax.ShapeDtypeStruct((2, width, 2 * pixels // SIDE * EDGE), BF),
        ],
        1,
        4,
        8 * pixels * width * width,
        16 * pixels * width,
        12,
        [pltpu.VMEM((2, 2 * pixels, width), BF)],
        name="turn",
    )(pos, centre, *got)


def split_pair(pos, kept, got):
    width = kept.shape[1]
    slices = kept.shape[0] // 64
    shape = (slices, 16, width)
    return call(
        share_rows,
        [jax.ShapeDtypeStruct(shape, F32)] + [jax.ShapeDtypeStruct(shape, BF)] * 3,
        1,
        3,
        0,
        0,
        10,
        [pltpu.VMEM((slices, 4, 16, width), F32)],
        name="rows",
    )(pos, kept, *got)


def sum_pair(blocks):
    mine = blocks[0] + sum(block.astype(F32) for block in blocks[1:])
    return mine, swap_core(mine.astype(BF))


def place_slots(bucket_slot, core, slot_count):
    replicas = lax.axis_size(DP)
    capacity = slot_count // replicas
    owner = bucket_slot // capacity
    other = jnp.bitwise_xor(owner % 2, core)
    return other * (slot_count // 2) + (owner // 2) * capacity + bucket_slot % capacity


def tap_slots(pos, place, deltas, turned, slot_count):
    pixels, width = deltas[0].shape
    half = slot_count // 2
    return call(
        tap_grads,
        [jax.ShapeDtypeStruct((half, 16, width), F32), jax.ShapeDtypeStruct((half, 16, width), BF)],
        2,
        6,
        2 * 7 * 4 * pixels * width * width,
        8 * 1024 * 1024,
        26,
        [
            pltpu.VMEM((2, 2 * pixels, width), BF),
            pltpu.VMEM((3, 2, 2 * pixels + 2 * RATE_C * SIDE, width), BF),
            pltpu.VMEM((2, (2 * SIDE + 2 * RATE_C) * EDGE, width), BF),
            pltpu.VMEM((slot_count, 16, width), F32),
        ],
        name="taps",
    )(pos, place, *deltas, *turned)


def reduce_slots(pos, place, kept, sent, mine, other):
    half, rows, width = kept.shape
    chips = lax.axis_size("dp_0") * lax.axis_size("dp_1")
    each = half // chips
    total = call(
        join_owners,
        jax.ShapeDtypeStruct((chips, each * rows, width), BF),
        2,
        4,
        kept.size,
        8 * kept.size,
        8,
        name="owners",
    )(pos, place, kept, swap_core(sent), mine, other)
    total = lax.all_to_all(total, ("dp_0", "dp_1"), 0, 0, tiled=True)
    return call(
        fold_last,
        jax.ShapeDtypeStruct((each, rows * width), F32),
        0,
        1,
        kept.size,
        2 * kept.size,
        8,
        [pltpu.VMEM((each, rows, width), F32)],
        name="last",
    )(total)


def sigmoid(value):
    return 0.5 + 0.5 * jnp.tanh(0.5 * value)


def silu_slope(value):
    sig = sigmoid(value)
    return sig * (1.0 + value * (1.0 - sig))


RATES = (RATE_A, RATE_B, RATE_C)
SIDE = 24


def turned_by(x, shift, far):
    return jnp.where(far == 0, roll_cols(x, shift), roll_cols(x, SIDE - shift))


def rank_of(shape, far):
    at = lax.broadcasted_iota(jnp.int32, shape, 1)
    return jnp.where(far == 0, at, SIDE - 1 - at)


def row_marks(low, rate):
    lead = rate * SIDE
    whole = SIDE * SIDE

    def either(upper, lower):
        return pl.multiple_of(jnp.where(low == 0, upper, lower), 16)

    return dict(
        own=either(0, lead),
        out=either(lead, 0),
        theirs=either(whole, 0),
        inward_from=either(lead, 0),
        inward=either(0, 2 * lead),
        kept=either(lead, 0),
        inner=either(0, lead),
    )


def blocks(x):
    return x.reshape(x.shape[0] // SIDE, SIDE, x.shape[1])


def flat(x):
    return x.reshape(x.shape[0] * SIDE, x.shape[2])


def tap_copies(pos_ref, refs, jobs, held, sems):
    copies = []
    for branch, ref in enumerate(refs):
        for n, (above, across) in enumerate(jobs):
            a = 1 if above == 1 else jnp.where(pos_ref[2] == 0, above, 2 - above)
            b = 1 if across == 1 else jnp.where(pos_ref[3] == 0, across, 2 - across)
            width = ref.shape[3]
            to = held.at[branch, :, n * width : (n + 1) * width]
            copies.append(pltpu.make_async_copy(ref.at[a, b], to, sems.at[branch, n]))
    return copies


BRANCHES = ((2, RATE_C), (1, RATE_B), (0, RATE_A))
OUTER = ((0, 0), (1, 0), (0, 1), (0, 2), (2, 0))
INNER = ((1, 1), (1, 2), (2, 1), (2, 2))


def outer_parts(pos_ref, x_ref, wc_ref, wb_ref, wa_ref, pre_ref, row_ref, col_ref, diag_ref, ext, acc, y, held, sems):
    low, far = pos_ref[2], pos_ref[3]
    whole = SIDE * SIDE
    width = pre_ref.shape[2]
    copies = tap_copies(pos_ref, (wc_ref, wb_ref, wa_ref), OUTER, held, sems)
    for copy in copies:
        copy.start()
    first = 0
    for turn, (index, rate) in enumerate(BRANCHES):
        lead = rate * SIDE
        inside = whole - lead
        at = row_marks(low, rate)
        own_rows = pl.ds(at["own"], whole)
        their_rows = pl.ds(at["theirs"], lead)
        kept_rows = pl.ds(at["kept"], inside)
        to_row = slice(first, first + lead)
        first += lead
        count = len(OUTER)
        for copy in copies[turn * count : (turn + 1) * count]:
            copy.wait()
        y[...] = jnp.dot(x_ref[...], held[turn, :, : 4 * width], preferred_element_type=F32)
        ext[pl.ds(pl.multiple_of(whole - at["theirs"], 16), lead), :] = jnp.zeros((lead, width), F32)
        ext[pl.ds(at["out"], whole), :] = y[:, :width]
        ext[own_rows, :] += y[:, width : 2 * width]
        ext[pl.ds(at["inward"], inside), :] += jnp.dot(
            x_ref[pl.ds(at["inward_from"], inside), :], held[turn, :, 4 * width :], preferred_element_type=F32
        )
        own = blocks(ext[own_rows, :])
        ours = turned_by(own, rate, far)
        rank = rank_of(own.shape, far)
        pre_ref[index] = flat(jnp.where(rank >= rate, ours, 0.0))
        below = blocks(ext[their_rows, :])
        theirs = turned_by(below, rate, far)
        place = rank_of(below.shape, far)
        acc[:lead, :] = flat(jnp.where(place >= rate, theirs, 0.0))
        if rate == RATE_C:
            col_ref[:whole, :] = flat(jnp.where(rank < rate, ours, 0.0)).astype(BF)
            diag_ref[:lead, :] = flat(jnp.where(place < rate, theirs, 0.0)).astype(BF)
        elif rate == RATE_B:
            half = rate // 2
            col_ref[whole:, :] = flat(jnp.where(rank[:rate] < rate, ours[:rate], own[rate:])).astype(BF)
            part = place[:half] < rate
            diag_ref[RATE_C * SIDE :, :] = flat(jnp.where(part, theirs[:half], below[half:])).astype(BF)
        else:
            have = blocks(col_ref[:whole, :].astype(F32))
            col_ref[:whole, :] = flat(jnp.where(rank >= RATE_C, own, have)).astype(BF)
            have = blocks(diag_ref[:lead, :].astype(F32))
            diag_ref[:lead, :] = flat(jnp.where(place >= RATE_C, below, have)).astype(BF)
        next_from = pl.multiple_of(jnp.where(low == 0, inside, 0), 16)
        keep_from = pl.multiple_of(jnp.where(low == 0, 0, lead), 16)
        pre_ref[index, kept_rows, :] += y[pl.ds(keep_from, inside), 2 * width : 3 * width]
        own = blocks(y[pl.ds(keep_from, inside), 3 * width :])
        rank = rank_of(own.shape, far)
        pre_ref[index, kept_rows, :] += flat(jnp.where(rank < SIDE - rate, turned_by(own, rate, 1 - far), 0.0))
        below = blocks(y[pl.ds(next_from, lead), 3 * width :])
        theirs = flat(jnp.where(place < SIDE - rate, turned_by(below, rate, 1 - far), 0.0))
        row_ref[to_row, :] = (acc[:lead, :] + y[pl.ds(next_from, lead), 2 * width : 3 * width] + theirs).astype(BF)


def inner_parts(pos_ref, x_ref, part_ref, wp_ref, wc_ref, wb_ref, wa_ref, joined_ref, slope_ref, pre_ref, y, z, held, sems):
    low, far = pos_ref[2], pos_ref[3]
    whole = SIDE * SIDE
    width = joined_ref.shape[1]
    copies = tap_copies(pos_ref, (wc_ref, wb_ref, wa_ref), INNER, held, sems)
    for copy in copies:
        copy.start()
    value = jnp.dot(x_ref[...], wp_ref[...], preferred_element_type=F32)
    sig = sigmoid(value)
    joined_ref[...] = (value * sig).astype(BF)
    slope_ref[...] = sig * (1.0 + value * (1.0 - sig))
    for turn, (index, rate) in enumerate(BRANCHES):
        lead = rate * SIDE
        inside = whole - lead
        at = row_marks(low, rate)
        from_rows = pl.ds(at["inward_from"], inside)
        to_rows = pl.ds(at["inner"], inside)
        count = len(INNER)
        for copy in copies[turn * count : (turn + 1) * count]:
            copy.wait()
        y[...] = jnp.dot(x_ref[...], held[turn, :, : 2 * width], preferred_element_type=F32)
        z[:inside, :] = jnp.dot(x_ref[from_rows, :], held[turn, :, 2 * width :], preferred_element_type=F32)
        y[to_rows, :] += z[:inside, :]
        own = blocks(y[:, width:])
        rank = rank_of(own.shape, far)
        moved = flat(jnp.where(rank < SIDE - rate, turned_by(own, rate, 1 - far), 0.0))
        pre_ref[index] = part_ref[index] + y[:, :width] + moved


def outer(pos, centre, w_rate_a, w_rate_b, w_rate_c):
    pixels, chans = centre.shape
    width = w_rate_a.shape[3]
    sends = (RATE_A + RATE_B + RATE_C) * SIDE
    shapes = [((3, pixels, width), F32), ((sends, width), BF), ((sends, width), BF), ((pixels, width), BF)]
    return call(
        outer_parts,
        [jax.ShapeDtypeStruct(*s) for s in shapes],
        1,
        1,
        2 * pixels * chans * width * 14,
        10 * MIB,
        28,
        [
            pltpu.VMEM(((SIDE + RATE_C) * SIDE, width), F32),
            pltpu.VMEM((RATE_C * SIDE, width), F32),
            pltpu.VMEM((pixels, 4 * width), F32),
            pltpu.VMEM((3, chans, len(OUTER) * width), BF),
            pltpu.SemaphoreType.DMA((3, len(OUTER))),
        ],
        name="outer",
        n_any=3,
    )(pos, centre, w_rate_c, w_rate_b, w_rate_a)


def inner(pos, centre, part, w_point, w_rate_a, w_rate_b, w_rate_c):
    pixels, chans = centre.shape
    width = w_point.shape[1]
    return call(
        inner_parts,
        [
            jax.ShapeDtypeStruct((pixels, width), BF),
            jax.ShapeDtypeStruct((pixels, width), F32),
            jax.ShapeDtypeStruct((3, pixels, width), F32),
        ],
        1,
        3,
        2 * pixels * chans * width * 10,
        10 * MIB,
        26,
        [
            pltpu.VMEM((pixels, 2 * width), F32),
            pltpu.VMEM((pixels, 2 * width), F32),
            pltpu.VMEM((3, chans, len(INNER) * width), BF),
            pltpu.SemaphoreType.DMA((3, len(INNER))),
        ],
        name="inner",
        n_any=3,
    )(pos, centre, part, w_point, w_rate_c, w_rate_b, w_rate_a)


def merge_parts(
    pos_ref, joined0_ref, own_ref, row_ref, col_ref, diag_ref, cot_ref, wp_ref, joined_ref, g_ref, d3_ref, pre
):
    low = pos_ref[2]
    theirs = 1 - pos_ref[3]
    width = joined0_ref.shape[1]
    whole = SIDE * SIDE

    def rows_of(rate):
        return pl.multiple_of(jnp.where(low == 0, (SIDE - rate) * SIDE, 0), 16)

    part = blocks(col_ref[:whole, :].astype(F32))
    rank = rank_of(part.shape, theirs)
    pre[2] = own_ref[2] + flat(jnp.where(rank < RATE_C, part, 0.0))
    pre[0] = own_ref[0] + flat(turned_by(jnp.where(rank >= RATE_C, part, 0.0), RATE_A, theirs))
    part = blocks(col_ref[whole:, :].astype(F32))
    rank = rank_of(part.shape, theirs)
    half = RATE_B * SIDE
    pre[1, :half, :] = own_ref[1, :half, :] + flat(jnp.where(rank < RATE_B, part, 0.0))
    pre[1, half:, :] = own_ref[1, half:, :] + flat(roll_cols(jnp.where(rank >= RATE_B, part, 0.0), RATE_B))
    first = 0
    for index, rate in ((2, RATE_C), (1, RATE_B), (0, RATE_A)):
        lead = rate * SIDE
        pre[index, pl.ds(rows_of(rate), lead), :] += row_ref[first : first + lead, :].astype(F32)
        first += lead

    part = blocks(diag_ref[: RATE_C * SIDE, :].astype(F32))
    rank = rank_of(part.shape, theirs)
    pre[2, pl.ds(rows_of(RATE_C), RATE_C * SIDE), :] += flat(jnp.where(rank < RATE_C, part, 0.0))
    few = part[:RATE_A]
    few = turned_by(jnp.where(rank[:RATE_A] >= RATE_C, few, 0.0), RATE_A, theirs)
    pre[0, pl.ds(rows_of(RATE_A), RATE_A * SIDE), :] += flat(few)
    part = blocks(diag_ref[RATE_C * SIDE :, :].astype(F32))
    rank = rank_of(part.shape, theirs)
    half = RATE_B // 2
    at = rows_of(RATE_B)
    pre[1, pl.ds(at, half * SIDE), :] += flat(jnp.where(rank < RATE_B, part, 0.0))
    last = pl.multiple_of(at + half * SIDE, 16)
    pre[1, pl.ds(last, half * SIDE), :] += flat(roll_cols(jnp.where(rank >= RATE_B, part, 0.0), RATE_B))

    joined_ref[:, :width] = joined0_ref[...]
    for k in range(1, 4):
        value = pre[k - 1]
        sig = sigmoid(value)
        joined_ref[:, k * width : (k + 1) * width] = (value * sig).astype(BF)
    slope = sig * (1.0 + value * (1.0 - sig))
    proj_pre = jnp.dot(joined_ref[...], wp_ref[...], preferred_element_type=F32)
    g_proj = (cot_ref[...].astype(F32) * silu_slope(proj_pre)).astype(BF)
    g_ref[...] = g_proj
    d3_ref[...] = (back_through(g_proj, wp_ref, 3) * slope).astype(BF)


def back_through(g_proj, wp_ref, k):
    width = g_proj.shape[1]
    return lax.dot_general(
        g_proj, wp_ref[k * width : (k + 1) * width, :], (((1,), (1,)), ((), ())), preferred_element_type=F32
    )


def merge(pos, joined0, own, row, col, diag, cot, w_proj):
    pixels, width = joined0.shape
    block = jax.ShapeDtypeStruct((pixels, width), BF)
    return call(
        merge_parts,
        [jax.ShapeDtypeStruct((pixels, 4 * width), BF), block, block],
        1,
        7,
        2 * pixels * width * width * 6,
        6 * 1024 * 1024,
        18,
        [pltpu.VMEM((3, pixels, width), F32)],
        name="merge",
    )(pos, joined0, own, row, col, diag, cot, w_proj)


def pair_grads(pos_ref, joined_ref, g_ref, x_ref, slope_ref, wp_ref, keep_ref, *send_refs):
    core = pos_ref[4]
    over = (((0,), (0,)), ((), ()))
    grad_proj = lax.dot_general(joined_ref[...], g_ref[...], over, preferred_element_type=F32)
    delta = (back_through(g_ref[...], wp_ref, 0) * slope_ref[...]).astype(BF)
    grad_point = lax.dot_general(x_ref[...], delta, over, preferred_element_type=F32)
    keep_ref[...] = jnp.where(core == 0, grad_proj, grad_point)
    half = send_refs[0].shape[0]
    for k, send_ref in enumerate(send_refs):
        part = slice(k * half, (k + 1) * half)
        send_ref[...] = jnp.where(core == 0, grad_point[part], grad_proj[part]).astype(BF)


def shards(features, cotangent, w_point, w_rate_a, w_rate_b, w_rate_c, w_proj, bucket_slot):
    image = features[0]
    rows_dev, cols_dev, chans = image.shape
    pixels = rows_dev * cols_dev
    width = w_point.shape[1]
    row, col, core = (lax.axis_index(n) for n in ("row", "col", "dp_2"))
    at_y, at_z = lax.axis_index("dp_0"), lax.axis_index("dp_1")
    pos = jnp.stack([2 * row + col, at_y, row, col, core, at_z]).astype(jnp.int32)
    replicas = lax.axis_size(DP)
    slot_count = replicas * (bucket_slot.shape[0] // replicas + 1)
    place = place_slots(bucket_slot, core, slot_count)
    centre = image.reshape(pixels, chans)
    weights = [pltpu.with_memory_space_constraint(w, pltpu.HBM) for w in (w_rate_a, w_rate_b, w_rate_c)]
    centre, *picked = pick(pos, centre)
    got = [flip(picked[k - 1], k) for k in (1, 2, 3)]
    part, *parts = outer(pos, centre, *weights)
    part, got = lax.optimization_barrier((part, got))
    to_row, to_col, to_diag = parts
    parts = [flip(to_row, 2), flip(to_col, 1), flip(to_diag, 3)]
    turned = turn(pos, centre, got)
    joined0, slope0, own = inner(pos, centre, part, w_point, *weights)
    parts, joined0, own, turned = lax.optimization_barrier((parts, joined0, own, turned))
    joined, g_proj, delta3 = merge(
        pos, joined0, own, *parts, cotangent[0].reshape(pixels, width), w_proj
    )
    shared = [delta3] + [flip(delta3, k) for k in (1, 2, 3)]
    block = (4 * width, width)
    kept, *sent = call(
        pair_grads,
        [jax.ShapeDtypeStruct(block, F32)] + [jax.ShapeDtypeStruct((2 * width, width), BF)] * 2,
        1,
        5,
        4 * pixels * chans * width,
        4 * 1024 * 1024,
        16,
        name="pair",
    )(pos, joined, g_proj, centre, slope0, w_proj)
    got = [swap_core(part) for part in sent]
    by_owner = split_pair(pos, kept, got)
    by_owner, shared = lax.optimization_barrier((by_owner, shared))
    by_owner = [by_owner[0]] + [flip(by_owner[k], k) for k in (1, 2, 3)]
    kept, sent = tap_slots(pos, place, shared, turned, slot_count)
    sent, by_owner = lax.optimization_barrier((sent, by_owner))
    mine, other = sum_pair(by_owner)
    return reduce_slots(pos, place, kept, sent, mine, other)


def solution(mesh):
    torus = Mesh(
        mesh.devices.reshape(mesh.shape["row"], mesh.shape["col"], 4, 4, 2),
        ("row", "col", "dp_0", "dp_1", "dp_2"),
    )
    in_specs = (P(DP, "row", "col", None), P(DP, "row", "col", None), P(), P(), P(), P(), P(), P())
    out_specs = P(DP, ("row", "col"))
    return jax.shard_map(
        shards, mesh=torus, in_specs=in_specs, out_specs=out_specs, check_vma=False
    )
```
